128 devices in a mesh: seq: 16 (over z, x), req: 8 (over y, core).
Axes of the slice: x: 4, y: 4, z: 4, core: 2. Of those that a mesh axis runs over, the one named last changes fastest.
Arguments:
- given_token_index: int32 [128], replicated, may hold values from 0 to 31999
- hidden: bfloat16 [128, 3584], P('req'), may hold values from -6 to 6
- token_embedding_table: bfloat16 [32000, 3584], P(('seq', 'req')), may hold values from -6 to 6
- attention_norm_gain: bfloat16 [7168], replicated, may hold values from 0.099609375 to 1.8984375
- query_key_value_weight: bfloat16 [7168, 10752], P('req', 'seq'), may hold values from -0.0625 to 0.0625
- rotated_key_cache: bfloat16 [96, 8, 128, 3584], P('seq', 'req'), may hold values from -240 to 240
- cached_value_pages: bfloat16 [96, 8, 128, 3584], P('seq', 'req'), may hold values from -6 to 6
- lengths: int32 [32], P('req'), may hold values from 1 to 6144, as said below
- request_page_slots: int32 [32, 48], P('req'), may hold values from 0 to 95, as said below
- attention_output_weight: bfloat16 [3584, 7168], P('seq'), may hold values from -0.375 to 0.375
- feedforward_norm_gain: bfloat16 [7168], replicated, may hold values from 0.099609375 to 1.8984375
- gate_weight: bfloat16 [7168, 14336], P('req', 'seq'), may hold values from -0.0625 to 0.0625
- up_weight: bfloat16 [7168, 14336], P('req', 'seq'), may hold values from -0.0625 to 0.0625
- adapter_down_map: bfloat16 [7168, 128], P('req'), may hold values from -0.0625 to 0.0625
- adapter_gate_map: bfloat16 [128, 14336], P(None, 'seq'), may hold values from -0.5 to 0.5
- adapter_up_map: bfloat16 [128, 14336], P(None, 'seq'), may hold values from -0.5 to 0.5
- down_weight: bfloat16 [14336, 7168], P('seq', 'req'), may hold values from -0.046875 to 0.046875
Outputs:
- block_out: bfloat16 [128, 7168], P('seq', 'req')
The draws below stay inside these ranges and needn't reach their ends.
Inputs may be any that keep to these rules, and one draw needn't show every extreme that they name: `lengths`: in each group of 4 requests exactly one has 6144 tokens, and the pages of a group's requests number at most 96 together. `request_page_slots`: entry p of request i names a slot of its group, 0 to 95; the entries with p * 128 below lengths[i] are distinct within a group, the others name any slot. Slot g of a group lies on the seq index g // 6, at place g % 6.
All inputs are finite; a program needn't handle non-finite values.
Results may differ from the reference program's by a relative error of at most 0.028.
The reference program's roundings to bfloat16 on the way count: a program that leaves them out, or rounds other values in their place, can miss the bound.
Values may be sent and summed in bfloat16 or wider, within the bound.
A program may use at most 128 MiB of HBM per device.

```python
import math
import jax
import jax.numpy as jnp
import numpy as np
from jax import lax

HALF = 3584
MODEL_WIDTH = 7168
HEADS = 16
HD = 224
HHD = 3584
FEEDFORWARD_UNITS = 14336
ADAPTER_RANK = 128
VOCAB = 32000
PAGE = 128
STEPS = 4
REQ_DEV = 4
PAGES_DEV = 6
REQS = 32
ROWS = 128
GSLOTS = 96
MAXPG = 48
N_SEQ = 16
N_REQ = 8


def plan_pages(key):
    base_key = jax.random.fold_in(key, 7)
    draw_keys = jax.random.split(base_key, 6)
    group_total = REQS // REQ_DEV
    half_pages = GSLOTS // 2
    long_place = jax.random.randint(draw_keys[0], (group_total,), 0, REQ_DEV)
    is_long = jnp.arange(REQ_DEV, dtype=jnp.int32)[None, :] == long_place[:, None]
    weight_base = 2 ** jax.random.randint(draw_keys[1], (group_total, REQ_DEV), 0, 7)
    weight_all = weight_base * jax.random.randint(draw_keys[2], (group_total, REQ_DEV), 1, 4)
    weight_all = jnp.where(is_long, 0, weight_all)
    share_pages = half_pages - (REQ_DEV - 1)
    weight_sum = jnp.maximum(jnp.sum(weight_all, axis=1, keepdims=True), 1)
    page_counts = jnp.maximum(1, weight_all * share_pages // weight_sum)
    page_counts = jnp.where(is_long, half_pages, page_counts)
    tail_tokens = jax.random.randint(draw_keys[3], (group_total, REQ_DEV), 1, PAGE + 1)
    length_all = jnp.where(is_long, half_pages * PAGE, (page_counts - 1) * PAGE + tail_tokens)
    offsets = jnp.cumsum(page_counts, axis=1) - page_counts
    orders = jax.vmap(lambda sub_key: jax.random.permutation(sub_key, GSLOTS))(jax.random.split(draw_keys[4], group_total))
    logical = offsets[:, :, None] + jnp.arange(MAXPG, dtype=jnp.int32)[None, None, :]
    is_live = jnp.arange(MAXPG, dtype=jnp.int32)[None, None, :] < page_counts[:, :, None]
    spread_orders = jnp.broadcast_to(orders[:, None, :], (group_total, REQ_DEV, GSLOTS))
    chosen = jnp.take_along_axis(spread_orders, jnp.minimum(logical, GSLOTS - 1), axis=2)
    filler = jax.random.randint(draw_keys[5], (group_total, REQ_DEV, MAXPG), 0, GSLOTS)
    table_all = jnp.where(is_live, chosen, filler)
    return (length_all.reshape(REQS).astype(jnp.int32), table_all.reshape(REQS, MAXPG).astype(jnp.int32))


def draw_lengths(key, part):
    return plan_pages(key)[0]


def draw_request_page_slots(key, part):
    return plan_pages(key)[1]


def draw_rotated_key_cache(key, part):
    shape_all = (GSLOTS, REQS // REQ_DEV, PAGE, HEADS * HD)
    values_all = jnp.clip(jax.random.normal(jax.random.fold_in(key, 11), shape_all, jnp.float32) * 2.0, -8.0, 8.0)
    return values_all.astype(jnp.bfloat16)


def touch_ends(result, rng, low, high):
    index_at = [jax.random.randint(jax.random.fold_in(rng, axis), (), 0, length) for axis, length in enumerate(result.shape)]
    main_axis = result.shape.index(max(result.shape))
    beside = index_at[:main_axis] + [(index_at[main_axis] + 1) % result.shape[main_axis]] + index_at[main_axis + 1:]
    return result.at[tuple(index_at)].set(low).at[tuple(beside)].set(high)


def level_of(stream_key, dims, cuts, low, top_value):
    loudness, own = 1.0, jax.random.fold_in(stream_key, 6)
    for position, shards_of in cuts:
        heights = jnp.exp(jax.random.uniform(jax.random.fold_in(own, position), (shards_of,), jnp.float32, low / len(cuts), top_value / len(cuts)))
        loudness = loudness * jnp.repeat(heights, dims[position] // shards_of).reshape([-1 if axis == position else 1 for axis in range(len(dims))])
    return loudness


def rank_bounds(count, slope):
    portions = [(1 << 20) // math.isqrt(grade ** slope) + 1 for grade in range(1, count + 1)]
    spread = 1 + sum(portions) // (1 << 30)
    return np.cumsum(np.array([max(1, weight // spread) for weight in portions]))


def skewed_ids(rng, extent, number_of, slope):
    listing = rank_bounds(number_of, slope)
    lot = jax.random.randint(jax.random.fold_in(rng, 1), extent, 0, int(listing[number_of - 1]))
    rank = jnp.searchsorted(jnp.asarray(listing, jnp.int32), lot, side="right")
    return jax.random.permutation(jax.random.fold_in(rng, 2), number_of)[rank].astype(jnp.int32)


def noise(key, shape, spread, most, cuts=(), kind=jnp.bfloat16):
    values = spread * jax.random.normal(key, shape, jnp.float32)
    if cuts:
        values = values * level_of(key, shape, cuts, -0.22, 0.18)
    return jnp.clip(values, -most, most).astype(kind)


def setup_inputs(seed: int = 0) -> dict:
    seeds = jax.random.split(jax.random.key(seed), 18)
    given_token_index = touch_ends(skewed_ids(seeds[0], (ROWS,), VOCAB, 2), jax.random.fold_in(seeds[0], 3), 0, VOCAB - 1).astype(jnp.int32)
    hidden = noise(seeds[1], (ROWS, HALF), 1.0, 6.0, ((0, 8),))
    token_embedding_table = noise(seeds[2], (VOCAB, HALF), 1.0, 6.0, ((0, 128),))
    attention_norm_gain = jnp.clip(1.0 + 0.18 * jax.random.normal(seeds[3], (MODEL_WIDTH,), jnp.float32), 0.099609375, 1.8984375).astype(jnp.bfloat16)
    query_key_value_weight = noise(seeds[4], (MODEL_WIDTH, 3 * HHD), MODEL_WIDTH ** -0.5, 0.0625, ((0, 8), (1, 16)))
    rotated_key_cache = draw_rotated_key_cache(jax.random.fold_in(seeds[17], 71), 0)
    cached_value_pages = noise(seeds[6], (GSLOTS, N_REQ, PAGE, HHD), 1.0, 6.0, ((0, 16), (1, 8)))
    lengths = draw_lengths(jax.random.fold_in(seeds[17], 71), 0)
    request_page_slots = draw_request_page_slots(jax.random.fold_in(seeds[17], 71), 0)
    attention_output_weight = noise(seeds[9], (HHD, MODEL_WIDTH), (HHD // 16) ** -0.5, 0.375, ((0, 16),))
    feedforward_norm_gain = jnp.clip(1.0 + 0.18 * jax.random.normal(seeds[10], (MODEL_WIDTH,), jnp.float32), 0.099609375, 1.8984375).astype(jnp.bfloat16)
    gate_weight = noise(seeds[11], (MODEL_WIDTH, FEEDFORWARD_UNITS), MODEL_WIDTH ** -0.5, 0.0625, ((0, 8), (1, 16)))
    up_weight = noise(seeds[12], (MODEL_WIDTH, FEEDFORWARD_UNITS), MODEL_WIDTH ** -0.5, 0.0625, ((0, 8), (1, 16)))
    adapter_down_map = noise(seeds[13], (MODEL_WIDTH, ADAPTER_RANK), MODEL_WIDTH ** -0.5, 0.0625, ((0, 8),))
    adapter_gate_map = noise(seeds[14], (ADAPTER_RANK, FEEDFORWARD_UNITS), ADAPTER_RANK ** -0.5, 0.5, ((1, 16),))
    adapter_up_map = noise(seeds[15], (ADAPTER_RANK, FEEDFORWARD_UNITS), ADAPTER_RANK ** -0.5, 0.5, ((1, 16),))
    down_weight = noise(seeds[16], (FEEDFORWARD_UNITS, MODEL_WIDTH), FEEDFORWARD_UNITS ** -0.5, 0.046875, ((0, 16), (1, 8)))
    return dict(given_token_index=given_token_index, hidden=hidden, token_embedding_table=token_embedding_table, attention_norm_gain=attention_norm_gain, query_key_value_weight=query_key_value_weight, rotated_key_cache=rotated_key_cache, cached_value_pages=cached_value_pages, lengths=lengths, request_page_slots=request_page_slots, attention_output_weight=attention_output_weight, feedforward_norm_gain=feedforward_norm_gain, gate_weight=gate_weight, up_weight=up_weight, adapter_down_map=adapter_down_map, adapter_gate_map=adapter_gate_map, adapter_up_map=adapter_up_map, down_weight=down_weight)


NEGATIVE = -1e+30
EPSILON = 1e-05
ROTARY_BASE = 10000.0

def rms_norm(matrix, gain_vec):
    widened = matrix.astype(jnp.float32)
    factor = lax.rsqrt(lax.optimization_barrier(jnp.mean(widened * widened, axis=-1, keepdims=True)) + EPSILON)
    return (widened * factor * gain_vec.astype(jnp.float32)).astype(jnp.bfloat16)

def rotate(vectors, positions):
    half_dim = vectors.shape[-1] // 2
    frequency = ROTARY_BASE ** (-2.0 * jnp.arange(half_dim, dtype=jnp.float32) / vectors.shape[-1])
    angles = positions.astype(jnp.float32)[..., None, None] * frequency
    cosine = jnp.cos(angles)
    sine_part = jnp.sin(angles)
    front_half = vectors[..., :half_dim]
    back_half = vectors[..., half_dim:]
    return jnp.concatenate([front_half * cosine - back_half * sine_part, back_half * cosine + front_half * sine_part], axis=-1)

def reference(given_token_index, hidden, token_embedding_table, attention_norm_gain, query_key_value_weight, rotated_key_cache, cached_value_pages, lengths, request_page_slots, attention_output_weight, feedforward_norm_gain, gate_weight, up_weight, adapter_down_map, adapter_gate_map, adapter_up_map, down_weight):
    embedded = jnp.take(token_embedding_table, given_token_index, axis=0)
    joined = jnp.concatenate([hidden, embedded], axis=1)
    normed = rms_norm(joined, attention_norm_gain)
    projected = jnp.dot(normed, query_key_value_weight, preferred_element_type=jnp.float32).astype(jnp.bfloat16)
    head_cols = HEADS * HD
    queries = projected[:, :head_cols].reshape(REQS, STEPS, HEADS, HD)
    new_keys = projected[:, head_cols:2 * head_cols].reshape(REQS, STEPS, HEADS, HD)
    new_values = projected[:, 2 * head_cols:].reshape(REQS, STEPS, HEADS, HD)
    positions = lengths[:, None] + jnp.arange(STEPS, dtype=jnp.int32)[None, :]
    queries = rotate(queries.astype(jnp.float32), positions).astype(jnp.bfloat16)
    new_keys = rotate(new_keys.astype(jnp.float32), positions).astype(jnp.bfloat16)
    groups = (jnp.arange(REQS, dtype=jnp.int32) // REQ_DEV).astype(jnp.int32)
    score_scale = 1.0 / math.sqrt(HD)
    causal = jnp.arange(STEPS)[:, None] >= jnp.arange(STEPS)[None, :]

    def attend_one(packed):
        query_rows, fresh_key, fresh_value, length, table_row, group_id = packed
        cache_k = lax.dynamic_index_in_dim(rotated_key_cache, group_id, 1, keepdims=False)
        cache_v = lax.dynamic_index_in_dim(cached_value_pages, group_id, 1, keepdims=False)
        cache_k = cache_k.reshape(N_SEQ, PAGES_DEV * PAGE, HEADS, HD).astype(jnp.float32)
        cache_v = cache_v.reshape(N_SEQ, PAGES_DEV * PAGE, HEADS, HD).astype(jnp.float32)
        slot_ids = jnp.arange(GSLOTS, dtype=jnp.int32)
        page_ids = jnp.arange(MAXPG, dtype=jnp.int32)
        is_live = page_ids < (length + PAGE - 1) // PAGE
        matches = (table_row[:, None] == slot_ids[None, :]) & is_live[:, None]
        is_owned = jnp.any(matches, axis=0)
        page_of = lax.optimization_barrier(jnp.sum(jnp.where(matches, page_ids[:, None], 0), axis=0))
        token_pos = page_of[:, None] * PAGE + jnp.arange(PAGE, dtype=jnp.int32)[None, :]
        is_valid = (is_owned[:, None] & (token_pos < length)).reshape(N_SEQ, PAGES_DEV * PAGE)
        scores = jnp.einsum('thd,gkhd->thgk', query_rows.astype(jnp.float32), cache_k) * score_scale
        mask_b = is_valid[None, None]
        part_max = lax.optimization_barrier(jnp.max(jnp.where(mask_b, scores, NEGATIVE), axis=-1))
        weights = jnp.where(mask_b, jnp.exp(scores - part_max[..., None]), 0.0)
        part_sum = lax.optimization_barrier(jnp.sum(weights, axis=-1))
        rounded = lax.optimization_barrier(weights.astype(jnp.bfloat16)).astype(jnp.float32)
        part_out = jnp.einsum('thgk,gkhd->thgd', rounded, cache_v)
        fresh_scores = jnp.einsum('thd,shd->ths', query_rows.astype(jnp.float32), fresh_key.astype(jnp.float32)) * score_scale
        fresh_mask = causal[:, None, :]
        fresh_max = lax.optimization_barrier(jnp.max(jnp.where(fresh_mask, fresh_scores, NEGATIVE), axis=-1))
        fresh_w = jnp.where(fresh_mask, jnp.exp(fresh_scores - fresh_max[..., None]), 0.0)
        fresh_sum = lax.optimization_barrier(jnp.sum(fresh_w, axis=-1))
        fresh_round = lax.optimization_barrier(fresh_w.astype(jnp.bfloat16)).astype(jnp.float32)
        fresh_out = jnp.einsum('ths,shd->thd', fresh_round, fresh_value.astype(jnp.float32))
        overall = jnp.maximum(lax.optimization_barrier(jnp.max(part_max, axis=-1)), fresh_max)
        cache_factor = jnp.exp(part_max - overall[..., None])
        fresh_factor = jnp.exp(fresh_max - overall)
        denominator = lax.optimization_barrier(jnp.sum(part_sum * cache_factor, axis=-1)) + fresh_sum * fresh_factor
        summed = lax.optimization_barrier(jnp.sum(part_out * cache_factor[..., None], axis=2)) + fresh_out * fresh_factor[..., None]
        return (summed / denominator[..., None]).astype(jnp.bfloat16)
    attended = lax.map(attend_one, (queries, new_keys, new_values, lengths, request_page_slots, groups))
    attention = attended.reshape(REQS * STEPS, head_cols)
    after_attn = (joined.astype(jnp.float32) + jnp.dot(attention, attention_output_weight, preferred_element_type=jnp.float32)).astype(jnp.bfloat16)
    second_normed_state = rms_norm(after_attn, feedforward_norm_gain)
    adapter_hidden = jnp.dot(second_normed_state, adapter_down_map, preferred_element_type=jnp.float32).astype(jnp.bfloat16)
    gate_preactivation = jnp.dot(second_normed_state, gate_weight, preferred_element_type=jnp.float32) + jnp.dot(adapter_hidden, adapter_gate_map, preferred_element_type=jnp.float32)
    up_projection_part = jnp.dot(second_normed_state, up_weight, preferred_element_type=jnp.float32) + jnp.dot(adapter_hidden, adapter_up_map, preferred_element_type=jnp.float32)
    inner_act = (jax.nn.silu(gate_preactivation) * up_projection_part).astype(jnp.bfloat16)
    return (after_attn.astype(jnp.float32) + jnp.dot(inner_act, down_weight, preferred_element_type=jnp.float32)).astype(jnp.bfloat16)
```

```python
import functools
import math

import jax
import jax.numpy as jnp
from jax import lax
from jax.experimental import pallas as pl
from jax.experimental.pallas import tpu as pltpu
from jax.sharding import PartitionSpec as P

HEADS = 16
HD = 224


NEGATIVE = -1e30
EPSILON = 1e-05
ROTARY_BASE = 10000.0


MESH_ID = pl.DeviceIdType.MESH


def _exchange_kernel(axis, n, gather, x_ref, y_ref, send_sem, recv_sem, local_sem):
    me = lax.axis_index(axis)
    barrier = pltpu.get_barrier_semaphore()
    for k in range(1, n):
        peer = lax.rem(me + k, n)
        pl.semaphore_signal(barrier, 1, device_id={axis: peer}, device_id_type=MESH_ID)
    pl.semaphore_wait(barrier, n - 1)
    copies = []
    for k in range(1, n):
        peer = lax.rem(me + k, n)
        source = x_ref if gather else x_ref.at[peer]
        copy = pltpu.make_async_remote_copy(
            src_ref=source,
            dst_ref=y_ref.at[me],
            send_sem=send_sem.at[k],
            recv_sem=recv_sem.at[k],
            device_id={axis: peer},
            device_id_type=MESH_ID,
        )
        copy.start()
        copies.append(copy)
    local = pltpu.make_async_copy(x_ref if gather else x_ref.at[me], y_ref.at[me], local_sem)
    local.start()
    local.wait()
    for copy in copies:
        copy.wait()


def exchange(x, axis, cid, gather=False):
    n = lax.axis_size(axis)
    out_shape = (n,) + x.shape if gather else x.shape
    return pl.pallas_call(
        functools.partial(_exchange_kernel, axis, n, gather),
        out_shape=jax.ShapeDtypeStruct(out_shape, x.dtype),
        in_specs=[pl.BlockSpec(memory_space=pltpu.VMEM)],
        out_specs=pl.BlockSpec(memory_space=pltpu.VMEM),
        scratch_shapes=[
            pltpu.SemaphoreType.DMA((n,)),
            pltpu.SemaphoreType.DMA((n,)),
            pltpu.SemaphoreType.DMA(()),
        ],
        compiler_params=pltpu.CompilerParams(collective_id=cid, has_side_effects=True),
    )(x)


def merged_2(array, axis, combine):
    everything = jax.tree.map(lambda part: lax.all_gather(part, axis), array)
    first = jax.tree.map(lambda part: part[0], everything)

    def hop(k, so_far):
        return combine(so_far, jax.tree.map(lambda part: part[k], everything))

    return lax.fori_loop(1, lax.axis_size(axis), hop, first)


def rms_norm(matrix, gain_vec):
    widened = matrix.astype(jnp.float32)
    factor = lax.rsqrt(jnp.mean(widened * widened, axis=-1, keepdims=True) + EPSILON)
    return (widened * factor * gain_vec.astype(jnp.float32)).astype(jnp.bfloat16)


def rotate(vectors, positions):
    half_dim = vectors.shape[-1] // 2
    frequency = ROTARY_BASE ** (-2.0 * jnp.arange(half_dim, dtype=jnp.float32) / vectors.shape[-1])
    angles = positions.astype(jnp.float32)[..., None, None] * frequency
    cosine = jnp.cos(angles)
    sine_part = jnp.sin(angles)
    front_half = vectors[..., :half_dim]
    back_half = vectors[..., half_dim:]
    return jnp.concatenate(
        [front_half * cosine - back_half * sine_part, back_half * cosine + front_half * sine_part],
        axis=-1,
    )


def softmax_join(earlier, later):
    first_max, first_sum, first_out = earlier
    second_max, second_sum, second_out = later
    overall = jnp.maximum(first_max, second_max)
    first_factor = jnp.exp(first_max - overall)
    second_factor = jnp.exp(second_max - overall)
    return (
        overall,
        first_sum * first_factor + second_sum * second_factor,
        first_out * first_factor[..., None] + second_out * second_factor[..., None],
    )


def body(
    given_token_index,
    hidden,
    token_embedding_table,
    attention_norm_gain,
    query_key_value_weight,
    rotated_key_cache,
    cached_value_pages,
    lengths,
    request_page_slots,
    attention_output_weight,
    feedforward_norm_gain,
    gate_weight,
    up_weight,
    adapter_down_map,
    adapter_gate_map,
    adapter_up_map,
    down_weight,
):
    seq_devices = lax.axis_size("seq")
    req_devices = lax.axis_size("req")
    seq_index = lax.axis_index("seq")
    req_index = lax.axis_index("req")
    group_rows = hidden.shape[0]
    requests = lengths.shape[0]
    steps_each = group_rows // requests
    vocab_rows = token_embedding_table.shape[0]
    first_id = (seq_index * req_devices + req_index) * vocab_rows
    local_ids = given_token_index - first_id
    present = (local_ids >= 0) & (local_ids < vocab_rows)
    looked = jnp.take(token_embedding_table, jnp.clip(local_ids, 0, vocab_rows - 1), axis=0).astype(
        jnp.float32
    )
    looked = jnp.where(present[:, None], looked, 0.0).astype(jnp.bfloat16)
    everywhere = lax.psum(looked, ("seq", "req"))
    embedded = lax.dynamic_slice_in_dim(everywhere, req_index * group_rows, group_rows, 0)
    joined = jnp.concatenate([hidden, embedded.astype(jnp.bfloat16)], axis=1)
    normed = rms_norm(joined, attention_norm_gain)
    spread = lax.all_to_all(normed, "req", split_axis=1, concat_axis=0, tiled=True)
    block_rows = spread
    qkv_part = lax.psum_scatter(
        jnp.dot(block_rows, query_key_value_weight, preferred_element_type=jnp.float32),
        "req",
        scatter_dimension=0,
        tiled=True,
    )
    projected = lax.all_gather(qkv_part.astype(jnp.bfloat16), "seq", axis=1, tiled=True)
    head_cols = HEADS * HD
    queries = projected[:, :head_cols].reshape(requests, steps_each, HEADS, HD)
    new_keys = projected[:, head_cols : 2 * head_cols].reshape(requests, steps_each, HEADS, HD)
    new_values = projected[:, 2 * head_cols :].reshape(requests, steps_each, HEADS, HD)
    positions = lengths[:, None] + jnp.arange(steps_each, dtype=jnp.int32)[None, :]
    queries = rotate(queries.astype(jnp.float32), positions).astype(jnp.bfloat16)
    new_keys = rotate(new_keys.astype(jnp.float32), positions).astype(jnp.bfloat16)
    slots = rotated_key_cache.shape[0]
    page_len = rotated_key_cache.shape[2]
    cache_k = rotated_key_cache.reshape(slots * page_len, HEADS, HD)
    cache_v = cached_value_pages.reshape(slots * page_len, HEADS, HD)
    slot_ids = seq_index * slots + jnp.arange(slots, dtype=jnp.int32)
    page_ids = jnp.arange(request_page_slots.shape[1], dtype=jnp.int32)
    is_live = page_ids[None, :] < ((lengths + page_len - 1) // page_len)[:, None]
    matches = (request_page_slots[:, :, None] == slot_ids[None, None, :]) & is_live[:, :, None]
    is_owned = jnp.any(matches, axis=1)
    page_of = jnp.sum(jnp.where(matches, page_ids[None, :, None], 0), axis=1)
    token_pos = (
        page_of[:, :, None] * page_len + jnp.arange(page_len, dtype=jnp.int32)[None, None, :]
    )
    is_valid = (is_owned[:, :, None] & (token_pos < lengths[:, None, None])).reshape(
        requests, slots * page_len
    )
    score_scale = 1.0 / math.sqrt(HD)
    scores = (
        jnp.einsum("rthd,khd->rthk", queries, cache_k, preferred_element_type=jnp.float32)
        * score_scale
    )
    mask_b = is_valid[:, None, None, :]
    local_max = jnp.max(jnp.where(mask_b, scores, NEGATIVE), axis=-1)
    weights = jnp.where(mask_b, jnp.exp(scores - local_max[..., None]), 0.0)
    local_sum = jnp.sum(weights, axis=-1)
    local_out = jnp.einsum(
        "rthk,khd->rthd", weights.astype(jnp.bfloat16), cache_v, preferred_element_type=jnp.float32
    )
    fresh_scores = (
        jnp.einsum("rthd,rshd->rths", queries, new_keys, preferred_element_type=jnp.float32)
        * score_scale
    )
    causal = jnp.arange(steps_each)[:, None] >= jnp.arange(steps_each)[None, :]
    fresh_mask = causal[None, :, None, :]
    fresh_max = jnp.max(jnp.where(fresh_mask, fresh_scores, NEGATIVE), axis=-1)
    fresh_w = jnp.where(fresh_mask, jnp.exp(fresh_scores - fresh_max[..., None]), 0.0)
    fresh_sum = jnp.sum(fresh_w, axis=-1)
    fresh_out = jnp.einsum(
        "rths,rshd->rthd",
        fresh_w.astype(jnp.bfloat16),
        new_values,
        preferred_element_type=jnp.float32,
    )
    own_heads = HEADS // seq_devices
    first_head = seq_index * own_heads

    def own_slice(member):
        return lax.dynamic_slice_in_dim(member, first_head, own_heads, 2)

    pad_cols = 256 - HD - 2
    packed = jnp.concatenate(
        [
            local_out,
            local_max[..., None],
            local_sum[..., None],
            jnp.zeros(local_out.shape[:-1] + (pad_cols,), jnp.float32),
        ],
        axis=-1,
    )
    packed = packed.reshape(requests * steps_each, seq_devices, own_heads, 256)
    packed = jnp.transpose(packed, (1, 0, 2, 3)).reshape(seq_devices, group_rows * own_heads, 256)
    arrived = exchange(packed, "seq", 0).reshape(seq_devices, requests, steps_each, own_heads, 256)
    part_o = arrived[..., :HD]
    part_m = arrived[..., HD]
    part_l = arrived[..., HD + 1]
    f_max, f_sum, f_out = own_slice(fresh_max), own_slice(fresh_sum), own_slice(fresh_out)
    overall = jnp.maximum(jnp.max(part_m, axis=0), f_max)
    part_factor = jnp.exp(part_m - overall[None])
    fresh_factor = jnp.exp(f_max - overall)
    denominator = jnp.sum(part_l * part_factor, axis=0) + f_sum * fresh_factor
    numerator = jnp.sum(part_o * part_factor[..., None], axis=0) + f_out * fresh_factor[..., None]
    attention = (
        (numerator / denominator[..., None])
        .astype(jnp.bfloat16)
        .reshape(group_rows, own_heads * HD)
    )
    projected_out = jnp.dot(attention, attention_output_weight, preferred_element_type=jnp.float32)
    model_width = projected_out.shape[1]
    row_share = group_rows // seq_devices
    out_parts = exchange(projected_out.reshape(seq_devices, row_share, model_width), "seq", 1)
    own_rows = lax.dynamic_slice_in_dim(joined, seq_index * row_share, row_share, 0)
    after_rows = (own_rows.astype(jnp.float32) + jnp.sum(out_parts, axis=0)).astype(jnp.bfloat16)
    after_attn = exchange(after_rows, "seq", 2, gather=True).reshape(group_rows, model_width)
    second_normed_state = rms_norm(after_attn, feedforward_norm_gain)
    residual_cols, second_spread_state = (
        lax.all_to_all(after_attn, "req", split_axis=1, concat_axis=0, tiled=True),
        lax.all_to_all(second_normed_state, "req", split_axis=1, concat_axis=0, tiled=True),
    )
    gate_total, up_total, low_sum = lax.psum(
        (
            jnp.dot(second_spread_state, gate_weight, preferred_element_type=jnp.float32),
            jnp.dot(second_spread_state, up_weight, preferred_element_type=jnp.float32),
            jnp.dot(second_spread_state, adapter_down_map, preferred_element_type=jnp.float32),
        ),
        "req",
    )
    adapter_hidden = low_sum.astype(jnp.bfloat16)
    gate_preactivation = gate_total + jnp.dot(
        adapter_hidden, adapter_gate_map, preferred_element_type=jnp.float32
    )
    up_projection_part = up_total + jnp.dot(
        adapter_hidden, adapter_up_map, preferred_element_type=jnp.float32
    )
    inner_act = (jax.nn.silu(gate_preactivation) * up_projection_part).astype(jnp.bfloat16)
    out_rows = residual_cols.shape[0] // seq_devices
    block_rows = inner_act
    down_full = jnp.dot(block_rows, down_weight, preferred_element_type=jnp.float32)
    down_parts = exchange(down_full.reshape(seq_devices, out_rows, down_full.shape[1]), "seq", 3)
    down_sum = jnp.sum(down_parts, axis=0)
    residual_rows = lax.dynamic_slice_in_dim(residual_cols, seq_index * out_rows, out_rows, 0)
    return (residual_rows.astype(jnp.float32) + down_sum).astype(jnp.bfloat16)


def solution(mesh):
    placed = (
        P(),
        P("req", None),
        P(("seq", "req"), None),
        P(),
        P("req", "seq"),
        P("seq", "req", None, None),
        P("seq", "req", None, None),
        P("req"),
        P("req", None),
        P("seq", None),
        P(),
        P("req", "seq"),
        P("req", "seq"),
        P("req", None),
        P(None, "seq"),
        P(None, "seq"),
        P("seq", "req"),
    )
    return jax.shard_map(
        body, mesh=mesh, in_specs=placed, out_specs=P("seq", "req"), check_vma=False
    )
```

```python
import functools
import math

import jax
import jax.numpy as jnp
from jax import lax
from jax.experimental import pallas as pl
from jax.experimental.pallas import tpu as pltpu
from jax.sharding import PartitionSpec as P

HEADS = 16
HD = 224


NEGATIVE = -1e30
EPSILON = 1e-05
ROTARY_BASE = 10000.0


MESH_ID = pl.DeviceIdType.MESH


def _exchange_kernel(axis, n, gather, x_ref, y_ref, send_sem, recv_sem, local_sem):
    me = lax.axis_index(axis)
    barrier = pltpu.get_barrier_semaphore()
    for k in range(1, n):
        peer = lax.rem(me + k, n)
        pl.semaphore_signal(barrier, 1, device_id={axis: peer}, device_id_type=MESH_ID)
    pl.semaphore_wait(barrier, n - 1)
    copies = []
    for k in range(1, n):
        peer = lax.rem(me + k, n)
        source = x_ref if gather else x_ref.at[peer]
        copy = pltpu.make_async_remote_copy(
            src_ref=source,
            dst_ref=y_ref.at[me],
            send_sem=send_sem.at[k],
            recv_sem=recv_sem.at[k],
            device_id={axis: peer},
            device_id_type=MESH_ID,
        )
        copy.start()
        copies.append(copy)
    local = pltpu.make_async_copy(x_ref if gather else x_ref.at[me], y_ref.at[me], local_sem)
    local.start()
    local.wait()
    for copy in copies:
        copy.wait()


def exchange(x, axis, cid, gather=False):
    n = lax.axis_size(axis)
    out_shape = (n,) + x.shape if gather else x.shape
    return pl.pallas_call(
        functools.partial(_exchange_kernel, axis, n, gather),
        out_shape=jax.ShapeDtypeStruct(out_shape, x.dtype),
        in_specs=[pl.BlockSpec(memory_space=pltpu.VMEM)],
        out_specs=pl.BlockSpec(memory_space=pltpu.VMEM),
        scratch_shapes=[
            pltpu.SemaphoreType.DMA((n,)),
            pltpu.SemaphoreType.DMA((n,)),
            pltpu.SemaphoreType.DMA(()),
        ],
        compiler_params=pltpu.CompilerParams(collective_id=cid, has_side_effects=True),
    )(x)


def merged_2(array, axis, combine):
    everything = jax.tree.map(lambda part: lax.all_gather(part, axis), array)
    first = jax.tree.map(lambda part: part[0], everything)

    def hop(k, so_far):
        return combine(so_far, jax.tree.map(lambda part: part[k], everything))

    return lax.fori_loop(1, lax.axis_size(axis), hop, first)


def rms_norm(matrix, gain_vec):
    widened = matrix.astype(jnp.float32)
    factor = lax.rsqrt(jnp.mean(widened * widened, axis=-1, keepdims=True) + EPSILON)
    return (widened * factor * gain_vec.astype(jnp.float32)).astype(jnp.bfloat16)


def rotate(vectors, positions):
    half_dim = vectors.shape[-1] // 2
    frequency = ROTARY_BASE ** (-2.0 * jnp.arange(half_dim, dtype=jnp.float32) / vectors.shape[-1])
    angles = positions.astype(jnp.float32)[..., None, None] * frequency
    cosine = jnp.cos(angles)
    sine_part = jnp.sin(angles)
    front_half = vectors[..., :half_dim]
    back_half = vectors[..., half_dim:]
    return jnp.concatenate(
        [front_half * cosine - back_half * sine_part, back_half * cosine + front_half * sine_part],
        axis=-1,
    )


def softmax_join(earlier, later):
    first_max, first_sum, first_out = earlier
    second_max, second_sum, second_out = later
    overall = jnp.maximum(first_max, second_max)
    first_factor = jnp.exp(first_max - overall)
    second_factor = jnp.exp(second_max - overall)
    return (
        overall,
        first_sum * first_factor + second_sum * second_factor,
        first_out * first_factor[..., None] + second_out * second_factor[..., None],
    )


def body(
    given_token_index,
    hidden,
    token_embedding_table,
    attention_norm_gain,
    query_key_value_weight,
    rotated_key_cache,
    cached_value_pages,
    lengths,
    request_page_slots,
    attention_output_weight,
    feedforward_norm_gain,
    gate_weight,
    up_weight,
    adapter_down_map,
    adapter_gate_map,
    adapter_up_map,
    down_weight,
):
    seq_devices = lax.axis_size("seq")
    req_devices = lax.axis_size("req")
    seq_index = lax.axis_index("seq")
    req_index = lax.axis_index("req")
    group_rows = hidden.shape[0]
    requests = lengths.shape[0]
    steps_each = group_rows // requests
    vocab_rows = token_embedding_table.shape[0]
    first_id = (seq_index * req_devices + req_index) * vocab_rows
    local_ids = given_token_index - first_id
    present = (local_ids >= 0) & (local_ids < vocab_rows)
    looked = jnp.take(token_embedding_table, jnp.clip(local_ids, 0, vocab_rows - 1), axis=0).astype(
        jnp.float32
    )
    looked = jnp.where(present[:, None], looked, 0.0)
    everywhere = lax.psum(looked, ("seq", "req"))
    embedded = lax.dynamic_slice_in_dim(everywhere, req_index * group_rows, group_rows, 0)
    joined = jnp.concatenate([hidden, embedded.astype(jnp.bfloat16)], axis=1)
    normed = rms_norm(joined, attention_norm_gain)
    width_share = normed.shape[1] // req_devices
    to_owners = jnp.transpose(normed.reshape(group_rows, req_devices, width_share), (1, 0, 2))
    block_rows = exchange(to_owners, "req", 4).reshape(req_devices * group_rows, width_share)
    qkv_full = jnp.dot(block_rows, query_key_value_weight, preferred_element_type=jnp.float32)
    qkv_parts = exchange(qkv_full.reshape(req_devices, group_rows, qkv_full.shape[1]), "req", 5)
    qkv_part = jnp.sum(qkv_parts, axis=0).astype(jnp.bfloat16)
    qkv_all = exchange(qkv_part, "seq", 6, gather=True)
    projected = jnp.transpose(qkv_all, (1, 0, 2)).reshape(group_rows, seq_devices * qkv_part.shape[1])
    head_cols = HEADS * HD
    queries = projected[:, :head_cols].reshape(requests, steps_each, HEADS, HD)
    new_keys = projected[:, head_cols : 2 * head_cols].reshape(requests, steps_each, HEADS, HD)
    new_values = projected[:, 2 * head_cols :].reshape(requests, steps_each, HEADS, HD)
    positions = lengths[:, None] + jnp.arange(steps_each, dtype=jnp.int32)[None, :]
    queries = rotate(queries.astype(jnp.float32), positions).astype(jnp.bfloat16)
    new_keys = rotate(new_keys.astype(jnp.float32), positions).astype(jnp.bfloat16)
    slots = rotated_key_cache.shape[0]
    page_len = rotated_key_cache.shape[2]
    cache_k = rotated_key_cache.reshape(slots * page_len, HEADS, HD)
    cache_v = cached_value_pages.reshape(slots * page_len, HEADS, HD)
    slot_ids = seq_index * slots + jnp.arange(slots, dtype=jnp.int32)
    page_ids = jnp.arange(request_page_slots.shape[1], dtype=jnp.int32)
    is_live = page_ids[None, :] < ((lengths + page_len - 1) // page_len)[:, None]
    matches = (request_page_slots[:, :, None] == slot_ids[None, None, :]) & is_live[:, :, None]
    is_owned = jnp.any(matches, axis=1)
    page_of = jnp.sum(jnp.where(matches, page_ids[None, :, None], 0), axis=1)
    token_pos = (
        page_of[:, :, None] * page_len + jnp.arange(page_len, dtype=jnp.int32)[None, None, :]
    )
    is_valid = (is_owned[:, :, None] & (token_pos < lengths[:, None, None])).reshape(
        requests, slots * page_len
    )
    score_scale = 1.0 / math.sqrt(HD)
    scores = (
        jnp.einsum("rthd,khd->rthk", queries, cache_k, preferred_element_type=jnp.float32)
        * score_scale
    )
    mask_b = is_valid[:, None, None, :]
    local_max = jnp.max(jnp.where(mask_b, scores, NEGATIVE), axis=-1)
    weights = jnp.where(mask_b, jnp.exp(scores - local_max[..., None]), 0.0)
    local_sum = jnp.sum(weights, axis=-1)
    local_out = jnp.einsum(
        "rthk,khd->rthd", weights.astype(jnp.bfloat16), cache_v, preferred_element_type=jnp.float32
    )
    fresh_scores = (
        jnp.einsum("rthd,rshd->rths", queries, new_keys, preferred_element_type=jnp.float32)
        * score_scale
    )
    causal = jnp.arange(steps_each)[:, None] >= jnp.arange(steps_each)[None, :]
    fresh_mask = causal[None, :, None, :]
    fresh_max = jnp.max(jnp.where(fresh_mask, fresh_scores, NEGATIVE), axis=-1)
    fresh_w = jnp.where(fresh_mask, jnp.exp(fresh_scores - fresh_max[..., None]), 0.0)
    fresh_sum = jnp.sum(fresh_w, axis=-1)
    fresh_out = jnp.einsum(
        "rths,rshd->rthd",
        fresh_w.astype(jnp.bfloat16),
        new_values,
        preferred_element_type=jnp.float32,
    )
    own_heads = HEADS // seq_devices
    first_head = seq_index * own_heads

    def own_slice(member):
        return lax.dynamic_slice_in_dim(member, first_head, own_heads, 2)

    pad_cols = 256 - HD - 2
    packed = jnp.concatenate(
        [
            local_out,
            local_max[..., None],
            local_sum[..., None],
            jnp.zeros(local_out.shape[:-1] + (pad_cols,), jnp.float32),
        ],
        axis=-1,
    )
    packed = packed.reshape(requests * steps_each, seq_devices, own_heads, 256)
    packed = jnp.transpose(packed, (1, 0, 2, 3)).reshape(seq_devices, group_rows * own_heads, 256)
    arrived = exchange(packed, "seq", 0).reshape(seq_devices, requests, steps_each, own_heads, 256)
    part_o = arrived[..., :HD]
    part_m = arrived[..., HD]
    part_l = arrived[..., HD + 1]
    f_max, f_sum, f_out = own_slice(fresh_max), own_slice(fresh_sum), own_slice(fresh_out)
    overall = jnp.maximum(jnp.max(part_m, axis=0), f_max)
    part_factor = jnp.exp(part_m - overall[None])
    fresh_factor = jnp.exp(f_max - overall)
    denominator = jnp.sum(part_l * part_factor, axis=0) + f_sum * fresh_factor
    numerator = jnp.sum(part_o * part_factor[..., None], axis=0) + f_out * fresh_factor[..., None]
    attention = (
        (numerator / denominator[..., None])
        .astype(jnp.bfloat16)
        .reshape(group_rows, own_heads * HD)
    )
    projected_out = jnp.dot(attention, attention_output_weight, preferred_element_type=jnp.float32)
    model_width = projected_out.shape[1]
    row_share = group_rows // seq_devices
    out_parts = exchange(projected_out.reshape(seq_devices, row_share, model_width), "seq", 1)
    own_rows = lax.dynamic_slice_in_dim(joined, seq_index * row_share, row_share, 0)
    after_rows = (own_rows.astype(jnp.float32) + jnp.sum(out_parts, axis=0)).astype(jnp.bfloat16)
    after_attn = exchange(after_rows, "seq", 2, gather=True).reshape(group_rows, model_width)
    second_normed_state = rms_norm(after_attn, feedforward_norm_gain)
    both = jnp.stack([after_attn, second_normed_state]).reshape(2, group_rows, req_devices, width_share)
    both_parts = exchange(jnp.transpose(both, (2, 0, 1, 3)), "req", 7)
    residual_cols = both_parts[:, 0].reshape(req_devices * group_rows, width_share)
    second_spread_state = both_parts[:, 1].reshape(req_devices * group_rows, width_share)
    units = gate_weight.shape[1]
    mlp_full = jnp.concatenate(
        [
            jnp.dot(second_spread_state, gate_weight, preferred_element_type=jnp.float32),
            jnp.dot(second_spread_state, up_weight, preferred_element_type=jnp.float32),
            jnp.dot(second_spread_state, adapter_down_map, preferred_element_type=jnp.float32),
        ],
        axis=1,
    )
    mlp_parts = exchange(mlp_full.reshape(req_devices, group_rows, mlp_full.shape[1]), "req", 8)
    mlp_sum = jnp.sum(mlp_parts, axis=0)
    gate_total = mlp_sum[:, :units]
    up_total = mlp_sum[:, units : 2 * units]
    low_sum = mlp_sum[:, 2 * units :]
    adapter_hidden = low_sum.astype(jnp.bfloat16)
    gate_preactivation = gate_total + jnp.dot(
        adapter_hidden, adapter_gate_map, preferred_element_type=jnp.float32
    )
    up_projection_part = up_total + jnp.dot(
        adapter_hidden, adapter_up_map, preferred_element_type=jnp.float32
    )
    group_act = (jax.nn.silu(gate_preactivation) * up_projection_part).astype(jnp.bfloat16)
    inner_act = exchange(group_act, "req", 9, gather=True).reshape(req_devices * group_rows, units)
    out_rows = residual_cols.shape[0] // seq_devices
    block_rows = inner_act
    down_full = jnp.dot(block_rows, down_weight, preferred_element_type=jnp.float32)
    down_parts = exchange(down_full.reshape(seq_devices, out_rows, down_full.shape[1]), "seq", 3)
    down_sum = jnp.sum(down_parts, axis=0)
    residual_rows = lax.dynamic_slice_in_dim(residual_cols, seq_index * out_rows, out_rows, 0)
    return (residual_rows.astype(jnp.float32) + down_sum).astype(jnp.bfloat16)


def solution(mesh):
    placed = (
        P(),
        P("req", None),
        P(("seq", "req"), None),
        P(),
        P("req", "seq"),
        P("seq", "req", None, None),
        P("seq", "req", None, None),
        P("req"),
        P("req", None),
        P("seq", None),
        P(),
        P("req", "seq"),
        P("req", "seq"),
        P("req", None),
        P(None, "seq"),
        P(None, "seq"),
        P("seq", "req"),
    )
    return jax.shard_map(
        body, mesh=mesh, in_specs=placed, out_specs=P("seq", "req"), check_vma=False
    )
```

```python
import functools
import math

import jax
import jax.numpy as jnp
from jax import lax
from jax.experimental import pallas as pl
from jax.experimental.pallas import tpu as pltpu
from jax.sharding import PartitionSpec as P

HEADS = 16
HD = 224


NEGATIVE = -1e30
EPSILON = 1e-05
ROTARY_BASE = 10000.0


MESH_ID = pl.DeviceIdType.MESH


def _exchange_kernel(axis, n, gather, x_ref, y_ref, send_sem, recv_sem, local_sem):
    me = lax.axis_index(axis)
    barrier = pltpu.get_barrier_semaphore()
    for k in range(1, n):
        peer = lax.rem(me + k, n)
        pl.semaphore_signal(barrier, 1, device_id={axis: peer}, device_id_type=MESH_ID)
    pl.semaphore_wait(barrier, n - 1)
    copies = []
    for k in range(1, n):
        peer = lax.rem(me + k, n)
        source = x_ref if gather else x_ref.at[peer]
        copy = pltpu.make_async_remote_copy(
            src_ref=source,
            dst_ref=y_ref.at[me],
            send_sem=send_sem.at[k],
            recv_sem=recv_sem.at[k],
            device_id={axis: peer},
            device_id_type=MESH_ID,
        )
        copy.start()
        copies.append(copy)
    local = pltpu.make_async_copy(x_ref if gather else x_ref.at[me], y_ref.at[me], local_sem)
    local.start()
    local.wait()
    for copy in copies:
        copy.wait()


def exchange(x, axis, cid, gather=False):
    n = lax.axis_size(axis)
    out_shape = (n,) + x.shape if gather else x.shape
    return pl.pallas_call(
        functools.partial(_exchange_kernel, axis, n, gather),
        out_shape=jax.ShapeDtypeStruct(out_shape, x.dtype),
        in_specs=[pl.BlockSpec(memory_space=pltpu.VMEM)],
        out_specs=pl.BlockSpec(memory_space=pltpu.VMEM),
        scratch_shapes=[
            pltpu.SemaphoreType.DMA((n,)),
            pltpu.SemaphoreType.DMA((n,)),
            pltpu.SemaphoreType.DMA(()),
        ],
        compiler_params=pltpu.CompilerParams(collective_id=cid, has_side_effects=True),
    )(x)


def merged_2(array, axis, combine):
    everything = jax.tree.map(lambda part: lax.all_gather(part, axis), array)
    first = jax.tree.map(lambda part: part[0], everything)

    def hop(k, so_far):
        return combine(so_far, jax.tree.map(lambda part: part[k], everything))

    return lax.fori_loop(1, lax.axis_size(axis), hop, first)


def rms_norm(matrix, gain_vec):
    widened = matrix.astype(jnp.float32)
    factor = lax.rsqrt(jnp.mean(widened * widened, axis=-1, keepdims=True) + EPSILON)
    return (widened * factor * gain_vec.astype(jnp.float32)).astype(jnp.bfloat16)


def rotate(vectors, positions):
    half_dim = vectors.shape[-1] // 2
    frequency = ROTARY_BASE ** (-2.0 * jnp.arange(half_dim, dtype=jnp.float32) / vectors.shape[-1])
    angles = positions.astype(jnp.float32)[..., None, None] * frequency
    cosine = jnp.cos(angles)
    sine_part = jnp.sin(angles)
    front_half = vectors[..., :half_dim]
    back_half = vectors[..., half_dim:]
    return jnp.concatenate(
        [front_half * cosine - back_half * sine_part, back_half * cosine + front_half * sine_part],
        axis=-1,
    )


def softmax_join(earlier, later):
    first_max, first_sum, first_out = earlier
    second_max, second_sum, second_out = later
    overall = jnp.maximum(first_max, second_max)
    first_factor = jnp.exp(first_max - overall)
    second_factor = jnp.exp(second_max - overall)
    return (
        overall,
        first_sum * first_factor + second_sum * second_factor,
        first_out * first_factor[..., None] + second_out * second_factor[..., None],
    )


def body(
    given_token_index,
    hidden,
    token_embedding_table,
    attention_norm_gain,
    query_key_value_weight,
    rotated_key_cache,
    cached_value_pages,
    lengths,
    request_page_slots,
    attention_output_weight,
    feedforward_norm_gain,
    gate_weight,
    up_weight,
    adapter_down_map,
    adapter_gate_map,
    adapter_up_map,
    down_weight,
):
    seq_devices = lax.axis_size("seq")
    req_devices = lax.axis_size("req")
    seq_index = lax.axis_index("seq")
    req_index = lax.axis_index("req")
    group_rows = hidden.shape[0]
    requests = lengths.shape[0]
    steps_each = group_rows // requests
    vocab_rows = token_embedding_table.shape[0]
    first_id = (seq_index * req_devices + req_index) * vocab_rows
    local_ids = given_token_index - first_id
    present = (local_ids >= 0) & (local_ids < vocab_rows)
    looked = jnp.take(token_embedding_table, jnp.clip(local_ids, 0, vocab_rows - 1), axis=0).astype(
        jnp.float32
    )
    looked = jnp.where(present[:, None], looked, 0.0).astype(jnp.bfloat16)
    by_group = exchange(looked.reshape(req_devices, group_rows, looked.shape[1]), "req", 10)
    column_part = jnp.sum(by_group.astype(jnp.float32), axis=0).astype(jnp.bfloat16)
    from_columns = exchange(column_part, "seq", 11, gather=True)
    embedded = jnp.sum(from_columns.astype(jnp.float32), axis=0)
    joined = jnp.concatenate([hidden, embedded.astype(jnp.bfloat16)], axis=1)
    normed = rms_norm(joined, attention_norm_gain)
    width_share = normed.shape[1] // req_devices
    to_owners = jnp.transpose(normed.reshape(group_rows, req_devices, width_share), (1, 0, 2))
    block_rows = exchange(to_owners, "req", 4).reshape(req_devices * group_rows, width_share)
    qkv_full = jnp.dot(block_rows, query_key_value_weight, preferred_element_type=jnp.float32)
    qkv_parts = exchange(qkv_full.reshape(req_devices, group_rows, qkv_full.shape[1]), "req", 5)
    qkv_part = jnp.sum(qkv_parts, axis=0).astype(jnp.bfloat16)
    qkv_all = exchange(qkv_part, "seq", 6, gather=True)
    projected = jnp.transpose(qkv_all, (1, 0, 2)).reshape(group_rows, seq_devices * qkv_part.shape[1])
    head_cols = HEADS * HD
    queries = projected[:, :head_cols].reshape(requests, steps_each, HEADS, HD)
    new_keys = projected[:, head_cols : 2 * head_cols].reshape(requests, steps_each, HEADS, HD)
    new_values = projected[:, 2 * head_cols :].reshape(requests, steps_each, HEADS, HD)
    positions = lengths[:, None] + jnp.arange(steps_each, dtype=jnp.int32)[None, :]
    queries = rotate(queries.astype(jnp.float32), positions).astype(jnp.bfloat16)
    new_keys = rotate(new_keys.astype(jnp.float32), positions).astype(jnp.bfloat16)
    slots = rotated_key_cache.shape[0]
    page_len = rotated_key_cache.shape[2]
    cache_k = rotated_key_cache.reshape(slots * page_len, head_cols)
    cache_v = cached_value_pages.reshape(slots * page_len, head_cols)
    slot_ids = seq_index * slots + jnp.arange(slots, dtype=jnp.int32)
    page_ids = jnp.arange(request_page_slots.shape[1], dtype=jnp.int32)
    is_live = page_ids[None, :] < ((lengths + page_len - 1) // page_len)[:, None]
    matches = (request_page_slots[:, :, None] == slot_ids[None, None, :]) & is_live[:, :, None]
    is_owned = jnp.any(matches, axis=1)
    page_of = jnp.sum(jnp.where(matches, page_ids[None, :, None], 0), axis=1)
    token_pos = (
        page_of[:, :, None] * page_len + jnp.arange(page_len, dtype=jnp.int32)[None, None, :]
    )
    is_valid = (is_owned[:, :, None] & (token_pos < lengths[:, None, None])).reshape(
        requests, slots * page_len
    )
    score_scale = 1.0 / math.sqrt(HD)
    head_mask = (jnp.arange(head_cols, dtype=jnp.int32)[None, :] // HD) == jnp.arange(
        HEADS, dtype=jnp.int32
    )[:, None]
    query_rows = queries.reshape(group_rows, head_cols)
    spread_queries = jnp.where(head_mask[None], query_rows[:, None, :], jnp.zeros((), jnp.bfloat16))
    scores = (
        jnp.dot(
            spread_queries.reshape(group_rows * HEADS, head_cols),
            cache_k.T,
            preferred_element_type=jnp.float32,
        )
        * score_scale
    ).reshape(requests, steps_each, HEADS, slots * page_len)
    mask_b = is_valid[:, None, None, :]
    local_max = jnp.max(jnp.where(mask_b, scores, NEGATIVE), axis=-1)
    weights = jnp.where(mask_b, jnp.exp(scores - local_max[..., None]), 0.0)
    local_sum = jnp.sum(weights, axis=-1)
    spread_out = jnp.dot(
        weights.astype(jnp.bfloat16).reshape(group_rows * HEADS, slots * page_len),
        cache_v,
        preferred_element_type=jnp.float32,
    ).reshape(group_rows, HEADS, head_cols)
    local_out = jnp.sum(jnp.where(head_mask[None], spread_out, 0.0), axis=1).reshape(
        requests, steps_each, HEADS, HD
    )
    fresh_scores = (
        jnp.einsum("rthd,rshd->rths", queries, new_keys, preferred_element_type=jnp.float32)
        * score_scale
    )
    causal = jnp.arange(steps_each)[:, None] >= jnp.arange(steps_each)[None, :]
    fresh_mask = causal[None, :, None, :]
    fresh_max = jnp.max(jnp.where(fresh_mask, fresh_scores, NEGATIVE), axis=-1)
    fresh_w = jnp.where(fresh_mask, jnp.exp(fresh_scores - fresh_max[..., None]), 0.0)
    fresh_sum = jnp.sum(fresh_w, axis=-1)
    fresh_out = jnp.einsum(
        "rths,rshd->rthd",
        fresh_w.astype(jnp.bfloat16),
        new_values,
        preferred_element_type=jnp.float32,
    )
    own_heads = HEADS // seq_devices
    first_head = seq_index * own_heads

    def own_slice(member):
        return lax.dynamic_slice_in_dim(member, first_head, own_heads, 2)

    pad_cols = 256 - HD - 2
    packed = jnp.concatenate(
        [
            local_out,
            local_max[..., None],
            local_sum[..., None],
            jnp.zeros(local_out.shape[:-1] + (pad_cols,), jnp.float32),
        ],
        axis=-1,
    )
    packed = packed.reshape(requests * steps_each, seq_devices, own_heads, 256)
    packed = jnp.transpose(packed, (1, 0, 2, 3)).reshape(seq_devices, group_rows * own_heads, 256)
    arrived = exchange(packed, "seq", 0).reshape(seq_devices, requests, steps_each, own_heads, 256)
    part_o = arrived[..., :HD]
    part_m = arrived[..., HD]
    part_l = arrived[..., HD + 1]
    f_max, f_sum, f_out = own_slice(fresh_max), own_slice(fresh_sum), own_slice(fresh_out)
    overall = jnp.maximum(jnp.max(part_m, axis=0), f_max)
    part_factor = jnp.exp(part_m - overall[None])
    fresh_factor = jnp.exp(f_max - overall)
    denominator = jnp.sum(part_l * part_factor, axis=0) + f_sum * fresh_factor
    numerator = jnp.sum(part_o * part_factor[..., None], axis=0) + f_out * fresh_factor[..., None]
    attention = (
        (numerator / denominator[..., None])
        .astype(jnp.bfloat16)
        .reshape(group_rows, own_heads * HD)
    )
    projected_out = jnp.dot(attention, attention_output_weight, preferred_element_type=jnp.float32)
    model_width = projected_out.shape[1]
    row_share = group_rows // seq_devices
    out_parts = exchange(projected_out.reshape(seq_devices, row_share, model_width), "seq", 1)
    own_rows = lax.dynamic_slice_in_dim(joined, seq_index * row_share, row_share, 0)
    after_rows = (own_rows.astype(jnp.float32) + jnp.sum(out_parts, axis=0)).astype(jnp.bfloat16)
    after_attn = exchange(after_rows, "seq", 2, gather=True).reshape(group_rows, model_width)
    second_normed_state = rms_norm(after_attn, feedforward_norm_gain)
    both = jnp.stack([after_attn, second_normed_state]).reshape(2, group_rows, req_devices, width_share)
    both_parts = exchange(jnp.transpose(both, (2, 0, 1, 3)), "req", 7)
    residual_cols = both_parts[:, 0].reshape(req_devices * group_rows, width_share)
    second_spread_state = both_parts[:, 1].reshape(req_devices * group_rows, width_share)
    units = gate_weight.shape[1]
    mlp_full = jnp.concatenate(
        [
            jnp.dot(second_spread_state, gate_weight, preferred_element_type=jnp.float32),
            jnp.dot(second_spread_state, up_weight, preferred_element_type=jnp.float32),
            jnp.dot(second_spread_state, adapter_down_map, preferred_element_type=jnp.float32),
        ],
        axis=1,
    )
    mlp_parts = exchange(mlp_full.reshape(req_devices, group_rows, mlp_full.shape[1]), "req", 8)
    mlp_sum = jnp.sum(mlp_parts, axis=0)
    gate_total = mlp_sum[:, :units]
    up_total = mlp_sum[:, units : 2 * units]
    low_sum = mlp_sum[:, 2 * units :]
    adapter_hidden = low_sum.astype(jnp.bfloat16)
    gate_preactivation = gate_total + jnp.dot(
        adapter_hidden, adapter_gate_map, preferred_element_type=jnp.float32
    )
    up_projection_part = up_total + jnp.dot(
        adapter_hidden, adapter_up_map, preferred_element_type=jnp.float32
    )
    group_act = (jax.nn.silu(gate_preactivation) * up_projection_part).astype(jnp.bfloat16)
    inner_act = exchange(group_act, "req", 9, gather=True).reshape(req_devices * group_rows, units)
    out_rows = residual_cols.shape[0] // seq_devices
    block_rows = inner_act
    down_full = jnp.dot(block_rows, down_weight, preferred_element_type=jnp.float32)
    down_parts = exchange(down_full.reshape(seq_devices, out_rows, down_full.shape[1]), "seq", 3)
    down_sum = jnp.sum(down_parts, axis=0)
    residual_rows = lax.dynamic_slice_in_dim(residual_cols, seq_index * out_rows, out_rows, 0)
    return (residual_rows.astype(jnp.float32) + down_sum).astype(jnp.bfloat16)


def solution(mesh):
    placed = (
        P(),
        P("req", None),
        P(("seq", "req"), None),
        P(),
        P("req", "seq"),
        P("seq", "req", None, None),
        P("seq", "req", None, None),
        P("req"),
        P("req", None),
        P("seq", None),
        P(),
        P("req", "seq"),
        P("req", "seq"),
        P("req", None),
        P(None, "seq"),
        P(None, "seq"),
        P("seq", "req"),
    )
    return jax.shard_map(
        body, mesh=mesh, in_specs=placed, out_specs=P("seq", "req"), check_vma=False
    )
```

```python
import functools
import math

import jax
import jax.numpy as jnp
from jax import lax
from jax.experimental import pallas as pl
from jax.experimental.pallas import tpu as pltpu
from jax.sharding import PartitionSpec as P

HEADS = 16
HD = 224


NEGATIVE = -1e30
EPSILON = 1e-05
ROTARY_BASE = 10000.0


MESH_ID = pl.DeviceIdType.MESH


def _exchange_kernel(axis, n, gather, x_ref, y_ref, send_sem, recv_sem, local_sem):
    me = lax.axis_index(axis)
    barrier = pltpu.get_barrier_semaphore()
    for k in range(1, n):
        peer = lax.rem(me + k, n)
        pl.semaphore_signal(barrier, 1, device_id={axis: peer}, device_id_type=MESH_ID)
    pl.semaphore_wait(barrier, n - 1)
    copies = []
    for k in range(1, n):
        peer = lax.rem(me + k, n)
        source = x_ref if gather else x_ref.at[peer]
        copy = pltpu.make_async_remote_copy(
            src_ref=source,
            dst_ref=y_ref.at[me],
            send_sem=send_sem.at[k],
            recv_sem=recv_sem.at[k],
            device_id={axis: peer},
            device_id_type=MESH_ID,
        )
        copy.start()
        copies.append(copy)
    local = pltpu.make_async_copy(x_ref if gather else x_ref.at[me], y_ref.at[me], local_sem)
    local.start()
    local.wait()
    for copy in copies:
        copy.wait()


def exchange(x, axis, cid, gather=False):
    n = lax.axis_size(axis)
    out_shape = (n,) + x.shape if gather else x.shape
    return pl.pallas_call(
        functools.partial(_exchange_kernel, axis, n, gather),
        out_shape=jax.ShapeDtypeStruct(out_shape, x.dtype),
        in_specs=[pl.BlockSpec(memory_space=pltpu.VMEM)],
        out_specs=pl.BlockSpec(memory_space=pltpu.VMEM),
        scratch_shapes=[
            pltpu.SemaphoreType.DMA((n,)),
            pltpu.SemaphoreType.DMA((n,)),
            pltpu.SemaphoreType.DMA(()),
        ],
        compiler_params=pltpu.CompilerParams(collective_id=cid, has_side_effects=True),
    )(x)


def merged_2(array, axis, combine):
    everything = jax.tree.map(lambda part: lax.all_gather(part, axis), array)
    first = jax.tree.map(lambda part: part[0], everything)

    def hop(k, so_far):
        return combine(so_far, jax.tree.map(lambda part: part[k], everything))

    return lax.fori_loop(1, lax.axis_size(axis), hop, first)


def rms_norm(matrix, gain_vec):
    widened = matrix.astype(jnp.float32)
    factor = lax.rsqrt(jnp.mean(widened * widened, axis=-1, keepdims=True) + EPSILON)
    return (widened * factor * gain_vec.astype(jnp.float32)).astype(jnp.bfloat16)


def rotate(vectors, positions):
    half_dim = vectors.shape[-1] // 2
    frequency = ROTARY_BASE ** (-2.0 * jnp.arange(half_dim, dtype=jnp.float32) / vectors.shape[-1])
    angles = positions.astype(jnp.float32)[..., None, None] * frequency
    cosine = jnp.cos(angles)
    sine_part = jnp.sin(angles)
    front_half = vectors[..., :half_dim]
    back_half = vectors[..., half_dim:]
    return jnp.concatenate(
        [front_half * cosine - back_half * sine_part, back_half * cosine + front_half * sine_part],
        axis=-1,
    )


def softmax_join(earlier, later):
    first_max, first_sum, first_out = earlier
    second_max, second_sum, second_out = later
    overall = jnp.maximum(first_max, second_max)
    first_factor = jnp.exp(first_max - overall)
    second_factor = jnp.exp(second_max - overall)
    return (
        overall,
        first_sum * first_factor + second_sum * second_factor,
        first_out * first_factor[..., None] + second_out * second_factor[..., None],
    )


def body(
    given_token_index,
    hidden,
    token_embedding_table,
    attention_norm_gain,
    query_key_value_weight,
    rotated_key_cache,
    cached_value_pages,
    lengths,
    request_page_slots,
    attention_output_weight,
    feedforward_norm_gain,
    gate_weight,
    up_weight,
    adapter_down_map,
    adapter_gate_map,
    adapter_up_map,
    down_weight,
):
    seq_devices = lax.axis_size("seq")
    req_devices = lax.axis_size("req")
    seq_index = lax.axis_index("seq")
    req_index = lax.axis_index("req")
    group_rows = hidden.shape[0]
    requests = lengths.shape[0]
    steps_each = group_rows // requests
    vocab_rows = token_embedding_table.shape[0]
    first_id = (seq_index * req_devices + req_index) * vocab_rows
    local_ids = given_token_index - first_id
    present = (local_ids >= 0) & (local_ids < vocab_rows)
    looked = jnp.take(token_embedding_table, jnp.clip(local_ids, 0, vocab_rows - 1), axis=0).astype(
        jnp.float32
    )
    looked = jnp.where(present[:, None], looked, 0.0).astype(jnp.bfloat16)
    by_group = exchange(looked.reshape(req_devices, group_rows, looked.shape[1]), "req", 10)
    column_part = jnp.sum(by_group.astype(jnp.float32), axis=0).astype(jnp.bfloat16)
    row_share = group_rows // seq_devices
    row_parts = exchange(column_part.reshape(seq_devices, row_share, column_part.shape[1]), "seq", 11)
    embedded_rows = jnp.sum(row_parts.astype(jnp.float32), axis=0).astype(jnp.bfloat16)
    own_hidden = lax.dynamic_slice_in_dim(hidden, seq_index * row_share, row_share, 0)
    own_rows = jnp.concatenate([own_hidden, embedded_rows], axis=1)
    normed_rows = rms_norm(own_rows, attention_norm_gain)
    normed = exchange(normed_rows, "seq", 12, gather=True).reshape(group_rows, own_rows.shape[1])
    width_share = normed.shape[1] // req_devices
    to_owners = jnp.transpose(normed.reshape(group_rows, req_devices, width_share), (1, 0, 2))
    block_rows = exchange(to_owners, "req", 4).reshape(req_devices * group_rows, width_share)
    qkv_full = jnp.dot(block_rows, query_key_value_weight, preferred_element_type=jnp.float32)
    qkv_parts = exchange(qkv_full.reshape(req_devices, group_rows, qkv_full.shape[1]), "req", 5)
    qkv_part = jnp.sum(qkv_parts, axis=0).astype(jnp.bfloat16)
    qkv_all = exchange(qkv_part, "seq", 6, gather=True)
    projected = jnp.transpose(qkv_all, (1, 0, 2)).reshape(group_rows, seq_devices * qkv_part.shape[1])
    head_cols = HEADS * HD
    queries = projected[:, :head_cols].reshape(requests, steps_each, HEADS, HD)
    new_keys = projected[:, head_cols : 2 * head_cols].reshape(requests, steps_each, HEADS, HD)
    new_values = projected[:, 2 * head_cols :].reshape(requests, steps_each, HEADS, HD)
    positions = lengths[:, None] + jnp.arange(steps_each, dtype=jnp.int32)[None, :]
    queries = rotate(queries.astype(jnp.float32), positions).astype(jnp.bfloat16)
    new_keys = rotate(new_keys.astype(jnp.float32), positions).astype(jnp.bfloat16)
    slots = rotated_key_cache.shape[0]
    page_len = rotated_key_cache.shape[2]
    cache_k = rotated_key_cache.reshape(slots * page_len, head_cols)
    cache_v = cached_value_pages.reshape(slots * page_len, head_cols)
    slot_ids = seq_index * slots + jnp.arange(slots, dtype=jnp.int32)
    page_ids = jnp.arange(request_page_slots.shape[1], dtype=jnp.int32)
    is_live = page_ids[None, :] < ((lengths + page_len - 1) // page_len)[:, None]
    matches = (request_page_slots[:, :, None] == slot_ids[None, None, :]) & is_live[:, :, None]
    is_owned = jnp.any(matches, axis=1)
    page_of = jnp.sum(jnp.where(matches, page_ids[None, :, None], 0), axis=1)
    token_pos = (
        page_of[:, :, None] * page_len + jnp.arange(page_len, dtype=jnp.int32)[None, None, :]
    )
    is_valid = (is_owned[:, :, None] & (token_pos < lengths[:, None, None])).reshape(
        requests, slots * page_len
    )
    score_scale = 1.0 / math.sqrt(HD)
    head_mask = (jnp.arange(head_cols, dtype=jnp.int32)[None, :] // HD) == jnp.arange(
        HEADS, dtype=jnp.int32
    )[:, None]
    query_rows = queries.reshape(group_rows, head_cols)
    spread_queries = jnp.where(head_mask[None], query_rows[:, None, :], jnp.zeros((), jnp.bfloat16))
    scores = (
        jnp.dot(
            spread_queries.reshape(group_rows * HEADS, head_cols),
            cache_k.T,
            preferred_element_type=jnp.float32,
        )
        * score_scale
    ).reshape(requests, steps_each, HEADS, slots * page_len)
    mask_b = is_valid[:, None, None, :]
    local_max = jnp.max(jnp.where(mask_b, scores, NEGATIVE), axis=-1)
    weights = jnp.where(mask_b, jnp.exp(scores - local_max[..., None]), 0.0)
    local_sum = jnp.sum(weights, axis=-1)
    spread_out = jnp.dot(
        weights.astype(jnp.bfloat16).reshape(group_rows * HEADS, slots * page_len),
        cache_v,
        preferred_element_type=jnp.float32,
    ).reshape(group_rows, HEADS, head_cols)
    local_out = jnp.sum(jnp.where(head_mask[None], spread_out, 0.0), axis=1).reshape(
        requests, steps_each, HEADS, HD
    )
    fresh_scores = (
        jnp.einsum("rthd,rshd->rths", queries, new_keys, preferred_element_type=jnp.float32)
        * score_scale
    )
    causal = jnp.arange(steps_each)[:, None] >= jnp.arange(steps_each)[None, :]
    fresh_mask = causal[None, :, None, :]
    fresh_max = jnp.max(jnp.where(fresh_mask, fresh_scores, NEGATIVE), axis=-1)
    fresh_w = jnp.where(fresh_mask, jnp.exp(fresh_scores - fresh_max[..., None]), 0.0)
    fresh_sum = jnp.sum(fresh_w, axis=-1)
    fresh_out = jnp.einsum(
        "rths,rshd->rthd",
        fresh_w.astype(jnp.bfloat16),
        new_values,
        preferred_element_type=jnp.float32,
    )
    own_heads = HEADS // seq_devices
    first_head = seq_index * own_heads

    def own_slice(member):
        return lax.dynamic_slice_in_dim(member, first_head, own_heads, 2)

    pad_cols = 256 - HD - 2
    packed = jnp.concatenate(
        [
            local_out,
            local_max[..., None],
            local_sum[..., None],
            jnp.zeros(local_out.shape[:-1] + (pad_cols,), jnp.float32),
        ],
        axis=-1,
    )
    packed = packed.reshape(requests * steps_each, seq_devices, own_heads, 256)
    packed = jnp.transpose(packed, (1, 0, 2, 3)).reshape(seq_devices, group_rows * own_heads, 256)
    arrived = exchange(packed, "seq", 0).reshape(seq_devices, requests, steps_each, own_heads, 256)
    part_o = arrived[..., :HD]
    part_m = arrived[..., HD]
    part_l = arrived[..., HD + 1]
    f_max, f_sum, f_out = own_slice(fresh_max), own_slice(fresh_sum), own_slice(fresh_out)
    overall = jnp.maximum(jnp.max(part_m, axis=0), f_max)
    part_factor = jnp.exp(part_m - overall[None])
    fresh_factor = jnp.exp(f_max - overall)
    denominator = jnp.sum(part_l * part_factor, axis=0) + f_sum * fresh_factor
    numerator = jnp.sum(part_o * part_factor[..., None], axis=0) + f_out * fresh_factor[..., None]
    attention = (
        (numerator / denominator[..., None])
        .astype(jnp.bfloat16)
        .reshape(group_rows, own_heads * HD)
    )
    projected_out = jnp.dot(attention, attention_output_weight, preferred_element_type=jnp.float32)
    model_width = projected_out.shape[1]
    out_parts = exchange(projected_out.reshape(seq_devices, row_share, model_width), "seq", 1)
    after_rows = (own_rows.astype(jnp.float32) + jnp.sum(out_parts, axis=0)).astype(jnp.bfloat16)
    after_attn = exchange(after_rows, "seq", 2, gather=True).reshape(group_rows, model_width)
    second_normed_state = rms_norm(after_attn, feedforward_norm_gain)
    both = jnp.stack([after_attn, second_normed_state]).reshape(2, group_rows, req_devices, width_share)
    both_parts = exchange(jnp.transpose(both, (2, 0, 1, 3)), "req", 7)
    residual_cols = both_parts[:, 0].reshape(req_devices * group_rows, width_share)
    second_spread_state = both_parts[:, 1].reshape(req_devices * group_rows, width_share)
    units = gate_weight.shape[1]
    mlp_full = jnp.concatenate(
        [
            jnp.dot(second_spread_state, gate_weight, preferred_element_type=jnp.float32),
            jnp.dot(second_spread_state, up_weight, preferred_element_type=jnp.float32),
            jnp.dot(second_spread_state, adapter_down_map, preferred_element_type=jnp.float32),
        ],
        axis=1,
    )
    mlp_parts = exchange(mlp_full.reshape(req_devices, group_rows, mlp_full.shape[1]), "req", 8)
    mlp_sum = jnp.sum(mlp_parts, axis=0)
    gate_total = mlp_sum[:, :units]
    up_total = mlp_sum[:, units : 2 * units]
    low_sum = mlp_sum[:, 2 * units :]
    adapter_hidden = low_sum.astype(jnp.bfloat16)
    gate_preactivation = gate_total + jnp.dot(
        adapter_hidden, adapter_gate_map, preferred_element_type=jnp.float32
    )
    up_projection_part = up_total + jnp.dot(
        adapter_hidden, adapter_up_map, preferred_element_type=jnp.float32
    )
    group_act = (jax.nn.silu(gate_preactivation) * up_projection_part).astype(jnp.bfloat16)
    inner_act = exchange(group_act, "req", 9, gather=True).reshape(req_devices * group_rows, units)
    out_rows = residual_cols.shape[0] // seq_devices
    block_rows = inner_act
    down_full = jnp.dot(block_rows, down_weight, preferred_element_type=jnp.float32)
    down_parts = exchange(down_full.reshape(seq_devices, out_rows, down_full.shape[1]), "seq", 3)
    down_sum = jnp.sum(down_parts, axis=0)
    residual_rows = lax.dynamic_slice_in_dim(residual_cols, seq_index * out_rows, out_rows, 0)
    return (residual_rows.astype(jnp.float32) + down_sum).astype(jnp.bfloat16)


def solution(mesh):
    placed = (
        P(),
        P("req", None),
        P(("seq", "req"), None),
        P(),
        P("req", "seq"),
        P("seq", "req", None, None),
        P("seq", "req", None, None),
        P("req"),
        P("req", None),
        P("seq", None),
        P(),
        P("req", "seq"),
        P("req", "seq"),
        P("req", None),
        P(None, "seq"),
        P(None, "seq"),
        P("seq", "req"),
    )
    return jax.shard_map(
        body, mesh=mesh, in_specs=placed, out_specs=P("seq", "req"), check_vma=False
    )
```

```python
import functools
import math

import jax
import jax.numpy as jnp
from jax import lax
from jax.experimental import pallas as pl
from jax.experimental.pallas import tpu as pltpu
from jax.sharding import PartitionSpec as P

HEADS = 16
HD = 224


NEGATIVE = -1e30
EPSILON = 1e-05
ROTARY_BASE = 10000.0


MESH_ID = pl.DeviceIdType.MESH


def _exchange_kernel(axis, n, gather, x_ref, y_ref, send_sem, recv_sem, local_sem):
    me = lax.axis_index(axis)
    barrier = pltpu.get_barrier_semaphore()
    for k in range(1, n):
        peer = lax.rem(me + k, n)
        pl.semaphore_signal(barrier, 1, device_id={axis: peer}, device_id_type=MESH_ID)
    pl.semaphore_wait(barrier, n - 1)
    copies = []
    for k in range(1, n):
        peer = lax.rem(me + k, n)
        source = x_ref if gather else x_ref.at[peer]
        copy = pltpu.make_async_remote_copy(
            src_ref=source,
            dst_ref=y_ref.at[me],
            send_sem=send_sem.at[k],
            recv_sem=recv_sem.at[k],
            device_id={axis: peer},
            device_id_type=MESH_ID,
        )
        copy.start()
        copies.append(copy)
    local = pltpu.make_async_copy(x_ref if gather else x_ref.at[me], y_ref.at[me], local_sem)
    local.start()
    local.wait()
    for copy in copies:
        copy.wait()


def exchange(x, axis, cid, gather=False):
    n = lax.axis_size(axis)
    out_shape = (n,) + x.shape if gather else x.shape
    return pl.pallas_call(
        functools.partial(_exchange_kernel, axis, n, gather),
        out_shape=jax.ShapeDtypeStruct(out_shape, x.dtype),
        in_specs=[pl.BlockSpec(memory_space=pltpu.VMEM)],
        out_specs=pl.BlockSpec(memory_space=pltpu.VMEM),
        scratch_shapes=[
            pltpu.SemaphoreType.DMA((n,)),
            pltpu.SemaphoreType.DMA((n,)),
            pltpu.SemaphoreType.DMA(()),
        ],
        compiler_params=pltpu.CompilerParams(collective_id=cid, has_side_effects=True),
    )(x)


def _greet(axes_sizes):
    barrier = pltpu.get_barrier_semaphore()
    total = 0
    for axis, n in axes_sizes:
        me = lax.axis_index(axis)
        for k in range(1, n):
            peer = lax.rem(me + k, n)
            pl.semaphore_signal(barrier, 1, device_id={axis: peer}, device_id_type=MESH_ID)
        total += n - 1
    pl.semaphore_wait(barrier, total)


def _start_round(axis, n, gather, source, target, send_sem, recv_sem, local_sem):
    me = lax.axis_index(axis)
    copies = []
    for k in range(1, n):
        peer = lax.rem(me + k, n)
        copy = pltpu.make_async_remote_copy(
            src_ref=source if gather else source.at[peer],
            dst_ref=target.at[me],
            send_sem=send_sem.at[k],
            recv_sem=recv_sem.at[k],
            device_id={axis: peer},
            device_id_type=MESH_ID,
        )
        copy.start()
        copies.append(copy)
    local = pltpu.make_async_copy(source if gather else source.at[me], target.at[me], local_sem)
    local.start()
    copies.append(local)
    return copies


def _two_round_kernel(first, second, mid, n_extra, x_ref, *refs):
    extra = refs[:n_extra]
    y_ref, landed, staged, send_a, recv_a, send_b, recv_b, local_sems = refs[n_extra:]
    axis_a, n_a, gather_a = first
    axis_b, n_b, gather_b = second
    greeted = [(axis_a, n_a)] if axis_a == axis_b else [(axis_a, n_a), (axis_b, n_b)]
    _greet(greeted)
    for copy in _start_round(axis_a, n_a, gather_a, x_ref, landed, send_a, recv_a, local_sems.at[0]):
        copy.wait()
    staged[...] = mid(landed, *extra)
    for copy in _start_round(axis_b, n_b, gather_b, staged, y_ref, send_b, recv_b, local_sems.at[1]):
        copy.wait()


def two_rounds(x, first, second, mid, staged_shape, staged_dtype, cid, extra=()):
    axis_a, gather_a = first
    axis_b, gather_b = second
    n_a, n_b = lax.axis_size(axis_a), lax.axis_size(axis_b)
    landed_shape = (n_a,) + x.shape if gather_a else x.shape
    out_shape = (n_b,) + staged_shape if gather_b else staged_shape
    return pl.pallas_call(
        functools.partial(
            _two_round_kernel, (axis_a, n_a, gather_a), (axis_b, n_b, gather_b), mid, len(extra)
        ),
        out_shape=jax.ShapeDtypeStruct(out_shape, staged_dtype),
        in_specs=[pl.BlockSpec(memory_space=pltpu.VMEM)] * (1 + len(extra)),
        out_specs=pl.BlockSpec(memory_space=pltpu.VMEM),
        scratch_shapes=[
            pltpu.VMEM(landed_shape, x.dtype),
            pltpu.VMEM(staged_shape, staged_dtype),
            pltpu.SemaphoreType.DMA((n_a,)),
            pltpu.SemaphoreType.DMA((n_a,)),
            pltpu.SemaphoreType.DMA((n_b,)),
            pltpu.SemaphoreType.DMA((n_b,)),
            pltpu.SemaphoreType.DMA((2,)),
        ],
        compiler_params=pltpu.CompilerParams(collective_id=cid, has_side_effects=True),
    )(x, *extra)


def _block_sum(landed):
    total = landed[0].astype(jnp.float32)
    for k in range(1, landed.shape[0]):
        total = total + landed[k].astype(jnp.float32)
    return total


def merged_2(array, axis, combine):
    everything = jax.tree.map(lambda part: lax.all_gather(part, axis), array)
    first = jax.tree.map(lambda part: part[0], everything)

    def hop(k, so_far):
        return combine(so_far, jax.tree.map(lambda part: part[k], everything))

    return lax.fori_loop(1, lax.axis_size(axis), hop, first)


def rms_norm(matrix, gain_vec):
    widened = matrix.astype(jnp.float32)
    factor = lax.rsqrt(jnp.mean(widened * widened, axis=-1, keepdims=True) + EPSILON)
    return (widened * factor * gain_vec.astype(jnp.float32)).astype(jnp.bfloat16)


def rotate(vectors, positions):
    half_dim = vectors.shape[-1] // 2
    frequency = ROTARY_BASE ** (-2.0 * jnp.arange(half_dim, dtype=jnp.float32) / vectors.shape[-1])
    angles = positions.astype(jnp.float32)[..., None, None] * frequency
    cosine = jnp.cos(angles)
    sine_part = jnp.sin(angles)
    front_half = vectors[..., :half_dim]
    back_half = vectors[..., half_dim:]
    return jnp.concatenate(
        [front_half * cosine - back_half * sine_part, back_half * cosine + front_half * sine_part],
        axis=-1,
    )


def softmax_join(earlier, later):
    first_max, first_sum, first_out = earlier
    second_max, second_sum, second_out = later
    overall = jnp.maximum(first_max, second_max)
    first_factor = jnp.exp(first_max - overall)
    second_factor = jnp.exp(second_max - overall)
    return (
        overall,
        first_sum * first_factor + second_sum * second_factor,
        first_out * first_factor[..., None] + second_out * second_factor[..., None],
    )


def body(
    given_token_index,
    hidden,
    token_embedding_table,
    attention_norm_gain,
    query_key_value_weight,
    rotated_key_cache,
    cached_value_pages,
    lengths,
    request_page_slots,
    attention_output_weight,
    feedforward_norm_gain,
    gate_weight,
    up_weight,
    adapter_down_map,
    adapter_gate_map,
    adapter_up_map,
    down_weight,
):
    seq_devices = lax.axis_size("seq")
    req_devices = lax.axis_size("req")
    seq_index = lax.axis_index("seq")
    req_index = lax.axis_index("req")
    group_rows = hidden.shape[0]
    requests = lengths.shape[0]
    steps_each = group_rows // requests
    vocab_rows = token_embedding_table.shape[0]
    first_id = (seq_index * req_devices + req_index) * vocab_rows
    local_ids = given_token_index - first_id
    present = (local_ids >= 0) & (local_ids < vocab_rows)
    looked = jnp.take(token_embedding_table, jnp.clip(local_ids, 0, vocab_rows - 1), axis=0).astype(
        jnp.float32
    )
    looked = jnp.where(present[:, None], looked, 0.0).astype(jnp.bfloat16)
    row_share = group_rows // seq_devices
    by_group = looked.reshape(req_devices, seq_devices, row_share, looked.shape[1])
    row_parts = two_rounds(
        by_group,
        ("req", False),
        ("seq", False),
        lambda landed: _block_sum(landed).astype(jnp.bfloat16),
        by_group.shape[1:],
        jnp.bfloat16,
        10,
    )
    embedded_rows = jnp.sum(row_parts.astype(jnp.float32), axis=0).astype(jnp.bfloat16)
    own_hidden = lax.dynamic_slice_in_dim(hidden, seq_index * row_share, row_share, 0)
    own_rows = jnp.concatenate([own_hidden, embedded_rows], axis=1)
    normed_rows = rms_norm(own_rows, attention_norm_gain)
    normed = exchange(normed_rows, "seq", 12, gather=True).reshape(group_rows, own_rows.shape[1])
    width_share = normed.shape[1] // req_devices
    to_owners = jnp.transpose(normed.reshape(group_rows, req_devices, width_share), (1, 0, 2))
    block_rows = exchange(to_owners, "req", 4).reshape(req_devices * group_rows, width_share)
    qkv_full = jnp.dot(block_rows, query_key_value_weight, preferred_element_type=jnp.float32)
    qkv_all = two_rounds(
        qkv_full.reshape(req_devices, group_rows, qkv_full.shape[1]),
        ("req", False),
        ("seq", True),
        lambda landed: _block_sum(landed).astype(jnp.bfloat16),
        (group_rows, qkv_full.shape[1]),
        jnp.bfloat16,
        5,
    )
    projected = jnp.transpose(qkv_all, (1, 0, 2)).reshape(group_rows, seq_devices * qkv_all.shape[2])
    head_cols = HEADS * HD
    queries = projected[:, :head_cols].reshape(requests, steps_each, HEADS, HD)
    new_keys = projected[:, head_cols : 2 * head_cols].reshape(requests, steps_each, HEADS, HD)
    new_values = projected[:, 2 * head_cols :].reshape(requests, steps_each, HEADS, HD)
    positions = lengths[:, None] + jnp.arange(steps_each, dtype=jnp.int32)[None, :]
    queries = rotate(queries.astype(jnp.float32), positions).astype(jnp.bfloat16)
    new_keys = rotate(new_keys.astype(jnp.float32), positions).astype(jnp.bfloat16)
    slots = rotated_key_cache.shape[0]
    page_len = rotated_key_cache.shape[2]
    cache_k = rotated_key_cache.reshape(slots * page_len, head_cols)
    cache_v = cached_value_pages.reshape(slots * page_len, head_cols)
    slot_ids = seq_index * slots + jnp.arange(slots, dtype=jnp.int32)
    page_ids = jnp.arange(request_page_slots.shape[1], dtype=jnp.int32)
    is_live = page_ids[None, :] < ((lengths + page_len - 1) // page_len)[:, None]
    matches = (request_page_slots[:, :, None] == slot_ids[None, None, :]) & is_live[:, :, None]
    is_owned = jnp.any(matches, axis=1)
    page_of = jnp.sum(jnp.where(matches, page_ids[None, :, None], 0), axis=1)
    token_pos = (
        page_of[:, :, None] * page_len + jnp.arange(page_len, dtype=jnp.int32)[None, None, :]
    )
    is_valid = (is_owned[:, :, None] & (token_pos < lengths[:, None, None])).reshape(
        requests, slots * page_len
    )
    score_scale = 1.0 / math.sqrt(HD)
    head_mask = (jnp.arange(head_cols, dtype=jnp.int32)[None, :] // HD) == jnp.arange(
        HEADS, dtype=jnp.int32
    )[:, None]
    query_rows = queries.reshape(group_rows, head_cols)
    spread_queries = jnp.where(head_mask[None], query_rows[:, None, :], jnp.zeros((), jnp.bfloat16))
    scores = (
        jnp.dot(
            spread_queries.reshape(group_rows * HEADS, head_cols),
            cache_k.T,
            preferred_element_type=jnp.float32,
        )
        * score_scale
    ).reshape(requests, steps_each, HEADS, slots * page_len)
    mask_b = is_valid[:, None, None, :]
    local_max = jnp.max(jnp.where(mask_b, scores, NEGATIVE), axis=-1)
    weights = jnp.where(mask_b, jnp.exp(scores - local_max[..., None]), 0.0)
    local_sum = jnp.sum(weights, axis=-1)
    spread_out = jnp.dot(
        weights.astype(jnp.bfloat16).reshape(group_rows * HEADS, slots * page_len),
        cache_v,
        preferred_element_type=jnp.float32,
    ).reshape(group_rows, HEADS, head_cols)
    local_out = jnp.sum(jnp.where(head_mask[None], spread_out, 0.0), axis=1).reshape(
        requests, steps_each, HEADS, HD
    )
    fresh_scores = (
        jnp.einsum("rthd,rshd->rths", queries, new_keys, preferred_element_type=jnp.float32)
        * score_scale
    )
    causal = jnp.arange(steps_each)[:, None] >= jnp.arange(steps_each)[None, :]
    fresh_mask = causal[None, :, None, :]
    fresh_max = jnp.max(jnp.where(fresh_mask, fresh_scores, NEGATIVE), axis=-1)
    fresh_w = jnp.where(fresh_mask, jnp.exp(fresh_scores - fresh_max[..., None]), 0.0)
    fresh_sum = jnp.sum(fresh_w, axis=-1)
    fresh_out = jnp.einsum(
        "rths,rshd->rthd",
        fresh_w.astype(jnp.bfloat16),
        new_values,
        preferred_element_type=jnp.float32,
    )
    own_heads = HEADS // seq_devices
    first_head = seq_index * own_heads

    def own_slice(member):
        return lax.dynamic_slice_in_dim(member, first_head, own_heads, 2)

    pad_cols = 256 - HD - 2
    packed = jnp.concatenate(
        [
            local_out,
            local_max[..., None],
            local_sum[..., None],
            jnp.zeros(local_out.shape[:-1] + (pad_cols,), jnp.float32),
        ],
        axis=-1,
    )
    packed = packed.reshape(requests * steps_each, seq_devices, own_heads, 256)
    packed = jnp.transpose(packed, (1, 0, 2, 3)).reshape(seq_devices, group_rows * own_heads, 256)
    arrived = exchange(packed, "seq", 0).reshape(seq_devices, requests, steps_each, own_heads, 256)
    part_o = arrived[..., :HD]
    part_m = arrived[..., HD]
    part_l = arrived[..., HD + 1]
    f_max, f_sum, f_out = own_slice(fresh_max), own_slice(fresh_sum), own_slice(fresh_out)
    overall = jnp.maximum(jnp.max(part_m, axis=0), f_max)
    part_factor = jnp.exp(part_m - overall[None])
    fresh_factor = jnp.exp(f_max - overall)
    denominator = jnp.sum(part_l * part_factor, axis=0) + f_sum * fresh_factor
    numerator = jnp.sum(part_o * part_factor[..., None], axis=0) + f_out * fresh_factor[..., None]
    attention = (
        (numerator / denominator[..., None])
        .astype(jnp.bfloat16)
        .reshape(group_rows, own_heads * HD)
    )
    projected_out = jnp.dot(attention, attention_output_weight, preferred_element_type=jnp.float32)
    model_width = projected_out.shape[1]
    after_attn = two_rounds(
        projected_out.reshape(seq_devices, row_share, model_width),
        ("seq", False),
        ("seq", True),
        lambda landed, own: (own[...].astype(jnp.float32) + _block_sum(landed)).astype(jnp.bfloat16),
        (row_share, model_width),
        jnp.bfloat16,
        1,
        extra=(own_rows,),
    ).reshape(group_rows, model_width)
    second_normed_state = rms_norm(after_attn, feedforward_norm_gain)
    both = jnp.stack([after_attn, second_normed_state]).reshape(2, group_rows, req_devices, width_share)
    both_parts = exchange(jnp.transpose(both, (2, 0, 1, 3)), "req", 7)
    residual_cols = both_parts[:, 0].reshape(req_devices * group_rows, width_share)
    second_spread_state = both_parts[:, 1].reshape(req_devices * group_rows, width_share)
    units = gate_weight.shape[1]
    mlp_full = jnp.concatenate(
        [
            jnp.dot(second_spread_state, gate_weight, preferred_element_type=jnp.float32),
            jnp.dot(second_spread_state, up_weight, preferred_element_type=jnp.float32),
            jnp.dot(second_spread_state, adapter_down_map, preferred_element_type=jnp.float32),
        ],
        axis=1,
    )
    def activate(landed, gate_map, up_map):
        total = _block_sum(landed)
        low = total[:, 2 * units :].astype(jnp.bfloat16)
        gate_pre = total[:, :units] + jnp.dot(low, gate_map[...], preferred_element_type=jnp.float32)
        up_part = total[:, units : 2 * units] + jnp.dot(
            low, up_map[...], preferred_element_type=jnp.float32
        )
        return (gate_pre / (1.0 + jnp.exp(-gate_pre)) * up_part).astype(jnp.bfloat16)

    inner_act = two_rounds(
        mlp_full.reshape(req_devices, group_rows, mlp_full.shape[1]),
        ("req", False),
        ("req", True),
        activate,
        (group_rows, units),
        jnp.bfloat16,
        8,
        extra=(adapter_gate_map, adapter_up_map),
    ).reshape(req_devices * group_rows, units)
    out_rows = residual_cols.shape[0] // seq_devices
    block_rows = inner_act
    down_full = jnp.dot(block_rows, down_weight, preferred_element_type=jnp.float32)
    down_parts = exchange(down_full.reshape(seq_devices, out_rows, down_full.shape[1]), "seq", 3)
    down_sum = jnp.sum(down_parts, axis=0)
    residual_rows = lax.dynamic_slice_in_dim(residual_cols, seq_index * out_rows, out_rows, 0)
    return (residual_rows.astype(jnp.float32) + down_sum).astype(jnp.bfloat16)


def solution(mesh):
    placed = (
        P(),
        P("req", None),
        P(("seq", "req"), None),
        P(),
        P("req", "seq"),
        P("seq", "req", None, None),
        P("seq", "req", None, None),
        P("req"),
        P("req", None),
        P("seq", None),
        P(),
        P("req", "seq"),
        P("req", "seq"),
        P("req", None),
        P(None, "seq"),
        P(None, "seq"),
        P("seq", "req"),
    )
    return jax.shard_map(
        body, mesh=mesh, in_specs=placed, out_specs=P("seq", "req"), check_vma=False
    )
```

```python
import functools
import math

import jax
import jax.numpy as jnp
from jax import lax
from jax.experimental import pallas as pl
from jax.experimental.pallas import tpu as pltpu
from jax.sharding import PartitionSpec as P

HEADS = 16
HD = 224


NEGATIVE = -1e30
EPSILON = 1e-05
ROTARY_BASE = 10000.0


MESH_ID = pl.DeviceIdType.MESH


def _exchange_kernel(axis, n, gather, x_ref, y_ref, send_sem, recv_sem, local_sem):
    me = lax.axis_index(axis)
    barrier = pltpu.get_barrier_semaphore()
    for k in range(1, n):
        peer = lax.rem(me + k, n)
        pl.semaphore_signal(barrier, 1, device_id={axis: peer}, device_id_type=MESH_ID)
    pl.semaphore_wait(barrier, n - 1)
    copies = []
    for k in range(1, n):
        peer = lax.rem(me + k, n)
        source = x_ref if gather else x_ref.at[peer]
        copy = pltpu.make_async_remote_copy(
            src_ref=source,
            dst_ref=y_ref.at[me],
            send_sem=send_sem.at[k],
            recv_sem=recv_sem.at[k],
            device_id={axis: peer},
            device_id_type=MESH_ID,
        )
        copy.start()
        copies.append(copy)
    local = pltpu.make_async_copy(x_ref if gather else x_ref.at[me], y_ref.at[me], local_sem)
    local.start()
    local.wait()
    for copy in copies:
        copy.wait()


def exchange(x, axis, cid, gather=False):
    n = lax.axis_size(axis)
    out_shape = (n,) + x.shape if gather else x.shape
    return pl.pallas_call(
        functools.partial(_exchange_kernel, axis, n, gather),
        out_shape=jax.ShapeDtypeStruct(out_shape, x.dtype),
        in_specs=[pl.BlockSpec(memory_space=pltpu.VMEM)],
        out_specs=pl.BlockSpec(memory_space=pltpu.VMEM),
        scratch_shapes=[
            pltpu.SemaphoreType.DMA((n,)),
            pltpu.SemaphoreType.DMA((n,)),
            pltpu.SemaphoreType.DMA(()),
        ],
        compiler_params=pltpu.CompilerParams(collective_id=cid, has_side_effects=True),
    )(x)


def _greet(axes_sizes):
    barrier = pltpu.get_barrier_semaphore()
    total = 0
    for axis, n in axes_sizes:
        me = lax.axis_index(axis)
        for k in range(1, n):
            peer = lax.rem(me + k, n)
            pl.semaphore_signal(barrier, 1, device_id={axis: peer}, device_id_type=MESH_ID)
        total += n - 1
    pl.semaphore_wait(barrier, total)


def _start_round(axis, n, gather, source, target, send_sem, recv_sem, local_sem):
    me = lax.axis_index(axis)
    copies = []
    for k in range(1, n):
        peer = lax.rem(me + k, n)
        copy = pltpu.make_async_remote_copy(
            src_ref=source if gather else source.at[peer],
            dst_ref=target.at[me],
            send_sem=send_sem.at[k],
            recv_sem=recv_sem.at[k],
            device_id={axis: peer},
            device_id_type=MESH_ID,
        )
        copy.start()
        copies.append(copy)
    local = pltpu.make_async_copy(source if gather else source.at[me], target.at[me], local_sem)
    local.start()
    copies.append(local)
    return copies


def _two_round_kernel(first, second, mid, n_extra, x_ref, *refs):
    extra = refs[:n_extra]
    y_ref, landed, staged, send_a, recv_a, send_b, recv_b, local_sems = refs[n_extra:]
    axis_a, n_a, gather_a = first
    axis_b, n_b, gather_b = second
    greeted = [(axis_a, n_a)] if axis_a == axis_b else [(axis_a, n_a), (axis_b, n_b)]
    _greet(greeted)
    for copy in _start_round(axis_a, n_a, gather_a, x_ref, landed, send_a, recv_a, local_sems.at[0]):
        copy.wait()
    staged[...] = mid(landed, *extra)
    for copy in _start_round(axis_b, n_b, gather_b, staged, y_ref, send_b, recv_b, local_sems.at[1]):
        copy.wait()


def two_rounds(x, first, second, mid, staged_shape, staged_dtype, cid, extra=()):
    axis_a, gather_a = first
    axis_b, gather_b = second
    n_a, n_b = lax.axis_size(axis_a), lax.axis_size(axis_b)
    landed_shape = (n_a,) + x.shape if gather_a else x.shape
    out_shape = (n_b,) + staged_shape if gather_b else staged_shape
    return pl.pallas_call(
        functools.partial(
            _two_round_kernel, (axis_a, n_a, gather_a), (axis_b, n_b, gather_b), mid, len(extra)
        ),
        out_shape=jax.ShapeDtypeStruct(out_shape, staged_dtype),
        in_specs=[pl.BlockSpec(memory_space=pltpu.VMEM)] * (1 + len(extra)),
        out_specs=pl.BlockSpec(memory_space=pltpu.VMEM),
        scratch_shapes=[
            pltpu.VMEM(landed_shape, x.dtype),
            pltpu.VMEM(staged_shape, staged_dtype),
            pltpu.SemaphoreType.DMA((n_a,)),
            pltpu.SemaphoreType.DMA((n_a,)),
            pltpu.SemaphoreType.DMA((n_b,)),
            pltpu.SemaphoreType.DMA((n_b,)),
            pltpu.SemaphoreType.DMA((2,)),
        ],
        compiler_params=pltpu.CompilerParams(collective_id=cid, has_side_effects=True),
    )(x, *extra)


def _block_sum(landed):
    total = landed[0].astype(jnp.float32)
    for k in range(1, landed.shape[0]):
        total = total + landed[k].astype(jnp.float32)
    return total


def merged_2(array, axis, combine):
    everything = jax.tree.map(lambda part: lax.all_gather(part, axis), array)
    first = jax.tree.map(lambda part: part[0], everything)

    def hop(k, so_far):
        return combine(so_far, jax.tree.map(lambda part: part[k], everything))

    return lax.fori_loop(1, lax.axis_size(axis), hop, first)


def rms_norm(matrix, gain_vec):
    widened = matrix.astype(jnp.float32)
    factor = lax.rsqrt(jnp.mean(widened * widened, axis=-1, keepdims=True) + EPSILON)
    return (widened * factor * gain_vec.astype(jnp.float32)).astype(jnp.bfloat16)


def rotate(vectors, positions):
    half_dim = vectors.shape[-1] // 2
    frequency = ROTARY_BASE ** (-2.0 * jnp.arange(half_dim, dtype=jnp.float32) / vectors.shape[-1])
    angles = positions.astype(jnp.float32)[..., None, None] * frequency
    cosine = jnp.cos(angles)
    sine_part = jnp.sin(angles)
    front_half = vectors[..., :half_dim]
    back_half = vectors[..., half_dim:]
    return jnp.concatenate(
        [front_half * cosine - back_half * sine_part, back_half * cosine + front_half * sine_part],
        axis=-1,
    )


def softmax_join(earlier, later):
    first_max, first_sum, first_out = earlier
    second_max, second_sum, second_out = later
    overall = jnp.maximum(first_max, second_max)
    first_factor = jnp.exp(first_max - overall)
    second_factor = jnp.exp(second_max - overall)
    return (
        overall,
        first_sum * first_factor + second_sum * second_factor,
        first_out * first_factor[..., None] + second_out * second_factor[..., None],
    )


def body(
    given_token_index,
    hidden,
    token_embedding_table,
    attention_norm_gain,
    query_key_value_weight,
    rotated_key_cache,
    cached_value_pages,
    lengths,
    request_page_slots,
    attention_output_weight,
    feedforward_norm_gain,
    gate_weight,
    up_weight,
    adapter_down_map,
    adapter_gate_map,
    adapter_up_map,
    down_weight,
):
    seq_devices = lax.axis_size("seq")
    req_devices = lax.axis_size("req")
    seq_index = lax.axis_index("seq")
    req_index = lax.axis_index("req")
    group_rows = hidden.shape[0]
    requests = lengths.shape[0]
    steps_each = group_rows // requests
    vocab_rows = token_embedding_table.shape[0]
    first_id = (seq_index * req_devices + req_index) * vocab_rows
    local_ids = given_token_index - first_id
    present = (local_ids >= 0) & (local_ids < vocab_rows)
    looked = jnp.take(token_embedding_table, jnp.clip(local_ids, 0, vocab_rows - 1), axis=0).astype(
        jnp.float32
    )
    looked = jnp.where(present[:, None], looked, 0.0).astype(jnp.bfloat16)
    row_share = group_rows // seq_devices
    lanes = 128
    by_group = looked.reshape(req_devices, seq_devices, row_share * looked.shape[1] // lanes, lanes)
    row_parts = two_rounds(
        by_group,
        ("req", False),
        ("seq", False),
        lambda landed: _block_sum(landed).astype(jnp.bfloat16),
        by_group.shape[1:],
        jnp.bfloat16,
        10,
    )
    embedded_rows = (
        jnp.sum(row_parts.astype(jnp.float32), axis=0)
        .astype(jnp.bfloat16)
        .reshape(row_share, looked.shape[1])
    )
    own_hidden = lax.dynamic_slice_in_dim(hidden, seq_index * row_share, row_share, 0)
    own_rows = jnp.concatenate([own_hidden, embedded_rows], axis=1)
    normed_rows = rms_norm(own_rows, attention_norm_gain)
    normed = exchange(normed_rows.reshape(-1, lanes), "seq", 12, gather=True).reshape(
        group_rows, own_rows.shape[1]
    )
    width_share = normed.shape[1] // req_devices
    to_owners = jnp.transpose(normed.reshape(group_rows, req_devices, width_share), (1, 0, 2))
    block_rows = exchange(to_owners, "req", 4).reshape(req_devices * group_rows, width_share)
    qkv_full = jnp.dot(block_rows, query_key_value_weight, preferred_element_type=jnp.float32)
    qkv_all = two_rounds(
        qkv_full.reshape(req_devices, group_rows, qkv_full.shape[1]),
        ("req", False),
        ("seq", True),
        lambda landed: _block_sum(landed).astype(jnp.bfloat16),
        (group_rows, qkv_full.shape[1]),
        jnp.bfloat16,
        5,
    )
    projected = jnp.transpose(qkv_all, (1, 0, 2)).reshape(group_rows, seq_devices * qkv_all.shape[2])
    head_cols = HEADS * HD
    queries = projected[:, :head_cols].reshape(requests, steps_each, HEADS, HD)
    new_keys = projected[:, head_cols : 2 * head_cols].reshape(requests, steps_each, HEADS, HD)
    new_values = projected[:, 2 * head_cols :].reshape(requests, steps_each, HEADS, HD)
    positions = lengths[:, None] + jnp.arange(steps_each, dtype=jnp.int32)[None, :]
    queries = rotate(queries.astype(jnp.float32), positions).astype(jnp.bfloat16)
    new_keys = rotate(new_keys.astype(jnp.float32), positions).astype(jnp.bfloat16)
    slots = rotated_key_cache.shape[0]
    page_len = rotated_key_cache.shape[2]
    cache_k = rotated_key_cache.reshape(slots * page_len, head_cols)
    cache_v = cached_value_pages.reshape(slots * page_len, head_cols)
    slot_ids = seq_index * slots + jnp.arange(slots, dtype=jnp.int32)
    page_ids = jnp.arange(request_page_slots.shape[1], dtype=jnp.int32)
    is_live = page_ids[None, :] < ((lengths + page_len - 1) // page_len)[:, None]
    matches = (request_page_slots[:, :, None] == slot_ids[None, None, :]) & is_live[:, :, None]
    is_owned = jnp.any(matches, axis=1)
    page_of = jnp.sum(jnp.where(matches, page_ids[None, :, None], 0), axis=1)
    token_pos = (
        page_of[:, :, None] * page_len + jnp.arange(page_len, dtype=jnp.int32)[None, None, :]
    )
    is_valid = (is_owned[:, :, None] & (token_pos < lengths[:, None, None])).reshape(
        requests, slots * page_len
    )
    score_scale = 1.0 / math.sqrt(HD)
    head_mask = (jnp.arange(head_cols, dtype=jnp.int32)[None, :] // HD) == jnp.arange(
        HEADS, dtype=jnp.int32
    )[:, None]
    query_rows = queries.reshape(group_rows, head_cols)
    spread_queries = jnp.where(head_mask[None], query_rows[:, None, :], jnp.zeros((), jnp.bfloat16))
    scores = (
        jnp.dot(
            spread_queries.reshape(group_rows * HEADS, head_cols),
            cache_k.T,
            preferred_element_type=jnp.float32,
        )
        * score_scale
    ).reshape(requests, steps_each, HEADS, slots * page_len)
    mask_b = is_valid[:, None, None, :]
    local_max = jnp.max(jnp.where(mask_b, scores, NEGATIVE), axis=-1)
    weights = jnp.where(mask_b, jnp.exp(scores - local_max[..., None]), 0.0)
    local_sum = jnp.sum(weights, axis=-1)
    spread_out = jnp.dot(
        weights.astype(jnp.bfloat16).reshape(group_rows * HEADS, slots * page_len),
        cache_v,
        preferred_element_type=jnp.float32,
    ).reshape(group_rows, HEADS, head_cols)
    local_out = jnp.sum(jnp.where(head_mask[None], spread_out, 0.0), axis=1).reshape(
        requests, steps_each, HEADS, HD
    )
    fresh_scores = (
        jnp.einsum("rthd,rshd->rths", queries, new_keys, preferred_element_type=jnp.float32)
        * score_scale
    )
    causal = jnp.arange(steps_each)[:, None] >= jnp.arange(steps_each)[None, :]
    fresh_mask = causal[None, :, None, :]
    fresh_max = jnp.max(jnp.where(fresh_mask, fresh_scores, NEGATIVE), axis=-1)
    fresh_w = jnp.where(fresh_mask, jnp.exp(fresh_scores - fresh_max[..., None]), 0.0)
    fresh_sum = jnp.sum(fresh_w, axis=-1)
    fresh_out = jnp.einsum(
        "rths,rshd->rthd",
        fresh_w.astype(jnp.bfloat16),
        new_values,
        preferred_element_type=jnp.float32,
    )
    own_heads = HEADS // seq_devices
    first_head = seq_index * own_heads

    def own_slice(member):
        return lax.dynamic_slice_in_dim(member, first_head, own_heads, 2)

    pad_cols = 256 - HD - 2
    packed = jnp.concatenate(
        [
            local_out,
            local_max[..., None],
            local_sum[..., None],
            jnp.zeros(local_out.shape[:-1] + (pad_cols,), jnp.float32),
        ],
        axis=-1,
    )
    packed = packed.reshape(requests * steps_each, seq_devices, own_heads, 256)
    packed = jnp.transpose(packed, (1, 0, 2, 3)).reshape(seq_devices, group_rows * own_heads, 256)
    arrived = exchange(packed, "seq", 0).reshape(seq_devices, requests, steps_each, own_heads, 256)
    part_o = arrived[..., :HD]
    part_m = arrived[..., HD]
    part_l = arrived[..., HD + 1]
    f_max, f_sum, f_out = own_slice(fresh_max), own_slice(fresh_sum), own_slice(fresh_out)
    overall = jnp.maximum(jnp.max(part_m, axis=0), f_max)
    part_factor = jnp.exp(part_m - overall[None])
    fresh_factor = jnp.exp(f_max - overall)
    denominator = jnp.sum(part_l * part_factor, axis=0) + f_sum * fresh_factor
    numerator = jnp.sum(part_o * part_factor[..., None], axis=0) + f_out * fresh_factor[..., None]
    attention = (
        (numerator / denominator[..., None])
        .astype(jnp.bfloat16)
        .reshape(group_rows, own_heads * HD)
    )
    projected_out = jnp.dot(attention, attention_output_weight, preferred_element_type=jnp.float32)
    model_width = projected_out.shape[1]
    after_attn = two_rounds(
        projected_out.reshape(seq_devices, row_share * model_width // lanes, lanes),
        ("seq", False),
        ("seq", True),
        lambda landed, own: (own[...].astype(jnp.float32) + _block_sum(landed)).astype(jnp.bfloat16),
        (row_share * model_width // lanes, lanes),
        jnp.bfloat16,
        1,
        extra=(own_rows.reshape(-1, lanes),),
    ).reshape(group_rows, model_width)
    second_normed_state = rms_norm(after_attn, feedforward_norm_gain)
    both = jnp.stack([after_attn, second_normed_state]).reshape(2, group_rows, req_devices, width_share)
    both_parts = exchange(jnp.transpose(both, (2, 0, 1, 3)), "req", 7)
    residual_cols = both_parts[:, 0].reshape(req_devices * group_rows, width_share)
    second_spread_state = both_parts[:, 1].reshape(req_devices * group_rows, width_share)
    units = gate_weight.shape[1]
    mlp_full = jnp.concatenate(
        [
            jnp.dot(second_spread_state, gate_weight, preferred_element_type=jnp.float32),
            jnp.dot(second_spread_state, up_weight, preferred_element_type=jnp.float32),
            jnp.dot(second_spread_state, adapter_down_map, preferred_element_type=jnp.float32),
        ],
        axis=1,
    )
    def activate(landed, gate_map, up_map):
        total = _block_sum(landed)
        low = total[:, 2 * units :].astype(jnp.bfloat16)
        gate_pre = total[:, :units] + jnp.dot(low, gate_map[...], preferred_element_type=jnp.float32)
        up_part = total[:, units : 2 * units] + jnp.dot(
            low, up_map[...], preferred_element_type=jnp.float32
        )
        return (gate_pre / (1.0 + jnp.exp(-gate_pre)) * up_part).astype(jnp.bfloat16)

    inner_act = two_rounds(
        mlp_full.reshape(req_devices, group_rows, mlp_full.shape[1]),
        ("req", False),
        ("req", True),
        activate,
        (group_rows, units),
        jnp.bfloat16,
        8,
        extra=(adapter_gate_map, adapter_up_map),
    ).reshape(req_devices * group_rows, units)
    out_rows = residual_cols.shape[0] // seq_devices
    block_rows = inner_act
    down_full = jnp.dot(block_rows, down_weight, preferred_element_type=jnp.float32)
    down_parts = exchange(down_full.reshape(seq_devices, out_rows, down_full.shape[1]), "seq", 3)
    down_sum = jnp.sum(down_parts, axis=0)
    residual_rows = lax.dynamic_slice_in_dim(residual_cols, seq_index * out_rows, out_rows, 0)
    return (residual_rows.astype(jnp.float32) + down_sum).astype(jnp.bfloat16)


def solution(mesh):
    placed = (
        P(),
        P("req", None),
        P(("seq", "req"), None),
        P(),
        P("req", "seq"),
        P("seq", "req", None, None),
        P("seq", "req", None, None),
        P("req"),
        P("req", None),
        P("seq", None),
        P(),
        P("req", "seq"),
        P("req", "seq"),
        P("req", None),
        P(None, "seq"),
        P(None, "seq"),
        P("seq", "req"),
    )
    return jax.shard_map(
        body, mesh=mesh, in_specs=placed, out_specs=P("seq", "req"), check_vma=False
    )
```

```python
import functools
import math

import jax
import jax.numpy as jnp
from jax import lax
from jax.experimental import pallas as pl
from jax.experimental.pallas import tpu as pltpu
from jax.sharding import PartitionSpec as P

HEADS = 16
HD = 224


NEGATIVE = -1e30
EPSILON = 1e-05
ROTARY_BASE = 10000.0


MESH_ID = pl.DeviceIdType.MESH


def _exchange_kernel(axis, n, gather, x_ref, y_ref, send_sem, recv_sem, local_sem):
    me = lax.axis_index(axis)
    barrier = pltpu.get_barrier_semaphore()
    for k in range(1, n):
        peer = lax.rem(me + k, n)
        pl.semaphore_signal(barrier, 1, device_id={axis: peer}, device_id_type=MESH_ID)
    pl.semaphore_wait(barrier, n - 1)
    copies = []
    for k in range(1, n):
        peer = lax.rem(me + k, n)
        source = x_ref if gather else x_ref.at[peer]
        copy = pltpu.make_async_remote_copy(
            src_ref=source,
            dst_ref=y_ref.at[me],
            send_sem=send_sem.at[k],
            recv_sem=recv_sem.at[k],
            device_id={axis: peer},
            device_id_type=MESH_ID,
        )
        copy.start()
        copies.append(copy)
    local = pltpu.make_async_copy(x_ref if gather else x_ref.at[me], y_ref.at[me], local_sem)
    local.start()
    local.wait()
    for copy in copies:
        copy.wait()


def exchange(x, axis, cid, gather=False):
    n = lax.axis_size(axis)
    out_shape = (n,) + x.shape if gather else x.shape
    return pl.pallas_call(
        functools.partial(_exchange_kernel, axis, n, gather),
        out_shape=jax.ShapeDtypeStruct(out_shape, x.dtype),
        in_specs=[pl.BlockSpec(memory_space=pltpu.VMEM)],
        out_specs=pl.BlockSpec(memory_space=pltpu.VMEM),
        scratch_shapes=[
            pltpu.SemaphoreType.DMA((n,)),
            pltpu.SemaphoreType.DMA((n,)),
            pltpu.SemaphoreType.DMA(()),
        ],
        compiler_params=pltpu.CompilerParams(collective_id=cid, has_side_effects=True),
    )(x)


def _greet(axes_sizes):
    barrier = pltpu.get_barrier_semaphore()
    total = 0
    for axis, n in axes_sizes:
        me = lax.axis_index(axis)
        for k in range(1, n):
            peer = lax.rem(me + k, n)
            pl.semaphore_signal(barrier, 1, device_id={axis: peer}, device_id_type=MESH_ID)
        total += n - 1
    pl.semaphore_wait(barrier, total)


def _start_round(axis, n, gather, source, target, send_sem, recv_sem, local_sem):
    me = lax.axis_index(axis)
    copies = []
    for k in range(1, n):
        peer = lax.rem(me + k, n)
        copy = pltpu.make_async_remote_copy(
            src_ref=source if gather else source.at[peer],
            dst_ref=target.at[me],
            send_sem=send_sem.at[k],
            recv_sem=recv_sem.at[k],
            device_id={axis: peer},
            device_id_type=MESH_ID,
        )
        copy.start()
        copies.append(copy)
    local = pltpu.make_async_copy(source if gather else source.at[me], target.at[me], local_sem)
    local.start()
    copies.append(local)
    return copies


def _two_round_kernel(first, second, mid, n_extra, x_ref, *refs):
    extra = refs[:n_extra]
    y_ref, landed, staged, send_a, recv_a, send_b, recv_b, local_sems = refs[n_extra:]
    axis_a, n_a, gather_a = first
    axis_b, n_b, gather_b = second
    greeted = [(axis_a, n_a)] if axis_a == axis_b else [(axis_a, n_a), (axis_b, n_b)]
    _greet(greeted)
    for copy in _start_round(axis_a, n_a, gather_a, x_ref, landed, send_a, recv_a, local_sems.at[0]):
        copy.wait()
    staged[...] = mid(landed, *extra)
    for copy in _start_round(axis_b, n_b, gather_b, staged, y_ref, send_b, recv_b, local_sems.at[1]):
        copy.wait()


def two_rounds(x, first, second, mid, staged_shape, staged_dtype, cid, extra=()):
    axis_a, gather_a = first
    axis_b, gather_b = second
    n_a, n_b = lax.axis_size(axis_a), lax.axis_size(axis_b)
    landed_shape = (n_a,) + x.shape if gather_a else x.shape
    out_shape = (n_b,) + staged_shape if gather_b else staged_shape
    return pl.pallas_call(
        functools.partial(
            _two_round_kernel, (axis_a, n_a, gather_a), (axis_b, n_b, gather_b), mid, len(extra)
        ),
        out_shape=jax.ShapeDtypeStruct(out_shape, staged_dtype),
        in_specs=[pl.BlockSpec(memory_space=pltpu.VMEM)] * (1 + len(extra)),
        out_specs=pl.BlockSpec(memory_space=pltpu.VMEM),
        scratch_shapes=[
            pltpu.VMEM(landed_shape, x.dtype),
            pltpu.VMEM(staged_shape, staged_dtype),
            pltpu.SemaphoreType.DMA((n_a,)),
            pltpu.SemaphoreType.DMA((n_a,)),
            pltpu.SemaphoreType.DMA((n_b,)),
            pltpu.SemaphoreType.DMA((n_b,)),
            pltpu.SemaphoreType.DMA((2,)),
        ],
        compiler_params=pltpu.CompilerParams(collective_id=cid, has_side_effects=True),
    )(x, *extra)


def _block_sum(landed):
    total = landed[0].astype(jnp.float32)
    for k in range(1, landed.shape[0]):
        total = total + landed[k].astype(jnp.float32)
    return total


def _mlp_kernel(
    x_ref, gate_ref, up_ref, down_map_ref, gate_map_ref, up_map_ref, down_ref,
    out_ref, spread_ref, landed1, staged1, staged2, landed2, staged3, landed3,
    send0, recv0, send1, recv1, send2, recv2, send3, recv3, local_sems,
):
    n_req = spread_ref.shape[0]
    n_seq = landed3.shape[0]
    rows = n_req * spread_ref.shape[2]
    units = gate_ref.shape[1]
    _greet([("req", n_req), ("seq", n_seq)])
    for copy in _start_round("req", n_req, False, x_ref, spread_ref, send0, recv0, local_sems.at[0]):
        copy.wait()
    normed_all = spread_ref[:, 1].reshape(rows, spread_ref.shape[3])
    staged1[:, :, :units] = jnp.dot(
        normed_all, gate_ref[...], preferred_element_type=jnp.float32
    ).reshape(staged1.shape[0], staged1.shape[1], units)
    staged1[:, :, units : 2 * units] = jnp.dot(
        normed_all, up_ref[...], preferred_element_type=jnp.float32
    ).reshape(staged1.shape[0], staged1.shape[1], units)
    staged1[:, :, 2 * units :] = jnp.dot(
        normed_all, down_map_ref[...], preferred_element_type=jnp.float32
    ).reshape(staged1.shape[0], staged1.shape[1], staged1.shape[2] - 2 * units)
    for copy in _start_round("req", n_req, False, staged1, landed1, send1, recv1, local_sems.at[1]):
        copy.wait()
    total = _block_sum(landed1)
    low = total[:, 2 * units :].astype(jnp.bfloat16)
    gate_pre = total[:, :units] + jnp.dot(low, gate_map_ref[...], preferred_element_type=jnp.float32)
    up_part = total[:, units : 2 * units] + jnp.dot(
        low, up_map_ref[...], preferred_element_type=jnp.float32
    )
    staged2[...] = (gate_pre / (1.0 + jnp.exp(-gate_pre)) * up_part).astype(jnp.bfloat16)
    for copy in _start_round("req", n_req, True, staged2, landed2, send2, recv2, local_sems.at[2]):
        copy.wait()
    inner = landed2[...].reshape(rows, units)
    staged3[...] = jnp.dot(inner, down_ref[...], preferred_element_type=jnp.float32).reshape(
        staged3.shape
    )
    for copy in _start_round("seq", n_seq, False, staged3, landed3, send3, recv3, local_sems.at[3]):
        copy.wait()
    out_ref[...] = _block_sum(landed3)


def fused_mlp(both, gate_weight, up_weight, down_map, gate_map, up_map, down_weight, cid):
    n_req, n_seq = lax.axis_size("req"), lax.axis_size("seq")
    group_rows = both.shape[2]
    rows = n_req * group_rows
    units = gate_weight.shape[1]
    wide = 2 * units + down_map.shape[1]
    out_rows = rows // n_seq
    vmem = pltpu.VMEM
    return pl.pallas_call(
        _mlp_kernel,
        out_shape=(
            jax.ShapeDtypeStruct((out_rows, down_weight.shape[1]), jnp.float32),
            jax.ShapeDtypeStruct(both.shape, both.dtype),
        ),
        in_specs=[pl.BlockSpec(memory_space=vmem)] * 7,
        out_specs=(pl.BlockSpec(memory_space=vmem), pl.BlockSpec(memory_space=vmem)),
        scratch_shapes=[
            vmem((n_req, group_rows, wide), jnp.float32),
            vmem((n_req, group_rows, wide), jnp.float32),
            vmem((group_rows, units), jnp.bfloat16),
            vmem((n_req, group_rows, units), jnp.bfloat16),
            vmem((n_seq, out_rows, down_weight.shape[1]), jnp.float32),
            vmem((n_seq, out_rows, down_weight.shape[1]), jnp.float32),
            pltpu.SemaphoreType.DMA((n_req,)),
            pltpu.SemaphoreType.DMA((n_req,)),
            pltpu.SemaphoreType.DMA((n_req,)),
            pltpu.SemaphoreType.DMA((n_req,)),
            pltpu.SemaphoreType.DMA((n_req,)),
            pltpu.SemaphoreType.DMA((n_req,)),
            pltpu.SemaphoreType.DMA((n_seq,)),
            pltpu.SemaphoreType.DMA((n_seq,)),
            pltpu.SemaphoreType.DMA((4,)),
        ],
        compiler_params=pltpu.CompilerParams(
            collective_id=cid, has_side_effects=True, vmem_limit_bytes=48 * 1024 * 1024
        ),
    )(both, gate_weight, up_weight, down_map, gate_map, up_map, down_weight)


def merged_2(array, axis, combine):
    everything = jax.tree.map(lambda part: lax.all_gather(part, axis), array)
    first = jax.tree.map(lambda part: part[0], everything)

    def hop(k, so_far):
        return combine(so_far, jax.tree.map(lambda part: part[k], everything))

    return lax.fori_loop(1, lax.axis_size(axis), hop, first)


def rms_norm(matrix, gain_vec):
    widened = matrix.astype(jnp.float32)
    factor = lax.rsqrt(jnp.mean(widened * widened, axis=-1, keepdims=True) + EPSILON)
    return (widened * factor * gain_vec.astype(jnp.float32)).astype(jnp.bfloat16)


def rotate(vectors, positions):
    half_dim = vectors.shape[-1] // 2
    frequency = ROTARY_BASE ** (-2.0 * jnp.arange(half_dim, dtype=jnp.float32) / vectors.shape[-1])
    angles = positions.astype(jnp.float32)[..., None, None] * frequency
    cosine = jnp.cos(angles)
    sine_part = jnp.sin(angles)
    front_half = vectors[..., :half_dim]
    back_half = vectors[..., half_dim:]
    return jnp.concatenate(
        [front_half * cosine - back_half * sine_part, back_half * cosine + front_half * sine_part],
        axis=-1,
    )


def softmax_join(earlier, later):
    first_max, first_sum, first_out = earlier
    second_max, second_sum, second_out = later
    overall = jnp.maximum(first_max, second_max)
    first_factor = jnp.exp(first_max - overall)
    second_factor = jnp.exp(second_max - overall)
    return (
        overall,
        first_sum * first_factor + second_sum * second_factor,
        first_out * first_factor[..., None] + second_out * second_factor[..., None],
    )


def body(
    given_token_index,
    hidden,
    token_embedding_table,
    attention_norm_gain,
    query_key_value_weight,
    rotated_key_cache,
    cached_value_pages,
    lengths,
    request_page_slots,
    attention_output_weight,
    feedforward_norm_gain,
    gate_weight,
    up_weight,
    adapter_down_map,
    adapter_gate_map,
    adapter_up_map,
    down_weight,
):
    seq_devices = lax.axis_size("seq")
    req_devices = lax.axis_size("req")
    seq_index = lax.axis_index("seq")
    req_index = lax.axis_index("req")
    group_rows = hidden.shape[0]
    requests = lengths.shape[0]
    steps_each = group_rows // requests
    vocab_rows = token_embedding_table.shape[0]
    first_id = (seq_index * req_devices + req_index) * vocab_rows
    local_ids = given_token_index - first_id
    present = (local_ids >= 0) & (local_ids < vocab_rows)
    looked = jnp.take(token_embedding_table, jnp.clip(local_ids, 0, vocab_rows - 1), axis=0).astype(
        jnp.float32
    )
    looked = jnp.where(present[:, None], looked, 0.0).astype(jnp.bfloat16)
    row_share = group_rows // seq_devices
    lanes = 128
    by_group = looked.reshape(req_devices, seq_devices, row_share * looked.shape[1] // lanes, lanes)
    row_parts = two_rounds(
        by_group,
        ("req", False),
        ("seq", False),
        lambda landed: _block_sum(landed).astype(jnp.bfloat16),
        by_group.shape[1:],
        jnp.bfloat16,
        10,
    )
    embedded_rows = (
        jnp.sum(row_parts.astype(jnp.float32), axis=0)
        .astype(jnp.bfloat16)
        .reshape(row_share, looked.shape[1])
    )
    own_hidden = lax.dynamic_slice_in_dim(hidden, seq_index * row_share, row_share, 0)
    own_rows = jnp.concatenate([own_hidden, embedded_rows], axis=1)
    normed_rows = rms_norm(own_rows, attention_norm_gain)
    normed = exchange(normed_rows.reshape(-1, lanes), "seq", 12, gather=True).reshape(
        group_rows, own_rows.shape[1]
    )
    width_share = normed.shape[1] // req_devices
    to_owners = jnp.transpose(normed.reshape(group_rows, req_devices, width_share), (1, 0, 2))
    block_rows = exchange(to_owners, "req", 4).reshape(req_devices * group_rows, width_share)
    qkv_full = jnp.dot(block_rows, query_key_value_weight, preferred_element_type=jnp.float32)
    qkv_all = two_rounds(
        qkv_full.reshape(req_devices, group_rows, qkv_full.shape[1]),
        ("req", False),
        ("seq", True),
        lambda landed: _block_sum(landed).astype(jnp.bfloat16),
        (group_rows, qkv_full.shape[1]),
        jnp.bfloat16,
        5,
    )
    projected = jnp.transpose(qkv_all, (1, 0, 2)).reshape(group_rows, seq_devices * qkv_all.shape[2])
    head_cols = HEADS * HD
    queries = projected[:, :head_cols].reshape(requests, steps_each, HEADS, HD)
    new_keys = projected[:, head_cols : 2 * head_cols].reshape(requests, steps_each, HEADS, HD)
    new_values = projected[:, 2 * head_cols :].reshape(requests, steps_each, HEADS, HD)
    positions = lengths[:, None] + jnp.arange(steps_each, dtype=jnp.int32)[None, :]
    queries = rotate(queries.astype(jnp.float32), positions).astype(jnp.bfloat16)
    new_keys = rotate(new_keys.astype(jnp.float32), positions).astype(jnp.bfloat16)
    slots = rotated_key_cache.shape[0]
    page_len = rotated_key_cache.shape[2]
    cache_k = rotated_key_cache.reshape(slots * page_len, head_cols)
    cache_v = cached_value_pages.reshape(slots * page_len, head_cols)
    slot_ids = seq_index * slots + jnp.arange(slots, dtype=jnp.int32)
    page_ids = jnp.arange(request_page_slots.shape[1], dtype=jnp.int32)
    is_live = page_ids[None, :] < ((lengths + page_len - 1) // page_len)[:, None]
    matches = (request_page_slots[:, :, None] == slot_ids[None, None, :]) & is_live[:, :, None]
    is_owned = jnp.any(matches, axis=1)
    page_of = jnp.sum(jnp.where(matches, page_ids[None, :, None], 0), axis=1)
    token_pos = (
        page_of[:, :, None] * page_len + jnp.arange(page_len, dtype=jnp.int32)[None, None, :]
    )
    is_valid = (is_owned[:, :, None] & (token_pos < lengths[:, None, None])).reshape(
        requests, slots * page_len
    )
    score_scale = 1.0 / math.sqrt(HD)
    head_mask = (jnp.arange(head_cols, dtype=jnp.int32)[None, :] // HD) == jnp.arange(
        HEADS, dtype=jnp.int32
    )[:, None]
    query_rows = queries.reshape(group_rows, head_cols)
    spread_queries = jnp.where(head_mask[None], query_rows[:, None, :], jnp.zeros((), jnp.bfloat16))
    scores = (
        jnp.dot(
            spread_queries.reshape(group_rows * HEADS, head_cols),
            cache_k.T,
            preferred_element_type=jnp.float32,
        )
        * score_scale
    ).reshape(requests, steps_each, HEADS, slots * page_len)
    mask_b = is_valid[:, None, None, :]
    local_max = jnp.max(jnp.where(mask_b, scores, NEGATIVE), axis=-1)
    weights = jnp.where(mask_b, jnp.exp(scores - local_max[..., None]), 0.0)
    local_sum = jnp.sum(weights, axis=-1)
    spread_out = jnp.dot(
        weights.astype(jnp.bfloat16).reshape(group_rows * HEADS, slots * page_len),
        cache_v,
        preferred_element_type=jnp.float32,
    ).reshape(group_rows, HEADS, head_cols)
    local_out = jnp.sum(jnp.where(head_mask[None], spread_out, 0.0), axis=1).reshape(
        requests, steps_each, HEADS, HD
    )
    fresh_scores = (
        jnp.einsum("rthd,rshd->rths", queries, new_keys, preferred_element_type=jnp.float32)
        * score_scale
    )
    causal = jnp.arange(steps_each)[:, None] >= jnp.arange(steps_each)[None, :]
    fresh_mask = causal[None, :, None, :]
    fresh_max = jnp.max(jnp.where(fresh_mask, fresh_scores, NEGATIVE), axis=-1)
    fresh_w = jnp.where(fresh_mask, jnp.exp(fresh_scores - fresh_max[..., None]), 0.0)
    fresh_sum = jnp.sum(fresh_w, axis=-1)
    fresh_out = jnp.einsum(
        "rths,rshd->rthd",
        fresh_w.astype(jnp.bfloat16),
        new_values,
        preferred_element_type=jnp.float32,
    )
    own_heads = HEADS // seq_devices
    first_head = seq_index * own_heads

    def own_slice(member):
        return lax.dynamic_slice_in_dim(member, first_head, own_heads, 2)

    pad_cols = 256 - HD - 2
    packed = jnp.concatenate(
        [
            local_out,
            local_max[..., None],
            local_sum[..., None],
            jnp.zeros(local_out.shape[:-1] + (pad_cols,), jnp.float32),
        ],
        axis=-1,
    )
    packed = packed.reshape(requests * steps_each, seq_devices, own_heads, 256)
    packed = jnp.transpose(packed, (1, 0, 2, 3)).reshape(seq_devices, group_rows * own_heads, 256)
    arrived = exchange(packed, "seq", 0).reshape(seq_devices, requests, steps_each, own_heads, 256)
    part_o = arrived[..., :HD]
    part_m = arrived[..., HD]
    part_l = arrived[..., HD + 1]
    f_max, f_sum, f_out = own_slice(fresh_max), own_slice(fresh_sum), own_slice(fresh_out)
    overall = jnp.maximum(jnp.max(part_m, axis=0), f_max)
    part_factor = jnp.exp(part_m - overall[None])
    fresh_factor = jnp.exp(f_max - overall)
    denominator = jnp.sum(part_l * part_factor, axis=0) + f_sum * fresh_factor
    numerator = jnp.sum(part_o * part_factor[..., None], axis=0) + f_out * fresh_factor[..., None]
    attention = (
        (numerator / denominator[..., None])
        .astype(jnp.bfloat16)
        .reshape(group_rows, own_heads * HD)
    )
    projected_out = jnp.dot(attention, attention_output_weight, preferred_element_type=jnp.float32)
    model_width = projected_out.shape[1]
    after_attn = two_rounds(
        projected_out.reshape(seq_devices, row_share * model_width // lanes, lanes),
        ("seq", False),
        ("seq", True),
        lambda landed, own: (own[...].astype(jnp.float32) + _block_sum(landed)).astype(jnp.bfloat16),
        (row_share * model_width // lanes, lanes),
        jnp.bfloat16,
        1,
        extra=(own_rows.reshape(-1, lanes),),
    ).reshape(group_rows, model_width)
    second_normed_state = rms_norm(after_attn, feedforward_norm_gain)
    both = jnp.stack([after_attn, second_normed_state]).reshape(2, group_rows, req_devices, width_share)
    both = jnp.transpose(both, (2, 0, 1, 3))
    down_sum, both_parts = fused_mlp(
        both, gate_weight, up_weight, adapter_down_map, adapter_gate_map, adapter_up_map, down_weight, 7
    )
    residual_cols = both_parts[:, 0].reshape(req_devices * group_rows, width_share)
    out_rows = residual_cols.shape[0] // seq_devices
    residual_rows = lax.dynamic_slice_in_dim(residual_cols, seq_index * out_rows, out_rows, 0)
    return (residual_rows.astype(jnp.float32) + down_sum).astype(jnp.bfloat16)


def solution(mesh):
    placed = (
        P(),
        P("req", None),
        P(("seq", "req"), None),
        P(),
        P("req", "seq"),
        P("seq", "req", None, None),
        P("seq", "req", None, None),
        P("req"),
        P("req", None),
        P("seq", None),
        P(),
        P("req", "seq"),
        P("req", "seq"),
        P("req", None),
        P(None, "seq"),
        P(None, "seq"),
        P("seq", "req"),
    )
    return jax.shard_map(
        body, mesh=mesh, in_specs=placed, out_specs=P("seq", "req"), check_vma=False
    )
```

```python
import functools
import math

import jax
import jax.numpy as jnp
from jax import lax
from jax.experimental import pallas as pl
from jax.experimental.pallas import tpu as pltpu
from jax.sharding import PartitionSpec as P

HEADS = 16
HD = 224


NEGATIVE = -1e30
EPSILON = 1e-05
ROTARY_BASE = 10000.0


MESH_ID = pl.DeviceIdType.MESH


def _exchange_kernel(axis, n, gather, x_ref, y_ref, send_sem, recv_sem, local_sem):
    me = lax.axis_index(axis)
    barrier = pltpu.get_barrier_semaphore()
    for k in range(1, n):
        peer = lax.rem(me + k, n)
        pl.semaphore_signal(barrier, 1, device_id={axis: peer}, device_id_type=MESH_ID)
    pl.semaphore_wait(barrier, n - 1)
    copies = []
    for k in range(1, n):
        peer = lax.rem(me + k, n)
        source = x_ref if gather else x_ref.at[peer]
        copy = pltpu.make_async_remote_copy(
            src_ref=source,
            dst_ref=y_ref.at[me],
            send_sem=send_sem.at[k],
            recv_sem=recv_sem.at[k],
            device_id={axis: peer},
            device_id_type=MESH_ID,
        )
        copy.start()
        copies.append(copy)
    local = pltpu.make_async_copy(x_ref if gather else x_ref.at[me], y_ref.at[me], local_sem)
    local.start()
    local.wait()
    for copy in copies:
        copy.wait()


def exchange(x, axis, cid, gather=False):
    n = lax.axis_size(axis)
    out_shape = (n,) + x.shape if gather else x.shape
    return pl.pallas_call(
        functools.partial(_exchange_kernel, axis, n, gather),
        out_shape=jax.ShapeDtypeStruct(out_shape, x.dtype),
        in_specs=[pl.BlockSpec(memory_space=pltpu.VMEM)],
        out_specs=pl.BlockSpec(memory_space=pltpu.VMEM),
        scratch_shapes=[
            pltpu.SemaphoreType.DMA((n,)),
            pltpu.SemaphoreType.DMA((n,)),
            pltpu.SemaphoreType.DMA(()),
        ],
        compiler_params=pltpu.CompilerParams(collective_id=cid, has_side_effects=True),
    )(x)


def _greet(axes_sizes):
    barrier = pltpu.get_barrier_semaphore()
    total = 0
    for axis, n in axes_sizes:
        me = lax.axis_index(axis)
        for k in range(1, n):
            peer = lax.rem(me + k, n)
            pl.semaphore_signal(barrier, 1, device_id={axis: peer}, device_id_type=MESH_ID)
        total += n - 1
    pl.semaphore_wait(barrier, total)


def _start_round(axis, n, gather, source, target, send_sem, recv_sem, local_sem):
    me = lax.axis_index(axis)
    copies = []
    for k in range(1, n):
        peer = lax.rem(me + k, n)
        copy = pltpu.make_async_remote_copy(
            src_ref=source if gather else source.at[peer],
            dst_ref=target.at[me],
            send_sem=send_sem.at[k],
            recv_sem=recv_sem.at[k],
            device_id={axis: peer},
            device_id_type=MESH_ID,
        )
        copy.start()
        copies.append(copy)
    local = pltpu.make_async_copy(source if gather else source.at[me], target.at[me], local_sem)
    local.start()
    copies.append(local)
    return copies


def _two_round_kernel(first, second, mid, n_extra, x_ref, *refs):
    extra = refs[:n_extra]
    y_ref, landed, staged, send_a, recv_a, send_b, recv_b, local_sems = refs[n_extra:]
    axis_a, n_a, gather_a = first
    axis_b, n_b, gather_b = second
    greeted = [(axis_a, n_a)] if axis_a == axis_b else [(axis_a, n_a), (axis_b, n_b)]
    _greet(greeted)
    for copy in _start_round(axis_a, n_a, gather_a, x_ref, landed, send_a, recv_a, local_sems.at[0]):
        copy.wait()
    staged[...] = mid(landed, *extra)
    for copy in _start_round(axis_b, n_b, gather_b, staged, y_ref, send_b, recv_b, local_sems.at[1]):
        copy.wait()


def two_rounds(x, first, second, mid, staged_shape, staged_dtype, cid, extra=()):
    axis_a, gather_a = first
    axis_b, gather_b = second
    n_a, n_b = lax.axis_size(axis_a), lax.axis_size(axis_b)
    landed_shape = (n_a,) + x.shape if gather_a else x.shape
    out_shape = (n_b,) + staged_shape if gather_b else staged_shape
    return pl.pallas_call(
        functools.partial(
            _two_round_kernel, (axis_a, n_a, gather_a), (axis_b, n_b, gather_b), mid, len(extra)
        ),
        out_shape=jax.ShapeDtypeStruct(out_shape, staged_dtype),
        in_specs=[pl.BlockSpec(memory_space=pltpu.VMEM)] * (1 + len(extra)),
        out_specs=pl.BlockSpec(memory_space=pltpu.VMEM),
        scratch_shapes=[
            pltpu.VMEM(landed_shape, x.dtype),
            pltpu.VMEM(staged_shape, staged_dtype),
            pltpu.SemaphoreType.DMA((n_a,)),
            pltpu.SemaphoreType.DMA((n_a,)),
            pltpu.SemaphoreType.DMA((n_b,)),
            pltpu.SemaphoreType.DMA((n_b,)),
            pltpu.SemaphoreType.DMA((2,)),
        ],
        compiler_params=pltpu.CompilerParams(collective_id=cid, has_side_effects=True),
    )(x, *extra)


def _block_sum(landed):
    total = landed[0].astype(jnp.float32)
    for k in range(1, landed.shape[0]):
        total = total + landed[k].astype(jnp.float32)
    return total


def _mlp_kernel(
    x_ref, gate_ref, up_ref, down_map_ref, gate_map_ref, up_map_ref, down_ref,
    out_ref, spread_ref, landed1, staged1, staged2, landed2, staged3, landed3,
    send0, recv0, send1, recv1, send2, recv2, send3, recv3, local_sems,
):
    n_req = spread_ref.shape[0]
    n_seq = landed3.shape[0]
    rows = n_req * spread_ref.shape[2]
    units = gate_ref.shape[1]
    _greet([("req", n_req), ("seq", n_seq)])
    for copy in _start_round("req", n_req, False, x_ref, spread_ref, send0, recv0, local_sems.at[0]):
        copy.wait()
    normed_all = spread_ref[:, 1].reshape(rows, spread_ref.shape[3])
    staged1[:, :, :units] = jnp.dot(
        normed_all, gate_ref[...], preferred_element_type=jnp.float32
    ).reshape(staged1.shape[0], staged1.shape[1], units)
    staged1[:, :, units : 2 * units] = jnp.dot(
        normed_all, up_ref[...], preferred_element_type=jnp.float32
    ).reshape(staged1.shape[0], staged1.shape[1], units)
    staged1[:, :, 2 * units :] = jnp.dot(
        normed_all, down_map_ref[...], preferred_element_type=jnp.float32
    ).reshape(staged1.shape[0], staged1.shape[1], staged1.shape[2] - 2 * units)
    for copy in _start_round("req", n_req, False, staged1, landed1, send1, recv1, local_sems.at[1]):
        copy.wait()
    total = _block_sum(landed1)
    low = total[:, 2 * units :].astype(jnp.bfloat16)
    gate_pre = total[:, :units] + jnp.dot(low, gate_map_ref[...], preferred_element_type=jnp.float32)
    up_part = total[:, units : 2 * units] + jnp.dot(
        low, up_map_ref[...], preferred_element_type=jnp.float32
    )
    staged2[...] = (gate_pre / (1.0 + jnp.exp(-gate_pre)) * up_part).astype(jnp.bfloat16)
    for copy in _start_round("req", n_req, True, staged2, landed2, send2, recv2, local_sems.at[2]):
        copy.wait()
    inner = landed2[...].reshape(rows, units)
    staged3[...] = jnp.dot(inner, down_ref[...], preferred_element_type=jnp.float32).reshape(
        staged3.shape
    )
    for copy in _start_round("seq", n_seq, False, staged3, landed3, send3, recv3, local_sems.at[3]):
        copy.wait()
    out_ref[...] = _block_sum(landed3)


def fused_mlp(both, gate_weight, up_weight, down_map, gate_map, up_map, down_weight, cid):
    n_req, n_seq = lax.axis_size("req"), lax.axis_size("seq")
    group_rows = both.shape[2]
    rows = n_req * group_rows
    units = gate_weight.shape[1]
    wide = 2 * units + down_map.shape[1]
    out_rows = rows // n_seq
    vmem = pltpu.VMEM
    return pl.pallas_call(
        _mlp_kernel,
        out_shape=(
            jax.ShapeDtypeStruct((out_rows, down_weight.shape[1]), jnp.float32),
            jax.ShapeDtypeStruct(both.shape, both.dtype),
        ),
        in_specs=[pl.BlockSpec(memory_space=vmem)] * 7,
        out_specs=(pl.BlockSpec(memory_space=vmem), pl.BlockSpec(memory_space=vmem)),
        scratch_shapes=[
            vmem((n_req, group_rows, wide), jnp.float32),
            vmem((n_req, group_rows, wide), jnp.float32),
            vmem((group_rows, units), jnp.bfloat16),
            vmem((n_req, group_rows, units), jnp.bfloat16),
            vmem((n_seq, out_rows, down_weight.shape[1]), jnp.float32),
            vmem((n_seq, out_rows, down_weight.shape[1]), jnp.float32),
            pltpu.SemaphoreType.DMA((n_req,)),
            pltpu.SemaphoreType.DMA((n_req,)),
            pltpu.SemaphoreType.DMA((n_req,)),
            pltpu.SemaphoreType.DMA((n_req,)),
            pltpu.SemaphoreType.DMA((n_req,)),
            pltpu.SemaphoreType.DMA((n_req,)),
            pltpu.SemaphoreType.DMA((n_seq,)),
            pltpu.SemaphoreType.DMA((n_seq,)),
            pltpu.SemaphoreType.DMA((4,)),
        ],
        compiler_params=pltpu.CompilerParams(
            collective_id=cid, has_side_effects=True, vmem_limit_bytes=48 * 1024 * 1024
        ),
    )(both, gate_weight, up_weight, down_map, gate_map, up_map, down_weight)


def _chain_kernel(spec, n_extra, x_ref, *refs):
    extra = refs[:n_extra]
    y_ref = refs[n_extra]
    scratch = refs[n_extra + 1 :]
    count = len(spec)
    landed = list(scratch[: count - 1]) + [y_ref]
    staged = scratch[count - 1 : 2 * count - 2]
    sems = scratch[2 * count - 2 :]
    axes = []
    for axis, n, _, _ in spec:
        if (axis, n) not in axes:
            axes.append((axis, n))
    _greet(axes)
    source = x_ref
    for k, (axis, n, gather, mid) in enumerate(spec):
        copies = _start_round(
            axis, n, gather, source, landed[k], sems[2 * k], sems[2 * k + 1], sems[-1].at[k]
        )
        for copy in copies:
            copy.wait()
        if mid is not None:
            staged[k][...] = mid(landed[k], *extra)
            source = staged[k]


def chain(x, rounds, cid, extra=()):
    spec, landed_shapes, staged_shapes = [], [], []
    block = (x.shape, x.dtype)
    for index, (axis, gather, mid, made) in enumerate(rounds):
        n = lax.axis_size(axis)
        shape, dtype = block
        landed = ((n,) + shape if gather else shape, dtype)
        spec.append((axis, n, gather, mid))
        if index < len(rounds) - 1:
            landed_shapes.append(landed)
            staged_shapes.append(made)
            block = made
        else:
            out = landed
    sizes = [n for _, n, _, _ in spec]
    semaphores = []
    for n in sizes:
        semaphores += [pltpu.SemaphoreType.DMA((n,)), pltpu.SemaphoreType.DMA((n,))]
    return pl.pallas_call(
        functools.partial(_chain_kernel, spec, len(extra)),
        out_shape=jax.ShapeDtypeStruct(*out),
        in_specs=[pl.BlockSpec(memory_space=pltpu.VMEM)] * (1 + len(extra)),
        out_specs=pl.BlockSpec(memory_space=pltpu.VMEM),
        scratch_shapes=[pltpu.VMEM(*item) for item in landed_shapes]
        + [pltpu.VMEM(*item) for item in staged_shapes]
        + semaphores
        + [pltpu.SemaphoreType.DMA((len(spec),))],
        compiler_params=pltpu.CompilerParams(
            collective_id=cid, has_side_effects=True, vmem_limit_bytes=48 * 1024 * 1024
        ),
    )(x, *extra)


def merged_2(array, axis, combine):
    everything = jax.tree.map(lambda part: lax.all_gather(part, axis), array)
    first = jax.tree.map(lambda part: part[0], everything)

    def hop(k, so_far):
        return combine(so_far, jax.tree.map(lambda part: part[k], everything))

    return lax.fori_loop(1, lax.axis_size(axis), hop, first)


def rms_norm(matrix, gain_vec):
    widened = matrix.astype(jnp.float32)
    factor = lax.rsqrt(jnp.mean(widened * widened, axis=-1, keepdims=True) + EPSILON)
    return (widened * factor * gain_vec.astype(jnp.float32)).astype(jnp.bfloat16)


def rotate(vectors, positions):
    half_dim = vectors.shape[-1] // 2
    frequency = ROTARY_BASE ** (-2.0 * jnp.arange(half_dim, dtype=jnp.float32) / vectors.shape[-1])
    angles = positions.astype(jnp.float32)[..., None, None] * frequency
    cosine = jnp.cos(angles)
    sine_part = jnp.sin(angles)
    front_half = vectors[..., :half_dim]
    back_half = vectors[..., half_dim:]
    return jnp.concatenate(
        [front_half * cosine - back_half * sine_part, back_half * cosine + front_half * sine_part],
        axis=-1,
    )


def softmax_join(earlier, later):
    first_max, first_sum, first_out = earlier
    second_max, second_sum, second_out = later
    overall = jnp.maximum(first_max, second_max)
    first_factor = jnp.exp(first_max - overall)
    second_factor = jnp.exp(second_max - overall)
    return (
        overall,
        first_sum * first_factor + second_sum * second_factor,
        first_out * first_factor[..., None] + second_out * second_factor[..., None],
    )


def body(
    given_token_index,
    hidden,
    token_embedding_table,
    attention_norm_gain,
    query_key_value_weight,
    rotated_key_cache,
    cached_value_pages,
    lengths,
    request_page_slots,
    attention_output_weight,
    feedforward_norm_gain,
    gate_weight,
    up_weight,
    adapter_down_map,
    adapter_gate_map,
    adapter_up_map,
    down_weight,
):
    seq_devices = lax.axis_size("seq")
    req_devices = lax.axis_size("req")
    seq_index = lax.axis_index("seq")
    req_index = lax.axis_index("req")
    group_rows = hidden.shape[0]
    requests = lengths.shape[0]
    steps_each = group_rows // requests
    vocab_rows = token_embedding_table.shape[0]
    first_id = (seq_index * req_devices + req_index) * vocab_rows
    local_ids = given_token_index - first_id
    present = (local_ids >= 0) & (local_ids < vocab_rows)
    looked = jnp.take(token_embedding_table, jnp.clip(local_ids, 0, vocab_rows - 1), axis=0).astype(
        jnp.float32
    )
    looked = jnp.where(present[:, None], looked, 0.0).astype(jnp.bfloat16)
    row_share = group_rows // seq_devices
    lanes = 128
    by_group = looked.reshape(req_devices, seq_devices, row_share * looked.shape[1] // lanes, lanes)
    row_parts = two_rounds(
        by_group,
        ("req", False),
        ("seq", False),
        lambda landed: _block_sum(landed).astype(jnp.bfloat16),
        by_group.shape[1:],
        jnp.bfloat16,
        10,
    )
    embedded_rows = (
        jnp.sum(row_parts.astype(jnp.float32), axis=0)
        .astype(jnp.bfloat16)
        .reshape(row_share, looked.shape[1])
    )
    own_hidden = lax.dynamic_slice_in_dim(hidden, seq_index * row_share, row_share, 0)
    own_rows = jnp.concatenate([own_hidden, embedded_rows], axis=1)
    normed_rows = rms_norm(own_rows, attention_norm_gain)
    normed = exchange(normed_rows.reshape(-1, lanes), "seq", 12, gather=True).reshape(
        group_rows, own_rows.shape[1]
    )
    width_share = normed.shape[1] // req_devices
    to_owners = jnp.transpose(normed.reshape(group_rows, req_devices, width_share), (1, 0, 2))
    qkv_cols = query_key_value_weight.shape[1]

    def project(landed, weight):
        flat = landed[...].reshape(req_devices * group_rows, width_share)
        product = jnp.dot(flat, weight[...], preferred_element_type=jnp.float32)
        return product.reshape(req_devices, group_rows, qkv_cols)

    qkv_all = chain(
        to_owners,
        [
            ("req", False, project, ((req_devices, group_rows, qkv_cols), jnp.float32)),
            (
                "req",
                False,
                lambda landed, weight: _block_sum(landed).astype(jnp.bfloat16),
                ((group_rows, qkv_cols), jnp.bfloat16),
            ),
            ("seq", True, None, None),
        ],
        4,
        extra=(query_key_value_weight,),
    )
    projected = jnp.transpose(qkv_all, (1, 0, 2)).reshape(group_rows, seq_devices * qkv_all.shape[2])
    head_cols = HEADS * HD
    queries = projected[:, :head_cols].reshape(requests, steps_each, HEADS, HD)
    new_keys = projected[:, head_cols : 2 * head_cols].reshape(requests, steps_each, HEADS, HD)
    new_values = projected[:, 2 * head_cols :].reshape(requests, steps_each, HEADS, HD)
    positions = lengths[:, None] + jnp.arange(steps_each, dtype=jnp.int32)[None, :]
    queries = rotate(queries.astype(jnp.float32), positions).astype(jnp.bfloat16)
    new_keys = rotate(new_keys.astype(jnp.float32), positions).astype(jnp.bfloat16)
    slots = rotated_key_cache.shape[0]
    page_len = rotated_key_cache.shape[2]
    cache_k = rotated_key_cache.reshape(slots * page_len, head_cols)
    cache_v = cached_value_pages.reshape(slots * page_len, head_cols)
    slot_ids = seq_index * slots + jnp.arange(slots, dtype=jnp.int32)
    page_ids = jnp.arange(request_page_slots.shape[1], dtype=jnp.int32)
    is_live = page_ids[None, :] < ((lengths + page_len - 1) // page_len)[:, None]
    matches = (request_page_slots[:, :, None] == slot_ids[None, None, :]) & is_live[:, :, None]
    is_owned = jnp.any(matches, axis=1)
    page_of = jnp.sum(jnp.where(matches, page_ids[None, :, None], 0), axis=1)
    token_pos = (
        page_of[:, :, None] * page_len + jnp.arange(page_len, dtype=jnp.int32)[None, None, :]
    )
    is_valid = (is_owned[:, :, None] & (token_pos < lengths[:, None, None])).reshape(
        requests, slots * page_len
    )
    score_scale = 1.0 / math.sqrt(HD)
    head_mask = (jnp.arange(head_cols, dtype=jnp.int32)[None, :] // HD) == jnp.arange(
        HEADS, dtype=jnp.int32
    )[:, None]
    query_rows = queries.reshape(group_rows, head_cols)
    spread_queries = jnp.where(head_mask[None], query_rows[:, None, :], jnp.zeros((), jnp.bfloat16))
    scores = (
        jnp.dot(
            spread_queries.reshape(group_rows * HEADS, head_cols),
            cache_k.T,
            preferred_element_type=jnp.float32,
        )
        * score_scale
    ).reshape(requests, steps_each, HEADS, slots * page_len)
    mask_b = is_valid[:, None, None, :]
    local_max = jnp.max(jnp.where(mask_b, scores, NEGATIVE), axis=-1)
    weights = jnp.where(mask_b, jnp.exp(scores - local_max[..., None]), 0.0)
    local_sum = jnp.sum(weights, axis=-1)
    spread_out = jnp.dot(
        weights.astype(jnp.bfloat16).reshape(group_rows * HEADS, slots * page_len),
        cache_v,
        preferred_element_type=jnp.float32,
    ).reshape(group_rows, HEADS, head_cols)
    local_out = jnp.sum(jnp.where(head_mask[None], spread_out, 0.0), axis=1).reshape(
        requests, steps_each, HEADS, HD
    )
    fresh_scores = (
        jnp.einsum("rthd,rshd->rths", queries, new_keys, preferred_element_type=jnp.float32)
        * score_scale
    )
    causal = jnp.arange(steps_each)[:, None] >= jnp.arange(steps_each)[None, :]
    fresh_mask = causal[None, :, None, :]
    fresh_max = jnp.max(jnp.where(fresh_mask, fresh_scores, NEGATIVE), axis=-1)
    fresh_w = jnp.where(fresh_mask, jnp.exp(fresh_scores - fresh_max[..., None]), 0.0)
    fresh_sum = jnp.sum(fresh_w, axis=-1)
    fresh_out = jnp.einsum(
        "rths,rshd->rthd",
        fresh_w.astype(jnp.bfloat16),
        new_values,
        preferred_element_type=jnp.float32,
    )
    own_heads = HEADS // seq_devices
    first_head = seq_index * own_heads

    def own_slice(member):
        return lax.dynamic_slice_in_dim(member, first_head, own_heads, 2)

    pad_cols = 256 - HD - 2
    packed = jnp.concatenate(
        [
            local_out,
            local_max[..., None],
            local_sum[..., None],
            jnp.zeros(local_out.shape[:-1] + (pad_cols,), jnp.float32),
        ],
        axis=-1,
    )
    packed = packed.reshape(requests * steps_each, seq_devices, own_heads, 256)
    packed = jnp.transpose(packed, (1, 0, 2, 3)).reshape(seq_devices, group_rows * own_heads, 256)
    arrived = exchange(packed, "seq", 0).reshape(seq_devices, requests, steps_each, own_heads, 256)
    part_o = arrived[..., :HD]
    part_m = arrived[..., HD]
    part_l = arrived[..., HD + 1]
    f_max, f_sum, f_out = own_slice(fresh_max), own_slice(fresh_sum), own_slice(fresh_out)
    overall = jnp.maximum(jnp.max(part_m, axis=0), f_max)
    part_factor = jnp.exp(part_m - overall[None])
    fresh_factor = jnp.exp(f_max - overall)
    denominator = jnp.sum(part_l * part_factor, axis=0) + f_sum * fresh_factor
    numerator = jnp.sum(part_o * part_factor[..., None], axis=0) + f_out * fresh_factor[..., None]
    attention = (
        (numerator / denominator[..., None])
        .astype(jnp.bfloat16)
        .reshape(group_rows, own_heads * HD)
    )
    projected_out = jnp.dot(attention, attention_output_weight, preferred_element_type=jnp.float32)
    model_width = projected_out.shape[1]
    after_attn = two_rounds(
        projected_out.reshape(seq_devices, row_share * model_width // lanes, lanes),
        ("seq", False),
        ("seq", True),
        lambda landed, own: (own[...].astype(jnp.float32) + _block_sum(landed)).astype(jnp.bfloat16),
        (row_share * model_width // lanes, lanes),
        jnp.bfloat16,
        1,
        extra=(own_rows.reshape(-1, lanes),),
    ).reshape(group_rows, model_width)
    second_normed_state = rms_norm(after_attn, feedforward_norm_gain)
    both = jnp.stack([after_attn, second_normed_state]).reshape(2, group_rows, req_devices, width_share)
    both = jnp.transpose(both, (2, 0, 1, 3))
    down_sum, both_parts = fused_mlp(
        both, gate_weight, up_weight, adapter_down_map, adapter_gate_map, adapter_up_map, down_weight, 7
    )
    residual_cols = both_parts[:, 0].reshape(req_devices * group_rows, width_share)
    out_rows = residual_cols.shape[0] // seq_devices
    residual_rows = lax.dynamic_slice_in_dim(residual_cols, seq_index * out_rows, out_rows, 0)
    return (residual_rows.astype(jnp.float32) + down_sum).astype(jnp.bfloat16)


def solution(mesh):
    placed = (
        P(),
        P("req", None),
        P(("seq", "req"), None),
        P(),
        P("req", "seq"),
        P("seq", "req", None, None),
        P("seq", "req", None, None),
        P("req"),
        P("req", None),
        P("seq", None),
        P(),
        P("req", "seq"),
        P("req", "seq"),
        P("req", None),
        P(None, "seq"),
        P(None, "seq"),
        P("seq", "req"),
    )
    return jax.shard_map(
        body, mesh=mesh, in_specs=placed, out_specs=P("seq", "req"), check_vma=False
    )
```

```python
import functools
import math

import jax
import jax.numpy as jnp
from jax import lax
from jax.experimental import pallas as pl
from jax.experimental.pallas import tpu as pltpu
from jax.sharding import PartitionSpec as P

HEADS = 16
HD = 224


NEGATIVE = -1e30
EPSILON = 1e-05
ROTARY_BASE = 10000.0


MESH_ID = pl.DeviceIdType.MESH


def _exchange_kernel(axis, n, gather, x_ref, y_ref, send_sem, recv_sem, local_sem):
    me = lax.axis_index(axis)
    barrier = pltpu.get_barrier_semaphore()
    for k in range(1, n):
        peer = lax.rem(me + k, n)
        pl.semaphore_signal(barrier, 1, device_id={axis: peer}, device_id_type=MESH_ID)
    pl.semaphore_wait(barrier, n - 1)
    copies = []
    for k in range(1, n):
        peer = lax.rem(me + k, n)
        source = x_ref if gather else x_ref.at[peer]
        copy = pltpu.make_async_remote_copy(
            src_ref=source,
            dst_ref=y_ref.at[me],
            send_sem=send_sem.at[k],
            recv_sem=recv_sem.at[k],
            device_id={axis: peer},
            device_id_type=MESH_ID,
        )
        copy.start()
        copies.append(copy)
    local = pltpu.make_async_copy(x_ref if gather else x_ref.at[me], y_ref.at[me], local_sem)
    local.start()
    local.wait()
    for copy in copies:
        copy.wait()


def exchange(x, axis, cid, gather=False):
    n = lax.axis_size(axis)
    out_shape = (n,) + x.shape if gather else x.shape
    return pl.pallas_call(
        functools.partial(_exchange_kernel, axis, n, gather),
        out_shape=jax.ShapeDtypeStruct(out_shape, x.dtype),
        in_specs=[pl.BlockSpec(memory_space=pltpu.VMEM)],
        out_specs=pl.BlockSpec(memory_space=pltpu.VMEM),
        scratch_shapes=[
            pltpu.SemaphoreType.DMA((n,)),
            pltpu.SemaphoreType.DMA((n,)),
            pltpu.SemaphoreType.DMA(()),
        ],
        compiler_params=pltpu.CompilerParams(collective_id=cid, has_side_effects=True),
    )(x)


def _greet(axes_sizes):
    barrier = pltpu.get_barrier_semaphore()
    total = 0
    for axis, n in axes_sizes:
        me = lax.axis_index(axis)
        for k in range(1, n):
            peer = lax.rem(me + k, n)
            pl.semaphore_signal(barrier, 1, device_id={axis: peer}, device_id_type=MESH_ID)
        total += n - 1
    pl.semaphore_wait(barrier, total)


def _start_round(axis, n, gather, source, target, send_sem, recv_sem, local_sem):
    me = lax.axis_index(axis)
    copies = []
    for k in range(1, n):
        peer = lax.rem(me + k, n)
        copy = pltpu.make_async_remote_copy(
            src_ref=source if gather else source.at[peer],
            dst_ref=target.at[me],
            send_sem=send_sem.at[k],
            recv_sem=recv_sem.at[k],
            device_id={axis: peer},
            device_id_type=MESH_ID,
        )
        copy.start()
        copies.append(copy)
    local = pltpu.make_async_copy(source if gather else source.at[me], target.at[me], local_sem)
    local.start()
    copies.append(local)
    return copies


def _two_round_kernel(first, second, mid, n_extra, x_ref, *refs):
    extra = refs[:n_extra]
    y_ref, landed, staged, send_a, recv_a, send_b, recv_b, local_sems = refs[n_extra:]
    axis_a, n_a, gather_a = first
    axis_b, n_b, gather_b = second
    greeted = [(axis_a, n_a)] if axis_a == axis_b else [(axis_a, n_a), (axis_b, n_b)]
    _greet(greeted)
    for copy in _start_round(axis_a, n_a, gather_a, x_ref, landed, send_a, recv_a, local_sems.at[0]):
        copy.wait()
    staged[...] = mid(landed, *extra)
    for copy in _start_round(axis_b, n_b, gather_b, staged, y_ref, send_b, recv_b, local_sems.at[1]):
        copy.wait()


def two_rounds(x, first, second, mid, staged_shape, staged_dtype, cid, extra=()):
    axis_a, gather_a = first
    axis_b, gather_b = second
    n_a, n_b = lax.axis_size(axis_a), lax.axis_size(axis_b)
    landed_shape = (n_a,) + x.shape if gather_a else x.shape
    out_shape = (n_b,) + staged_shape if gather_b else staged_shape
    return pl.pallas_call(
        functools.partial(
            _two_round_kernel, (axis_a, n_a, gather_a), (axis_b, n_b, gather_b), mid, len(extra)
        ),
        out_shape=jax.ShapeDtypeStruct(out_shape, staged_dtype),
        in_specs=[pl.BlockSpec(memory_space=pltpu.VMEM)] * (1 + len(extra)),
        out_specs=pl.BlockSpec(memory_space=pltpu.VMEM),
        scratch_shapes=[
            pltpu.VMEM(landed_shape, x.dtype),
            pltpu.VMEM(staged_shape, staged_dtype),
            pltpu.SemaphoreType.DMA((n_a,)),
            pltpu.SemaphoreType.DMA((n_a,)),
            pltpu.SemaphoreType.DMA((n_b,)),
            pltpu.SemaphoreType.DMA((n_b,)),
            pltpu.SemaphoreType.DMA((2,)),
        ],
        compiler_params=pltpu.CompilerParams(collective_id=cid, has_side_effects=True),
    )(x, *extra)


def _block_sum(landed):
    total = landed[0].astype(jnp.float32)
    for k in range(1, landed.shape[0]):
        total = total + landed[k].astype(jnp.float32)
    return total


def _mlp_kernel(
    x_ref, gate_ref, up_ref, down_map_ref, gate_map_ref, up_map_ref, down_ref,
    out_ref, spread_ref, landed1, staged1, staged2, landed2, staged3, landed3,
    send0, recv0, send1, recv1, send2, recv2, send3, recv3, local_sems,
):
    n_req = spread_ref.shape[0]
    n_seq = landed3.shape[0]
    rows = n_req * spread_ref.shape[2]
    units = gate_ref.shape[1]
    _greet([("req", n_req), ("seq", n_seq)])
    for copy in _start_round("req", n_req, False, x_ref, spread_ref, send0, recv0, local_sems.at[0]):
        copy.wait()
    normed_all = spread_ref[:, 1].reshape(rows, spread_ref.shape[3])
    staged1[:, :, :units] = jnp.dot(
        normed_all, gate_ref[...], preferred_element_type=jnp.float32
    ).reshape(staged1.shape[0], staged1.shape[1], units)
    staged1[:, :, units : 2 * units] = jnp.dot(
        normed_all, up_ref[...], preferred_element_type=jnp.float32
    ).reshape(staged1.shape[0], staged1.shape[1], units)
    staged1[:, :, 2 * units :] = jnp.dot(
        normed_all, down_map_ref[...], preferred_element_type=jnp.float32
    ).reshape(staged1.shape[0], staged1.shape[1], staged1.shape[2] - 2 * units)
    for copy in _start_round("req", n_req, False, staged1, landed1, send1, recv1, local_sems.at[1]):
        copy.wait()
    total = _block_sum(landed1)
    low = total[:, 2 * units :].astype(jnp.bfloat16)
    gate_pre = total[:, :units] + jnp.dot(low, gate_map_ref[...], preferred_element_type=jnp.float32)
    up_part = total[:, units : 2 * units] + jnp.dot(
        low, up_map_ref[...], preferred_element_type=jnp.float32
    )
    staged2[...] = (gate_pre / (1.0 + jnp.exp(-gate_pre)) * up_part).astype(jnp.bfloat16)
    for copy in _start_round("req", n_req, True, staged2, landed2, send2, recv2, local_sems.at[2]):
        copy.wait()
    inner = landed2[...].reshape(rows, units)
    staged3[...] = jnp.dot(inner, down_ref[...], preferred_element_type=jnp.float32).reshape(
        staged3.shape
    )
    for copy in _start_round("seq", n_seq, False, staged3, landed3, send3, recv3, local_sems.at[3]):
        copy.wait()
    out_ref[...] = _block_sum(landed3)


def fused_mlp(both, gate_weight, up_weight, down_map, gate_map, up_map, down_weight, cid):
    n_req, n_seq = lax.axis_size("req"), lax.axis_size("seq")
    group_rows = both.shape[2]
    rows = n_req * group_rows
    units = gate_weight.shape[1]
    wide = 2 * units + down_map.shape[1]
    out_rows = rows // n_seq
    vmem = pltpu.VMEM
    return pl.pallas_call(
        _mlp_kernel,
        out_shape=(
            jax.ShapeDtypeStruct((out_rows, down_weight.shape[1]), jnp.float32),
            jax.ShapeDtypeStruct(both.shape, both.dtype),
        ),
        in_specs=[pl.BlockSpec(memory_space=vmem)] * 7,
        out_specs=(pl.BlockSpec(memory_space=vmem), pl.BlockSpec(memory_space=vmem)),
        scratch_shapes=[
            vmem((n_req, group_rows, wide), jnp.float32),
            vmem((n_req, group_rows, wide), jnp.float32),
            vmem((group_rows, units), jnp.bfloat16),
            vmem((n_req, group_rows, units), jnp.bfloat16),
            vmem((n_seq, out_rows, down_weight.shape[1]), jnp.float32),
            vmem((n_seq, out_rows, down_weight.shape[1]), jnp.float32),
            pltpu.SemaphoreType.DMA((n_req,)),
            pltpu.SemaphoreType.DMA((n_req,)),
            pltpu.SemaphoreType.DMA((n_req,)),
            pltpu.SemaphoreType.DMA((n_req,)),
            pltpu.SemaphoreType.DMA((n_req,)),
            pltpu.SemaphoreType.DMA((n_req,)),
            pltpu.SemaphoreType.DMA((n_seq,)),
            pltpu.SemaphoreType.DMA((n_seq,)),
            pltpu.SemaphoreType.DMA((4,)),
        ],
        compiler_params=pltpu.CompilerParams(
            collective_id=cid, has_side_effects=True, vmem_limit_bytes=48 * 1024 * 1024
        ),
    )(both, gate_weight, up_weight, down_map, gate_map, up_map, down_weight)


def _chain_kernel(spec, n_extra, x_ref, *refs):
    extra = refs[:n_extra]
    y_ref = refs[n_extra]
    scratch = refs[n_extra + 1 :]
    count = len(spec)
    landed = list(scratch[: count - 1]) + [y_ref]
    staged = scratch[count - 1 : 2 * count - 2]
    sems = scratch[2 * count - 2 :]
    axes = []
    for axis, n, _, _ in spec:
        if (axis, n) not in axes:
            axes.append((axis, n))
    _greet(axes)
    source = x_ref
    for k, (axis, n, gather, mid) in enumerate(spec):
        copies = _start_round(
            axis, n, gather, source, landed[k], sems[2 * k], sems[2 * k + 1], sems[-1].at[k]
        )
        for copy in copies:
            copy.wait()
        if mid is not None:
            staged[k][...] = mid(landed[k], *extra)
            source = staged[k]


def chain(x, rounds, cid, extra=()):
    spec, landed_shapes, staged_shapes = [], [], []
    block = (x.shape, x.dtype)
    for index, (axis, gather, mid, made) in enumerate(rounds):
        n = lax.axis_size(axis)
        shape, dtype = block
        landed = ((n,) + shape if gather else shape, dtype)
        spec.append((axis, n, gather, mid))
        if index < len(rounds) - 1:
            landed_shapes.append(landed)
            staged_shapes.append(made)
            block = made
        else:
            out = landed
    sizes = [n for _, n, _, _ in spec]
    semaphores = []
    for n in sizes:
        semaphores += [pltpu.SemaphoreType.DMA((n,)), pltpu.SemaphoreType.DMA((n,))]
    return pl.pallas_call(
        functools.partial(_chain_kernel, spec, len(extra)),
        out_shape=jax.ShapeDtypeStruct(*out),
        in_specs=[pl.BlockSpec(memory_space=pltpu.VMEM)] * (1 + len(extra)),
        out_specs=pl.BlockSpec(memory_space=pltpu.VMEM),
        scratch_shapes=[pltpu.VMEM(*item) for item in landed_shapes]
        + [pltpu.VMEM(*item) for item in staged_shapes]
        + semaphores
        + [pltpu.SemaphoreType.DMA((len(spec),))],
        compiler_params=pltpu.CompilerParams(
            collective_id=cid, has_side_effects=True, vmem_limit_bytes=48 * 1024 * 1024
        ),
    )(x, *extra)


def _embed_kernel(
    x_a, x_b, out_a, out_b, landed_a, landed_b, staged_a, staged_b, arrived_a, arrived_b,
    send_a, recv_a, send_b, recv_b, send_c, recv_c, send_d, recv_d, local_sems,
):
    n_req, n_seq = landed_a.shape[0], landed_b.shape[0]
    _greet([("req", n_req), ("seq", n_seq)])
    first = _start_round("req", n_req, False, x_a, landed_a, send_a, recv_a, local_sems.at[0])
    first += _start_round("seq", n_seq, False, x_b, landed_b, send_b, recv_b, local_sems.at[1])
    for copy in first:
        copy.wait()
    staged_a[...] = _block_sum(landed_a).astype(staged_a.dtype)
    staged_b[...] = _block_sum(landed_b).astype(staged_b.dtype)
    second = _start_round("seq", n_seq, False, staged_a, arrived_a, send_c, recv_c, local_sems.at[2])
    second += _start_round("req", n_req, False, staged_b, arrived_b, send_d, recv_d, local_sems.at[3])
    for copy in second:
        copy.wait()
    out_a[...] = _block_sum(arrived_a)
    out_b[...] = _block_sum(arrived_b)


def embed_rows(x_a, x_b, cid):
    n_req, n_seq = x_a.shape[0], x_b.shape[0]
    block_a, block_b = x_a.shape[2:], x_b.shape[2:]
    vmem = pltpu.VMEM
    return pl.pallas_call(
        _embed_kernel,
        out_shape=(
            jax.ShapeDtypeStruct(block_a, jnp.float32),
            jax.ShapeDtypeStruct(block_b, jnp.float32),
        ),
        in_specs=[pl.BlockSpec(memory_space=vmem)] * 2,
        out_specs=(pl.BlockSpec(memory_space=vmem), pl.BlockSpec(memory_space=vmem)),
        scratch_shapes=[
            vmem(x_a.shape, x_a.dtype),
            vmem(x_b.shape, x_b.dtype),
            vmem(x_a.shape[1:], x_a.dtype),
            vmem(x_b.shape[1:], x_b.dtype),
            vmem((n_seq,) + block_a, x_a.dtype),
            vmem((n_req,) + block_b, x_b.dtype),
            pltpu.SemaphoreType.DMA((n_req,)),
            pltpu.SemaphoreType.DMA((n_req,)),
            pltpu.SemaphoreType.DMA((n_seq,)),
            pltpu.SemaphoreType.DMA((n_seq,)),
            pltpu.SemaphoreType.DMA((n_seq,)),
            pltpu.SemaphoreType.DMA((n_seq,)),
            pltpu.SemaphoreType.DMA((n_req,)),
            pltpu.SemaphoreType.DMA((n_req,)),
            pltpu.SemaphoreType.DMA((4,)),
        ],
        compiler_params=pltpu.CompilerParams(
            collective_id=cid, has_side_effects=True, vmem_limit_bytes=48 * 1024 * 1024
        ),
    )(x_a, x_b)


def merged_2(array, axis, combine):
    everything = jax.tree.map(lambda part: lax.all_gather(part, axis), array)
    first = jax.tree.map(lambda part: part[0], everything)

    def hop(k, so_far):
        return combine(so_far, jax.tree.map(lambda part: part[k], everything))

    return lax.fori_loop(1, lax.axis_size(axis), hop, first)


def rms_norm(matrix, gain_vec):
    widened = matrix.astype(jnp.float32)
    factor = lax.rsqrt(jnp.mean(widened * widened, axis=-1, keepdims=True) + EPSILON)
    return (widened * factor * gain_vec.astype(jnp.float32)).astype(jnp.bfloat16)


def rotate(vectors, positions):
    half_dim = vectors.shape[-1] // 2
    frequency = ROTARY_BASE ** (-2.0 * jnp.arange(half_dim, dtype=jnp.float32) / vectors.shape[-1])
    angles = positions.astype(jnp.float32)[..., None, None] * frequency
    cosine = jnp.cos(angles)
    sine_part = jnp.sin(angles)
    front_half = vectors[..., :half_dim]
    back_half = vectors[..., half_dim:]
    return jnp.concatenate(
        [front_half * cosine - back_half * sine_part, back_half * cosine + front_half * sine_part],
        axis=-1,
    )


def softmax_join(earlier, later):
    first_max, first_sum, first_out = earlier
    second_max, second_sum, second_out = later
    overall = jnp.maximum(first_max, second_max)
    first_factor = jnp.exp(first_max - overall)
    second_factor = jnp.exp(second_max - overall)
    return (
        overall,
        first_sum * first_factor + second_sum * second_factor,
        first_out * first_factor[..., None] + second_out * second_factor[..., None],
    )


def body(
    given_token_index,
    hidden,
    token_embedding_table,
    attention_norm_gain,
    query_key_value_weight,
    rotated_key_cache,
    cached_value_pages,
    lengths,
    request_page_slots,
    attention_output_weight,
    feedforward_norm_gain,
    gate_weight,
    up_weight,
    adapter_down_map,
    adapter_gate_map,
    adapter_up_map,
    down_weight,
):
    seq_devices = lax.axis_size("seq")
    req_devices = lax.axis_size("req")
    seq_index = lax.axis_index("seq")
    req_index = lax.axis_index("req")
    group_rows = hidden.shape[0]
    requests = lengths.shape[0]
    steps_each = group_rows // requests
    vocab_rows = token_embedding_table.shape[0]
    first_id = (seq_index * req_devices + req_index) * vocab_rows
    local_ids = given_token_index - first_id
    present = (local_ids >= 0) & (local_ids < vocab_rows)
    looked = jnp.take(token_embedding_table, jnp.clip(local_ids, 0, vocab_rows - 1), axis=0).astype(
        jnp.float32
    )
    looked = jnp.where(present[:, None], looked, 0.0).astype(jnp.bfloat16)
    row_share = group_rows // seq_devices
    lanes = 128
    half = looked.shape[1] // 2
    per_row = looked.reshape(req_devices, seq_devices, row_share, looked.shape[1])
    x_a = per_row[..., :half].reshape(req_devices, seq_devices, row_share * half // lanes, lanes)
    x_b = jnp.transpose(per_row[..., half:], (1, 0, 2, 3)).reshape(
        seq_devices, req_devices, row_share * half // lanes, lanes
    )
    sum_a, sum_b = embed_rows(x_a, x_b, 10)
    embedded_rows = jnp.concatenate(
        [sum_a.reshape(row_share, half), sum_b.reshape(row_share, half)], axis=1
    ).astype(jnp.bfloat16)
    own_hidden = lax.dynamic_slice_in_dim(hidden, seq_index * row_share, row_share, 0)
    own_rows = jnp.concatenate([own_hidden, embedded_rows], axis=1)
    normed_rows = rms_norm(own_rows, attention_norm_gain)
    normed = exchange(normed_rows.reshape(-1, lanes), "seq", 12, gather=True).reshape(
        group_rows, own_rows.shape[1]
    )
    width_share = normed.shape[1] // req_devices
    to_owners = jnp.transpose(normed.reshape(group_rows, req_devices, width_share), (1, 0, 2))
    qkv_cols = query_key_value_weight.shape[1]

    def project(landed, weight):
        flat = landed[...].reshape(req_devices * group_rows, width_share)
        product = jnp.dot(flat, weight[...], preferred_element_type=jnp.float32)
        return product.reshape(req_devices, group_rows, qkv_cols)

    qkv_all = chain(
        to_owners,
        [
            ("req", False, project, ((req_devices, group_rows, qkv_cols), jnp.float32)),
            (
                "req",
                False,
                lambda landed, weight: _block_sum(landed).astype(jnp.bfloat16),
                ((group_rows, qkv_cols), jnp.bfloat16),
            ),
            ("seq", True, None, None),
        ],
        4,
        extra=(query_key_value_weight,),
    )
    projected = jnp.transpose(qkv_all, (1, 0, 2)).reshape(group_rows, seq_devices * qkv_all.shape[2])
    head_cols = HEADS * HD
    queries = projected[:, :head_cols].reshape(requests, steps_each, HEADS, HD)
    new_keys = projected[:, head_cols : 2 * head_cols].reshape(requests, steps_each, HEADS, HD)
    new_values = projected[:, 2 * head_cols :].reshape(requests, steps_each, HEADS, HD)
    positions = lengths[:, None] + jnp.arange(steps_each, dtype=jnp.int32)[None, :]
    queries = rotate(queries.astype(jnp.float32), positions).astype(jnp.bfloat16)
    new_keys = rotate(new_keys.astype(jnp.float32), positions).astype(jnp.bfloat16)
    slots = rotated_key_cache.shape[0]
    page_len = rotated_key_cache.shape[2]
    cache_k = rotated_key_cache.reshape(slots * page_len, head_cols)
    cache_v = cached_value_pages.reshape(slots * page_len, head_cols)
    slot_ids = seq_index * slots + jnp.arange(slots, dtype=jnp.int32)
    page_ids = jnp.arange(request_page_slots.shape[1], dtype=jnp.int32)
    is_live = page_ids[None, :] < ((lengths + page_len - 1) // page_len)[:, None]
    matches = (request_page_slots[:, :, None] == slot_ids[None, None, :]) & is_live[:, :, None]
    is_owned = jnp.any(matches, axis=1)
    page_of = jnp.sum(jnp.where(matches, page_ids[None, :, None], 0), axis=1)
    token_pos = (
        page_of[:, :, None] * page_len + jnp.arange(page_len, dtype=jnp.int32)[None, None, :]
    )
    is_valid = (is_owned[:, :, None] & (token_pos < lengths[:, None, None])).reshape(
        requests, slots * page_len
    )
    score_scale = 1.0 / math.sqrt(HD)
    head_mask = (jnp.arange(head_cols, dtype=jnp.int32)[None, :] // HD) == jnp.arange(
        HEADS, dtype=jnp.int32
    )[:, None]
    query_rows = queries.reshape(group_rows, head_cols)
    spread_queries = jnp.where(head_mask[None], query_rows[:, None, :], jnp.zeros((), jnp.bfloat16))
    scores = (
        jnp.dot(
            spread_queries.reshape(group_rows * HEADS, head_cols),
            cache_k.T,
            preferred_element_type=jnp.float32,
        )
        * score_scale
    ).reshape(requests, steps_each, HEADS, slots * page_len)
    mask_b = is_valid[:, None, None, :]
    local_max = jnp.max(jnp.where(mask_b, scores, NEGATIVE), axis=-1)
    weights = jnp.where(mask_b, jnp.exp(scores - local_max[..., None]), 0.0)
    local_sum = jnp.sum(weights, axis=-1)
    spread_out = jnp.dot(
        weights.astype(jnp.bfloat16).reshape(group_rows * HEADS, slots * page_len),
        cache_v,
        preferred_element_type=jnp.float32,
    ).reshape(group_rows, HEADS, head_cols)
    local_out = jnp.sum(jnp.where(head_mask[None], spread_out, 0.0), axis=1).reshape(
        requests, steps_each, HEADS, HD
    )
    fresh_scores = (
        jnp.einsum("rthd,rshd->rths", queries, new_keys, preferred_element_type=jnp.float32)
        * score_scale
    )
    causal = jnp.arange(steps_each)[:, None] >= jnp.arange(steps_each)[None, :]
    fresh_mask = causal[None, :, None, :]
    fresh_max = jnp.max(jnp.where(fresh_mask, fresh_scores, NEGATIVE), axis=-1)
    fresh_w = jnp.where(fresh_mask, jnp.exp(fresh_scores - fresh_max[..., None]), 0.0)
    fresh_sum = jnp.sum(fresh_w, axis=-1)
    fresh_out = jnp.einsum(
        "rths,rshd->rthd",
        fresh_w.astype(jnp.bfloat16),
        new_values,
        preferred_element_type=jnp.float32,
    )
    own_heads = HEADS // seq_devices
    first_head = seq_index * own_heads

    def own_slice(member):
        return lax.dynamic_slice_in_dim(member, first_head, own_heads, 2)

    pad_cols = 256 - HD - 2
    packed = jnp.concatenate(
        [
            local_out,
            local_max[..., None],
            local_sum[..., None],
            jnp.zeros(local_out.shape[:-1] + (pad_cols,), jnp.float32),
        ],
        axis=-1,
    )
    packed = packed.reshape(requests * steps_each, seq_devices, own_heads, 256)
    packed = jnp.transpose(packed, (1, 0, 2, 3)).reshape(seq_devices, group_rows * own_heads, 256)
    arrived = exchange(packed, "seq", 0).reshape(seq_devices, requests, steps_each, own_heads, 256)
    part_o = arrived[..., :HD]
    part_m = arrived[..., HD]
    part_l = arrived[..., HD + 1]
    f_max, f_sum, f_out = own_slice(fresh_max), own_slice(fresh_sum), own_slice(fresh_out)
    overall = jnp.maximum(jnp.max(part_m, axis=0), f_max)
    part_factor = jnp.exp(part_m - overall[None])
    fresh_factor = jnp.exp(f_max - overall)
    denominator = jnp.sum(part_l * part_factor, axis=0) + f_sum * fresh_factor
    numerator = jnp.sum(part_o * part_factor[..., None], axis=0) + f_out * fresh_factor[..., None]
    attention = (
        (numerator / denominator[..., None])
        .astype(jnp.bfloat16)
        .reshape(group_rows, own_heads * HD)
    )
    projected_out = jnp.dot(attention, attention_output_weight, preferred_element_type=jnp.float32)
    model_width = projected_out.shape[1]
    after_attn = two_rounds(
        projected_out.reshape(seq_devices, row_share * model_width // lanes, lanes),
        ("seq", False),
        ("seq", True),
        lambda landed, own: (own[...].astype(jnp.float32) + _block_sum(landed)).astype(jnp.bfloat16),
        (row_share * model_width // lanes, lanes),
        jnp.bfloat16,
        1,
        extra=(own_rows.reshape(-1, lanes),),
    ).reshape(group_rows, model_width)
    second_normed_state = rms_norm(after_attn, feedforward_norm_gain)
    both = jnp.stack([after_attn, second_normed_state]).reshape(2, group_rows, req_devices, width_share)
    both = jnp.transpose(both, (2, 0, 1, 3))
    down_sum, both_parts = fused_mlp(
        both, gate_weight, up_weight, adapter_down_map, adapter_gate_map, adapter_up_map, down_weight, 7
    )
    residual_cols = both_parts[:, 0].reshape(req_devices * group_rows, width_share)
    out_rows = residual_cols.shape[0] // seq_devices
    residual_rows = lax.dynamic_slice_in_dim(residual_cols, seq_index * out_rows, out_rows, 0)
    return (residual_rows.astype(jnp.float32) + down_sum).astype(jnp.bfloat16)


def solution(mesh):
    placed = (
        P(),
        P("req", None),
        P(("seq", "req"), None),
        P(),
        P("req", "seq"),
        P("seq", "req", None, None),
        P("seq", "req", None, None),
        P("req"),
        P("req", None),
        P("seq", None),
        P(),
        P("req", "seq"),
        P("req", "seq"),
        P("req", None),
        P(None, "seq"),
        P(None, "seq"),
        P("seq", "req"),
    )
    return jax.shard_map(
        body, mesh=mesh, in_specs=placed, out_specs=P("seq", "req"), check_vma=False
    )
```

```python
import functools
import math

import jax
import jax.numpy as jnp
from jax import lax
from jax.experimental import pallas as pl
from jax.experimental.pallas import tpu as pltpu
from jax.sharding import PartitionSpec as P

HEADS = 16
HD = 224


NEGATIVE = -1e30
EPSILON = 1e-05
ROTARY_BASE = 10000.0


MESH_ID = pl.DeviceIdType.MESH


def _exchange_kernel(axis, n, gather, x_ref, y_ref, send_sem, recv_sem, local_sem):
    me = lax.axis_index(axis)
    barrier = pltpu.get_barrier_semaphore()
    for k in range(1, n):
        peer = lax.rem(me + k, n)
        pl.semaphore_signal(barrier, 1, device_id={axis: peer}, device_id_type=MESH_ID)
    pl.semaphore_wait(barrier, n - 1)
    copies = []
    for k in range(1, n):
        peer = lax.rem(me + k, n)
        source = x_ref if gather else x_ref.at[peer]
        copy = pltpu.make_async_remote_copy(
            src_ref=source,
            dst_ref=y_ref.at[me],
            send_sem=send_sem.at[k],
            recv_sem=recv_sem.at[k],
            device_id={axis: peer},
            device_id_type=MESH_ID,
        )
        copy.start()
        copies.append(copy)
    local = pltpu.make_async_copy(x_ref if gather else x_ref.at[me], y_ref.at[me], local_sem)
    local.start()
    local.wait()
    for copy in copies:
        copy.wait()


def exchange(x, axis, cid, gather=False):
    n = lax.axis_size(axis)
    out_shape = (n,) + x.shape if gather else x.shape
    return pl.pallas_call(
        functools.partial(_exchange_kernel, axis, n, gather),
        out_shape=jax.ShapeDtypeStruct(out_shape, x.dtype),
        in_specs=[pl.BlockSpec(memory_space=pltpu.VMEM)],
        out_specs=pl.BlockSpec(memory_space=pltpu.VMEM),
        scratch_shapes=[
            pltpu.SemaphoreType.DMA((n,)),
            pltpu.SemaphoreType.DMA((n,)),
            pltpu.SemaphoreType.DMA(()),
        ],
        compiler_params=pltpu.CompilerParams(collective_id=cid, has_side_effects=True),
    )(x)


def _greet(axes_sizes):
    barrier = pltpu.get_barrier_semaphore()
    total = 0
    for axis, n in axes_sizes:
        me = lax.axis_index(axis)
        for k in range(1, n):
            peer = lax.rem(me + k, n)
            pl.semaphore_signal(barrier, 1, device_id={axis: peer}, device_id_type=MESH_ID)
        total += n - 1
    pl.semaphore_wait(barrier, total)


def _start_round(axis, n, gather, source, target, send_sem, recv_sem, local_sem):
    me = lax.axis_index(axis)
    copies = []
    for k in range(1, n):
        peer = lax.rem(me + k, n)
        copy = pltpu.make_async_remote_copy(
            src_ref=source if gather else source.at[peer],
            dst_ref=target.at[me],
            send_sem=send_sem.at[k],
            recv_sem=recv_sem.at[k],
            device_id={axis: peer},
            device_id_type=MESH_ID,
        )
        copy.start()
        copies.append(copy)
    local = pltpu.make_async_copy(source if gather else source.at[me], target.at[me], local_sem)
    local.start()
    copies.append(local)
    return copies


def _two_round_kernel(first, second, mid, n_extra, x_ref, *refs):
    extra = refs[:n_extra]
    y_ref, landed, staged, send_a, recv_a, send_b, recv_b, local_sems = refs[n_extra:]
    axis_a, n_a, gather_a = first
    axis_b, n_b, gather_b = second
    greeted = [(axis_a, n_a)] if axis_a == axis_b else [(axis_a, n_a), (axis_b, n_b)]
    _greet(greeted)
    for copy in _start_round(axis_a, n_a, gather_a, x_ref, landed, send_a, recv_a, local_sems.at[0]):
        copy.wait()
    staged[...] = mid(landed, *extra)
    for copy in _start_round(axis_b, n_b, gather_b, staged, y_ref, send_b, recv_b, local_sems.at[1]):
        copy.wait()


def two_rounds(x, first, second, mid, staged_shape, staged_dtype, cid, extra=()):
    axis_a, gather_a = first
    axis_b, gather_b = second
    n_a, n_b = lax.axis_size(axis_a), lax.axis_size(axis_b)
    landed_shape = (n_a,) + x.shape if gather_a else x.shape
    out_shape = (n_b,) + staged_shape if gather_b else staged_shape
    return pl.pallas_call(
        functools.partial(
            _two_round_kernel, (axis_a, n_a, gather_a), (axis_b, n_b, gather_b), mid, len(extra)
        ),
        out_shape=jax.ShapeDtypeStruct(out_shape, staged_dtype),
        in_specs=[pl.BlockSpec(memory_space=pltpu.VMEM)] * (1 + len(extra)),
        out_specs=pl.BlockSpec(memory_space=pltpu.VMEM),
        scratch_shapes=[
            pltpu.VMEM(landed_shape, x.dtype),
            pltpu.VMEM(staged_shape, staged_dtype),
            pltpu.SemaphoreType.DMA((n_a,)),
            pltpu.SemaphoreType.DMA((n_a,)),
            pltpu.SemaphoreType.DMA((n_b,)),
            pltpu.SemaphoreType.DMA((n_b,)),
            pltpu.SemaphoreType.DMA((2,)),
        ],
        compiler_params=pltpu.CompilerParams(collective_id=cid, has_side_effects=True),
    )(x, *extra)


def _block_sum(landed):
    total = landed[0].astype(jnp.float32)
    for k in range(1, landed.shape[0]):
        total = total + landed[k].astype(jnp.float32)
    return total


def _mlp_kernel(
    x_ref, gate_hbm, up_hbm, down_map_hbm, gate_map_hbm, up_map_hbm, down_hbm,
    out_ref, spread_ref, landed1, staged1, staged2, landed2, staged3, landed3,
    send0, recv0, send1, recv1, send2, recv2, send3, recv3, local_sems,
    gate_ref, up_ref, down_map_ref, gate_map_ref, up_map_ref, down_ref, weight_sems,
):
    n_req = spread_ref.shape[0]
    n_seq = landed3.shape[0]
    rows = n_req * spread_ref.shape[2]
    units = gate_ref.shape[1]
    loads = []
    pairs = (
        (gate_hbm, gate_ref), (up_hbm, up_ref), (down_map_hbm, down_map_ref),
        (gate_map_hbm, gate_map_ref), (up_map_hbm, up_map_ref), (down_hbm, down_ref),
    )
    for index, (source, target) in enumerate(pairs):
        load = pltpu.make_async_copy(source, target, weight_sems.at[index])
        load.start()
        loads.append(load)
    _greet([("req", n_req), ("seq", n_seq)])
    for copy in _start_round("req", n_req, False, x_ref, spread_ref, send0, recv0, local_sems.at[0]):
        copy.wait()
    for load in loads[:3]:
        load.wait()
    normed_all = spread_ref[:, 1].reshape(rows, spread_ref.shape[3])
    staged1[:, :, :units] = jnp.dot(
        normed_all, gate_ref[...], preferred_element_type=jnp.float32
    ).reshape(staged1.shape[0], staged1.shape[1], units)
    staged1[:, :, units : 2 * units] = jnp.dot(
        normed_all, up_ref[...], preferred_element_type=jnp.float32
    ).reshape(staged1.shape[0], staged1.shape[1], units)
    staged1[:, :, 2 * units :] = jnp.dot(
        normed_all, down_map_ref[...], preferred_element_type=jnp.float32
    ).reshape(staged1.shape[0], staged1.shape[1], staged1.shape[2] - 2 * units)
    for copy in _start_round("req", n_req, False, staged1, landed1, send1, recv1, local_sems.at[1]):
        copy.wait()
    for load in loads[3:5]:
        load.wait()
    total = _block_sum(landed1)
    low = total[:, 2 * units :].astype(jnp.bfloat16)
    gate_pre = total[:, :units] + jnp.dot(low, gate_map_ref[...], preferred_element_type=jnp.float32)
    up_part = total[:, units : 2 * units] + jnp.dot(
        low, up_map_ref[...], preferred_element_type=jnp.float32
    )
    staged2[...] = (gate_pre / (1.0 + jnp.exp(-gate_pre)) * up_part).astype(jnp.bfloat16)
    for copy in _start_round("req", n_req, True, staged2, landed2, send2, recv2, local_sems.at[2]):
        copy.wait()
    loads[5].wait()
    inner = landed2[...].reshape(rows, units)
    staged3[...] = jnp.dot(inner, down_ref[...], preferred_element_type=jnp.float32).reshape(
        staged3.shape
    )
    for copy in _start_round("seq", n_seq, False, staged3, landed3, send3, recv3, local_sems.at[3]):
        copy.wait()
    out_ref[...] = _block_sum(landed3)


def fused_mlp(both, gate_weight, up_weight, down_map, gate_map, up_map, down_weight, cid):
    n_req, n_seq = lax.axis_size("req"), lax.axis_size("seq")
    group_rows = both.shape[2]
    rows = n_req * group_rows
    units = gate_weight.shape[1]
    wide = 2 * units + down_map.shape[1]
    out_rows = rows // n_seq
    vmem = pltpu.VMEM
    return pl.pallas_call(
        _mlp_kernel,
        out_shape=(
            jax.ShapeDtypeStruct((out_rows, down_weight.shape[1]), jnp.float32),
            jax.ShapeDtypeStruct(both.shape, both.dtype),
        ),
        in_specs=[pl.BlockSpec(memory_space=vmem)] + [pl.BlockSpec(memory_space=pl.ANY)] * 6,
        out_specs=(pl.BlockSpec(memory_space=vmem), pl.BlockSpec(memory_space=vmem)),
        scratch_shapes=[
            vmem((n_req, group_rows, wide), jnp.float32),
            vmem((n_req, group_rows, wide), jnp.float32),
            vmem((group_rows, units), jnp.bfloat16),
            vmem((n_req, group_rows, units), jnp.bfloat16),
            vmem((n_seq, out_rows, down_weight.shape[1]), jnp.float32),
            vmem((n_seq, out_rows, down_weight.shape[1]), jnp.float32),
            pltpu.SemaphoreType.DMA((n_req,)),
            pltpu.SemaphoreType.DMA((n_req,)),
            pltpu.SemaphoreType.DMA((n_req,)),
            pltpu.SemaphoreType.DMA((n_req,)),
            pltpu.SemaphoreType.DMA((n_req,)),
            pltpu.SemaphoreType.DMA((n_req,)),
            pltpu.SemaphoreType.DMA((n_seq,)),
            pltpu.SemaphoreType.DMA((n_seq,)),
            pltpu.SemaphoreType.DMA((4,)),
        ]
        + [
            vmem(weight.shape, weight.dtype)
            for weight in (gate_weight, up_weight, down_map, gate_map, up_map, down_weight)
        ]
        + [pltpu.SemaphoreType.DMA((6,))],
        compiler_params=pltpu.CompilerParams(
            collective_id=cid, has_side_effects=True, vmem_limit_bytes=48 * 1024 * 1024
        ),
    )(both, gate_weight, up_weight, down_map, gate_map, up_map, down_weight)


def _chain_kernel(spec, n_extra, x_ref, *refs):
    extra_hbm = refs[:n_extra]
    y_ref = refs[n_extra]
    scratch = refs[n_extra + 1 :]
    count = len(spec)
    landed = list(scratch[: count - 1]) + [y_ref]
    staged = scratch[count - 1 : 2 * count - 2]
    extra = scratch[2 * count - 2 : 2 * count - 2 + n_extra]
    extra_sems = scratch[2 * count - 2 + n_extra]
    sems = scratch[2 * count - 1 + n_extra :]
    loads = []
    for index in range(n_extra):
        load = pltpu.make_async_copy(extra_hbm[index], extra[index], extra_sems.at[index])
        load.start()
        loads.append(load)
    axes = []
    for axis, n, _, _ in spec:
        if (axis, n) not in axes:
            axes.append((axis, n))
    _greet(axes)
    source = x_ref
    for k, (axis, n, gather, mid) in enumerate(spec):
        copies = _start_round(
            axis, n, gather, source, landed[k], sems[2 * k], sems[2 * k + 1], sems[-1].at[k]
        )
        for copy in copies:
            copy.wait()
        if k == 0:
            for load in loads:
                load.wait()
        if mid is not None:
            staged[k][...] = mid(landed[k], *extra)
            source = staged[k]


def chain(x, rounds, cid, extra=()):
    spec, landed_shapes, staged_shapes = [], [], []
    block = (x.shape, x.dtype)
    for index, (axis, gather, mid, made) in enumerate(rounds):
        n = lax.axis_size(axis)
        shape, dtype = block
        landed = ((n,) + shape if gather else shape, dtype)
        spec.append((axis, n, gather, mid))
        if index < len(rounds) - 1:
            landed_shapes.append(landed)
            staged_shapes.append(made)
            block = made
        else:
            out = landed
    sizes = [n for _, n, _, _ in spec]
    semaphores = []
    for n in sizes:
        semaphores += [pltpu.SemaphoreType.DMA((n,)), pltpu.SemaphoreType.DMA((n,))]
    return pl.pallas_call(
        functools.partial(_chain_kernel, spec, len(extra)),
        out_shape=jax.ShapeDtypeStruct(*out),
        in_specs=[pl.BlockSpec(memory_space=pltpu.VMEM)]
        + [pl.BlockSpec(memory_space=pl.ANY)] * len(extra),
        out_specs=pl.BlockSpec(memory_space=pltpu.VMEM),
        scratch_shapes=[pltpu.VMEM(*item) for item in landed_shapes]
        + [pltpu.VMEM(*item) for item in staged_shapes]
        + [pltpu.VMEM(item.shape, item.dtype) for item in extra]
        + [pltpu.SemaphoreType.DMA((max(len(extra), 1),))]
        + semaphores
        + [pltpu.SemaphoreType.DMA((len(spec),))],
        compiler_params=pltpu.CompilerParams(
            collective_id=cid, has_side_effects=True, vmem_limit_bytes=48 * 1024 * 1024
        ),
    )(x, *extra)


def merged_2(array, axis, combine):
    everything = jax.tree.map(lambda part: lax.all_gather(part, axis), array)
    first = jax.tree.map(lambda part: part[0], everything)

    def hop(k, so_far):
        return combine(so_far, jax.tree.map(lambda part: part[k], everything))

    return lax.fori_loop(1, lax.axis_size(axis), hop, first)


def rms_norm(matrix, gain_vec):
    widened = matrix.astype(jnp.float32)
    factor = lax.rsqrt(jnp.mean(widened * widened, axis=-1, keepdims=True) + EPSILON)
    return (widened * factor * gain_vec.astype(jnp.float32)).astype(jnp.bfloat16)


def rotate(vectors, positions):
    half_dim = vectors.shape[-1] // 2
    frequency = ROTARY_BASE ** (-2.0 * jnp.arange(half_dim, dtype=jnp.float32) / vectors.shape[-1])
    angles = positions.astype(jnp.float32)[..., None, None] * frequency
    cosine = jnp.cos(angles)
    sine_part = jnp.sin(angles)
    front_half = vectors[..., :half_dim]
    back_half = vectors[..., half_dim:]
    return jnp.concatenate(
        [front_half * cosine - back_half * sine_part, back_half * cosine + front_half * sine_part],
        axis=-1,
    )


def softmax_join(earlier, later):
    first_max, first_sum, first_out = earlier
    second_max, second_sum, second_out = later
    overall = jnp.maximum(first_max, second_max)
    first_factor = jnp.exp(first_max - overall)
    second_factor = jnp.exp(second_max - overall)
    return (
        overall,
        first_sum * first_factor + second_sum * second_factor,
        first_out * first_factor[..., None] + second_out * second_factor[..., None],
    )


def body(
    given_token_index,
    hidden,
    token_embedding_table,
    attention_norm_gain,
    query_key_value_weight,
    rotated_key_cache,
    cached_value_pages,
    lengths,
    request_page_slots,
    attention_output_weight,
    feedforward_norm_gain,
    gate_weight,
    up_weight,
    adapter_down_map,
    adapter_gate_map,
    adapter_up_map,
    down_weight,
):
    seq_devices = lax.axis_size("seq")
    req_devices = lax.axis_size("req")
    seq_index = lax.axis_index("seq")
    req_index = lax.axis_index("req")
    group_rows = hidden.shape[0]
    requests = lengths.shape[0]
    steps_each = group_rows // requests
    vocab_rows = token_embedding_table.shape[0]
    first_id = (seq_index * req_devices + req_index) * vocab_rows
    local_ids = given_token_index - first_id
    present = (local_ids >= 0) & (local_ids < vocab_rows)
    looked = jnp.take(token_embedding_table, jnp.clip(local_ids, 0, vocab_rows - 1), axis=0).astype(
        jnp.float32
    )
    looked = jnp.where(present[:, None], looked, 0.0).astype(jnp.bfloat16)
    row_share = group_rows // seq_devices
    lanes = 128
    by_group = looked.reshape(req_devices, seq_devices, row_share * looked.shape[1] // lanes, lanes)
    row_parts = two_rounds(
        by_group,
        ("req", False),
        ("seq", False),
        lambda landed: _block_sum(landed).astype(jnp.bfloat16),
        by_group.shape[1:],
        jnp.bfloat16,
        10,
    )
    embedded_rows = (
        jnp.sum(row_parts.astype(jnp.float32), axis=0)
        .astype(jnp.bfloat16)
        .reshape(row_share, looked.shape[1])
    )
    own_hidden = lax.dynamic_slice_in_dim(hidden, seq_index * row_share, row_share, 0)
    own_rows = jnp.concatenate([own_hidden, embedded_rows], axis=1)
    normed_rows = rms_norm(own_rows, attention_norm_gain)
    normed = exchange(normed_rows.reshape(-1, lanes), "seq", 12, gather=True).reshape(
        group_rows, own_rows.shape[1]
    )
    width_share = normed.shape[1] // req_devices
    to_owners = jnp.transpose(normed.reshape(group_rows, req_devices, width_share), (1, 0, 2))
    qkv_cols = query_key_value_weight.shape[1]

    def project(landed, weight):
        flat = landed[...].reshape(req_devices * group_rows, width_share)
        product = jnp.dot(flat, weight[...], preferred_element_type=jnp.float32)
        return product.reshape(req_devices, group_rows, qkv_cols)

    qkv_all = chain(
        to_owners,
        [
            ("req", False, project, ((req_devices, group_rows, qkv_cols), jnp.float32)),
            (
                "req",
                False,
                lambda landed, weight: _block_sum(landed).astype(jnp.bfloat16),
                ((group_rows, qkv_cols), jnp.bfloat16),
            ),
            ("seq", True, None, None),
        ],
        4,
        extra=(query_key_value_weight,),
    )
    projected = jnp.transpose(qkv_all, (1, 0, 2)).reshape(group_rows, seq_devices * qkv_all.shape[2])
    head_cols = HEADS * HD
    queries = projected[:, :head_cols].reshape(requests, steps_each, HEADS, HD)
    new_keys = projected[:, head_cols : 2 * head_cols].reshape(requests, steps_each, HEADS, HD)
    new_values = projected[:, 2 * head_cols :].reshape(requests, steps_each, HEADS, HD)
    positions = lengths[:, None] + jnp.arange(steps_each, dtype=jnp.int32)[None, :]
    queries = rotate(queries.astype(jnp.float32), positions).astype(jnp.bfloat16)
    new_keys = rotate(new_keys.astype(jnp.float32), positions).astype(jnp.bfloat16)
    slots = rotated_key_cache.shape[0]
    page_len = rotated_key_cache.shape[2]
    cache_k = rotated_key_cache.reshape(slots * page_len, head_cols)
    cache_v = cached_value_pages.reshape(slots * page_len, head_cols)
    slot_ids = seq_index * slots + jnp.arange(slots, dtype=jnp.int32)
    page_ids = jnp.arange(request_page_slots.shape[1], dtype=jnp.int32)
    is_live = page_ids[None, :] < ((lengths + page_len - 1) // page_len)[:, None]
    matches = (request_page_slots[:, :, None] == slot_ids[None, None, :]) & is_live[:, :, None]
    is_owned = jnp.any(matches, axis=1)
    page_of = jnp.sum(jnp.where(matches, page_ids[None, :, None], 0), axis=1)
    token_pos = (
        page_of[:, :, None] * page_len + jnp.arange(page_len, dtype=jnp.int32)[None, None, :]
    )
    is_valid = (is_owned[:, :, None] & (token_pos < lengths[:, None, None])).reshape(
        requests, slots * page_len
    )
    score_scale = 1.0 / math.sqrt(HD)
    head_mask = (jnp.arange(head_cols, dtype=jnp.int32)[None, :] // HD) == jnp.arange(
        HEADS, dtype=jnp.int32
    )[:, None]
    query_rows = queries.reshape(group_rows, head_cols)
    spread_queries = jnp.where(head_mask[None], query_rows[:, None, :], jnp.zeros((), jnp.bfloat16))
    scores = (
        jnp.dot(
            spread_queries.reshape(group_rows * HEADS, head_cols),
            cache_k.T,
            preferred_element_type=jnp.float32,
        )
        * score_scale
    ).reshape(requests, steps_each, HEADS, slots * page_len)
    mask_b = is_valid[:, None, None, :]
    local_max = jnp.max(jnp.where(mask_b, scores, NEGATIVE), axis=-1)
    weights = jnp.where(mask_b, jnp.exp(scores - local_max[..., None]), 0.0)
    local_sum = jnp.sum(weights, axis=-1)
    spread_out = jnp.dot(
        weights.astype(jnp.bfloat16).reshape(group_rows * HEADS, slots * page_len),
        cache_v,
        preferred_element_type=jnp.float32,
    ).reshape(group_rows, HEADS, head_cols)
    local_out = jnp.sum(jnp.where(head_mask[None], spread_out, 0.0), axis=1).reshape(
        requests, steps_each, HEADS, HD
    )
    fresh_scores = (
        jnp.einsum("rthd,rshd->rths", queries, new_keys, preferred_element_type=jnp.float32)
        * score_scale
    )
    causal = jnp.arange(steps_each)[:, None] >= jnp.arange(steps_each)[None, :]
    fresh_mask = causal[None, :, None, :]
    fresh_max = jnp.max(jnp.where(fresh_mask, fresh_scores, NEGATIVE), axis=-1)
    fresh_w = jnp.where(fresh_mask, jnp.exp(fresh_scores - fresh_max[..., None]), 0.0)
    fresh_sum = jnp.sum(fresh_w, axis=-1)
    fresh_out = jnp.einsum(
        "rths,rshd->rthd",
        fresh_w.astype(jnp.bfloat16),
        new_values,
        preferred_element_type=jnp.float32,
    )
    own_heads = HEADS // seq_devices
    first_head = seq_index * own_heads

    def own_slice(member):
        return lax.dynamic_slice_in_dim(member, first_head, own_heads, 2)

    pad_cols = 256 - HD - 2
    packed = jnp.concatenate(
        [
            local_out,
            local_max[..., None],
            local_sum[..., None],
            jnp.zeros(local_out.shape[:-1] + (pad_cols,), jnp.float32),
        ],
        axis=-1,
    )
    packed = packed.reshape(requests * steps_each, seq_devices, own_heads, 256)
    packed = jnp.transpose(packed, (1, 0, 2, 3)).reshape(seq_devices, group_rows * own_heads, 256)
    arrived = exchange(packed, "seq", 0).reshape(seq_devices, requests, steps_each, own_heads, 256)
    part_o = arrived[..., :HD]
    part_m = arrived[..., HD]
    part_l = arrived[..., HD + 1]
    f_max, f_sum, f_out = own_slice(fresh_max), own_slice(fresh_sum), own_slice(fresh_out)
    overall = jnp.maximum(jnp.max(part_m, axis=0), f_max)
    part_factor = jnp.exp(part_m - overall[None])
    fresh_factor = jnp.exp(f_max - overall)
    denominator = jnp.sum(part_l * part_factor, axis=0) + f_sum * fresh_factor
    numerator = jnp.sum(part_o * part_factor[..., None], axis=0) + f_out * fresh_factor[..., None]
    attention = (
        (numerator / denominator[..., None])
        .astype(jnp.bfloat16)
        .reshape(group_rows, own_heads * HD)
    )
    projected_out = jnp.dot(attention, attention_output_weight, preferred_element_type=jnp.float32)
    model_width = projected_out.shape[1]
    after_attn = two_rounds(
        projected_out.reshape(seq_devices, row_share * model_width // lanes, lanes),
        ("seq", False),
        ("seq", True),
        lambda landed, own: (own[...].astype(jnp.float32) + _block_sum(landed)).astype(jnp.bfloat16),
        (row_share * model_width // lanes, lanes),
        jnp.bfloat16,
        1,
        extra=(own_rows.reshape(-1, lanes),),
    ).reshape(group_rows, model_width)
    second_normed_state = rms_norm(after_attn, feedforward_norm_gain)
    both = jnp.stack([after_attn, second_normed_state]).reshape(2, group_rows, req_devices, width_share)
    both = jnp.transpose(both, (2, 0, 1, 3))
    down_sum, both_parts = fused_mlp(
        both, gate_weight, up_weight, adapter_down_map, adapter_gate_map, adapter_up_map, down_weight, 7
    )
    residual_cols = both_parts[:, 0].reshape(req_devices * group_rows, width_share)
    out_rows = residual_cols.shape[0] // seq_devices
    residual_rows = lax.dynamic_slice_in_dim(residual_cols, seq_index * out_rows, out_rows, 0)
    return (residual_rows.astype(jnp.float32) + down_sum).astype(jnp.bfloat16)


def solution(mesh):
    placed = (
        P(),
        P("req", None),
        P(("seq", "req"), None),
        P(),
        P("req", "seq"),
        P("seq", "req", None, None),
        P("seq", "req", None, None),
        P("req"),
        P("req", None),
        P("seq", None),
        P(),
        P("req", "seq"),
        P("req", "seq"),
        P("req", None),
        P(None, "seq"),
        P(None, "seq"),
        P("seq", "req"),
    )
    return jax.shard_map(
        body, mesh=mesh, in_specs=placed, out_specs=P("seq", "req"), check_vma=False
    )
```

```python
import functools
import math

import jax
import jax.numpy as jnp
from jax import lax
from jax.experimental import pallas as pl
from jax.experimental.pallas import tpu as pltpu
from jax.sharding import PartitionSpec as P

HEADS = 16
HD = 224


NEGATIVE = -1e30
EPSILON = 1e-05
ROTARY_BASE = 10000.0


MESH_ID = pl.DeviceIdType.MESH


def _exchange_kernel(axis, n, gather, x_ref, y_ref, send_sem, recv_sem, local_sem):
    me = lax.axis_index(axis)
    barrier = pltpu.get_barrier_semaphore()
    for k in range(1, n):
        peer = lax.rem(me + k, n)
        pl.semaphore_signal(barrier, 1, device_id={axis: peer}, device_id_type=MESH_ID)
    pl.semaphore_wait(barrier, n - 1)
    copies = []
    for k in range(1, n):
        peer = lax.rem(me + k, n)
        source = x_ref if gather else x_ref.at[peer]
        copy = pltpu.make_async_remote_copy(
            src_ref=source,
            dst_ref=y_ref.at[me],
            send_sem=send_sem.at[k],
            recv_sem=recv_sem.at[k],
            device_id={axis: peer},
            device_id_type=MESH_ID,
        )
        copy.start()
        copies.append(copy)
    local = pltpu.make_async_copy(x_ref if gather else x_ref.at[me], y_ref.at[me], local_sem)
    local.start()
    local.wait()
    for copy in copies:
        copy.wait()


def exchange(x, axis, cid, gather=False):
    n = lax.axis_size(axis)
    out_shape = (n,) + x.shape if gather else x.shape
    return pl.pallas_call(
        functools.partial(_exchange_kernel, axis, n, gather),
        out_shape=jax.ShapeDtypeStruct(out_shape, x.dtype),
        in_specs=[pl.BlockSpec(memory_space=pltpu.VMEM)],
        out_specs=pl.BlockSpec(memory_space=pltpu.VMEM),
        scratch_shapes=[
            pltpu.SemaphoreType.DMA((n,)),
            pltpu.SemaphoreType.DMA((n,)),
            pltpu.SemaphoreType.DMA(()),
        ],
        compiler_params=pltpu.CompilerParams(collective_id=cid, has_side_effects=True),
    )(x)


def _greet(axes_sizes):
    barrier = pltpu.get_barrier_semaphore()
    total = 0
    for axis, n in axes_sizes:
        me = lax.axis_index(axis)
        for k in range(1, n):
            peer = lax.rem(me + k, n)
            pl.semaphore_signal(barrier, 1, device_id={axis: peer}, device_id_type=MESH_ID)
        total += n - 1
    pl.semaphore_wait(barrier, total)


def _start_round(axis, n, gather, source, target, send_sem, recv_sem, local_sem):
    me = lax.axis_index(axis)
    copies = []
    for k in range(1, n):
        peer = lax.rem(me + k, n)
        copy = pltpu.make_async_remote_copy(
            src_ref=source if gather else source.at[peer],
            dst_ref=target.at[me],
            send_sem=send_sem.at[k],
            recv_sem=recv_sem.at[k],
            device_id={axis: peer},
            device_id_type=MESH_ID,
        )
        copy.start()
        copies.append(copy)
    local = pltpu.make_async_copy(source if gather else source.at[me], target.at[me], local_sem)
    local.start()
    copies.append(local)
    return copies


def _two_round_kernel(first, second, mid, n_extra, x_ref, *refs):
    extra = refs[:n_extra]
    y_ref, landed, staged, send_a, recv_a, send_b, recv_b, local_sems = refs[n_extra:]
    axis_a, n_a, gather_a = first
    axis_b, n_b, gather_b = second
    greeted = [(axis_a, n_a)] if axis_a == axis_b else [(axis_a, n_a), (axis_b, n_b)]
    _greet(greeted)
    for copy in _start_round(axis_a, n_a, gather_a, x_ref, landed, send_a, recv_a, local_sems.at[0]):
        copy.wait()
    staged[...] = mid(landed, *extra)
    for copy in _start_round(axis_b, n_b, gather_b, staged, y_ref, send_b, recv_b, local_sems.at[1]):
        copy.wait()


def two_rounds(x, first, second, mid, staged_shape, staged_dtype, cid, extra=()):
    axis_a, gather_a = first
    axis_b, gather_b = second
    n_a, n_b = lax.axis_size(axis_a), lax.axis_size(axis_b)
    landed_shape = (n_a,) + x.shape if gather_a else x.shape
    out_shape = (n_b,) + staged_shape if gather_b else staged_shape
    return pl.pallas_call(
        functools.partial(
            _two_round_kernel, (axis_a, n_a, gather_a), (axis_b, n_b, gather_b), mid, len(extra)
        ),
        out_shape=jax.ShapeDtypeStruct(out_shape, staged_dtype),
        in_specs=[pl.BlockSpec(memory_space=pltpu.VMEM)] * (1 + len(extra)),
        out_specs=pl.BlockSpec(memory_space=pltpu.VMEM),
        scratch_shapes=[
            pltpu.VMEM(landed_shape, x.dtype),
            pltpu.VMEM(staged_shape, staged_dtype),
            pltpu.SemaphoreType.DMA((n_a,)),
            pltpu.SemaphoreType.DMA((n_a,)),
            pltpu.SemaphoreType.DMA((n_b,)),
            pltpu.SemaphoreType.DMA((n_b,)),
            pltpu.SemaphoreType.DMA((2,)),
        ],
        compiler_params=pltpu.CompilerParams(collective_id=cid, has_side_effects=True),
    )(x, *extra)


def _block_sum(landed):
    total = landed[0].astype(jnp.float32)
    for k in range(1, landed.shape[0]):
        total = total + landed[k].astype(jnp.float32)
    return total


def _mlp_kernel(
    x_ref, gate_hbm, up_hbm, down_map_hbm, gate_map_hbm, up_map_hbm, down_hbm,
    out_ref, spread_ref, landed1, staged1, staged2, landed2, staged3, landed3,
    send0, recv0, send1, recv1, send2, recv2, send3, recv3, local_sems,
    gate_ref, up_ref, down_map_ref, gate_map_ref, up_map_ref, down_ref, weight_sems,
):
    n_req = spread_ref.shape[0]
    n_seq = landed3.shape[0]
    rows = n_req * spread_ref.shape[2]
    units = gate_ref.shape[1]
    loads = []
    pairs = (
        (gate_hbm, gate_ref), (up_hbm, up_ref), (down_map_hbm, down_map_ref),
        (gate_map_hbm, gate_map_ref), (up_map_hbm, up_map_ref), (down_hbm, down_ref),
    )
    for index, (source, target) in enumerate(pairs):
        load = pltpu.make_async_copy(source, target, weight_sems.at[index])
        load.start()
        loads.append(load)
    _greet([("req", n_req), ("seq", n_seq)])
    for copy in _start_round("req", n_req, False, x_ref, spread_ref, send0, recv0, local_sems.at[0]):
        copy.wait()
    for load in loads[:3]:
        load.wait()
    normed_all = spread_ref[:, 1].reshape(rows, spread_ref.shape[3])
    staged1[:, :, :units] = jnp.dot(
        normed_all, gate_ref[...], preferred_element_type=jnp.float32
    ).reshape(staged1.shape[0], staged1.shape[1], units)
    staged1[:, :, units : 2 * units] = jnp.dot(
        normed_all, up_ref[...], preferred_element_type=jnp.float32
    ).reshape(staged1.shape[0], staged1.shape[1], units)
    staged1[:, :, 2 * units :] = jnp.dot(
        normed_all, down_map_ref[...], preferred_element_type=jnp.float32
    ).reshape(staged1.shape[0], staged1.shape[1], staged1.shape[2] - 2 * units)
    for copy in _start_round("req", n_req, False, staged1, landed1, send1, recv1, local_sems.at[1]):
        copy.wait()
    for load in loads[3:5]:
        load.wait()
    total = _block_sum(landed1)
    low = total[:, 2 * units :].astype(jnp.bfloat16)
    gate_pre = total[:, :units] + jnp.dot(low, gate_map_ref[...], preferred_element_type=jnp.float32)
    up_part = total[:, units : 2 * units] + jnp.dot(
        low, up_map_ref[...], preferred_element_type=jnp.float32
    )
    staged2[...] = (gate_pre / (1.0 + jnp.exp(-gate_pre)) * up_part).astype(jnp.bfloat16)
    for copy in _start_round("req", n_req, True, staged2, landed2, send2, recv2, local_sems.at[2]):
        copy.wait()
    loads[5].wait()
    inner = landed2[...].reshape(rows, units)
    staged3[...] = jnp.dot(inner, down_ref[...], preferred_element_type=jnp.float32).reshape(
        staged3.shape
    )
    for copy in _start_round("seq", n_seq, False, staged3, landed3, send3, recv3, local_sems.at[3]):
        copy.wait()
    out_ref[...] = _block_sum(landed3)


def fused_mlp(both, gate_weight, up_weight, down_map, gate_map, up_map, down_weight, cid):
    n_req, n_seq = lax.axis_size("req"), lax.axis_size("seq")
    group_rows = both.shape[2]
    rows = n_req * group_rows
    units = gate_weight.shape[1]
    wide = 2 * units + down_map.shape[1]
    out_rows = rows // n_seq
    vmem = pltpu.VMEM
    return pl.pallas_call(
        _mlp_kernel,
        out_shape=(
            jax.ShapeDtypeStruct((out_rows, down_weight.shape[1]), jnp.float32),
            jax.ShapeDtypeStruct(both.shape, both.dtype),
        ),
        in_specs=[pl.BlockSpec(memory_space=vmem)] + [pl.BlockSpec(memory_space=pl.ANY)] * 6,
        out_specs=(pl.BlockSpec(memory_space=vmem), pl.BlockSpec(memory_space=vmem)),
        scratch_shapes=[
            vmem((n_req, group_rows, wide), jnp.float32),
            vmem((n_req, group_rows, wide), jnp.float32),
            vmem((group_rows, units), jnp.bfloat16),
            vmem((n_req, group_rows, units), jnp.bfloat16),
            vmem((n_seq, out_rows, down_weight.shape[1]), jnp.float32),
            vmem((n_seq, out_rows, down_weight.shape[1]), jnp.float32),
            pltpu.SemaphoreType.DMA((n_req,)),
            pltpu.SemaphoreType.DMA((n_req,)),
            pltpu.SemaphoreType.DMA((n_req,)),
            pltpu.SemaphoreType.DMA((n_req,)),
            pltpu.SemaphoreType.DMA((n_req,)),
            pltpu.SemaphoreType.DMA((n_req,)),
            pltpu.SemaphoreType.DMA((n_seq,)),
            pltpu.SemaphoreType.DMA((n_seq,)),
            pltpu.SemaphoreType.DMA((4,)),
        ]
        + [
            vmem(weight.shape, weight.dtype)
            for weight in (gate_weight, up_weight, down_map, gate_map, up_map, down_weight)
        ]
        + [pltpu.SemaphoreType.DMA((6,))],
        compiler_params=pltpu.CompilerParams(
            collective_id=cid, has_side_effects=True
        ),
    )(both, gate_weight, up_weight, down_map, gate_map, up_map, down_weight)


def _chain_kernel(spec, n_extra, x_ref, *refs):
    extra_hbm = refs[:n_extra]
    y_ref = refs[n_extra]
    scratch = refs[n_extra + 1 :]
    count = len(spec)
    landed = list(scratch[: count - 1]) + [y_ref]
    staged = scratch[count - 1 : 2 * count - 2]
    extra = scratch[2 * count - 2 : 2 * count - 2 + n_extra]
    extra_sems = scratch[2 * count - 2 + n_extra]
    sems = scratch[2 * count - 1 + n_extra :]
    loads = []
    for index in range(n_extra):
        load = pltpu.make_async_copy(extra_hbm[index], extra[index], extra_sems.at[index])
        load.start()
        loads.append(load)
    axes = []
    for axis, n, _, _ in spec:
        if (axis, n) not in axes:
            axes.append((axis, n))
    _greet(axes)
    source = x_ref
    for k, (axis, n, gather, mid) in enumerate(spec):
        copies = _start_round(
            axis, n, gather, source, landed[k], sems[2 * k], sems[2 * k + 1], sems[-1].at[k]
        )
        for copy in copies:
            copy.wait()
        if k == 0:
            for load in loads:
                load.wait()
        if mid is not None:
            staged[k][...] = mid(landed[k], *extra)
            source = staged[k]


def chain(x, rounds, cid, extra=()):
    spec, landed_shapes, staged_shapes = [], [], []
    block = (x.shape, x.dtype)
    for index, (axis, gather, mid, made) in enumerate(rounds):
        n = lax.axis_size(axis)
        shape, dtype = block
        landed = ((n,) + shape if gather else shape, dtype)
        spec.append((axis, n, gather, mid))
        if index < len(rounds) - 1:
            landed_shapes.append(landed)
            staged_shapes.append(made)
            block = made
        else:
            out = landed
    sizes = [n for _, n, _, _ in spec]
    semaphores = []
    for n in sizes:
        semaphores += [pltpu.SemaphoreType.DMA((n,)), pltpu.SemaphoreType.DMA((n,))]
    return pl.pallas_call(
        functools.partial(_chain_kernel, spec, len(extra)),
        out_shape=jax.ShapeDtypeStruct(*out),
        in_specs=[pl.BlockSpec(memory_space=pltpu.VMEM)]
        + [pl.BlockSpec(memory_space=pl.ANY)] * len(extra),
        out_specs=pl.BlockSpec(memory_space=pltpu.VMEM),
        scratch_shapes=[pltpu.VMEM(*item) for item in landed_shapes]
        + [pltpu.VMEM(*item) for item in staged_shapes]
        + [pltpu.VMEM(item.shape, item.dtype) for item in extra]
        + [pltpu.SemaphoreType.DMA((max(len(extra), 1),))]
        + semaphores
        + [pltpu.SemaphoreType.DMA((len(spec),))],
        compiler_params=pltpu.CompilerParams(
            collective_id=cid, has_side_effects=True
        ),
    )(x, *extra)


def merged_2(array, axis, combine):
    everything = jax.tree.map(lambda part: lax.all_gather(part, axis), array)
    first = jax.tree.map(lambda part: part[0], everything)

    def hop(k, so_far):
        return combine(so_far, jax.tree.map(lambda part: part[k], everything))

    return lax.fori_loop(1, lax.axis_size(axis), hop, first)


def rms_norm(matrix, gain_vec):
    widened = matrix.astype(jnp.float32)
    factor = lax.rsqrt(jnp.mean(widened * widened, axis=-1, keepdims=True) + EPSILON)
    return (widened * factor * gain_vec.astype(jnp.float32)).astype(jnp.bfloat16)


def rotate(vectors, positions):
    half_dim = vectors.shape[-1] // 2
    frequency = ROTARY_BASE ** (-2.0 * jnp.arange(half_dim, dtype=jnp.float32) / vectors.shape[-1])
    angles = positions.astype(jnp.float32)[..., None, None] * frequency
    cosine = jnp.cos(angles)
    sine_part = jnp.sin(angles)
    front_half = vectors[..., :half_dim]
    back_half = vectors[..., half_dim:]
    return jnp.concatenate(
        [front_half * cosine - back_half * sine_part, back_half * cosine + front_half * sine_part],
        axis=-1,
    )


def softmax_join(earlier, later):
    first_max, first_sum, first_out = earlier
    second_max, second_sum, second_out = later
    overall = jnp.maximum(first_max, second_max)
    first_factor = jnp.exp(first_max - overall)
    second_factor = jnp.exp(second_max - overall)
    return (
        overall,
        first_sum * first_factor + second_sum * second_factor,
        first_out * first_factor[..., None] + second_out * second_factor[..., None],
    )


def body(
    given_token_index,
    hidden,
    token_embedding_table,
    attention_norm_gain,
    query_key_value_weight,
    rotated_key_cache,
    cached_value_pages,
    lengths,
    request_page_slots,
    attention_output_weight,
    feedforward_norm_gain,
    gate_weight,
    up_weight,
    adapter_down_map,
    adapter_gate_map,
    adapter_up_map,
    down_weight,
):
    seq_devices = lax.axis_size("seq")
    req_devices = lax.axis_size("req")
    seq_index = lax.axis_index("seq")
    req_index = lax.axis_index("req")
    group_rows = hidden.shape[0]
    requests = lengths.shape[0]
    steps_each = group_rows // requests
    vocab_rows = token_embedding_table.shape[0]
    first_id = (seq_index * req_devices + req_index) * vocab_rows
    local_ids = given_token_index - first_id
    present = (local_ids >= 0) & (local_ids < vocab_rows)
    looked = jnp.take(token_embedding_table, jnp.clip(local_ids, 0, vocab_rows - 1), axis=0).astype(
        jnp.float32
    )
    looked = jnp.where(present[:, None], looked, 0.0).astype(jnp.bfloat16)
    row_share = group_rows // seq_devices
    lanes = 128
    by_group = looked.reshape(req_devices, seq_devices, row_share * looked.shape[1] // lanes, lanes)
    row_parts = two_rounds(
        by_group,
        ("req", False),
        ("seq", False),
        lambda landed: _block_sum(landed).astype(jnp.bfloat16),
        by_group.shape[1:],
        jnp.bfloat16,
        10,
    )
    embedded_rows = (
        jnp.sum(row_parts.astype(jnp.float32), axis=0)
        .astype(jnp.bfloat16)
        .reshape(row_share, looked.shape[1])
    )
    own_hidden = lax.dynamic_slice_in_dim(hidden, seq_index * row_share, row_share, 0)
    own_rows = jnp.concatenate([own_hidden, embedded_rows], axis=1)
    normed_rows = rms_norm(own_rows, attention_norm_gain)
    normed = exchange(normed_rows.reshape(-1, lanes), "seq", 12, gather=True).reshape(
        group_rows, own_rows.shape[1]
    )
    width_share = normed.shape[1] // req_devices
    to_owners = jnp.transpose(normed.reshape(group_rows, req_devices, width_share), (1, 0, 2))
    qkv_cols = query_key_value_weight.shape[1]

    def project(landed, weight):
        flat = landed[...].reshape(req_devices * group_rows, width_share)
        product = jnp.dot(flat, weight[...], preferred_element_type=jnp.float32)
        return product.reshape(req_devices, group_rows, qkv_cols)

    qkv_all = chain(
        to_owners,
        [
            ("req", False, project, ((req_devices, group_rows, qkv_cols), jnp.float32)),
            (
                "req",
                False,
                lambda landed, weight: _block_sum(landed).astype(jnp.bfloat16),
                ((group_rows, qkv_cols), jnp.bfloat16),
            ),
            ("seq", True, None, None),
        ],
        4,
        extra=(query_key_value_weight,),
    )
    projected = jnp.transpose(qkv_all, (1, 0, 2)).reshape(group_rows, seq_devices * qkv_all.shape[2])
    head_cols = HEADS * HD
    queries = projected[:, :head_cols].reshape(requests, steps_each, HEADS, HD)
    new_keys = projected[:, head_cols : 2 * head_cols].reshape(requests, steps_each, HEADS, HD)
    new_values = projected[:, 2 * head_cols :].reshape(requests, steps_each, HEADS, HD)
    positions = lengths[:, None] + jnp.arange(steps_each, dtype=jnp.int32)[None, :]
    queries = rotate(queries.astype(jnp.float32), positions).astype(jnp.bfloat16)
    new_keys = rotate(new_keys.astype(jnp.float32), positions).astype(jnp.bfloat16)
    slots = rotated_key_cache.shape[0]
    page_len = rotated_key_cache.shape[2]
    cache_k = rotated_key_cache.reshape(slots * page_len, head_cols)
    cache_v = cached_value_pages.reshape(slots * page_len, head_cols)
    slot_ids = seq_index * slots + jnp.arange(slots, dtype=jnp.int32)
    page_ids = jnp.arange(request_page_slots.shape[1], dtype=jnp.int32)
    is_live = page_ids[None, :] < ((lengths + page_len - 1) // page_len)[:, None]
    matches = (request_page_slots[:, :, None] == slot_ids[None, None, :]) & is_live[:, :, None]
    is_owned = jnp.any(matches, axis=1)
    page_of = jnp.sum(jnp.where(matches, page_ids[None, :, None], 0), axis=1)
    token_pos = (
        page_of[:, :, None] * page_len + jnp.arange(page_len, dtype=jnp.int32)[None, None, :]
    )
    is_valid = (is_owned[:, :, None] & (token_pos < lengths[:, None, None])).reshape(
        requests, slots * page_len
    )
    score_scale = 1.0 / math.sqrt(HD)
    head_mask = (jnp.arange(head_cols, dtype=jnp.int32)[None, :] // HD) == jnp.arange(
        HEADS, dtype=jnp.int32
    )[:, None]
    query_rows = queries.reshape(group_rows, head_cols)
    spread_queries = jnp.where(head_mask[None], query_rows[:, None, :], jnp.zeros((), jnp.bfloat16))
    scores = (
        jnp.dot(
            spread_queries.reshape(group_rows * HEADS, head_cols),
            cache_k.T,
            preferred_element_type=jnp.float32,
        )
        * score_scale
    ).reshape(requests, steps_each, HEADS, slots * page_len)
    mask_b = is_valid[:, None, None, :]
    local_max = jnp.max(jnp.where(mask_b, scores, NEGATIVE), axis=-1)
    weights = jnp.where(mask_b, jnp.exp(scores - local_max[..., None]), 0.0)
    local_sum = jnp.sum(weights, axis=-1)
    spread_out = jnp.dot(
        weights.astype(jnp.bfloat16).reshape(group_rows * HEADS, slots * page_len),
        cache_v,
        preferred_element_type=jnp.float32,
    ).reshape(group_rows, HEADS, head_cols)
    local_out = jnp.sum(jnp.where(head_mask[None], spread_out, 0.0), axis=1).reshape(
        requests, steps_each, HEADS, HD
    )
    fresh_scores = (
        jnp.einsum("rthd,rshd->rths", queries, new_keys, preferred_element_type=jnp.float32)
        * score_scale
    )
    causal = jnp.arange(steps_each)[:, None] >= jnp.arange(steps_each)[None, :]
    fresh_mask = causal[None, :, None, :]
    fresh_max = jnp.max(jnp.where(fresh_mask, fresh_scores, NEGATIVE), axis=-1)
    fresh_w = jnp.where(fresh_mask, jnp.exp(fresh_scores - fresh_max[..., None]), 0.0)
    fresh_sum = jnp.sum(fresh_w, axis=-1)
    fresh_out = jnp.einsum(
        "rths,rshd->rthd",
        fresh_w.astype(jnp.bfloat16),
        new_values,
        preferred_element_type=jnp.float32,
    )
    own_heads = HEADS // seq_devices
    first_head = seq_index * own_heads

    def own_slice(member):
        return lax.dynamic_slice_in_dim(member, first_head, own_heads, 2)

    pad_cols = 256 - HD - 2
    packed = jnp.concatenate(
        [
            local_out,
            local_max[..., None],
            local_sum[..., None],
            jnp.zeros(local_out.shape[:-1] + (pad_cols,), jnp.float32),
        ],
        axis=-1,
    )
    packed = packed.reshape(requests * steps_each, seq_devices, own_heads, 256)
    packed = jnp.transpose(packed, (1, 0, 2, 3)).reshape(seq_devices, group_rows * own_heads, 256)
    arrived = exchange(packed, "seq", 0).reshape(seq_devices, requests, steps_each, own_heads, 256)
    part_o = arrived[..., :HD]
    part_m = arrived[..., HD]
    part_l = arrived[..., HD + 1]
    f_max, f_sum, f_out = own_slice(fresh_max), own_slice(fresh_sum), own_slice(fresh_out)
    overall = jnp.maximum(jnp.max(part_m, axis=0), f_max)
    part_factor = jnp.exp(part_m - overall[None])
    fresh_factor = jnp.exp(f_max - overall)
    denominator = jnp.sum(part_l * part_factor, axis=0) + f_sum * fresh_factor
    numerator = jnp.sum(part_o * part_factor[..., None], axis=0) + f_out * fresh_factor[..., None]
    attention = (
        (numerator / denominator[..., None])
        .astype(jnp.bfloat16)
        .reshape(group_rows, own_heads * HD)
    )
    projected_out = jnp.dot(attention, attention_output_weight, preferred_element_type=jnp.float32)
    model_width = projected_out.shape[1]
    after_attn = two_rounds(
        projected_out.reshape(seq_devices, row_share * model_width // lanes, lanes),
        ("seq", False),
        ("seq", True),
        lambda landed, own: (own[...].astype(jnp.float32) + _block_sum(landed)).astype(jnp.bfloat16),
        (row_share * model_width // lanes, lanes),
        jnp.bfloat16,
        1,
        extra=(own_rows.reshape(-1, lanes),),
    ).reshape(group_rows, model_width)
    second_normed_state = rms_norm(after_attn, feedforward_norm_gain)
    both = jnp.stack([after_attn, second_normed_state]).reshape(2, group_rows, req_devices, width_share)
    both = jnp.transpose(both, (2, 0, 1, 3))
    down_sum, both_parts = fused_mlp(
        both, gate_weight, up_weight, adapter_down_map, adapter_gate_map, adapter_up_map, down_weight, 7
    )
    residual_cols = both_parts[:, 0].reshape(req_devices * group_rows, width_share)
    out_rows = residual_cols.shape[0] // seq_devices
    residual_rows = lax.dynamic_slice_in_dim(residual_cols, seq_index * out_rows, out_rows, 0)
    return (residual_rows.astype(jnp.float32) + down_sum).astype(jnp.bfloat16)


def solution(mesh):
    placed = (
        P(),
        P("req", None),
        P(("seq", "req"), None),
        P(),
        P("req", "seq"),
        P("seq", "req", None, None),
        P("seq", "req", None, None),
        P("req"),
        P("req", None),
        P("seq", None),
        P(),
        P("req", "seq"),
        P("req", "seq"),
        P("req", None),
        P(None, "seq"),
        P(None, "seq"),
        P("seq", "req"),
    )
    return jax.shard_map(
        body, mesh=mesh, in_specs=placed, out_specs=P("seq", "req"), check_vma=False
    )
```

```python
import functools
import math

import jax
import jax.numpy as jnp
from jax import lax
from jax.experimental import pallas as pl
from jax.experimental.pallas import tpu as pltpu
from jax.sharding import PartitionSpec as P

HEADS = 16
HD = 224


NEGATIVE = -1e30
EPSILON = 1e-05
ROTARY_BASE = 10000.0


MESH_ID = pl.DeviceIdType.MESH


def _exchange_kernel(axis, n, gather, x_ref, y_ref, send_sem, recv_sem, local_sem):
    me = lax.axis_index(axis)
    barrier = pltpu.get_barrier_semaphore()
    for k in range(1, n):
        peer = lax.rem(me + k, n)
        pl.semaphore_signal(barrier, 1, device_id={axis: peer}, device_id_type=MESH_ID)
    pl.semaphore_wait(barrier, n - 1)
    copies = []
    for k in range(1, n):
        peer = lax.rem(me + k, n)
        source = x_ref if gather else x_ref.at[peer]
        copy = pltpu.make_async_remote_copy(
            src_ref=source,
            dst_ref=y_ref.at[me],
            send_sem=send_sem.at[k],
            recv_sem=recv_sem.at[k],
            device_id={axis: peer},
            device_id_type=MESH_ID,
        )
        copy.start()
        copies.append(copy)
    local = pltpu.make_async_copy(x_ref if gather else x_ref.at[me], y_ref.at[me], local_sem)
    local.start()
    local.wait()
    for copy in copies:
        copy.wait()


def exchange(x, axis, cid, gather=False):
    n = lax.axis_size(axis)
    out_shape = (n,) + x.shape if gather else x.shape
    return pl.pallas_call(
        functools.partial(_exchange_kernel, axis, n, gather),
        out_shape=jax.ShapeDtypeStruct(out_shape, x.dtype),
        in_specs=[pl.BlockSpec(memory_space=pltpu.VMEM)],
        out_specs=pl.BlockSpec(memory_space=pltpu.VMEM),
        scratch_shapes=[
            pltpu.SemaphoreType.DMA((n,)),
            pltpu.SemaphoreType.DMA((n,)),
            pltpu.SemaphoreType.DMA(()),
        ],
        compiler_params=pltpu.CompilerParams(collective_id=cid, has_side_effects=True),
    )(x)


def _greet(axes_sizes):
    barrier = pltpu.get_barrier_semaphore()
    total = 0
    for axis, n in axes_sizes:
        me = lax.axis_index(axis)
        for k in range(1, n):
            peer = lax.rem(me + k, n)
            pl.semaphore_signal(barrier, 1, device_id={axis: peer}, device_id_type=MESH_ID)
        total += n - 1
    pl.semaphore_wait(barrier, total)


def _start_round(axis, n, gather, source, target, send_sem, recv_sem, local_sem):
    me = lax.axis_index(axis)
    copies = []
    for k in range(1, n):
        peer = lax.rem(me + k, n)
        copy = pltpu.make_async_remote_copy(
            src_ref=source if gather else source.at[peer],
            dst_ref=target.at[me],
            send_sem=send_sem.at[k],
            recv_sem=recv_sem.at[k],
            device_id={axis: peer},
            device_id_type=MESH_ID,
        )
        copy.start()
        copies.append(copy)
    local = pltpu.make_async_copy(source if gather else source.at[me], target.at[me], local_sem)
    local.start()
    copies.append(local)
    return copies


def _two_round_kernel(first, second, mid, n_extra, x_ref, *refs):
    extra = refs[:n_extra]
    y_ref, landed, staged, send_a, recv_a, send_b, recv_b, local_sems = refs[n_extra:]
    axis_a, n_a, gather_a = first
    axis_b, n_b, gather_b = second
    greeted = [(axis_a, n_a)] if axis_a == axis_b else [(axis_a, n_a), (axis_b, n_b)]
    _greet(greeted)
    for copy in _start_round(axis_a, n_a, gather_a, x_ref, landed, send_a, recv_a, local_sems.at[0]):
        copy.wait()
    staged[...] = mid(landed, *extra)
    for copy in _start_round(axis_b, n_b, gather_b, staged, y_ref, send_b, recv_b, local_sems.at[1]):
        copy.wait()


def two_rounds(x, first, second, mid, staged_shape, staged_dtype, cid, extra=()):
    axis_a, gather_a = first
    axis_b, gather_b = second
    n_a, n_b = lax.axis_size(axis_a), lax.axis_size(axis_b)
    landed_shape = (n_a,) + x.shape if gather_a else x.shape
    out_shape = (n_b,) + staged_shape if gather_b else staged_shape
    return pl.pallas_call(
        functools.partial(
            _two_round_kernel, (axis_a, n_a, gather_a), (axis_b, n_b, gather_b), mid, len(extra)
        ),
        out_shape=jax.ShapeDtypeStruct(out_shape, staged_dtype),
        in_specs=[pl.BlockSpec(memory_space=pltpu.VMEM)] * (1 + len(extra)),
        out_specs=pl.BlockSpec(memory_space=pltpu.VMEM),
        scratch_shapes=[
            pltpu.VMEM(landed_shape, x.dtype),
            pltpu.VMEM(staged_shape, staged_dtype),
            pltpu.SemaphoreType.DMA((n_a,)),
            pltpu.SemaphoreType.DMA((n_a,)),
            pltpu.SemaphoreType.DMA((n_b,)),
            pltpu.SemaphoreType.DMA((n_b,)),
            pltpu.SemaphoreType.DMA((2,)),
        ],
        compiler_params=pltpu.CompilerParams(collective_id=cid, has_side_effects=True),
    )(x, *extra)


def _block_sum(landed):
    total = landed[0].astype(jnp.float32)
    for k in range(1, landed.shape[0]):
        total = total + landed[k].astype(jnp.float32)
    return total


def _mlp_kernel(
    x_ref, gate_hbm, up_hbm, down_map_hbm, gate_map_hbm, up_map_hbm, down_hbm,
    out_ref, spread_ref, landed1, staged1, staged2, landed2, staged3, landed3,
    send0, recv0, send1, recv1, send2, recv2, send3, recv3, local_sems,
    gate_ref, up_ref, down_map_ref, gate_map_ref, up_map_ref, down_ref, weight_sems,
):
    n_req = spread_ref.shape[0]
    n_seq = landed3.shape[0]
    rows = n_req * spread_ref.shape[2]
    units = gate_ref.shape[1]
    loads = []
    pairs = (
        (gate_hbm, gate_ref), (up_hbm, up_ref), (down_map_hbm, down_map_ref),
        (gate_map_hbm, gate_map_ref), (up_map_hbm, up_map_ref), (down_hbm, down_ref),
    )
    for index, (source, target) in enumerate(pairs):
        load = pltpu.make_async_copy(source, target, weight_sems.at[index])
        load.start()
        loads.append(load)
    _greet([("req", n_req), ("seq", n_seq)])
    for copy in _start_round("req", n_req, False, x_ref, spread_ref, send0, recv0, local_sems.at[0]):
        copy.wait()
    for load in loads[:3]:
        load.wait()
    normed_all = spread_ref[:, 1].reshape(rows, spread_ref.shape[3])
    staged1[:, :, :units] = jnp.dot(
        normed_all, gate_ref[...], preferred_element_type=jnp.float32
    ).reshape(staged1.shape[0], staged1.shape[1], units)
    staged1[:, :, units : 2 * units] = jnp.dot(
        normed_all, up_ref[...], preferred_element_type=jnp.float32
    ).reshape(staged1.shape[0], staged1.shape[1], units)
    staged1[:, :, 2 * units :] = jnp.dot(
        normed_all, down_map_ref[...], preferred_element_type=jnp.float32
    ).reshape(staged1.shape[0], staged1.shape[1], staged1.shape[2] - 2 * units)
    for copy in _start_round("req", n_req, False, staged1, landed1, send1, recv1, local_sems.at[1]):
        copy.wait()
    for load in loads[3:5]:
        load.wait()
    total = _block_sum(landed1)
    low = total[:, 2 * units :].astype(jnp.bfloat16)
    gate_pre = total[:, :units] + jnp.dot(low, gate_map_ref[...], preferred_element_type=jnp.float32)
    up_part = total[:, units : 2 * units] + jnp.dot(
        low, up_map_ref[...], preferred_element_type=jnp.float32
    )
    staged2[...] = (gate_pre / (1.0 + jnp.exp(-gate_pre)) * up_part).astype(jnp.bfloat16)
    for copy in _start_round("req", n_req, True, staged2, landed2, send2, recv2, local_sems.at[2]):
        copy.wait()
    loads[5].wait()
    inner = landed2[...].reshape(rows, units)
    staged3[...] = jnp.dot(inner, down_ref[...], preferred_element_type=jnp.float32).reshape(
        staged3.shape
    )
    for copy in _start_round("seq", n_seq, False, staged3, landed3, send3, recv3, local_sems.at[3]):
        copy.wait()
    out_ref[...] = _block_sum(landed3)


def fused_mlp(both, gate_weight, up_weight, down_map, gate_map, up_map, down_weight, cid):
    n_req, n_seq = lax.axis_size("req"), lax.axis_size("seq")
    group_rows = both.shape[2]
    rows = n_req * group_rows
    units = gate_weight.shape[1]
    wide = 2 * units + down_map.shape[1]
    out_rows = rows // n_seq
    vmem = pltpu.VMEM
    return pl.pallas_call(
        _mlp_kernel,
        out_shape=(
            jax.ShapeDtypeStruct((out_rows, down_weight.shape[1]), jnp.float32),
            jax.ShapeDtypeStruct(both.shape, both.dtype),
        ),
        in_specs=[pl.BlockSpec(memory_space=vmem)] + [pl.BlockSpec(memory_space=pl.ANY)] * 6,
        out_specs=(pl.BlockSpec(memory_space=vmem), pl.BlockSpec(memory_space=vmem)),
        scratch_shapes=[
            vmem((n_req, group_rows, wide), jnp.float32),
            vmem((n_req, group_rows, wide), jnp.float32),
            vmem((group_rows, units), jnp.bfloat16),
            vmem((n_req, group_rows, units), jnp.bfloat16),
            vmem((n_seq, out_rows, down_weight.shape[1]), jnp.float32),
            vmem((n_seq, out_rows, down_weight.shape[1]), jnp.float32),
            pltpu.SemaphoreType.DMA((n_req,)),
            pltpu.SemaphoreType.DMA((n_req,)),
            pltpu.SemaphoreType.DMA((n_req,)),
            pltpu.SemaphoreType.DMA((n_req,)),
            pltpu.SemaphoreType.DMA((n_req,)),
            pltpu.SemaphoreType.DMA((n_req,)),
            pltpu.SemaphoreType.DMA((n_seq,)),
            pltpu.SemaphoreType.DMA((n_seq,)),
            pltpu.SemaphoreType.DMA((4,)),
        ]
        + [
            vmem(weight.shape, weight.dtype)
            for weight in (gate_weight, up_weight, down_map, gate_map, up_map, down_weight)
        ]
        + [pltpu.SemaphoreType.DMA((6,))],
        compiler_params=pltpu.CompilerParams(
            collective_id=cid, has_side_effects=True
        ),
    )(both, gate_weight, up_weight, down_map, gate_map, up_map, down_weight)


def _chain_kernel(spec, n_extra, x_ref, *refs):
    extra_hbm = refs[:n_extra]
    y_ref = refs[n_extra]
    scratch = refs[n_extra + 1 :]
    count = len(spec)
    landed = list(scratch[: count - 1]) + [y_ref]
    staged = scratch[count - 1 : 2 * count - 2]
    extra = scratch[2 * count - 2 : 2 * count - 2 + n_extra]
    extra_sems = scratch[2 * count - 2 + n_extra]
    sems = scratch[2 * count - 1 + n_extra :]
    loads = []
    for index in range(n_extra):
        load = pltpu.make_async_copy(extra_hbm[index], extra[index], extra_sems.at[index])
        load.start()
        loads.append(load)
    axes = []
    for axis, n, _, _ in spec:
        if (axis, n) not in axes:
            axes.append((axis, n))
    _greet(axes)
    source = x_ref
    for k, (axis, n, gather, mid) in enumerate(spec):
        copies = _start_round(
            axis, n, gather, source, landed[k], sems[2 * k], sems[2 * k + 1], sems[-1].at[k]
        )
        for copy in copies:
            copy.wait()
        if k == 0:
            for load in loads:
                load.wait()
        if mid is not None:
            staged[k][...] = mid(landed[k], *extra)
            source = staged[k]


def chain(x, rounds, cid, extra=()):
    spec, landed_shapes, staged_shapes = [], [], []
    block = (x.shape, x.dtype)
    for index, (axis, gather, mid, made) in enumerate(rounds):
        n = lax.axis_size(axis)
        shape, dtype = block
        landed = ((n,) + shape if gather else shape, dtype)
        spec.append((axis, n, gather, mid))
        if index < len(rounds) - 1:
            landed_shapes.append(landed)
            staged_shapes.append(made)
            block = made
        else:
            out = landed
    sizes = [n for _, n, _, _ in spec]
    semaphores = []
    for n in sizes:
        semaphores += [pltpu.SemaphoreType.DMA((n,)), pltpu.SemaphoreType.DMA((n,))]
    return pl.pallas_call(
        functools.partial(_chain_kernel, spec, len(extra)),
        out_shape=jax.ShapeDtypeStruct(*out),
        in_specs=[pl.BlockSpec(memory_space=pltpu.VMEM)]
        + [pl.BlockSpec(memory_space=pl.ANY)] * len(extra),
        out_specs=pl.BlockSpec(memory_space=pltpu.VMEM),
        scratch_shapes=[pltpu.VMEM(*item) for item in landed_shapes]
        + [pltpu.VMEM(*item) for item in staged_shapes]
        + [pltpu.VMEM(item.shape, item.dtype) for item in extra]
        + [pltpu.SemaphoreType.DMA((max(len(extra), 1),))]
        + semaphores
        + [pltpu.SemaphoreType.DMA((len(spec),))],
        compiler_params=pltpu.CompilerParams(
            collective_id=cid, has_side_effects=True
        ),
    )(x, *extra)


def merged_2(array, axis, combine):
    everything = jax.tree.map(lambda part: lax.all_gather(part, axis), array)
    first = jax.tree.map(lambda part: part[0], everything)

    def hop(k, so_far):
        return combine(so_far, jax.tree.map(lambda part: part[k], everything))

    return lax.fori_loop(1, lax.axis_size(axis), hop, first)


def rms_norm(matrix, gain_vec):
    widened = matrix.astype(jnp.float32)
    factor = lax.rsqrt(jnp.mean(widened * widened, axis=-1, keepdims=True) + EPSILON)
    return (widened * factor * gain_vec.astype(jnp.float32)).astype(jnp.bfloat16)


def rotate(vectors, positions):
    half_dim = vectors.shape[-1] // 2
    frequency = ROTARY_BASE ** (-2.0 * jnp.arange(half_dim, dtype=jnp.float32) / vectors.shape[-1])
    angles = positions.astype(jnp.float32)[..., None, None] * frequency
    cosine = jnp.cos(angles)
    sine_part = jnp.sin(angles)
    front_half = vectors[..., :half_dim]
    back_half = vectors[..., half_dim:]
    return jnp.concatenate(
        [front_half * cosine - back_half * sine_part, back_half * cosine + front_half * sine_part],
        axis=-1,
    )


def softmax_join(earlier, later):
    first_max, first_sum, first_out = earlier
    second_max, second_sum, second_out = later
    overall = jnp.maximum(first_max, second_max)
    first_factor = jnp.exp(first_max - overall)
    second_factor = jnp.exp(second_max - overall)
    return (
        overall,
        first_sum * first_factor + second_sum * second_factor,
        first_out * first_factor[..., None] + second_out * second_factor[..., None],
    )


def body(
    given_token_index,
    hidden,
    token_embedding_table,
    attention_norm_gain,
    query_key_value_weight,
    rotated_key_cache,
    cached_value_pages,
    lengths,
    request_page_slots,
    attention_output_weight,
    feedforward_norm_gain,
    gate_weight,
    up_weight,
    adapter_down_map,
    adapter_gate_map,
    adapter_up_map,
    down_weight,
):
    seq_devices = lax.axis_size("seq")
    req_devices = lax.axis_size("req")
    seq_index = lax.axis_index("seq")
    req_index = lax.axis_index("req")
    group_rows = hidden.shape[0]
    requests = lengths.shape[0]
    steps_each = group_rows // requests
    vocab_rows = token_embedding_table.shape[0]
    first_id = (seq_index * req_devices + req_index) * vocab_rows
    local_ids = given_token_index - first_id
    present = (local_ids >= 0) & (local_ids < vocab_rows)
    looked = jnp.take(token_embedding_table, jnp.clip(local_ids, 0, vocab_rows - 1), axis=0).astype(
        jnp.float32
    )
    looked = jnp.where(present[:, None], looked, 0.0).astype(jnp.bfloat16)
    row_share = group_rows // seq_devices
    lanes = 128
    tile_rows = row_share * looked.shape[1] // lanes
    by_group = looked.reshape(req_devices, seq_devices, tile_rows, lanes)
    own_hidden = lax.dynamic_slice_in_dim(hidden, seq_index * row_share, row_share, 0)
    model_width = hidden.shape[1] + looked.shape[1]

    def normalize(landed, hidden_tiles, gain_tiles):
        emb = _block_sum(landed)
        front = hidden_tiles[...].astype(jnp.float32)
        squares = jnp.sum(front * front) + jnp.sum(emb * emb)
        factor = lax.rsqrt(squares / model_width + EPSILON)
        gains = gain_tiles[...].astype(jnp.float32)
        return jnp.stack(
            [
                (front * factor * gains[0]).astype(jnp.bfloat16),
                (emb * factor * gains[1]).astype(jnp.bfloat16),
                emb.astype(jnp.bfloat16),
            ]
        )

    gathered = chain(
        by_group,
        [
            (
                "req",
                False,
                lambda landed, *rest: _block_sum(landed).astype(jnp.bfloat16),
                ((seq_devices, tile_rows, lanes), jnp.bfloat16),
            ),
            ("seq", False, normalize, ((3, tile_rows, lanes), jnp.bfloat16)),
            ("seq", True, None, None),
        ],
        12,
        extra=(
            own_hidden.reshape(tile_rows, lanes),
            attention_norm_gain.reshape(2, tile_rows, lanes),
        ),
    )
    normed = gathered[:, :2].reshape(group_rows, model_width)
    embedded_rows = lax.dynamic_index_in_dim(gathered, seq_index, 0, keepdims=False)[2].reshape(
        row_share, looked.shape[1]
    )
    own_rows = jnp.concatenate([own_hidden, embedded_rows], axis=1)
    width_share = normed.shape[1] // req_devices
    to_owners = jnp.transpose(normed.reshape(group_rows, req_devices, width_share), (1, 0, 2))
    qkv_cols = query_key_value_weight.shape[1]

    def project(landed, weight):
        flat = landed[...].reshape(req_devices * group_rows, width_share)
        product = jnp.dot(flat, weight[...], preferred_element_type=jnp.float32)
        return product.reshape(req_devices, group_rows, qkv_cols)

    qkv_all = chain(
        to_owners,
        [
            ("req", False, project, ((req_devices, group_rows, qkv_cols), jnp.float32)),
            (
                "req",
                False,
                lambda landed, weight: _block_sum(landed).astype(jnp.bfloat16),
                ((group_rows, qkv_cols), jnp.bfloat16),
            ),
            ("seq", True, None, None),
        ],
        4,
        extra=(query_key_value_weight,),
    )
    projected = jnp.transpose(qkv_all, (1, 0, 2)).reshape(group_rows, seq_devices * qkv_all.shape[2])
    head_cols = HEADS * HD
    queries = projected[:, :head_cols].reshape(requests, steps_each, HEADS, HD)
    new_keys = projected[:, head_cols : 2 * head_cols].reshape(requests, steps_each, HEADS, HD)
    new_values = projected[:, 2 * head_cols :].reshape(requests, steps_each, HEADS, HD)
    positions = lengths[:, None] + jnp.arange(steps_each, dtype=jnp.int32)[None, :]
    queries = rotate(queries.astype(jnp.float32), positions).astype(jnp.bfloat16)
    new_keys = rotate(new_keys.astype(jnp.float32), positions).astype(jnp.bfloat16)
    slots = rotated_key_cache.shape[0]
    page_len = rotated_key_cache.shape[2]
    cache_k = rotated_key_cache.reshape(slots * page_len, head_cols)
    cache_v = cached_value_pages.reshape(slots * page_len, head_cols)
    slot_ids = seq_index * slots + jnp.arange(slots, dtype=jnp.int32)
    page_ids = jnp.arange(request_page_slots.shape[1], dtype=jnp.int32)
    is_live = page_ids[None, :] < ((lengths + page_len - 1) // page_len)[:, None]
    matches = (request_page_slots[:, :, None] == slot_ids[None, None, :]) & is_live[:, :, None]
    is_owned = jnp.any(matches, axis=1)
    page_of = jnp.sum(jnp.where(matches, page_ids[None, :, None], 0), axis=1)
    token_pos = (
        page_of[:, :, None] * page_len + jnp.arange(page_len, dtype=jnp.int32)[None, None, :]
    )
    is_valid = (is_owned[:, :, None] & (token_pos < lengths[:, None, None])).reshape(
        requests, slots * page_len
    )
    score_scale = 1.0 / math.sqrt(HD)
    head_mask = (jnp.arange(head_cols, dtype=jnp.int32)[None, :] // HD) == jnp.arange(
        HEADS, dtype=jnp.int32
    )[:, None]
    query_rows = queries.reshape(group_rows, head_cols)
    spread_queries = jnp.where(head_mask[None], query_rows[:, None, :], jnp.zeros((), jnp.bfloat16))
    scores = (
        jnp.dot(
            spread_queries.reshape(group_rows * HEADS, head_cols),
            cache_k.T,
            preferred_element_type=jnp.float32,
        )
        * score_scale
    ).reshape(requests, steps_each, HEADS, slots * page_len)
    mask_b = is_valid[:, None, None, :]
    local_max = jnp.max(jnp.where(mask_b, scores, NEGATIVE), axis=-1)
    weights = jnp.where(mask_b, jnp.exp(scores - local_max[..., None]), 0.0)
    local_sum = jnp.sum(weights, axis=-1)
    spread_out = jnp.dot(
        weights.astype(jnp.bfloat16).reshape(group_rows * HEADS, slots * page_len),
        cache_v,
        preferred_element_type=jnp.float32,
    ).reshape(group_rows, HEADS, head_cols)
    local_out = jnp.sum(jnp.where(head_mask[None], spread_out, 0.0), axis=1).reshape(
        requests, steps_each, HEADS, HD
    )
    fresh_scores = (
        jnp.einsum("rthd,rshd->rths", queries, new_keys, preferred_element_type=jnp.float32)
        * score_scale
    )
    causal = jnp.arange(steps_each)[:, None] >= jnp.arange(steps_each)[None, :]
    fresh_mask = causal[None, :, None, :]
    fresh_max = jnp.max(jnp.where(fresh_mask, fresh_scores, NEGATIVE), axis=-1)
    fresh_w = jnp.where(fresh_mask, jnp.exp(fresh_scores - fresh_max[..., None]), 0.0)
    fresh_sum = jnp.sum(fresh_w, axis=-1)
    fresh_out = jnp.einsum(
        "rths,rshd->rthd",
        fresh_w.astype(jnp.bfloat16),
        new_values,
        preferred_element_type=jnp.float32,
    )
    own_heads = HEADS // seq_devices
    first_head = seq_index * own_heads

    def own_slice(member):
        return lax.dynamic_slice_in_dim(member, first_head, own_heads, 2)

    pad_cols = 256 - HD - 2
    packed = jnp.concatenate(
        [
            local_out,
            local_max[..., None],
            local_sum[..., None],
            jnp.zeros(local_out.shape[:-1] + (pad_cols,), jnp.float32),
        ],
        axis=-1,
    )
    packed = packed.reshape(requests * steps_each, seq_devices, own_heads, 256)
    packed = jnp.transpose(packed, (1, 0, 2, 3)).reshape(seq_devices, group_rows * own_heads, 256)
    arrived = exchange(packed, "seq", 0).reshape(seq_devices, requests, steps_each, own_heads, 256)
    part_o = arrived[..., :HD]
    part_m = arrived[..., HD]
    part_l = arrived[..., HD + 1]
    f_max, f_sum, f_out = own_slice(fresh_max), own_slice(fresh_sum), own_slice(fresh_out)
    overall = jnp.maximum(jnp.max(part_m, axis=0), f_max)
    part_factor = jnp.exp(part_m - overall[None])
    fresh_factor = jnp.exp(f_max - overall)
    denominator = jnp.sum(part_l * part_factor, axis=0) + f_sum * fresh_factor
    numerator = jnp.sum(part_o * part_factor[..., None], axis=0) + f_out * fresh_factor[..., None]
    attention = (
        (numerator / denominator[..., None])
        .astype(jnp.bfloat16)
        .reshape(group_rows, own_heads * HD)
    )
    projected_out = jnp.dot(attention, attention_output_weight, preferred_element_type=jnp.float32)
    model_width = projected_out.shape[1]
    after_attn = two_rounds(
        projected_out.reshape(seq_devices, row_share * model_width // lanes, lanes),
        ("seq", False),
        ("seq", True),
        lambda landed, own: (own[...].astype(jnp.float32) + _block_sum(landed)).astype(jnp.bfloat16),
        (row_share * model_width // lanes, lanes),
        jnp.bfloat16,
        1,
        extra=(own_rows.reshape(-1, lanes),),
    ).reshape(group_rows, model_width)
    second_normed_state = rms_norm(after_attn, feedforward_norm_gain)
    both = jnp.stack([after_attn, second_normed_state]).reshape(2, group_rows, req_devices, width_share)
    both = jnp.transpose(both, (2, 0, 1, 3))
    down_sum, both_parts = fused_mlp(
        both, gate_weight, up_weight, adapter_down_map, adapter_gate_map, adapter_up_map, down_weight, 7
    )
    residual_cols = both_parts[:, 0].reshape(req_devices * group_rows, width_share)
    out_rows = residual_cols.shape[0] // seq_devices
    residual_rows = lax.dynamic_slice_in_dim(residual_cols, seq_index * out_rows, out_rows, 0)
    return (residual_rows.astype(jnp.float32) + down_sum).astype(jnp.bfloat16)


def solution(mesh):
    placed = (
        P(),
        P("req", None),
        P(("seq", "req"), None),
        P(),
        P("req", "seq"),
        P("seq", "req", None, None),
        P("seq", "req", None, None),
        P("req"),
        P("req", None),
        P("seq", None),
        P(),
        P("req", "seq"),
        P("req", "seq"),
        P("req", None),
        P(None, "seq"),
        P(None, "seq"),
        P("seq", "req"),
    )
    return jax.shard_map(
        body, mesh=mesh, in_specs=placed, out_specs=P("seq", "req"), check_vma=False
    )
```

```python
import functools
import math

import jax
import jax.numpy as jnp
from jax import lax
from jax.experimental import pallas as pl
from jax.experimental.pallas import tpu as pltpu
from jax.sharding import PartitionSpec as P

HEADS = 16
HD = 224


NEGATIVE = -1e30
EPSILON = 1e-05
ROTARY_BASE = 10000.0


MESH_ID = pl.DeviceIdType.MESH


def _exchange_kernel(axis, n, gather, x_ref, y_ref, send_sem, recv_sem, local_sem):
    me = lax.axis_index(axis)
    barrier = pltpu.get_barrier_semaphore()
    for k in range(1, n):
        peer = lax.rem(me + k, n)
        pl.semaphore_signal(barrier, 1, device_id={axis: peer}, device_id_type=MESH_ID)
    pl.semaphore_wait(barrier, n - 1)
    copies = []
    for k in range(1, n):
        peer = lax.rem(me + k, n)
        source = x_ref if gather else x_ref.at[peer]
        copy = pltpu.make_async_remote_copy(
            src_ref=source,
            dst_ref=y_ref.at[me],
            send_sem=send_sem.at[k],
            recv_sem=recv_sem.at[k],
            device_id={axis: peer},
            device_id_type=MESH_ID,
        )
        copy.start()
        copies.append(copy)
    local = pltpu.make_async_copy(x_ref if gather else x_ref.at[me], y_ref.at[me], local_sem)
    local.start()
    local.wait()
    for copy in copies:
        copy.wait()


def exchange(x, axis, cid, gather=False):
    n = lax.axis_size(axis)
    out_shape = (n,) + x.shape if gather else x.shape
    return pl.pallas_call(
        functools.partial(_exchange_kernel, axis, n, gather),
        out_shape=jax.ShapeDtypeStruct(out_shape, x.dtype),
        in_specs=[pl.BlockSpec(memory_space=pltpu.VMEM)],
        out_specs=pl.BlockSpec(memory_space=pltpu.VMEM),
        scratch_shapes=[
            pltpu.SemaphoreType.DMA((n,)),
            pltpu.SemaphoreType.DMA((n,)),
            pltpu.SemaphoreType.DMA(()),
        ],
        compiler_params=pltpu.CompilerParams(collective_id=cid, has_side_effects=True),
    )(x)


def _greet(axes_sizes):
    barrier = pltpu.get_barrier_semaphore()
    total = 0
    for axis, n in axes_sizes:
        me = lax.axis_index(axis)
        for k in range(1, n):
            peer = lax.rem(me + k, n)
            pl.semaphore_signal(barrier, 1, device_id={axis: peer}, device_id_type=MESH_ID)
        total += n - 1
    pl.semaphore_wait(barrier, total)


def _start_round(axis, n, gather, source, target, send_sem, recv_sem, local_sem):
    me = lax.axis_index(axis)
    copies = []
    for k in range(1, n):
        peer = lax.rem(me + k, n)
        copy = pltpu.make_async_remote_copy(
            src_ref=source if gather else source.at[peer],
            dst_ref=target.at[me],
            send_sem=send_sem.at[k],
            recv_sem=recv_sem.at[k],
            device_id={axis: peer},
            device_id_type=MESH_ID,
        )
        copy.start()
        copies.append(copy)
    local = pltpu.make_async_copy(source if gather else source.at[me], target.at[me], local_sem)
    local.start()
    copies.append(local)
    return copies


def _two_round_kernel(first, second, mid, n_extra, x_ref, *refs):
    extra = refs[:n_extra]
    y_ref, landed, staged, send_a, recv_a, send_b, recv_b, local_sems = refs[n_extra:]
    axis_a, n_a, gather_a = first
    axis_b, n_b, gather_b = second
    greeted = [(axis_a, n_a)] if axis_a == axis_b else [(axis_a, n_a), (axis_b, n_b)]
    _greet(greeted)
    for copy in _start_round(axis_a, n_a, gather_a, x_ref, landed, send_a, recv_a, local_sems.at[0]):
        copy.wait()
    staged[...] = mid(landed, *extra)
    for copy in _start_round(axis_b, n_b, gather_b, staged, y_ref, send_b, recv_b, local_sems.at[1]):
        copy.wait()


def two_rounds(x, first, second, mid, staged_shape, staged_dtype, cid, extra=()):
    axis_a, gather_a = first
    axis_b, gather_b = second
    n_a, n_b = lax.axis_size(axis_a), lax.axis_size(axis_b)
    landed_shape = (n_a,) + x.shape if gather_a else x.shape
    out_shape = (n_b,) + staged_shape if gather_b else staged_shape
    return pl.pallas_call(
        functools.partial(
            _two_round_kernel, (axis_a, n_a, gather_a), (axis_b, n_b, gather_b), mid, len(extra)
        ),
        out_shape=jax.ShapeDtypeStruct(out_shape, staged_dtype),
        in_specs=[pl.BlockSpec(memory_space=pltpu.VMEM)] * (1 + len(extra)),
        out_specs=pl.BlockSpec(memory_space=pltpu.VMEM),
        scratch_shapes=[
            pltpu.VMEM(landed_shape, x.dtype),
            pltpu.VMEM(staged_shape, staged_dtype),
            pltpu.SemaphoreType.DMA((n_a,)),
            pltpu.SemaphoreType.DMA((n_a,)),
            pltpu.SemaphoreType.DMA((n_b,)),
            pltpu.SemaphoreType.DMA((n_b,)),
            pltpu.SemaphoreType.DMA((2,)),
        ],
        compiler_params=pltpu.CompilerParams(collective_id=cid, has_side_effects=True),
    )(x, *extra)


def _block_sum(landed):
    total = landed[0].astype(jnp.float32)
    for k in range(1, landed.shape[0]):
        total = total + landed[k].astype(jnp.float32)
    return total


def _mlp_kernel(
    x_ref, gate_hbm, up_hbm, down_map_hbm, gate_map_hbm, up_map_hbm, down_hbm,
    out_ref, spread_ref, landed1, staged1, staged2, landed2, staged3, landed3,
    send0, recv0, send1, recv1, send2, recv2, send3, recv3, local_sems,
    gate_ref, up_ref, down_map_ref, gate_map_ref, up_map_ref, down_ref, weight_sems,
):
    n_req = spread_ref.shape[0]
    n_seq = landed3.shape[0]
    rows = n_req * spread_ref.shape[2]
    units = gate_ref.shape[1]
    loads = []
    pairs = (
        (gate_hbm, gate_ref), (up_hbm, up_ref), (down_map_hbm, down_map_ref),
        (gate_map_hbm, gate_map_ref), (up_map_hbm, up_map_ref), (down_hbm, down_ref),
    )
    for index, (source, target) in enumerate(pairs):
        load = pltpu.make_async_copy(source, target, weight_sems.at[index])
        load.start()
        loads.append(load)
    _greet([("req", n_req), ("seq", n_seq)])
    for copy in _start_round("req", n_req, False, x_ref, spread_ref, send0, recv0, local_sems.at[0]):
        copy.wait()
    for load in loads[:3]:
        load.wait()
    normed_all = spread_ref[:, 1].reshape(rows, spread_ref.shape[3])
    staged1[:, :, :units] = jnp.dot(
        normed_all, gate_ref[...], preferred_element_type=jnp.float32
    ).reshape(staged1.shape[0], staged1.shape[1], units)
    staged1[:, :, units : 2 * units] = jnp.dot(
        normed_all, up_ref[...], preferred_element_type=jnp.float32
    ).reshape(staged1.shape[0], staged1.shape[1], units)
    staged1[:, :, 2 * units :] = jnp.dot(
        normed_all, down_map_ref[...], preferred_element_type=jnp.float32
    ).reshape(staged1.shape[0], staged1.shape[1], staged1.shape[2] - 2 * units)
    for copy in _start_round("req", n_req, False, staged1, landed1, send1, recv1, local_sems.at[1]):
        copy.wait()
    for load in loads[3:5]:
        load.wait()
    total = _block_sum(landed1)
    low = total[:, 2 * units :].astype(jnp.bfloat16)
    gate_pre = total[:, :units] + jnp.dot(low, gate_map_ref[...], preferred_element_type=jnp.float32)
    up_part = total[:, units : 2 * units] + jnp.dot(
        low, up_map_ref[...], preferred_element_type=jnp.float32
    )
    staged2[...] = (gate_pre / (1.0 + jnp.exp(-gate_pre)) * up_part).astype(jnp.bfloat16)
    for copy in _start_round("req", n_req, True, staged2, landed2, send2, recv2, local_sems.at[2]):
        copy.wait()
    loads[5].wait()
    inner = landed2[...].reshape(rows, units)
    staged3[...] = jnp.dot(inner, down_ref[...], preferred_element_type=jnp.float32).reshape(
        staged3.shape
    )
    for copy in _start_round("seq", n_seq, False, staged3, landed3, send3, recv3, local_sems.at[3]):
        copy.wait()
    out_ref[...] = _block_sum(landed3)


def fused_mlp(both, gate_weight, up_weight, down_map, gate_map, up_map, down_weight, cid):
    n_req, n_seq = lax.axis_size("req"), lax.axis_size("seq")
    group_rows = both.shape[2]
    rows = n_req * group_rows
    units = gate_weight.shape[1]
    wide = 2 * units + down_map.shape[1]
    out_rows = rows // n_seq
    vmem = pltpu.VMEM
    return pl.pallas_call(
        _mlp_kernel,
        out_shape=(
            jax.ShapeDtypeStruct((out_rows, down_weight.shape[1]), jnp.float32),
            jax.ShapeDtypeStruct(both.shape, both.dtype),
        ),
        in_specs=[pl.BlockSpec(memory_space=vmem)] + [pl.BlockSpec(memory_space=pl.ANY)] * 6,
        out_specs=(pl.BlockSpec(memory_space=vmem), pl.BlockSpec(memory_space=vmem)),
        scratch_shapes=[
            vmem((n_req, group_rows, wide), jnp.float32),
            vmem((n_req, group_rows, wide), jnp.float32),
            vmem((group_rows, units), jnp.bfloat16),
            vmem((n_req, group_rows, units), jnp.bfloat16),
            vmem((n_seq, out_rows, down_weight.shape[1]), jnp.float32),
            vmem((n_seq, out_rows, down_weight.shape[1]), jnp.float32),
            pltpu.SemaphoreType.DMA((n_req,)),
            pltpu.SemaphoreType.DMA((n_req,)),
            pltpu.SemaphoreType.DMA((n_req,)),
            pltpu.SemaphoreType.DMA((n_req,)),
            pltpu.SemaphoreType.DMA((n_req,)),
            pltpu.SemaphoreType.DMA((n_req,)),
            pltpu.SemaphoreType.DMA((n_seq,)),
            pltpu.SemaphoreType.DMA((n_seq,)),
            pltpu.SemaphoreType.DMA((4,)),
        ]
        + [
            vmem(weight.shape, weight.dtype)
            for weight in (gate_weight, up_weight, down_map, gate_map, up_map, down_weight)
        ]
        + [pltpu.SemaphoreType.DMA((6,))],
        compiler_params=pltpu.CompilerParams(
            collective_id=cid, has_side_effects=True
        ),
    )(both, gate_weight, up_weight, down_map, gate_map, up_map, down_weight)


def _chain_kernel(spec, n_extra, x_ref, *refs):
    extra_hbm = refs[:n_extra]
    y_ref = refs[n_extra]
    scratch = refs[n_extra + 1 :]
    count = len(spec)
    landed = list(scratch[: count - 1]) + [y_ref]
    staged = scratch[count - 1 : 2 * count - 2]
    extra = scratch[2 * count - 2 : 2 * count - 2 + n_extra]
    extra_sems = scratch[2 * count - 2 + n_extra]
    sems = scratch[2 * count - 1 + n_extra :]
    loads = []
    for index in range(n_extra):
        load = pltpu.make_async_copy(extra_hbm[index], extra[index], extra_sems.at[index])
        load.start()
        loads.append(load)
    axes = []
    for axis, n, _, _ in spec:
        if (axis, n) not in axes:
            axes.append((axis, n))
    _greet(axes)
    source = x_ref
    for k, (axis, n, gather, mid) in enumerate(spec):
        copies = _start_round(
            axis, n, gather, source, landed[k], sems[2 * k], sems[2 * k + 1], sems[-1].at[k]
        )
        for copy in copies:
            copy.wait()
        if k == 0:
            for load in loads:
                load.wait()
        if mid is not None:
            staged[k][...] = mid(landed[k], *extra)
            source = staged[k]


def chain(x, rounds, cid, extra=()):
    spec, landed_shapes, staged_shapes = [], [], []
    block = (x.shape, x.dtype)
    for index, (axis, gather, mid, made) in enumerate(rounds):
        n = lax.axis_size(axis)
        shape, dtype = block
        landed = ((n,) + shape if gather else shape, dtype)
        spec.append((axis, n, gather, mid))
        if index < len(rounds) - 1:
            landed_shapes.append(landed)
            staged_shapes.append(made)
            block = made
        else:
            out = landed
    sizes = [n for _, n, _, _ in spec]
    semaphores = []
    for n in sizes:
        semaphores += [pltpu.SemaphoreType.DMA((n,)), pltpu.SemaphoreType.DMA((n,))]
    return pl.pallas_call(
        functools.partial(_chain_kernel, spec, len(extra)),
        out_shape=jax.ShapeDtypeStruct(*out),
        in_specs=[pl.BlockSpec(memory_space=pltpu.VMEM)]
        + [pl.BlockSpec(memory_space=pl.ANY)] * len(extra),
        out_specs=pl.BlockSpec(memory_space=pltpu.VMEM),
        scratch_shapes=[pltpu.VMEM(*item) for item in landed_shapes]
        + [pltpu.VMEM(*item) for item in staged_shapes]
        + [pltpu.VMEM(item.shape, item.dtype) for item in extra]
        + [pltpu.SemaphoreType.DMA((max(len(extra), 1),))]
        + semaphores
        + [pltpu.SemaphoreType.DMA((len(spec),))],
        compiler_params=pltpu.CompilerParams(
            collective_id=cid, has_side_effects=True
        ),
    )(x, *extra)


def merged_2(array, axis, combine):
    everything = jax.tree.map(lambda part: lax.all_gather(part, axis), array)
    first = jax.tree.map(lambda part: part[0], everything)

    def hop(k, so_far):
        return combine(so_far, jax.tree.map(lambda part: part[k], everything))

    return lax.fori_loop(1, lax.axis_size(axis), hop, first)


def rms_norm(matrix, gain_vec):
    widened = matrix.astype(jnp.float32)
    factor = lax.rsqrt(jnp.mean(widened * widened, axis=-1, keepdims=True) + EPSILON)
    return (widened * factor * gain_vec.astype(jnp.float32)).astype(jnp.bfloat16)


def rotate(vectors, positions):
    half_dim = vectors.shape[-1] // 2
    frequency = ROTARY_BASE ** (-2.0 * jnp.arange(half_dim, dtype=jnp.float32) / vectors.shape[-1])
    angles = positions.astype(jnp.float32)[..., None, None] * frequency
    cosine = jnp.cos(angles)
    sine_part = jnp.sin(angles)
    front_half = vectors[..., :half_dim]
    back_half = vectors[..., half_dim:]
    return jnp.concatenate(
        [front_half * cosine - back_half * sine_part, back_half * cosine + front_half * sine_part],
        axis=-1,
    )


def softmax_join(earlier, later):
    first_max, first_sum, first_out = earlier
    second_max, second_sum, second_out = later
    overall = jnp.maximum(first_max, second_max)
    first_factor = jnp.exp(first_max - overall)
    second_factor = jnp.exp(second_max - overall)
    return (
        overall,
        first_sum * first_factor + second_sum * second_factor,
        first_out * first_factor[..., None] + second_out * second_factor[..., None],
    )


def body(
    given_token_index,
    hidden,
    token_embedding_table,
    attention_norm_gain,
    query_key_value_weight,
    rotated_key_cache,
    cached_value_pages,
    lengths,
    request_page_slots,
    attention_output_weight,
    feedforward_norm_gain,
    gate_weight,
    up_weight,
    adapter_down_map,
    adapter_gate_map,
    adapter_up_map,
    down_weight,
):
    seq_devices = lax.axis_size("seq")
    req_devices = lax.axis_size("req")
    seq_index = lax.axis_index("seq")
    req_index = lax.axis_index("req")
    group_rows = hidden.shape[0]
    requests = lengths.shape[0]
    steps_each = group_rows // requests
    vocab_rows = token_embedding_table.shape[0]
    first_id = (seq_index * req_devices + req_index) * vocab_rows
    local_ids = given_token_index - first_id
    present = (local_ids >= 0) & (local_ids < vocab_rows)
    looked = jnp.take(token_embedding_table, jnp.clip(local_ids, 0, vocab_rows - 1), axis=0).astype(
        jnp.float32
    )
    looked = jnp.where(present[:, None], looked, 0.0).astype(jnp.bfloat16)
    row_share = group_rows // seq_devices
    lanes = 128
    by_group = looked.reshape(req_devices, seq_devices, row_share * looked.shape[1] // lanes, lanes)
    row_parts = two_rounds(
        by_group,
        ("req", False),
        ("seq", False),
        lambda landed: _block_sum(landed).astype(jnp.bfloat16),
        by_group.shape[1:],
        jnp.bfloat16,
        10,
    )
    embedded_rows = (
        jnp.sum(row_parts.astype(jnp.float32), axis=0)
        .astype(jnp.bfloat16)
        .reshape(row_share, looked.shape[1])
    )
    own_hidden = lax.dynamic_slice_in_dim(hidden, seq_index * row_share, row_share, 0)
    own_rows = jnp.concatenate([own_hidden, embedded_rows], axis=1)
    normed_rows = rms_norm(own_rows, attention_norm_gain)
    normed = exchange(normed_rows.reshape(-1, lanes), "seq", 12, gather=True).reshape(
        group_rows, own_rows.shape[1]
    )
    width_share = normed.shape[1] // req_devices
    to_owners = jnp.transpose(normed.reshape(group_rows, req_devices, width_share), (1, 0, 2))
    qkv_cols = query_key_value_weight.shape[1]

    def project(landed, weight):
        flat = landed[...].reshape(req_devices * group_rows, width_share)
        product = jnp.dot(flat, weight[...], preferred_element_type=jnp.float32)
        return product.reshape(req_devices, group_rows, qkv_cols)

    qkv_all = chain(
        to_owners,
        [
            ("req", False, project, ((req_devices, group_rows, qkv_cols), jnp.float32)),
            (
                "req",
                False,
                lambda landed, weight: _block_sum(landed).astype(jnp.bfloat16),
                ((group_rows, qkv_cols), jnp.bfloat16),
            ),
            ("seq", True, None, None),
        ],
        4,
        extra=(query_key_value_weight,),
    )
    projected = jnp.transpose(qkv_all, (1, 0, 2)).reshape(group_rows, seq_devices * qkv_all.shape[2])
    head_cols = HEADS * HD
    queries = projected[:, :head_cols].reshape(requests, steps_each, HEADS, HD)
    new_keys = projected[:, head_cols : 2 * head_cols].reshape(requests, steps_each, HEADS, HD)
    new_values = projected[:, 2 * head_cols :].reshape(requests, steps_each, HEADS, HD)
    positions = lengths[:, None] + jnp.arange(steps_each, dtype=jnp.int32)[None, :]
    queries = rotate(queries.astype(jnp.float32), positions).astype(jnp.bfloat16)
    new_keys = rotate(new_keys.astype(jnp.float32), positions).astype(jnp.bfloat16)
    slots = rotated_key_cache.shape[0]
    page_len = rotated_key_cache.shape[2]
    cache_k = rotated_key_cache.reshape(slots * page_len, head_cols)
    cache_v = cached_value_pages.reshape(slots * page_len, head_cols)
    slot_ids = seq_index * slots + jnp.arange(slots, dtype=jnp.int32)
    page_ids = jnp.arange(request_page_slots.shape[1], dtype=jnp.int32)
    is_live = page_ids[None, :] < ((lengths + page_len - 1) // page_len)[:, None]
    matches = (request_page_slots[:, :, None] == slot_ids[None, None, :]) & is_live[:, :, None]
    is_owned = jnp.any(matches, axis=1)
    page_of = jnp.sum(jnp.where(matches, page_ids[None, :, None], 0), axis=1)
    token_pos = (
        page_of[:, :, None] * page_len + jnp.arange(page_len, dtype=jnp.int32)[None, None, :]
    )
    is_valid = (is_owned[:, :, None] & (token_pos < lengths[:, None, None])).reshape(
        requests, slots * page_len
    )
    score_scale = 1.0 / math.sqrt(HD)
    head_mask = (jnp.arange(head_cols, dtype=jnp.int32)[None, :] // HD) == jnp.arange(
        HEADS, dtype=jnp.int32
    )[:, None]
    query_rows = queries.reshape(group_rows, head_cols)
    spread_queries = jnp.where(head_mask[None], query_rows[:, None, :], jnp.zeros((), jnp.bfloat16))
    scores = (
        jnp.dot(
            spread_queries.reshape(group_rows * HEADS, head_cols),
            cache_k.T,
            preferred_element_type=jnp.float32,
        )
        * score_scale
    ).reshape(requests, steps_each, HEADS, slots * page_len)
    mask_b = is_valid[:, None, None, :]
    local_max = jnp.max(jnp.where(mask_b, scores, NEGATIVE), axis=-1)
    weights = jnp.where(mask_b, jnp.exp(scores - local_max[..., None]), 0.0)
    local_sum = jnp.sum(weights, axis=-1)
    spread_out = jnp.dot(
        weights.astype(jnp.bfloat16).reshape(group_rows * HEADS, slots * page_len),
        cache_v,
        preferred_element_type=jnp.float32,
    ).reshape(group_rows, HEADS, head_cols)
    local_out = jnp.sum(jnp.where(head_mask[None], spread_out, 0.0), axis=1).reshape(
        requests, steps_each, HEADS, HD
    )
    fresh_scores = (
        jnp.einsum("rthd,rshd->rths", queries, new_keys, preferred_element_type=jnp.float32)
        * score_scale
    )
    causal = jnp.arange(steps_each)[:, None] >= jnp.arange(steps_each)[None, :]
    fresh_mask = causal[None, :, None, :]
    fresh_max = jnp.max(jnp.where(fresh_mask, fresh_scores, NEGATIVE), axis=-1)
    fresh_w = jnp.where(fresh_mask, jnp.exp(fresh_scores - fresh_max[..., None]), 0.0)
    fresh_sum = jnp.sum(fresh_w, axis=-1)
    fresh_out = jnp.einsum(
        "rths,rshd->rthd",
        fresh_w.astype(jnp.bfloat16),
        new_values,
        preferred_element_type=jnp.float32,
    )
    own_heads = HEADS // seq_devices
    first_head = seq_index * own_heads

    def own_slice(member):
        return lax.dynamic_slice_in_dim(member, first_head, own_heads, 2)

    pad_cols = 256 - HD - 2
    packed = jnp.concatenate(
        [
            local_out,
            local_max[..., None],
            local_sum[..., None],
            jnp.zeros(local_out.shape[:-1] + (pad_cols,), jnp.float32),
        ],
        axis=-1,
    )
    packed = packed.reshape(requests * steps_each, seq_devices, own_heads, 256)
    packed = jnp.transpose(packed, (1, 0, 2, 3)).reshape(seq_devices, group_rows * own_heads, 256)
    model_width = attention_output_weight.shape[1]
    head_rows = group_rows * own_heads
    tile_rows = row_share * model_width // lanes

    def merge_and_project(landed, fresh_max_ref, fresh_sum_ref, fresh_out_ref, weight, own):
        part_o = landed[:, :, :HD]
        part_m = landed[:, :, HD : HD + 1]
        part_l = landed[:, :, HD + 1 : HD + 2]
        f_max = fresh_max_ref[...]
        overall = jnp.maximum(jnp.max(part_m, axis=0), f_max)
        part_factor = jnp.exp(part_m - overall[None])
        fresh_factor = jnp.exp(f_max - overall)
        denominator = jnp.sum(part_l * part_factor, axis=0) + fresh_sum_ref[...] * fresh_factor
        numerator = jnp.sum(part_o * part_factor, axis=0) + fresh_out_ref[...] * fresh_factor
        attention = (numerator / denominator).astype(jnp.bfloat16).reshape(
            group_rows, own_heads * HD
        )
        product = jnp.dot(attention, weight[...], preferred_element_type=jnp.float32)
        return product.reshape(seq_devices, tile_rows, lanes)

    def add_residual(landed, fresh_max_ref, fresh_sum_ref, fresh_out_ref, weight, own):
        return (own[...].astype(jnp.float32) + _block_sum(landed)).astype(jnp.bfloat16)

    after_attn = chain(
        packed,
        [
            ("seq", False, merge_and_project, ((seq_devices, tile_rows, lanes), jnp.float32)),
            ("seq", False, add_residual, ((tile_rows, lanes), jnp.bfloat16)),
            ("seq", True, None, None),
        ],
        1,
        extra=(
            own_slice(fresh_max).reshape(head_rows, 1),
            own_slice(fresh_sum).reshape(head_rows, 1),
            own_slice(fresh_out).reshape(head_rows, HD),
            attention_output_weight,
            own_rows.reshape(tile_rows, lanes),
        ),
    ).reshape(group_rows, model_width)
    second_normed_state = rms_norm(after_attn, feedforward_norm_gain)
    both = jnp.stack([after_attn, second_normed_state]).reshape(2, group_rows, req_devices, width_share)
    both = jnp.transpose(both, (2, 0, 1, 3))
    down_sum, both_parts = fused_mlp(
        both, gate_weight, up_weight, adapter_down_map, adapter_gate_map, adapter_up_map, down_weight, 7
    )
    residual_cols = both_parts[:, 0].reshape(req_devices * group_rows, width_share)
    out_rows = residual_cols.shape[0] // seq_devices
    residual_rows = lax.dynamic_slice_in_dim(residual_cols, seq_index * out_rows, out_rows, 0)
    return (residual_rows.astype(jnp.float32) + down_sum).astype(jnp.bfloat16)


def solution(mesh):
    placed = (
        P(),
        P("req", None),
        P(("seq", "req"), None),
        P(),
        P("req", "seq"),
        P("seq", "req", None, None),
        P("seq", "req", None, None),
        P("req"),
        P("req", None),
        P("seq", None),
        P(),
        P("req", "seq"),
        P("req", "seq"),
        P("req", None),
        P(None, "seq"),
        P(None, "seq"),
        P("seq", "req"),
    )
    return jax.shard_map(
        body, mesh=mesh, in_specs=placed, out_specs=P("seq", "req"), check_vma=False
    )
```

```python
import functools
import math

import jax
import jax.numpy as jnp
from jax import lax
from jax.experimental import pallas as pl
from jax.experimental.pallas import tpu as pltpu
from jax.sharding import PartitionSpec as P

HEADS = 16
HD = 224


NEGATIVE = -1e30
EPSILON = 1e-05
ROTARY_BASE = 10000.0


MESH_ID = pl.DeviceIdType.MESH


def _exchange_kernel(axis, n, gather, x_ref, y_ref, send_sem, recv_sem, local_sem):
    me = lax.axis_index(axis)
    barrier = pltpu.get_barrier_semaphore()
    for k in range(1, n):
        peer = lax.rem(me + k, n)
        pl.semaphore_signal(barrier, 1, device_id={axis: peer}, device_id_type=MESH_ID)
    pl.semaphore_wait(barrier, n - 1)
    copies = []
    for k in range(1, n):
        peer = lax.rem(me + k, n)
        source = x_ref if gather else x_ref.at[peer]
        copy = pltpu.make_async_remote_copy(
            src_ref=source,
            dst_ref=y_ref.at[me],
            send_sem=send_sem.at[k],
            recv_sem=recv_sem.at[k],
            device_id={axis: peer},
            device_id_type=MESH_ID,
        )
        copy.start()
        copies.append(copy)
    local = pltpu.make_async_copy(x_ref if gather else x_ref.at[me], y_ref.at[me], local_sem)
    local.start()
    local.wait()
    for copy in copies:
        copy.wait()


def exchange(x, axis, cid, gather=False):
    n = lax.axis_size(axis)
    out_shape = (n,) + x.shape if gather else x.shape
    return pl.pallas_call(
        functools.partial(_exchange_kernel, axis, n, gather),
        out_shape=jax.ShapeDtypeStruct(out_shape, x.dtype),
        in_specs=[pl.BlockSpec(memory_space=pltpu.VMEM)],
        out_specs=pl.BlockSpec(memory_space=pltpu.VMEM),
        scratch_shapes=[
            pltpu.SemaphoreType.DMA((n,)),
            pltpu.SemaphoreType.DMA((n,)),
            pltpu.SemaphoreType.DMA(()),
        ],
        compiler_params=pltpu.CompilerParams(collective_id=cid, has_side_effects=True),
    )(x)


def _greet(axes_sizes):
    barrier = pltpu.get_barrier_semaphore()
    total = 0
    for axis, n in axes_sizes:
        me = lax.axis_index(axis)
        for k in range(1, n):
            peer = lax.rem(me + k, n)
            pl.semaphore_signal(barrier, 1, device_id={axis: peer}, device_id_type=MESH_ID)
        total += n - 1
    pl.semaphore_wait(barrier, total)


def _start_round(axis, n, gather, source, target, send_sem, recv_sem, local_sem):
    me = lax.axis_index(axis)
    copies = []
    for k in range(1, n):
        peer = lax.rem(me + k, n)
        copy = pltpu.make_async_remote_copy(
            src_ref=source if gather else source.at[peer],
            dst_ref=target.at[me],
            send_sem=send_sem.at[k],
            recv_sem=recv_sem.at[k],
            device_id={axis: peer},
            device_id_type=MESH_ID,
        )
        copy.start()
        copies.append(copy)
    local = pltpu.make_async_copy(source if gather else source.at[me], target.at[me], local_sem)
    local.start()
    copies.append(local)
    return copies


def _two_round_kernel(first, second, mid, n_extra, x_ref, *refs):
    extra = refs[:n_extra]
    y_ref, landed, staged, send_a, recv_a, send_b, recv_b, local_sems = refs[n_extra:]
    axis_a, n_a, gather_a = first
    axis_b, n_b, gather_b = second
    greeted = [(axis_a, n_a)] if axis_a == axis_b else [(axis_a, n_a), (axis_b, n_b)]
    _greet(greeted)
    for copy in _start_round(axis_a, n_a, gather_a, x_ref, landed, send_a, recv_a, local_sems.at[0]):
        copy.wait()
    staged[...] = mid(landed, *extra)
    for copy in _start_round(axis_b, n_b, gather_b, staged, y_ref, send_b, recv_b, local_sems.at[1]):
        copy.wait()


def two_rounds(x, first, second, mid, staged_shape, staged_dtype, cid, extra=()):
    axis_a, gather_a = first
    axis_b, gather_b = second
    n_a, n_b = lax.axis_size(axis_a), lax.axis_size(axis_b)
    landed_shape = (n_a,) + x.shape if gather_a else x.shape
    out_shape = (n_b,) + staged_shape if gather_b else staged_shape
    return pl.pallas_call(
        functools.partial(
            _two_round_kernel, (axis_a, n_a, gather_a), (axis_b, n_b, gather_b), mid, len(extra)
        ),
        out_shape=jax.ShapeDtypeStruct(out_shape, staged_dtype),
        in_specs=[pl.BlockSpec(memory_space=pltpu.VMEM)] * (1 + len(extra)),
        out_specs=pl.BlockSpec(memory_space=pltpu.VMEM),
        scratch_shapes=[
            pltpu.VMEM(landed_shape, x.dtype),
            pltpu.VMEM(staged_shape, staged_dtype),
            pltpu.SemaphoreType.DMA((n_a,)),
            pltpu.SemaphoreType.DMA((n_a,)),
            pltpu.SemaphoreType.DMA((n_b,)),
            pltpu.SemaphoreType.DMA((n_b,)),
            pltpu.SemaphoreType.DMA((2,)),
        ],
        compiler_params=pltpu.CompilerParams(collective_id=cid, has_side_effects=True),
    )(x, *extra)


def _block_sum(landed):
    total = landed[0].astype(jnp.float32)
    for k in range(1, landed.shape[0]):
        total = total + landed[k].astype(jnp.float32)
    return total


def _mlp_kernel(
    x_ref, gate_hbm, up_hbm, down_map_hbm, gate_map_hbm, up_map_hbm, down_hbm,
    out_ref, spread_ref, landed1, staged1, staged2, landed2, staged3, landed3,
    send0, recv0, send1, recv1, send2, recv2, send3, recv3, local_sems,
    gate_ref, up_ref, down_map_ref, gate_map_ref, up_map_ref, down_ref, weight_sems,
):
    n_req = spread_ref.shape[0]
    n_seq = landed3.shape[0]
    rows = n_req * spread_ref.shape[2]
    units = gate_ref.shape[1]
    loads = []
    pairs = (
        (gate_hbm, gate_ref), (up_hbm, up_ref), (down_map_hbm, down_map_ref),
        (gate_map_hbm, gate_map_ref), (up_map_hbm, up_map_ref), (down_hbm, down_ref),
    )
    for index, (source, target) in enumerate(pairs):
        load = pltpu.make_async_copy(source, target, weight_sems.at[index])
        load.start()
        loads.append(load)
    _greet([("req", n_req), ("seq", n_seq)])
    for copy in _start_round("req", n_req, False, x_ref, spread_ref, send0, recv0, local_sems.at[0]):
        copy.wait()
    for load in loads[:3]:
        load.wait()
    normed_all = spread_ref[:, 1].reshape(rows, spread_ref.shape[3])
    staged1[:, :, :units] = jnp.dot(
        normed_all, gate_ref[...], preferred_element_type=jnp.float32
    ).reshape(staged1.shape[0], staged1.shape[1], units)
    staged1[:, :, units : 2 * units] = jnp.dot(
        normed_all, up_ref[...], preferred_element_type=jnp.float32
    ).reshape(staged1.shape[0], staged1.shape[1], units)
    staged1[:, :, 2 * units :] = jnp.dot(
        normed_all, down_map_ref[...], preferred_element_type=jnp.float32
    ).reshape(staged1.shape[0], staged1.shape[1], staged1.shape[2] - 2 * units)
    for copy in _start_round("req", n_req, False, staged1, landed1, send1, recv1, local_sems.at[1]):
        copy.wait()
    for load in loads[3:5]:
        load.wait()
    total = _block_sum(landed1)
    low = total[:, 2 * units :].astype(jnp.bfloat16)
    gate_pre = total[:, :units] + jnp.dot(low, gate_map_ref[...], preferred_element_type=jnp.float32)
    up_part = total[:, units : 2 * units] + jnp.dot(
        low, up_map_ref[...], preferred_element_type=jnp.float32
    )
    staged2[...] = (gate_pre / (1.0 + jnp.exp(-gate_pre)) * up_part).astype(jnp.bfloat16)
    for copy in _start_round("req", n_req, True, staged2, landed2, send2, recv2, local_sems.at[2]):
        copy.wait()
    loads[5].wait()
    inner = landed2[...].reshape(rows, units)
    staged3[...] = jnp.dot(inner, down_ref[...], preferred_element_type=jnp.float32).reshape(
        staged3.shape
    )
    for copy in _start_round("seq", n_seq, False, staged3, landed3, send3, recv3, local_sems.at[3]):
        copy.wait()
    out_ref[...] = _block_sum(landed3)


def fused_mlp(both, gate_weight, up_weight, down_map, gate_map, up_map, down_weight, cid):
    n_req, n_seq = lax.axis_size("req"), lax.axis_size("seq")
    group_rows = both.shape[2]
    rows = n_req * group_rows
    units = gate_weight.shape[1]
    wide = 2 * units + down_map.shape[1]
    out_rows = rows // n_seq
    vmem = pltpu.VMEM
    return pl.pallas_call(
        _mlp_kernel,
        out_shape=(
            jax.ShapeDtypeStruct((out_rows, down_weight.shape[1]), jnp.float32),
            jax.ShapeDtypeStruct(both.shape, both.dtype),
        ),
        in_specs=[pl.BlockSpec(memory_space=vmem)] + [pl.BlockSpec(memory_space=pl.ANY)] * 6,
        out_specs=(pl.BlockSpec(memory_space=vmem), pl.BlockSpec(memory_space=vmem)),
        scratch_shapes=[
            vmem((n_req, group_rows, wide), jnp.float32),
            vmem((n_req, group_rows, wide), jnp.float32),
            vmem((group_rows, units), jnp.bfloat16),
            vmem((n_req, group_rows, units), jnp.bfloat16),
            vmem((n_seq, out_rows, down_weight.shape[1]), jnp.float32),
            vmem((n_seq, out_rows, down_weight.shape[1]), jnp.float32),
            pltpu.SemaphoreType.DMA((n_req,)),
            pltpu.SemaphoreType.DMA((n_req,)),
            pltpu.SemaphoreType.DMA((n_req,)),
            pltpu.SemaphoreType.DMA((n_req,)),
            pltpu.SemaphoreType.DMA((n_req,)),
            pltpu.SemaphoreType.DMA((n_req,)),
            pltpu.SemaphoreType.DMA((n_seq,)),
            pltpu.SemaphoreType.DMA((n_seq,)),
            pltpu.SemaphoreType.DMA((4,)),
        ]
        + [
            vmem(weight.shape, weight.dtype)
            for weight in (gate_weight, up_weight, down_map, gate_map, up_map, down_weight)
        ]
        + [pltpu.SemaphoreType.DMA((6,))],
        compiler_params=pltpu.CompilerParams(
            collective_id=cid, has_side_effects=True
        ),
    )(both, gate_weight, up_weight, down_map, gate_map, up_map, down_weight)


def _chain_kernel(spec, n_extra, x_ref, *refs):
    extra_hbm = refs[:n_extra]
    y_ref = refs[n_extra]
    scratch = refs[n_extra + 1 :]
    count = len(spec)
    landed = list(scratch[: count - 1]) + [y_ref]
    staged = scratch[count - 1 : 2 * count - 2]
    extra = scratch[2 * count - 2 : 2 * count - 2 + n_extra]
    extra_sems = scratch[2 * count - 2 + n_extra]
    sems = scratch[2 * count - 1 + n_extra :]
    loads = []
    for index in range(n_extra):
        load = pltpu.make_async_copy(extra_hbm[index], extra[index], extra_sems.at[index])
        load.start()
        loads.append(load)
    axes = []
    for axis, n, _, _ in spec:
        if (axis, n) not in axes:
            axes.append((axis, n))
    _greet(axes)
    source = x_ref
    for k, (axis, n, gather, mid) in enumerate(spec):
        copies = _start_round(
            axis, n, gather, source, landed[k], sems[2 * k], sems[2 * k + 1], sems[-1].at[k]
        )
        for copy in copies:
            copy.wait()
        if k == 0:
            for load in loads:
                load.wait()
        if mid is not None:
            staged[k][...] = mid(landed[k], *extra)
            source = staged[k]


def chain(x, rounds, cid, extra=()):
    spec, landed_shapes, staged_shapes = [], [], []
    block = (x.shape, x.dtype)
    for index, (axis, gather, mid, made) in enumerate(rounds):
        n = lax.axis_size(axis)
        shape, dtype = block
        landed = ((n,) + shape if gather else shape, dtype)
        spec.append((axis, n, gather, mid))
        if index < len(rounds) - 1:
            landed_shapes.append(landed)
            staged_shapes.append(made)
            block = made
        else:
            out = landed
    sizes = [n for _, n, _, _ in spec]
    semaphores = []
    for n in sizes:
        semaphores += [pltpu.SemaphoreType.DMA((n,)), pltpu.SemaphoreType.DMA((n,))]
    return pl.pallas_call(
        functools.partial(_chain_kernel, spec, len(extra)),
        out_shape=jax.ShapeDtypeStruct(*out),
        in_specs=[pl.BlockSpec(memory_space=pltpu.VMEM)]
        + [pl.BlockSpec(memory_space=pl.ANY)] * len(extra),
        out_specs=pl.BlockSpec(memory_space=pltpu.VMEM),
        scratch_shapes=[pltpu.VMEM(*item) for item in landed_shapes]
        + [pltpu.VMEM(*item) for item in staged_shapes]
        + [pltpu.VMEM(item.shape, item.dtype) for item in extra]
        + [pltpu.SemaphoreType.DMA((max(len(extra), 1),))]
        + semaphores
        + [pltpu.SemaphoreType.DMA((len(spec),))],
        compiler_params=pltpu.CompilerParams(
            collective_id=cid, has_side_effects=True
        ),
    )(x, *extra)


def merged_2(array, axis, combine):
    everything = jax.tree.map(lambda part: lax.all_gather(part, axis), array)
    first = jax.tree.map(lambda part: part[0], everything)

    def hop(k, so_far):
        return combine(so_far, jax.tree.map(lambda part: part[k], everything))

    return lax.fori_loop(1, lax.axis_size(axis), hop, first)


def rms_norm(matrix, gain_vec):
    widened = matrix.astype(jnp.float32)
    factor = lax.rsqrt(jnp.mean(widened * widened, axis=-1, keepdims=True) + EPSILON)
    return (widened * factor * gain_vec.astype(jnp.float32)).astype(jnp.bfloat16)


def rotate(vectors, positions):
    half_dim = vectors.shape[-1] // 2
    frequency = ROTARY_BASE ** (-2.0 * jnp.arange(half_dim, dtype=jnp.float32) / vectors.shape[-1])
    angles = positions.astype(jnp.float32)[..., None, None] * frequency
    cosine = jnp.cos(angles)
    sine_part = jnp.sin(angles)
    front_half = vectors[..., :half_dim]
    back_half = vectors[..., half_dim:]
    return jnp.concatenate(
        [front_half * cosine - back_half * sine_part, back_half * cosine + front_half * sine_part],
        axis=-1,
    )


def softmax_join(earlier, later):
    first_max, first_sum, first_out = earlier
    second_max, second_sum, second_out = later
    overall = jnp.maximum(first_max, second_max)
    first_factor = jnp.exp(first_max - overall)
    second_factor = jnp.exp(second_max - overall)
    return (
        overall,
        first_sum * first_factor + second_sum * second_factor,
        first_out * first_factor[..., None] + second_out * second_factor[..., None],
    )


def body(
    given_token_index,
    hidden,
    token_embedding_table,
    attention_norm_gain,
    query_key_value_weight,
    rotated_key_cache,
    cached_value_pages,
    lengths,
    request_page_slots,
    attention_output_weight,
    feedforward_norm_gain,
    gate_weight,
    up_weight,
    adapter_down_map,
    adapter_gate_map,
    adapter_up_map,
    down_weight,
):
    seq_devices = lax.axis_size("seq")
    req_devices = lax.axis_size("req")
    seq_index = lax.axis_index("seq")
    req_index = lax.axis_index("req")
    group_rows = hidden.shape[0]
    requests = lengths.shape[0]
    steps_each = group_rows // requests
    vocab_rows = token_embedding_table.shape[0]
    first_id = (seq_index * req_devices + req_index) * vocab_rows
    local_ids = given_token_index - first_id
    present = (local_ids >= 0) & (local_ids < vocab_rows)
    looked = jnp.take(token_embedding_table, jnp.clip(local_ids, 0, vocab_rows - 1), axis=0).astype(
        jnp.float32
    )
    looked = jnp.where(present[:, None], looked, 0.0).astype(jnp.bfloat16)
    row_share = group_rows // seq_devices
    lanes = 128
    by_group = looked.reshape(req_devices, seq_devices, row_share * looked.shape[1] // lanes, lanes)
    row_parts = two_rounds(
        by_group,
        ("req", False),
        ("seq", False),
        lambda landed: _block_sum(landed).astype(jnp.bfloat16),
        by_group.shape[1:],
        jnp.bfloat16,
        10,
    )
    embedded_rows = (
        jnp.sum(row_parts.astype(jnp.float32), axis=0)
        .astype(jnp.bfloat16)
        .reshape(row_share, looked.shape[1])
    )
    own_hidden = lax.dynamic_slice_in_dim(hidden, seq_index * row_share, row_share, 0)
    own_rows = jnp.concatenate([own_hidden, embedded_rows], axis=1)
    normed_rows = rms_norm(own_rows, attention_norm_gain)
    model_width = own_rows.shape[1]
    width_share = model_width // req_devices

    def to_owners(landed, weight):
        rows = landed[...].reshape(group_rows, model_width)
        return jnp.stack(
            [rows[:, part * width_share : (part + 1) * width_share] for part in range(req_devices)]
        )

    qkv_cols = query_key_value_weight.shape[1]

    def project(landed, weight):
        flat = landed[...].reshape(req_devices * group_rows, width_share)
        product = jnp.dot(flat, weight[...], preferred_element_type=jnp.float32)
        return product.reshape(req_devices, group_rows, qkv_cols)

    qkv_all = chain(
        normed_rows.reshape(-1, lanes),
        [
            ("seq", True, to_owners, ((req_devices, group_rows, width_share), jnp.bfloat16)),
            ("req", False, project, ((req_devices, group_rows, qkv_cols), jnp.float32)),
            (
                "req",
                False,
                lambda landed, weight: _block_sum(landed).astype(jnp.bfloat16),
                ((group_rows, qkv_cols), jnp.bfloat16),
            ),
            ("seq", True, None, None),
        ],
        4,
        extra=(query_key_value_weight,),
    )
    projected = jnp.transpose(qkv_all, (1, 0, 2)).reshape(group_rows, seq_devices * qkv_all.shape[2])
    head_cols = HEADS * HD
    queries = projected[:, :head_cols].reshape(requests, steps_each, HEADS, HD)
    new_keys = projected[:, head_cols : 2 * head_cols].reshape(requests, steps_each, HEADS, HD)
    new_values = projected[:, 2 * head_cols :].reshape(requests, steps_each, HEADS, HD)
    positions = lengths[:, None] + jnp.arange(steps_each, dtype=jnp.int32)[None, :]
    queries = rotate(queries.astype(jnp.float32), positions).astype(jnp.bfloat16)
    new_keys = rotate(new_keys.astype(jnp.float32), positions).astype(jnp.bfloat16)
    slots = rotated_key_cache.shape[0]
    page_len = rotated_key_cache.shape[2]
    cache_k = rotated_key_cache.reshape(slots * page_len, head_cols)
    cache_v = cached_value_pages.reshape(slots * page_len, head_cols)
    slot_ids = seq_index * slots + jnp.arange(slots, dtype=jnp.int32)
    page_ids = jnp.arange(request_page_slots.shape[1], dtype=jnp.int32)
    is_live = page_ids[None, :] < ((lengths + page_len - 1) // page_len)[:, None]
    matches = (request_page_slots[:, :, None] == slot_ids[None, None, :]) & is_live[:, :, None]
    is_owned = jnp.any(matches, axis=1)
    page_of = jnp.sum(jnp.where(matches, page_ids[None, :, None], 0), axis=1)
    token_pos = (
        page_of[:, :, None] * page_len + jnp.arange(page_len, dtype=jnp.int32)[None, None, :]
    )
    is_valid = (is_owned[:, :, None] & (token_pos < lengths[:, None, None])).reshape(
        requests, slots * page_len
    )
    score_scale = 1.0 / math.sqrt(HD)
    head_mask = (jnp.arange(head_cols, dtype=jnp.int32)[None, :] // HD) == jnp.arange(
        HEADS, dtype=jnp.int32
    )[:, None]
    query_rows = queries.reshape(group_rows, head_cols)
    spread_queries = jnp.where(head_mask[None], query_rows[:, None, :], jnp.zeros((), jnp.bfloat16))
    scores = (
        jnp.dot(
            spread_queries.reshape(group_rows * HEADS, head_cols),
            cache_k.T,
            preferred_element_type=jnp.float32,
        )
        * score_scale
    ).reshape(requests, steps_each, HEADS, slots * page_len)
    mask_b = is_valid[:, None, None, :]
    local_max = jnp.max(jnp.where(mask_b, scores, NEGATIVE), axis=-1)
    weights = jnp.where(mask_b, jnp.exp(scores - local_max[..., None]), 0.0)
    local_sum = jnp.sum(weights, axis=-1)
    spread_out = jnp.dot(
        weights.astype(jnp.bfloat16).reshape(group_rows * HEADS, slots * page_len),
        cache_v,
        preferred_element_type=jnp.float32,
    ).reshape(group_rows, HEADS, head_cols)
    local_out = jnp.sum(jnp.where(head_mask[None], spread_out, 0.0), axis=1).reshape(
        requests, steps_each, HEADS, HD
    )
    fresh_scores = (
        jnp.einsum("rthd,rshd->rths", queries, new_keys, preferred_element_type=jnp.float32)
        * score_scale
    )
    causal = jnp.arange(steps_each)[:, None] >= jnp.arange(steps_each)[None, :]
    fresh_mask = causal[None, :, None, :]
    fresh_max = jnp.max(jnp.where(fresh_mask, fresh_scores, NEGATIVE), axis=-1)
    fresh_w = jnp.where(fresh_mask, jnp.exp(fresh_scores - fresh_max[..., None]), 0.0)
    fresh_sum = jnp.sum(fresh_w, axis=-1)
    fresh_out = jnp.einsum(
        "rths,rshd->rthd",
        fresh_w.astype(jnp.bfloat16),
        new_values,
        preferred_element_type=jnp.float32,
    )
    own_heads = HEADS // seq_devices
    first_head = seq_index * own_heads

    def own_slice(member):
        return lax.dynamic_slice_in_dim(member, first_head, own_heads, 2)

    pad_cols = 256 - HD - 2
    packed = jnp.concatenate(
        [
            local_out,
            local_max[..., None],
            local_sum[..., None],
            jnp.zeros(local_out.shape[:-1] + (pad_cols,), jnp.float32),
        ],
        axis=-1,
    )
    packed = packed.reshape(requests * steps_each, seq_devices, own_heads, 256)
    packed = jnp.transpose(packed, (1, 0, 2, 3)).reshape(seq_devices, group_rows * own_heads, 256)
    model_width = attention_output_weight.shape[1]
    head_rows = group_rows * own_heads
    tile_rows = row_share * model_width // lanes

    def merge_and_project(landed, fresh_max_ref, fresh_sum_ref, fresh_out_ref, weight, own):
        part_o = landed[:, :, :HD]
        part_m = landed[:, :, HD : HD + 1]
        part_l = landed[:, :, HD + 1 : HD + 2]
        f_max = fresh_max_ref[...]
        overall = jnp.maximum(jnp.max(part_m, axis=0), f_max)
        part_factor = jnp.exp(part_m - overall[None])
        fresh_factor = jnp.exp(f_max - overall)
        denominator = jnp.sum(part_l * part_factor, axis=0) + fresh_sum_ref[...] * fresh_factor
        numerator = jnp.sum(part_o * part_factor, axis=0) + fresh_out_ref[...] * fresh_factor
        attention = (numerator / denominator).astype(jnp.bfloat16).reshape(
            group_rows, own_heads * HD
        )
        product = jnp.dot(attention, weight[...], preferred_element_type=jnp.float32)
        return product.reshape(seq_devices, tile_rows, lanes)

    def add_residual(landed, fresh_max_ref, fresh_sum_ref, fresh_out_ref, weight, own):
        return (own[...].astype(jnp.float32) + _block_sum(landed)).astype(jnp.bfloat16)

    after_attn = chain(
        packed,
        [
            ("seq", False, merge_and_project, ((seq_devices, tile_rows, lanes), jnp.float32)),
            ("seq", False, add_residual, ((tile_rows, lanes), jnp.bfloat16)),
            ("seq", True, None, None),
        ],
        1,
        extra=(
            own_slice(fresh_max).reshape(head_rows, 1),
            own_slice(fresh_sum).reshape(head_rows, 1),
            own_slice(fresh_out).reshape(head_rows, HD),
            attention_output_weight,
            own_rows.reshape(tile_rows, lanes),
        ),
    ).reshape(group_rows, model_width)
    second_normed_state = rms_norm(after_attn, feedforward_norm_gain)
    both = jnp.stack([after_attn, second_normed_state]).reshape(2, group_rows, req_devices, width_share)
    both = jnp.transpose(both, (2, 0, 1, 3))
    down_sum, both_parts = fused_mlp(
        both, gate_weight, up_weight, adapter_down_map, adapter_gate_map, adapter_up_map, down_weight, 7
    )
    residual_cols = both_parts[:, 0].reshape(req_devices * group_rows, width_share)
    out_rows = residual_cols.shape[0] // seq_devices
    residual_rows = lax.dynamic_slice_in_dim(residual_cols, seq_index * out_rows, out_rows, 0)
    return (residual_rows.astype(jnp.float32) + down_sum).astype(jnp.bfloat16)


def solution(mesh):
    placed = (
        P(),
        P("req", None),
        P(("seq", "req"), None),
        P(),
        P("req", "seq"),
        P("seq", "req", None, None),
        P("seq", "req", None, None),
        P("req"),
        P("req", None),
        P("seq", None),
        P(),
        P("req", "seq"),
        P("req", "seq"),
        P("req", None),
        P(None, "seq"),
        P(None, "seq"),
        P("seq", "req"),
    )
    return jax.shard_map(
        body, mesh=mesh, in_specs=placed, out_specs=P("seq", "req"), check_vma=False
    )
```

```python
import functools
import math

import jax
import jax.numpy as jnp
from jax import lax
from jax.experimental import pallas as pl
from jax.experimental.pallas import tpu as pltpu
from jax.sharding import PartitionSpec as P

HEADS = 16
HD = 224


NEGATIVE = -1e30
EPSILON = 1e-05
ROTARY_BASE = 10000.0


MESH_ID = pl.DeviceIdType.MESH


def _exchange_kernel(axis, n, gather, x_ref, y_ref, send_sem, recv_sem, local_sem):
    me = lax.axis_index(axis)
    barrier = pltpu.get_barrier_semaphore()
    for k in range(1, n):
        peer = lax.rem(me + k, n)
        pl.semaphore_signal(barrier, 1, device_id={axis: peer}, device_id_type=MESH_ID)
    pl.semaphore_wait(barrier, n - 1)
    copies = []
    for k in range(1, n):
        peer = lax.rem(me + k, n)
        source = x_ref if gather else x_ref.at[peer]
        copy = pltpu.make_async_remote_copy(
            src_ref=source,
            dst_ref=y_ref.at[me],
            send_sem=send_sem.at[k],
            recv_sem=recv_sem.at[k],
            device_id={axis: peer},
            device_id_type=MESH_ID,
        )
        copy.start()
        copies.append(copy)
    local = pltpu.make_async_copy(x_ref if gather else x_ref.at[me], y_ref.at[me], local_sem)
    local.start()
    local.wait()
    for copy in copies:
        copy.wait()


def exchange(x, axis, cid, gather=False):
    n = lax.axis_size(axis)
    out_shape = (n,) + x.shape if gather else x.shape
    return pl.pallas_call(
        functools.partial(_exchange_kernel, axis, n, gather),
        out_shape=jax.ShapeDtypeStruct(out_shape, x.dtype),
        in_specs=[pl.BlockSpec(memory_space=pltpu.VMEM)],
        out_specs=pl.BlockSpec(memory_space=pltpu.VMEM),
        scratch_shapes=[
            pltpu.SemaphoreType.DMA((n,)),
            pltpu.SemaphoreType.DMA((n,)),
            pltpu.SemaphoreType.DMA(()),
        ],
        compiler_params=pltpu.CompilerParams(collective_id=cid, has_side_effects=True),
    )(x)


def _greet(axes_sizes):
    barrier = pltpu.get_barrier_semaphore()
    total = 0
    for axis, n in axes_sizes:
        me = lax.axis_index(axis)
        for k in range(1, n):
            peer = lax.rem(me + k, n)
            pl.semaphore_signal(barrier, 1, device_id={axis: peer}, device_id_type=MESH_ID)
        total += n - 1
    pl.semaphore_wait(barrier, total)


def _start_round(axis, n, gather, source, target, send_sem, recv_sem, local_sem):
    me = lax.axis_index(axis)
    copies = []
    for k in range(1, n):
        peer = lax.rem(me + k, n)
        copy = pltpu.make_async_remote_copy(
            src_ref=source if gather else source.at[peer],
            dst_ref=target.at[me],
            send_sem=send_sem.at[k],
            recv_sem=recv_sem.at[k],
            device_id={axis: peer},
            device_id_type=MESH_ID,
        )
        copy.start()
        copies.append(copy)
    local = pltpu.make_async_copy(source if gather else source.at[me], target.at[me], local_sem)
    local.start()
    copies.append(local)
    return copies


def _two_round_kernel(first, second, mid, n_extra, x_ref, *refs):
    extra = refs[:n_extra]
    y_ref, landed, staged, send_a, recv_a, send_b, recv_b, local_sems = refs[n_extra:]
    axis_a, n_a, gather_a = first
    axis_b, n_b, gather_b = second
    greeted = [(axis_a, n_a)] if axis_a == axis_b else [(axis_a, n_a), (axis_b, n_b)]
    _greet(greeted)
    for copy in _start_round(axis_a, n_a, gather_a, x_ref, landed, send_a, recv_a, local_sems.at[0]):
        copy.wait()
    staged[...] = mid(landed, *extra)
    for copy in _start_round(axis_b, n_b, gather_b, staged, y_ref, send_b, recv_b, local_sems.at[1]):
        copy.wait()


def two_rounds(x, first, second, mid, staged_shape, staged_dtype, cid, extra=()):
    axis_a, gather_a = first
    axis_b, gather_b = second
    n_a, n_b = lax.axis_size(axis_a), lax.axis_size(axis_b)
    landed_shape = (n_a,) + x.shape if gather_a else x.shape
    out_shape = (n_b,) + staged_shape if gather_b else staged_shape
    return pl.pallas_call(
        functools.partial(
            _two_round_kernel, (axis_a, n_a, gather_a), (axis_b, n_b, gather_b), mid, len(extra)
        ),
        out_shape=jax.ShapeDtypeStruct(out_shape, staged_dtype),
        in_specs=[pl.BlockSpec(memory_space=pltpu.VMEM)] * (1 + len(extra)),
        out_specs=pl.BlockSpec(memory_space=pltpu.VMEM),
        scratch_shapes=[
            pltpu.VMEM(landed_shape, x.dtype),
            pltpu.VMEM(staged_shape, staged_dtype),
            pltpu.SemaphoreType.DMA((n_a,)),
            pltpu.SemaphoreType.DMA((n_a,)),
            pltpu.SemaphoreType.DMA((n_b,)),
            pltpu.SemaphoreType.DMA((n_b,)),
            pltpu.SemaphoreType.DMA((2,)),
        ],
        compiler_params=pltpu.CompilerParams(collective_id=cid, has_side_effects=True),
    )(x, *extra)


def _block_sum(landed):
    total = landed[0].astype(jnp.float32)
    for k in range(1, landed.shape[0]):
        total = total + landed[k].astype(jnp.float32)
    return total


def _mlp_kernel(
    x_ref, gate_hbm, up_hbm, down_map_hbm, gate_map_hbm, up_map_hbm, down_hbm,
    out_ref, spread_ref, landed1, staged1, staged2, landed2, staged3, landed3,
    send0, recv0, send1, recv1, send2, recv2, send3, recv3, local_sems,
    gate_ref, up_ref, down_map_ref, gate_map_ref, up_map_ref, down_ref, weight_sems,
):
    n_req = spread_ref.shape[0]
    n_seq = landed3.shape[0]
    rows = n_req * spread_ref.shape[2]
    units = gate_ref.shape[1]
    loads = []
    pairs = (
        (gate_hbm, gate_ref), (up_hbm, up_ref), (down_map_hbm, down_map_ref),
        (gate_map_hbm, gate_map_ref), (up_map_hbm, up_map_ref), (down_hbm, down_ref),
    )
    for index, (source, target) in enumerate(pairs):
        load = pltpu.make_async_copy(source, target, weight_sems.at[index])
        load.start()
        loads.append(load)
    _greet([("req", n_req), ("seq", n_seq)])
    for copy in _start_round("req", n_req, False, x_ref, spread_ref, send0, recv0, local_sems.at[0]):
        copy.wait()
    for load in loads[:3]:
        load.wait()
    normed_all = spread_ref[:, 1].reshape(rows, spread_ref.shape[3])
    staged1[:, :, :units] = jnp.dot(
        normed_all, gate_ref[...], preferred_element_type=jnp.float32
    ).reshape(staged1.shape[0], staged1.shape[1], units)
    staged1[:, :, units : 2 * units] = jnp.dot(
        normed_all, up_ref[...], preferred_element_type=jnp.float32
    ).reshape(staged1.shape[0], staged1.shape[1], units)
    staged1[:, :, 2 * units :] = jnp.dot(
        normed_all, down_map_ref[...], preferred_element_type=jnp.float32
    ).reshape(staged1.shape[0], staged1.shape[1], staged1.shape[2] - 2 * units)
    for copy in _start_round("req", n_req, False, staged1, landed1, send1, recv1, local_sems.at[1]):
        copy.wait()
    for load in loads[3:5]:
        load.wait()
    total = _block_sum(landed1)
    low = total[:, 2 * units :].astype(jnp.bfloat16)
    gate_pre = total[:, :units] + jnp.dot(low, gate_map_ref[...], preferred_element_type=jnp.float32)
    up_part = total[:, units : 2 * units] + jnp.dot(
        low, up_map_ref[...], preferred_element_type=jnp.float32
    )
    staged2[...] = (gate_pre / (1.0 + jnp.exp(-gate_pre)) * up_part).astype(jnp.bfloat16)
    for copy in _start_round("req", n_req, True, staged2, landed2, send2, recv2, local_sems.at[2]):
        copy.wait()
    loads[5].wait()
    inner = landed2[...].reshape(rows, units)
    staged3[...] = jnp.dot(inner, down_ref[...], preferred_element_type=jnp.float32).reshape(
        staged3.shape
    )
    for copy in _start_round("seq", n_seq, False, staged3, landed3, send3, recv3, local_sems.at[3]):
        copy.wait()
    out_ref[...] = _block_sum(landed3)


def fused_mlp(both, gate_weight, up_weight, down_map, gate_map, up_map, down_weight, cid):
    n_req, n_seq = lax.axis_size("req"), lax.axis_size("seq")
    group_rows = both.shape[2]
    rows = n_req * group_rows
    units = gate_weight.shape[1]
    wide = 2 * units + down_map.shape[1]
    out_rows = rows // n_seq
    vmem = pltpu.VMEM
    return pl.pallas_call(
        _mlp_kernel,
        out_shape=(
            jax.ShapeDtypeStruct((out_rows, down_weight.shape[1]), jnp.float32),
            jax.ShapeDtypeStruct(both.shape, both.dtype),
        ),
        in_specs=[pl.BlockSpec(memory_space=vmem)] + [pl.BlockSpec(memory_space=pl.ANY)] * 6,
        out_specs=(pl.BlockSpec(memory_space=vmem), pl.BlockSpec(memory_space=vmem)),
        scratch_shapes=[
            vmem((n_req, group_rows, wide), jnp.float32),
            vmem((n_req, group_rows, wide), jnp.float32),
            vmem((group_rows, units), jnp.bfloat16),
            vmem((n_req, group_rows, units), jnp.bfloat16),
            vmem((n_seq, out_rows, down_weight.shape[1]), jnp.float32),
            vmem((n_seq, out_rows, down_weight.shape[1]), jnp.float32),
            pltpu.SemaphoreType.DMA((n_req,)),
            pltpu.SemaphoreType.DMA((n_req,)),
            pltpu.SemaphoreType.DMA((n_req,)),
            pltpu.SemaphoreType.DMA((n_req,)),
            pltpu.SemaphoreType.DMA((n_req,)),
            pltpu.SemaphoreType.DMA((n_req,)),
            pltpu.SemaphoreType.DMA((n_seq,)),
            pltpu.SemaphoreType.DMA((n_seq,)),
            pltpu.SemaphoreType.DMA((4,)),
        ]
        + [
            vmem(weight.shape, weight.dtype)
            for weight in (gate_weight, up_weight, down_map, gate_map, up_map, down_weight)
        ]
        + [pltpu.SemaphoreType.DMA((6,))],
        compiler_params=pltpu.CompilerParams(
            collective_id=cid, has_side_effects=True
        ),
    )(both, gate_weight, up_weight, down_map, gate_map, up_map, down_weight)


def _chain_kernel(spec, n_extra, x_ref, *refs):
    extra_hbm = refs[:n_extra]
    y_ref = refs[n_extra]
    scratch = refs[n_extra + 1 :]
    count = len(spec)
    landed = list(scratch[: count - 1]) + [y_ref]
    staged = scratch[count - 1 : 2 * count - 2]
    extra = scratch[2 * count - 2 : 2 * count - 2 + n_extra]
    extra_sems = scratch[2 * count - 2 + n_extra]
    sems = scratch[2 * count - 1 + n_extra :]
    loads = []
    for index in range(n_extra):
        load = pltpu.make_async_copy(extra_hbm[index], extra[index], extra_sems.at[index])
        load.start()
        loads.append(load)
    axes = []
    for axis, n, _, _ in spec:
        if (axis, n) not in axes:
            axes.append((axis, n))
    _greet(axes)
    source = x_ref
    for k, (axis, n, gather, mid) in enumerate(spec):
        copies = _start_round(
            axis, n, gather, source, landed[k], sems[2 * k], sems[2 * k + 1], sems[-1].at[k]
        )
        for copy in copies:
            copy.wait()
        if k == 0:
            for load in loads:
                load.wait()
        if mid is not None:
            staged[k][...] = mid(landed[k], *extra)
            source = staged[k]


def chain(x, rounds, cid, extra=()):
    spec, landed_shapes, staged_shapes = [], [], []
    block = (x.shape, x.dtype)
    for index, (axis, gather, mid, made) in enumerate(rounds):
        n = lax.axis_size(axis)
        shape, dtype = block
        landed = ((n,) + shape if gather else shape, dtype)
        spec.append((axis, n, gather, mid))
        if index < len(rounds) - 1:
            landed_shapes.append(landed)
            staged_shapes.append(made)
            block = made
        else:
            out = landed
    sizes = [n for _, n, _, _ in spec]
    semaphores = []
    for n in sizes:
        semaphores += [pltpu.SemaphoreType.DMA((n,)), pltpu.SemaphoreType.DMA((n,))]
    return pl.pallas_call(
        functools.partial(_chain_kernel, spec, len(extra)),
        out_shape=jax.ShapeDtypeStruct(*out),
        in_specs=[pl.BlockSpec(memory_space=pltpu.VMEM)]
        + [pl.BlockSpec(memory_space=pl.ANY)] * len(extra),
        out_specs=pl.BlockSpec(memory_space=pltpu.VMEM),
        scratch_shapes=[pltpu.VMEM(*item) for item in landed_shapes]
        + [pltpu.VMEM(*item) for item in staged_shapes]
        + [pltpu.VMEM(item.shape, item.dtype) for item in extra]
        + [pltpu.SemaphoreType.DMA((max(len(extra), 1),))]
        + semaphores
        + [pltpu.SemaphoreType.DMA((len(spec),))],
        compiler_params=pltpu.CompilerParams(
            collective_id=cid, has_side_effects=True
        ),
    )(x, *extra)


def merged_2(array, axis, combine):
    everything = jax.tree.map(lambda part: lax.all_gather(part, axis), array)
    first = jax.tree.map(lambda part: part[0], everything)

    def hop(k, so_far):
        return combine(so_far, jax.tree.map(lambda part: part[k], everything))

    return lax.fori_loop(1, lax.axis_size(axis), hop, first)


def rms_norm(matrix, gain_vec):
    widened = matrix.astype(jnp.float32)
    factor = lax.rsqrt(jnp.mean(widened * widened, axis=-1, keepdims=True) + EPSILON)
    return (widened * factor * gain_vec.astype(jnp.float32)).astype(jnp.bfloat16)


def rotate(vectors, positions):
    half_dim = vectors.shape[-1] // 2
    frequency = ROTARY_BASE ** (-2.0 * jnp.arange(half_dim, dtype=jnp.float32) / vectors.shape[-1])
    angles = positions.astype(jnp.float32)[..., None, None] * frequency
    cosine = jnp.cos(angles)
    sine_part = jnp.sin(angles)
    front_half = vectors[..., :half_dim]
    back_half = vectors[..., half_dim:]
    return jnp.concatenate(
        [front_half * cosine - back_half * sine_part, back_half * cosine + front_half * sine_part],
        axis=-1,
    )


def softmax_join(earlier, later):
    first_max, first_sum, first_out = earlier
    second_max, second_sum, second_out = later
    overall = jnp.maximum(first_max, second_max)
    first_factor = jnp.exp(first_max - overall)
    second_factor = jnp.exp(second_max - overall)
    return (
        overall,
        first_sum * first_factor + second_sum * second_factor,
        first_out * first_factor[..., None] + second_out * second_factor[..., None],
    )


def body(
    given_token_index,
    hidden,
    token_embedding_table,
    attention_norm_gain,
    query_key_value_weight,
    rotated_key_cache,
    cached_value_pages,
    lengths,
    request_page_slots,
    attention_output_weight,
    feedforward_norm_gain,
    gate_weight,
    up_weight,
    adapter_down_map,
    adapter_gate_map,
    adapter_up_map,
    down_weight,
):
    seq_devices = lax.axis_size("seq")
    req_devices = lax.axis_size("req")
    seq_index = lax.axis_index("seq")
    req_index = lax.axis_index("req")
    group_rows = hidden.shape[0]
    requests = lengths.shape[0]
    steps_each = group_rows // requests
    vocab_rows = token_embedding_table.shape[0]
    first_id = (seq_index * req_devices + req_index) * vocab_rows
    local_ids = given_token_index - first_id
    present = (local_ids >= 0) & (local_ids < vocab_rows)
    looked = jnp.take(token_embedding_table, jnp.clip(local_ids, 0, vocab_rows - 1), axis=0).astype(
        jnp.float32
    )
    looked = jnp.where(present[:, None], looked, 0.0).astype(jnp.bfloat16)
    row_share = group_rows // seq_devices
    lanes = 128
    by_group = looked.reshape(req_devices, seq_devices, row_share * looked.shape[1] // lanes, lanes)
    row_parts = two_rounds(
        by_group,
        ("req", False),
        ("seq", False),
        lambda landed: _block_sum(landed).astype(jnp.bfloat16),
        by_group.shape[1:],
        jnp.bfloat16,
        10,
    )
    embedded_rows = (
        jnp.sum(row_parts.astype(jnp.float32), axis=0)
        .astype(jnp.bfloat16)
        .reshape(row_share, looked.shape[1])
    )
    own_hidden = lax.dynamic_slice_in_dim(hidden, seq_index * row_share, row_share, 0)
    own_rows = jnp.concatenate([own_hidden, embedded_rows], axis=1)
    normed_rows = rms_norm(own_rows, attention_norm_gain)
    model_width = own_rows.shape[1]
    width_share = model_width // req_devices

    def to_owners(landed, weight):
        rows = landed[...].reshape(group_rows, model_width)
        return jnp.stack(
            [rows[:, part * width_share : (part + 1) * width_share] for part in range(req_devices)]
        )

    qkv_cols = query_key_value_weight.shape[1]

    def project(landed, weight):
        flat = landed[...].reshape(req_devices * group_rows, width_share)
        product = jnp.dot(flat, weight[...], preferred_element_type=jnp.float32)
        return product.reshape(req_devices, group_rows, qkv_cols)

    qkv_all = chain(
        normed_rows.reshape(-1, lanes),
        [
            ("seq", True, to_owners, ((req_devices, group_rows, width_share), jnp.bfloat16)),
            ("req", False, project, ((req_devices, group_rows, qkv_cols), jnp.float32)),
            (
                "req",
                False,
                lambda landed, weight: _block_sum(landed).astype(jnp.bfloat16),
                ((group_rows, qkv_cols), jnp.bfloat16),
            ),
            ("seq", True, None, None),
        ],
        4,
        extra=(query_key_value_weight,),
    )
    projected = jnp.transpose(qkv_all, (1, 0, 2)).reshape(group_rows, seq_devices * qkv_all.shape[2])
    head_cols = HEADS * HD
    queries = projected[:, :head_cols].reshape(requests, steps_each, HEADS, HD)
    new_keys = projected[:, head_cols : 2 * head_cols].reshape(requests, steps_each, HEADS, HD)
    new_values = projected[:, 2 * head_cols :].reshape(requests, steps_each, HEADS, HD)
    positions = lengths[:, None] + jnp.arange(steps_each, dtype=jnp.int32)[None, :]
    queries = rotate(queries.astype(jnp.float32), positions).astype(jnp.bfloat16)
    new_keys = rotate(new_keys.astype(jnp.float32), positions).astype(jnp.bfloat16)
    slots = rotated_key_cache.shape[0]
    page_len = rotated_key_cache.shape[2]
    cache_k = rotated_key_cache.reshape(slots * page_len, head_cols)
    cache_v = cached_value_pages.reshape(slots * page_len, head_cols)
    slot_ids = seq_index * slots + jnp.arange(slots, dtype=jnp.int32)
    page_ids = jnp.arange(request_page_slots.shape[1], dtype=jnp.int32)
    is_live = page_ids[None, :] < ((lengths + page_len - 1) // page_len)[:, None]
    matches = (request_page_slots[:, :, None] == slot_ids[None, None, :]) & is_live[:, :, None]
    is_owned = jnp.any(matches, axis=1)
    page_of = jnp.sum(jnp.where(matches, page_ids[None, :, None], 0), axis=1)
    token_pos = (
        page_of[:, :, None] * page_len + jnp.arange(page_len, dtype=jnp.int32)[None, None, :]
    )
    is_valid = (is_owned[:, :, None] & (token_pos < lengths[:, None, None])).reshape(
        requests, slots * page_len
    )
    score_scale = 1.0 / math.sqrt(HD)
    head_mask = (jnp.arange(head_cols, dtype=jnp.int32)[None, :] // HD) == jnp.arange(
        HEADS, dtype=jnp.int32
    )[:, None]
    query_rows = queries.reshape(group_rows, head_cols)
    spread_queries = jnp.where(head_mask[None], query_rows[:, None, :], jnp.zeros((), jnp.bfloat16))
    scores = (
        jnp.dot(
            spread_queries.reshape(group_rows * HEADS, head_cols),
            cache_k.T,
            preferred_element_type=jnp.float32,
        )
        * score_scale
    ).reshape(requests, steps_each, HEADS, slots * page_len)
    mask_b = is_valid[:, None, None, :]
    local_max = jnp.max(jnp.where(mask_b, scores, NEGATIVE), axis=-1)
    weights = jnp.where(mask_b, jnp.exp(scores - local_max[..., None]), 0.0)
    local_sum = jnp.sum(weights, axis=-1)
    spread_out = jnp.dot(
        weights.astype(jnp.bfloat16).reshape(group_rows * HEADS, slots * page_len),
        cache_v,
        preferred_element_type=jnp.float32,
    ).reshape(group_rows, HEADS, head_cols)
    local_out = jnp.sum(jnp.where(head_mask[None], spread_out, 0.0), axis=1).reshape(
        requests, steps_each, HEADS, HD
    )
    fresh_scores = (
        jnp.einsum("rthd,rshd->rths", queries, new_keys, preferred_element_type=jnp.float32)
        * score_scale
    )
    causal = jnp.arange(steps_each)[:, None] >= jnp.arange(steps_each)[None, :]
    fresh_mask = causal[None, :, None, :]
    fresh_max = jnp.max(jnp.where(fresh_mask, fresh_scores, NEGATIVE), axis=-1)
    fresh_w = jnp.where(fresh_mask, jnp.exp(fresh_scores - fresh_max[..., None]), 0.0)
    fresh_sum = jnp.sum(fresh_w, axis=-1)
    fresh_out = jnp.einsum(
        "rths,rshd->rthd",
        fresh_w.astype(jnp.bfloat16),
        new_values,
        preferred_element_type=jnp.float32,
    )
    own_heads = HEADS // seq_devices
    first_head = seq_index * own_heads

    def own_slice(member):
        return lax.dynamic_slice_in_dim(member, first_head, own_heads, 2)

    pad_cols = 256 - HD - 2
    packed = jnp.concatenate(
        [
            local_out,
            local_max[..., None],
            local_sum[..., None],
            jnp.zeros(local_out.shape[:-1] + (pad_cols,), jnp.float32),
        ],
        axis=-1,
    )
    packed = packed.reshape(requests * steps_each, seq_devices, own_heads, 256)
    packed = jnp.transpose(packed, (1, 0, 2, 3)).reshape(seq_devices, group_rows * own_heads, 256)
    model_width = attention_output_weight.shape[1]
    head_rows = group_rows * own_heads
    tile_rows = row_share * model_width // lanes

    def merge_and_project(landed, fresh_max_ref, fresh_sum_ref, fresh_out_ref, weight, own, gain):
        part_o = landed[:, :, :HD]
        part_m = landed[:, :, HD : HD + 1]
        part_l = landed[:, :, HD + 1 : HD + 2]
        f_max = fresh_max_ref[...]
        overall = jnp.maximum(jnp.max(part_m, axis=0), f_max)
        part_factor = jnp.exp(part_m - overall[None])
        fresh_factor = jnp.exp(f_max - overall)
        denominator = jnp.sum(part_l * part_factor, axis=0) + fresh_sum_ref[...] * fresh_factor
        numerator = jnp.sum(part_o * part_factor, axis=0) + fresh_out_ref[...] * fresh_factor
        attention = (numerator / denominator).astype(jnp.bfloat16).reshape(
            group_rows, own_heads * HD
        )
        product = jnp.dot(attention, weight[...], preferred_element_type=jnp.float32)
        return product.reshape(seq_devices, tile_rows, lanes)

    def add_residual(landed, fresh_max_ref, fresh_sum_ref, fresh_out_ref, weight, own, gain):
        after = (own[...].astype(jnp.float32) + _block_sum(landed)).astype(jnp.bfloat16)
        widened = after.astype(jnp.float32)
        factor = lax.rsqrt(jnp.sum(widened * widened) / model_width + EPSILON)
        normed_two = (widened * factor * gain[...].astype(jnp.float32)).astype(jnp.bfloat16)
        return jnp.stack([after, normed_two])

    both_rows = chain(
        packed,
        [
            ("seq", False, merge_and_project, ((seq_devices, tile_rows, lanes), jnp.float32)),
            ("seq", False, add_residual, ((2, tile_rows, lanes), jnp.bfloat16)),
            ("seq", True, None, None),
        ],
        1,
        extra=(
            own_slice(fresh_max).reshape(head_rows, 1),
            own_slice(fresh_sum).reshape(head_rows, 1),
            own_slice(fresh_out).reshape(head_rows, HD),
            attention_output_weight,
            own_rows.reshape(tile_rows, lanes),
            feedforward_norm_gain.reshape(tile_rows, lanes),
        ),
    )
    both = both_rows.reshape(group_rows, 2, req_devices, width_share)
    both = jnp.transpose(both, (2, 1, 0, 3))
    down_sum, both_parts = fused_mlp(
        both, gate_weight, up_weight, adapter_down_map, adapter_gate_map, adapter_up_map, down_weight, 7
    )
    residual_cols = both_parts[:, 0].reshape(req_devices * group_rows, width_share)
    out_rows = residual_cols.shape[0] // seq_devices
    residual_rows = lax.dynamic_slice_in_dim(residual_cols, seq_index * out_rows, out_rows, 0)
    return (residual_rows.astype(jnp.float32) + down_sum).astype(jnp.bfloat16)


def solution(mesh):
    placed = (
        P(),
        P("req", None),
        P(("seq", "req"), None),
        P(),
        P("req", "seq"),
        P("seq", "req", None, None),
        P("seq", "req", None, None),
        P("req"),
        P("req", None),
        P("seq", None),
        P(),
        P("req", "seq"),
        P("req", "seq"),
        P("req", None),
        P(None, "seq"),
        P(None, "seq"),
        P("seq", "req"),
    )
    return jax.shard_map(
        body, mesh=mesh, in_specs=placed, out_specs=P("seq", "req"), check_vma=False
    )
```

```python
import functools
import math

import jax
import jax.numpy as jnp
from jax import lax
from jax.experimental import pallas as pl
from jax.experimental.pallas import tpu as pltpu
from jax.sharding import PartitionSpec as P

HEADS = 16
HD = 224


NEGATIVE = -1e30
EPSILON = 1e-05
ROTARY_BASE = 10000.0


MESH_ID = pl.DeviceIdType.MESH


def _exchange_kernel(axis, n, gather, x_ref, y_ref, send_sem, recv_sem, local_sem):
    me = lax.axis_index(axis)
    barrier = pltpu.get_barrier_semaphore()
    for k in range(1, n):
        peer = lax.rem(me + k, n)
        pl.semaphore_signal(barrier, 1, device_id={axis: peer}, device_id_type=MESH_ID)
    pl.semaphore_wait(barrier, n - 1)
    copies = []
    for k in range(1, n):
        peer = lax.rem(me + k, n)
        source = x_ref if gather else x_ref.at[peer]
        copy = pltpu.make_async_remote_copy(
            src_ref=source,
            dst_ref=y_ref.at[me],
            send_sem=send_sem.at[k],
            recv_sem=recv_sem.at[k],
            device_id={axis: peer},
            device_id_type=MESH_ID,
        )
        copy.start()
        copies.append(copy)
    local = pltpu.make_async_copy(x_ref if gather else x_ref.at[me], y_ref.at[me], local_sem)
    local.start()
    local.wait()
    for copy in copies:
        copy.wait()


def exchange(x, axis, cid, gather=False):
    n = lax.axis_size(axis)
    out_shape = (n,) + x.shape if gather else x.shape
    return pl.pallas_call(
        functools.partial(_exchange_kernel, axis, n, gather),
        out_shape=jax.ShapeDtypeStruct(out_shape, x.dtype),
        in_specs=[pl.BlockSpec(memory_space=pltpu.VMEM)],
        out_specs=pl.BlockSpec(memory_space=pltpu.VMEM),
        scratch_shapes=[
            pltpu.SemaphoreType.DMA((n,)),
            pltpu.SemaphoreType.DMA((n,)),
            pltpu.SemaphoreType.DMA(()),
        ],
        compiler_params=pltpu.CompilerParams(collective_id=cid, has_side_effects=True),
    )(x)


def _greet(axes_sizes):
    barrier = pltpu.get_barrier_semaphore()
    total = 0
    for axis, n in axes_sizes:
        me = lax.axis_index(axis)
        for k in range(1, n):
            peer = lax.rem(me + k, n)
            pl.semaphore_signal(barrier, 1, device_id={axis: peer}, device_id_type=MESH_ID)
        total += n - 1
    pl.semaphore_wait(barrier, total)


def _start_round(axis, n, gather, source, target, send_sem, recv_sem, local_sem):
    me = lax.axis_index(axis)
    copies = []
    for k in range(1, n):
        peer = lax.rem(me + k, n)
        copy = pltpu.make_async_remote_copy(
            src_ref=source if gather else source.at[peer],
            dst_ref=target.at[me],
            send_sem=send_sem.at[k],
            recv_sem=recv_sem.at[k],
            device_id={axis: peer},
            device_id_type=MESH_ID,
        )
        copy.start()
        copies.append(copy)
    local = pltpu.make_async_copy(source if gather else source.at[me], target.at[me], local_sem)
    local.start()
    copies.append(local)
    return copies


def _two_round_kernel(first, second, mid, n_extra, x_ref, *refs):
    extra = refs[:n_extra]
    y_ref, landed, staged, send_a, recv_a, send_b, recv_b, local_sems = refs[n_extra:]
    axis_a, n_a, gather_a = first
    axis_b, n_b, gather_b = second
    greeted = [(axis_a, n_a)] if axis_a == axis_b else [(axis_a, n_a), (axis_b, n_b)]
    _greet(greeted)
    for copy in _start_round(axis_a, n_a, gather_a, x_ref, landed, send_a, recv_a, local_sems.at[0]):
        copy.wait()
    staged[...] = mid(landed, *extra)
    for copy in _start_round(axis_b, n_b, gather_b, staged, y_ref, send_b, recv_b, local_sems.at[1]):
        copy.wait()


def two_rounds(x, first, second, mid, staged_shape, staged_dtype, cid, extra=()):
    axis_a, gather_a = first
    axis_b, gather_b = second
    n_a, n_b = lax.axis_size(axis_a), lax.axis_size(axis_b)
    landed_shape = (n_a,) + x.shape if gather_a else x.shape
    out_shape = (n_b,) + staged_shape if gather_b else staged_shape
    return pl.pallas_call(
        functools.partial(
            _two_round_kernel, (axis_a, n_a, gather_a), (axis_b, n_b, gather_b), mid, len(extra)
        ),
        out_shape=jax.ShapeDtypeStruct(out_shape, staged_dtype),
        in_specs=[pl.BlockSpec(memory_space=pltpu.VMEM)] * (1 + len(extra)),
        out_specs=pl.BlockSpec(memory_space=pltpu.VMEM),
        scratch_shapes=[
            pltpu.VMEM(landed_shape, x.dtype),
            pltpu.VMEM(staged_shape, staged_dtype),
            pltpu.SemaphoreType.DMA((n_a,)),
            pltpu.SemaphoreType.DMA((n_a,)),
            pltpu.SemaphoreType.DMA((n_b,)),
            pltpu.SemaphoreType.DMA((n_b,)),
            pltpu.SemaphoreType.DMA((2,)),
        ],
        compiler_params=pltpu.CompilerParams(collective_id=cid, has_side_effects=True),
    )(x, *extra)


def _block_sum(landed):
    total = landed[0].astype(jnp.float32)
    for k in range(1, landed.shape[0]):
        total = total + landed[k].astype(jnp.float32)
    return total


def _mlp_kernel(
    x_ref, gate_hbm, up_hbm, down_map_hbm, gate_map_hbm, up_map_hbm, down_hbm,
    out_ref, spread_ref, landed1, staged1, staged2, landed2, staged3, landed3,
    send0, recv0, send1, recv1, send2, recv2, send3, recv3, local_sems,
    gate_ref, up_ref, down_map_ref, gate_map_ref, up_map_ref, down_ref, weight_sems,
):
    n_req = spread_ref.shape[0]
    n_seq = landed3.shape[0]
    rows = n_req * spread_ref.shape[2]
    units = gate_ref.shape[1]
    loads = []
    pairs = (
        (gate_hbm, gate_ref), (up_hbm, up_ref), (down_map_hbm, down_map_ref),
        (gate_map_hbm, gate_map_ref), (up_map_hbm, up_map_ref), (down_hbm, down_ref),
    )
    for index, (source, target) in enumerate(pairs):
        load = pltpu.make_async_copy(source, target, weight_sems.at[index])
        load.start()
        loads.append(load)
    _greet([("req", n_req), ("seq", n_seq)])
    for copy in _start_round("req", n_req, False, x_ref, spread_ref, send0, recv0, local_sems.at[0]):
        copy.wait()
    for load in loads[:3]:
        load.wait()
    normed_all = spread_ref[:, 1].reshape(rows, spread_ref.shape[3])
    staged1[:, :, :units] = jnp.dot(
        normed_all, gate_ref[...], preferred_element_type=jnp.float32
    ).reshape(staged1.shape[0], staged1.shape[1], units)
    staged1[:, :, units : 2 * units] = jnp.dot(
        normed_all, up_ref[...], preferred_element_type=jnp.float32
    ).reshape(staged1.shape[0], staged1.shape[1], units)
    staged1[:, :, 2 * units :] = jnp.dot(
        normed_all, down_map_ref[...], preferred_element_type=jnp.float32
    ).reshape(staged1.shape[0], staged1.shape[1], staged1.shape[2] - 2 * units)
    for copy in _start_round("req", n_req, False, staged1, landed1, send1, recv1, local_sems.at[1]):
        copy.wait()
    for load in loads[3:5]:
        load.wait()
    total = _block_sum(landed1)
    low = total[:, 2 * units :].astype(jnp.bfloat16)
    gate_pre = total[:, :units] + jnp.dot(low, gate_map_ref[...], preferred_element_type=jnp.float32)
    up_part = total[:, units : 2 * units] + jnp.dot(
        low, up_map_ref[...], preferred_element_type=jnp.float32
    )
    staged2[...] = (gate_pre / (1.0 + jnp.exp(-gate_pre)) * up_part).astype(jnp.bfloat16)
    for copy in _start_round("req", n_req, True, staged2, landed2, send2, recv2, local_sems.at[2]):
        copy.wait()
    loads[5].wait()
    inner = landed2[...].reshape(rows, units)
    staged3[...] = jnp.dot(inner, down_ref[...], preferred_element_type=jnp.float32).reshape(
        staged3.shape
    )
    for copy in _start_round("seq", n_seq, False, staged3, landed3, send3, recv3, local_sems.at[3]):
        copy.wait()
    out_rows = landed3.shape[1]
    group_rows = spread_ref.shape[2]
    first_row = lax.axis_index("seq") * out_rows
    group_rows_all = spread_ref[first_row // group_rows, 0].astype(jnp.float32)
    chunk = (first_row % group_rows) // out_rows
    residual = group_rows_all[:out_rows]
    for index in range(1, group_rows // out_rows):
        piece = group_rows_all[index * out_rows : (index + 1) * out_rows]
        residual = jnp.where(chunk == index, piece, residual)
    out_ref[...] = (residual + _block_sum(landed3)).astype(out_ref.dtype)


def fused_mlp(both, gate_weight, up_weight, down_map, gate_map, up_map, down_weight, cid):
    n_req, n_seq = lax.axis_size("req"), lax.axis_size("seq")
    group_rows = both.shape[2]
    rows = n_req * group_rows
    units = gate_weight.shape[1]
    wide = 2 * units + down_map.shape[1]
    out_rows = rows // n_seq
    vmem = pltpu.VMEM
    return pl.pallas_call(
        _mlp_kernel,
        out_shape=(
            jax.ShapeDtypeStruct((out_rows, down_weight.shape[1]), jnp.bfloat16),
            jax.ShapeDtypeStruct(both.shape, both.dtype),
        ),
        in_specs=[pl.BlockSpec(memory_space=vmem)] + [pl.BlockSpec(memory_space=pl.ANY)] * 6,
        out_specs=(pl.BlockSpec(memory_space=vmem), pl.BlockSpec(memory_space=vmem)),
        scratch_shapes=[
            vmem((n_req, group_rows, wide), jnp.float32),
            vmem((n_req, group_rows, wide), jnp.float32),
            vmem((group_rows, units), jnp.bfloat16),
            vmem((n_req, group_rows, units), jnp.bfloat16),
            vmem((n_seq, out_rows, down_weight.shape[1]), jnp.float32),
            vmem((n_seq, out_rows, down_weight.shape[1]), jnp.float32),
            pltpu.SemaphoreType.DMA((n_req,)),
            pltpu.SemaphoreType.DMA((n_req,)),
            pltpu.SemaphoreType.DMA((n_req,)),
            pltpu.SemaphoreType.DMA((n_req,)),
            pltpu.SemaphoreType.DMA((n_req,)),
            pltpu.SemaphoreType.DMA((n_req,)),
            pltpu.SemaphoreType.DMA((n_seq,)),
            pltpu.SemaphoreType.DMA((n_seq,)),
            pltpu.SemaphoreType.DMA((4,)),
        ]
        + [
            vmem(weight.shape, weight.dtype)
            for weight in (gate_weight, up_weight, down_map, gate_map, up_map, down_weight)
        ]
        + [pltpu.SemaphoreType.DMA((6,))],
        compiler_params=pltpu.CompilerParams(
            collective_id=cid, has_side_effects=True
        ),
    )(both, gate_weight, up_weight, down_map, gate_map, up_map, down_weight)


def _chain_kernel(spec, n_extra, x_ref, *refs):
    extra_hbm = refs[:n_extra]
    y_ref = refs[n_extra]
    scratch = refs[n_extra + 1 :]
    count = len(spec)
    landed = list(scratch[: count - 1]) + [y_ref]
    staged = scratch[count - 1 : 2 * count - 2]
    extra = scratch[2 * count - 2 : 2 * count - 2 + n_extra]
    extra_sems = scratch[2 * count - 2 + n_extra]
    sems = scratch[2 * count - 1 + n_extra :]
    loads = []
    for index in range(n_extra):
        load = pltpu.make_async_copy(extra_hbm[index], extra[index], extra_sems.at[index])
        load.start()
        loads.append(load)
    axes = []
    for axis, n, _, _ in spec:
        if (axis, n) not in axes:
            axes.append((axis, n))
    _greet(axes)
    source = x_ref
    for k, (axis, n, gather, mid) in enumerate(spec):
        copies = _start_round(
            axis, n, gather, source, landed[k], sems[2 * k], sems[2 * k + 1], sems[-1].at[k]
        )
        for copy in copies:
            copy.wait()
        if k == 0:
            for load in loads:
                load.wait()
        if mid is not None:
            staged[k][...] = mid(landed[k], *extra)
            source = staged[k]


def chain(x, rounds, cid, extra=()):
    spec, landed_shapes, staged_shapes = [], [], []
    block = (x.shape, x.dtype)
    for index, (axis, gather, mid, made) in enumerate(rounds):
        n = lax.axis_size(axis)
        shape, dtype = block
        landed = ((n,) + shape if gather else shape, dtype)
        spec.append((axis, n, gather, mid))
        if index < len(rounds) - 1:
            landed_shapes.append(landed)
            staged_shapes.append(made)
            block = made
        else:
            out = landed
    sizes = [n for _, n, _, _ in spec]
    semaphores = []
    for n in sizes:
        semaphores += [pltpu.SemaphoreType.DMA((n,)), pltpu.SemaphoreType.DMA((n,))]
    return pl.pallas_call(
        functools.partial(_chain_kernel, spec, len(extra)),
        out_shape=jax.ShapeDtypeStruct(*out),
        in_specs=[pl.BlockSpec(memory_space=pltpu.VMEM)]
        + [pl.BlockSpec(memory_space=pl.ANY)] * len(extra),
        out_specs=pl.BlockSpec(memory_space=pltpu.VMEM),
        scratch_shapes=[pltpu.VMEM(*item) for item in landed_shapes]
        + [pltpu.VMEM(*item) for item in staged_shapes]
        + [pltpu.VMEM(item.shape, item.dtype) for item in extra]
        + [pltpu.SemaphoreType.DMA((max(len(extra), 1),))]
        + semaphores
        + [pltpu.SemaphoreType.DMA((len(spec),))],
        compiler_params=pltpu.CompilerParams(
            collective_id=cid, has_side_effects=True
        ),
    )(x, *extra)


def merged_2(array, axis, combine):
    everything = jax.tree.map(lambda part: lax.all_gather(part, axis), array)
    first = jax.tree.map(lambda part: part[0], everything)

    def hop(k, so_far):
        return combine(so_far, jax.tree.map(lambda part: part[k], everything))

    return lax.fori_loop(1, lax.axis_size(axis), hop, first)


def rms_norm(matrix, gain_vec):
    widened = matrix.astype(jnp.float32)
    factor = lax.rsqrt(jnp.mean(widened * widened, axis=-1, keepdims=True) + EPSILON)
    return (widened * factor * gain_vec.astype(jnp.float32)).astype(jnp.bfloat16)


def rotate(vectors, positions):
    half_dim = vectors.shape[-1] // 2
    frequency = ROTARY_BASE ** (-2.0 * jnp.arange(half_dim, dtype=jnp.float32) / vectors.shape[-1])
    angles = positions.astype(jnp.float32)[..., None, None] * frequency
    cosine = jnp.cos(angles)
    sine_part = jnp.sin(angles)
    front_half = vectors[..., :half_dim]
    back_half = vectors[..., half_dim:]
    return jnp.concatenate(
        [front_half * cosine - back_half * sine_part, back_half * cosine + front_half * sine_part],
        axis=-1,
    )


def softmax_join(earlier, later):
    first_max, first_sum, first_out = earlier
    second_max, second_sum, second_out = later
    overall = jnp.maximum(first_max, second_max)
    first_factor = jnp.exp(first_max - overall)
    second_factor = jnp.exp(second_max - overall)
    return (
        overall,
        first_sum * first_factor + second_sum * second_factor,
        first_out * first_factor[..., None] + second_out * second_factor[..., None],
    )


def body(
    given_token_index,
    hidden,
    token_embedding_table,
    attention_norm_gain,
    query_key_value_weight,
    rotated_key_cache,
    cached_value_pages,
    lengths,
    request_page_slots,
    attention_output_weight,
    feedforward_norm_gain,
    gate_weight,
    up_weight,
    adapter_down_map,
    adapter_gate_map,
    adapter_up_map,
    down_weight,
):
    seq_devices = lax.axis_size("seq")
    req_devices = lax.axis_size("req")
    seq_index = lax.axis_index("seq")
    req_index = lax.axis_index("req")
    group_rows = hidden.shape[0]
    requests = lengths.shape[0]
    steps_each = group_rows // requests
    vocab_rows = token_embedding_table.shape[0]
    first_id = (seq_index * req_devices + req_index) * vocab_rows
    local_ids = given_token_index - first_id
    present = (local_ids >= 0) & (local_ids < vocab_rows)
    looked = jnp.take(token_embedding_table, jnp.clip(local_ids, 0, vocab_rows - 1), axis=0).astype(
        jnp.float32
    )
    looked = jnp.where(present[:, None], looked, 0.0).astype(jnp.bfloat16)
    row_share = group_rows // seq_devices
    lanes = 128
    by_group = looked.reshape(req_devices, seq_devices, row_share * looked.shape[1] // lanes, lanes)
    row_parts = two_rounds(
        by_group,
        ("req", False),
        ("seq", False),
        lambda landed: _block_sum(landed).astype(jnp.bfloat16),
        by_group.shape[1:],
        jnp.bfloat16,
        10,
    )
    embedded_rows = (
        jnp.sum(row_parts.astype(jnp.float32), axis=0)
        .astype(jnp.bfloat16)
        .reshape(row_share, looked.shape[1])
    )
    own_hidden = lax.dynamic_slice_in_dim(hidden, seq_index * row_share, row_share, 0)
    own_rows = jnp.concatenate([own_hidden, embedded_rows], axis=1)
    normed_rows = rms_norm(own_rows, attention_norm_gain)
    model_width = own_rows.shape[1]
    width_share = model_width // req_devices

    def to_owners(landed, weight):
        rows = landed[...].reshape(group_rows, model_width)
        return jnp.stack(
            [rows[:, part * width_share : (part + 1) * width_share] for part in range(req_devices)]
        )

    qkv_cols = query_key_value_weight.shape[1]

    def project(landed, weight):
        flat = landed[...].reshape(req_devices * group_rows, width_share)
        product = jnp.dot(flat, weight[...], preferred_element_type=jnp.float32)
        return product.reshape(req_devices, group_rows, qkv_cols)

    qkv_all = chain(
        normed_rows.reshape(-1, lanes),
        [
            ("seq", True, to_owners, ((req_devices, group_rows, width_share), jnp.bfloat16)),
            ("req", False, project, ((req_devices, group_rows, qkv_cols), jnp.float32)),
            (
                "req",
                False,
                lambda landed, weight: _block_sum(landed).astype(jnp.bfloat16),
                ((group_rows, qkv_cols), jnp.bfloat16),
            ),
            ("seq", True, None, None),
        ],
        4,
        extra=(query_key_value_weight,),
    )
    projected = jnp.transpose(qkv_all, (1, 0, 2)).reshape(group_rows, seq_devices * qkv_all.shape[2])
    head_cols = HEADS * HD
    queries = projected[:, :head_cols].reshape(requests, steps_each, HEADS, HD)
    new_keys = projected[:, head_cols : 2 * head_cols].reshape(requests, steps_each, HEADS, HD)
    new_values = projected[:, 2 * head_cols :].reshape(requests, steps_each, HEADS, HD)
    positions = lengths[:, None] + jnp.arange(steps_each, dtype=jnp.int32)[None, :]
    queries = rotate(queries.astype(jnp.float32), positions).astype(jnp.bfloat16)
    new_keys = rotate(new_keys.astype(jnp.float32), positions).astype(jnp.bfloat16)
    slots = rotated_key_cache.shape[0]
    page_len = rotated_key_cache.shape[2]
    cache_k = rotated_key_cache.reshape(slots * page_len, head_cols)
    cache_v = cached_value_pages.reshape(slots * page_len, head_cols)
    slot_ids = seq_index * slots + jnp.arange(slots, dtype=jnp.int32)
    page_ids = jnp.arange(request_page_slots.shape[1], dtype=jnp.int32)
    is_live = page_ids[None, :] < ((lengths + page_len - 1) // page_len)[:, None]
    matches = (request_page_slots[:, :, None] == slot_ids[None, None, :]) & is_live[:, :, None]
    is_owned = jnp.any(matches, axis=1)
    page_of = jnp.sum(jnp.where(matches, page_ids[None, :, None], 0), axis=1)
    token_pos = (
        page_of[:, :, None] * page_len + jnp.arange(page_len, dtype=jnp.int32)[None, None, :]
    )
    is_valid = (is_owned[:, :, None] & (token_pos < lengths[:, None, None])).reshape(
        requests, slots * page_len
    )
    score_scale = 1.0 / math.sqrt(HD)
    head_mask = (jnp.arange(head_cols, dtype=jnp.int32)[None, :] // HD) == jnp.arange(
        HEADS, dtype=jnp.int32
    )[:, None]
    query_rows = queries.reshape(group_rows, head_cols)
    spread_queries = jnp.where(head_mask[None], query_rows[:, None, :], jnp.zeros((), jnp.bfloat16))
    scores = (
        jnp.dot(
            spread_queries.reshape(group_rows * HEADS, head_cols),
            cache_k.T,
            preferred_element_type=jnp.float32,
        )
        * score_scale
    ).reshape(requests, steps_each, HEADS, slots * page_len)
    mask_b = is_valid[:, None, None, :]
    local_max = jnp.max(jnp.where(mask_b, scores, NEGATIVE), axis=-1)
    weights = jnp.where(mask_b, jnp.exp(scores - local_max[..., None]), 0.0)
    local_sum = jnp.sum(weights, axis=-1)
    spread_out = jnp.dot(
        weights.astype(jnp.bfloat16).reshape(group_rows * HEADS, slots * page_len),
        cache_v,
        preferred_element_type=jnp.float32,
    ).reshape(group_rows, HEADS, head_cols)
    local_out = jnp.sum(jnp.where(head_mask[None], spread_out, 0.0), axis=1).reshape(
        requests, steps_each, HEADS, HD
    )
    fresh_scores = (
        jnp.einsum("rthd,rshd->rths", queries, new_keys, preferred_element_type=jnp.float32)
        * score_scale
    )
    causal = jnp.arange(steps_each)[:, None] >= jnp.arange(steps_each)[None, :]
    fresh_mask = causal[None, :, None, :]
    fresh_max = jnp.max(jnp.where(fresh_mask, fresh_scores, NEGATIVE), axis=-1)
    fresh_w = jnp.where(fresh_mask, jnp.exp(fresh_scores - fresh_max[..., None]), 0.0)
    fresh_sum = jnp.sum(fresh_w, axis=-1)
    fresh_out = jnp.einsum(
        "rths,rshd->rthd",
        fresh_w.astype(jnp.bfloat16),
        new_values,
        preferred_element_type=jnp.float32,
    )
    own_heads = HEADS // seq_devices
    first_head = seq_index * own_heads

    def own_slice(member):
        return lax.dynamic_slice_in_dim(member, first_head, own_heads, 2)

    pad_cols = 256 - HD - 2
    packed = jnp.concatenate(
        [
            local_out,
            local_max[..., None],
            local_sum[..., None],
            jnp.zeros(local_out.shape[:-1] + (pad_cols,), jnp.float32),
        ],
        axis=-1,
    )
    packed = packed.reshape(requests * steps_each, seq_devices, own_heads, 256)
    packed = jnp.transpose(packed, (1, 0, 2, 3)).reshape(seq_devices, group_rows * own_heads, 256)
    model_width = attention_output_weight.shape[1]
    head_rows = group_rows * own_heads
    tile_rows = row_share * model_width // lanes

    def merge_and_project(landed, fresh_max_ref, fresh_sum_ref, fresh_out_ref, weight, own, gain):
        part_o = landed[:, :, :HD]
        part_m = landed[:, :, HD : HD + 1]
        part_l = landed[:, :, HD + 1 : HD + 2]
        f_max = fresh_max_ref[...]
        overall = jnp.maximum(jnp.max(part_m, axis=0), f_max)
        part_factor = jnp.exp(part_m - overall[None])
        fresh_factor = jnp.exp(f_max - overall)
        denominator = jnp.sum(part_l * part_factor, axis=0) + fresh_sum_ref[...] * fresh_factor
        numerator = jnp.sum(part_o * part_factor, axis=0) + fresh_out_ref[...] * fresh_factor
        attention = (numerator / denominator).astype(jnp.bfloat16).reshape(
            group_rows, own_heads * HD
        )
        product = jnp.dot(attention, weight[...], preferred_element_type=jnp.float32)
        return product.reshape(seq_devices, tile_rows, lanes)

    def add_residual(landed, fresh_max_ref, fresh_sum_ref, fresh_out_ref, weight, own, gain):
        after = (own[...].astype(jnp.float32) + _block_sum(landed)).astype(jnp.bfloat16)
        widened = after.astype(jnp.float32)
        factor = lax.rsqrt(jnp.sum(widened * widened) / model_width + EPSILON)
        normed_two = (widened * factor * gain[...].astype(jnp.float32)).astype(jnp.bfloat16)
        return jnp.stack([after, normed_two])

    both_rows = chain(
        packed,
        [
            ("seq", False, merge_and_project, ((seq_devices, tile_rows, lanes), jnp.float32)),
            ("seq", False, add_residual, ((2, tile_rows, lanes), jnp.bfloat16)),
            ("seq", True, None, None),
        ],
        1,
        extra=(
            own_slice(fresh_max).reshape(head_rows, 1),
            own_slice(fresh_sum).reshape(head_rows, 1),
            own_slice(fresh_out).reshape(head_rows, HD),
            attention_output_weight,
            own_rows.reshape(tile_rows, lanes),
            feedforward_norm_gain.reshape(tile_rows, lanes),
        ),
    )
    both = both_rows.reshape(group_rows, 2, req_devices, width_share)
    both = jnp.transpose(both, (2, 1, 0, 3))
    block_out, _ = fused_mlp(
        both, gate_weight, up_weight, adapter_down_map, adapter_gate_map, adapter_up_map, down_weight, 7
    )
    return block_out


def solution(mesh):
    placed = (
        P(),
        P("req", None),
        P(("seq", "req"), None),
        P(),
        P("req", "seq"),
        P("seq", "req", None, None),
        P("seq", "req", None, None),
        P("req"),
        P("req", None),
        P("seq", None),
        P(),
        P("req", "seq"),
        P("req", "seq"),
        P("req", None),
        P(None, "seq"),
        P(None, "seq"),
        P("seq", "req"),
    )
    return jax.shard_map(
        body, mesh=mesh, in_specs=placed, out_specs=P("seq", "req"), check_vma=False
    )
```

```python
import functools
import math

import jax
import jax.numpy as jnp
from jax import lax
from jax.experimental import pallas as pl
from jax.experimental.pallas import tpu as pltpu
from jax.sharding import PartitionSpec as P

HEADS = 16
HD = 224


NEGATIVE = -1e30
EPSILON = 1e-05
ROTARY_BASE = 10000.0


MESH_ID = pl.DeviceIdType.MESH


def _exchange_kernel(axis, n, gather, x_ref, y_ref, send_sem, recv_sem, local_sem):
    me = lax.axis_index(axis)
    barrier = pltpu.get_barrier_semaphore()
    for k in range(1, n):
        peer = lax.rem(me + k, n)
        pl.semaphore_signal(barrier, 1, device_id={axis: peer}, device_id_type=MESH_ID)
    pl.semaphore_wait(barrier, n - 1)
    copies = []
    for k in range(1, n):
        peer = lax.rem(me + k, n)
        source = x_ref if gather else x_ref.at[peer]
        copy = pltpu.make_async_remote_copy(
            src_ref=source,
            dst_ref=y_ref.at[me],
            send_sem=send_sem.at[k],
            recv_sem=recv_sem.at[k],
            device_id={axis: peer},
            device_id_type=MESH_ID,
        )
        copy.start()
        copies.append(copy)
    local = pltpu.make_async_copy(x_ref if gather else x_ref.at[me], y_ref.at[me], local_sem)
    local.start()
    local.wait()
    for copy in copies:
        copy.wait()


def exchange(x, axis, cid, gather=False):
    n = lax.axis_size(axis)
    out_shape = (n,) + x.shape if gather else x.shape
    return pl.pallas_call(
        functools.partial(_exchange_kernel, axis, n, gather),
        out_shape=jax.ShapeDtypeStruct(out_shape, x.dtype),
        in_specs=[pl.BlockSpec(memory_space=pltpu.VMEM)],
        out_specs=pl.BlockSpec(memory_space=pltpu.VMEM),
        scratch_shapes=[
            pltpu.SemaphoreType.DMA((n,)),
            pltpu.SemaphoreType.DMA((n,)),
            pltpu.SemaphoreType.DMA(()),
        ],
        compiler_params=pltpu.CompilerParams(collective_id=cid, has_side_effects=True),
    )(x)


def _greet(axes_sizes):
    barrier = pltpu.get_barrier_semaphore()
    total = 0
    for axis, n in axes_sizes:
        me = lax.axis_index(axis)
        for k in range(1, n):
            peer = lax.rem(me + k, n)
            pl.semaphore_signal(barrier, 1, device_id={axis: peer}, device_id_type=MESH_ID)
        total += n - 1
    pl.semaphore_wait(barrier, total)


def _start_round(axis, n, gather, source, target, send_sem, recv_sem, local_sem):
    me = lax.axis_index(axis)
    copies = []
    for k in range(1, n):
        peer = lax.rem(me + k, n)
        copy = pltpu.make_async_remote_copy(
            src_ref=source if gather else source.at[peer],
            dst_ref=target.at[me],
            send_sem=send_sem.at[k],
            recv_sem=recv_sem.at[k],
            device_id={axis: peer},
            device_id_type=MESH_ID,
        )
        copy.start()
        copies.append(copy)
    local = pltpu.make_async_copy(source if gather else source.at[me], target.at[me], local_sem)
    local.start()
    copies.append(local)
    return copies


def _two_round_kernel(first, second, mid, n_extra, x_ref, *refs):
    extra = refs[:n_extra]
    y_ref, landed, staged, send_a, recv_a, send_b, recv_b, local_sems = refs[n_extra:]
    axis_a, n_a, gather_a = first
    axis_b, n_b, gather_b = second
    greeted = [(axis_a, n_a)] if axis_a == axis_b else [(axis_a, n_a), (axis_b, n_b)]
    _greet(greeted)
    for copy in _start_round(axis_a, n_a, gather_a, x_ref, landed, send_a, recv_a, local_sems.at[0]):
        copy.wait()
    staged[...] = mid(landed, *extra)
    for copy in _start_round(axis_b, n_b, gather_b, staged, y_ref, send_b, recv_b, local_sems.at[1]):
        copy.wait()


def two_rounds(x, first, second, mid, staged_shape, staged_dtype, cid, extra=()):
    axis_a, gather_a = first
    axis_b, gather_b = second
    n_a, n_b = lax.axis_size(axis_a), lax.axis_size(axis_b)
    landed_shape = (n_a,) + x.shape if gather_a else x.shape
    out_shape = (n_b,) + staged_shape if gather_b else staged_shape
    return pl.pallas_call(
        functools.partial(
            _two_round_kernel, (axis_a, n_a, gather_a), (axis_b, n_b, gather_b), mid, len(extra)
        ),
        out_shape=jax.ShapeDtypeStruct(out_shape, staged_dtype),
        in_specs=[pl.BlockSpec(memory_space=pltpu.VMEM)] * (1 + len(extra)),
        out_specs=pl.BlockSpec(memory_space=pltpu.VMEM),
        scratch_shapes=[
            pltpu.VMEM(landed_shape, x.dtype),
            pltpu.VMEM(staged_shape, staged_dtype),
            pltpu.SemaphoreType.DMA((n_a,)),
            pltpu.SemaphoreType.DMA((n_a,)),
            pltpu.SemaphoreType.DMA((n_b,)),
            pltpu.SemaphoreType.DMA((n_b,)),
            pltpu.SemaphoreType.DMA((2,)),
        ],
        compiler_params=pltpu.CompilerParams(collective_id=cid, has_side_effects=True),
    )(x, *extra)


def _block_sum(landed):
    total = landed[0].astype(jnp.float32)
    for k in range(1, landed.shape[0]):
        total = total + landed[k].astype(jnp.float32)
    return total


def _mlp_kernel(
    x_ref, gate_hbm, up_hbm, down_map_hbm, gate_map_hbm, up_map_hbm, down_hbm,
    out_ref, spread_ref, landed1, staged1, staged2, landed2, staged3, landed3,
    send0, recv0, send1, recv1, send2, recv2, send3, recv3, local_sems,
    gate_ref, up_ref, down_map_ref, gate_map_ref, up_map_ref, down_ref, weight_sems, staged0,
):
    n_req = spread_ref.shape[0]
    n_seq = landed3.shape[0]
    rows = n_req * spread_ref.shape[2]
    units = gate_ref.shape[1]
    loads = []
    pairs = (
        (gate_hbm, gate_ref), (up_hbm, up_ref), (down_map_hbm, down_map_ref),
        (gate_map_hbm, gate_map_ref), (up_map_hbm, up_map_ref), (down_hbm, down_ref),
    )
    for index, (source, target) in enumerate(pairs):
        load = pltpu.make_async_copy(source, target, weight_sems.at[index])
        load.start()
        loads.append(load)
    _greet([("req", n_req), ("seq", n_seq)])
    share = staged0.shape[3]
    for kind in range(staged0.shape[1]):
        full_rows = x_ref[:, kind].reshape(staged0.shape[2], n_req * share)
        for part in range(n_req):
            staged0[part, kind] = full_rows[:, part * share : (part + 1) * share]
    for copy in _start_round("req", n_req, False, staged0, spread_ref, send0, recv0, local_sems.at[0]):
        copy.wait()
    for load in loads[:3]:
        load.wait()
    normed_all = spread_ref[:, 1].reshape(rows, spread_ref.shape[3])
    staged1[:, :, :units] = jnp.dot(
        normed_all, gate_ref[...], preferred_element_type=jnp.float32
    ).reshape(staged1.shape[0], staged1.shape[1], units)
    staged1[:, :, units : 2 * units] = jnp.dot(
        normed_all, up_ref[...], preferred_element_type=jnp.float32
    ).reshape(staged1.shape[0], staged1.shape[1], units)
    staged1[:, :, 2 * units :] = jnp.dot(
        normed_all, down_map_ref[...], preferred_element_type=jnp.float32
    ).reshape(staged1.shape[0], staged1.shape[1], staged1.shape[2] - 2 * units)
    for copy in _start_round("req", n_req, False, staged1, landed1, send1, recv1, local_sems.at[1]):
        copy.wait()
    for load in loads[3:5]:
        load.wait()
    total = _block_sum(landed1)
    low = total[:, 2 * units :].astype(jnp.bfloat16)
    gate_pre = total[:, :units] + jnp.dot(low, gate_map_ref[...], preferred_element_type=jnp.float32)
    up_part = total[:, units : 2 * units] + jnp.dot(
        low, up_map_ref[...], preferred_element_type=jnp.float32
    )
    staged2[...] = (gate_pre / (1.0 + jnp.exp(-gate_pre)) * up_part).astype(jnp.bfloat16)
    for copy in _start_round("req", n_req, True, staged2, landed2, send2, recv2, local_sems.at[2]):
        copy.wait()
    loads[5].wait()
    inner = landed2[...].reshape(rows, units)
    staged3[...] = jnp.dot(inner, down_ref[...], preferred_element_type=jnp.float32).reshape(
        staged3.shape
    )
    for copy in _start_round("seq", n_seq, False, staged3, landed3, send3, recv3, local_sems.at[3]):
        copy.wait()
    out_rows = landed3.shape[1]
    group_rows = spread_ref.shape[2]
    first_row = lax.axis_index("seq") * out_rows
    group_rows_all = spread_ref[first_row // group_rows, 0].astype(jnp.float32)
    chunk = (first_row % group_rows) // out_rows
    residual = group_rows_all[:out_rows]
    for index in range(1, group_rows // out_rows):
        piece = group_rows_all[index * out_rows : (index + 1) * out_rows]
        residual = jnp.where(chunk == index, piece, residual)
    out_ref[...] = (residual + _block_sum(landed3)).astype(out_ref.dtype)


def fused_mlp(both, gate_weight, up_weight, down_map, gate_map, up_map, down_weight, cid):
    n_req, n_seq = lax.axis_size("req"), lax.axis_size("seq")
    group_rows = both.shape[0]
    spread_shape = (n_req, both.shape[1], group_rows, both.shape[2] * both.shape[3] // n_req)
    rows = n_req * group_rows
    units = gate_weight.shape[1]
    wide = 2 * units + down_map.shape[1]
    out_rows = rows // n_seq
    vmem = pltpu.VMEM
    return pl.pallas_call(
        _mlp_kernel,
        out_shape=(
            jax.ShapeDtypeStruct((out_rows, down_weight.shape[1]), jnp.bfloat16),
            jax.ShapeDtypeStruct(spread_shape, both.dtype),
        ),
        in_specs=[pl.BlockSpec(memory_space=vmem)] + [pl.BlockSpec(memory_space=pl.ANY)] * 6,
        out_specs=(pl.BlockSpec(memory_space=vmem), pl.BlockSpec(memory_space=vmem)),
        scratch_shapes=[
            vmem((n_req, group_rows, wide), jnp.float32),
            vmem((n_req, group_rows, wide), jnp.float32),
            vmem((group_rows, units), jnp.bfloat16),
            vmem((n_req, group_rows, units), jnp.bfloat16),
            vmem((n_seq, out_rows, down_weight.shape[1]), jnp.float32),
            vmem((n_seq, out_rows, down_weight.shape[1]), jnp.float32),
            pltpu.SemaphoreType.DMA((n_req,)),
            pltpu.SemaphoreType.DMA((n_req,)),
            pltpu.SemaphoreType.DMA((n_req,)),
            pltpu.SemaphoreType.DMA((n_req,)),
            pltpu.SemaphoreType.DMA((n_req,)),
            pltpu.SemaphoreType.DMA((n_req,)),
            pltpu.SemaphoreType.DMA((n_seq,)),
            pltpu.SemaphoreType.DMA((n_seq,)),
            pltpu.SemaphoreType.DMA((4,)),
        ]
        + [
            vmem(weight.shape, weight.dtype)
            for weight in (gate_weight, up_weight, down_map, gate_map, up_map, down_weight)
        ]
        + [pltpu.SemaphoreType.DMA((6,)), vmem(spread_shape, both.dtype)],
        compiler_params=pltpu.CompilerParams(
            collective_id=cid, has_side_effects=True
        ),
    )(both, gate_weight, up_weight, down_map, gate_map, up_map, down_weight)


def _chain_kernel(spec, n_extra, x_ref, *refs):
    extra_hbm = refs[:n_extra]
    y_ref = refs[n_extra]
    scratch = refs[n_extra + 1 :]
    count = len(spec)
    landed = list(scratch[: count - 1]) + [y_ref]
    staged = scratch[count - 1 : 2 * count - 2]
    extra = scratch[2 * count - 2 : 2 * count - 2 + n_extra]
    extra_sems = scratch[2 * count - 2 + n_extra]
    sems = scratch[2 * count - 1 + n_extra :]
    loads = []
    for index in range(n_extra):
        load = pltpu.make_async_copy(extra_hbm[index], extra[index], extra_sems.at[index])
        load.start()
        loads.append(load)
    axes = []
    for axis, n, _, _ in spec:
        if (axis, n) not in axes:
            axes.append((axis, n))
    _greet(axes)
    source = x_ref
    for k, (axis, n, gather, mid) in enumerate(spec):
        copies = _start_round(
            axis, n, gather, source, landed[k], sems[2 * k], sems[2 * k + 1], sems[-1].at[k]
        )
        for copy in copies:
            copy.wait()
        if k == 0:
            for load in loads:
                load.wait()
        if mid is not None:
            staged[k][...] = mid(landed[k], *extra)
            source = staged[k]


def chain(x, rounds, cid, extra=()):
    spec, landed_shapes, staged_shapes = [], [], []
    block = (x.shape, x.dtype)
    for index, (axis, gather, mid, made) in enumerate(rounds):
        n = lax.axis_size(axis)
        shape, dtype = block
        landed = ((n,) + shape if gather else shape, dtype)
        spec.append((axis, n, gather, mid))
        if index < len(rounds) - 1:
            landed_shapes.append(landed)
            staged_shapes.append(made)
            block = made
        else:
            out = landed
    sizes = [n for _, n, _, _ in spec]
    semaphores = []
    for n in sizes:
        semaphores += [pltpu.SemaphoreType.DMA((n,)), pltpu.SemaphoreType.DMA((n,))]
    return pl.pallas_call(
        functools.partial(_chain_kernel, spec, len(extra)),
        out_shape=jax.ShapeDtypeStruct(*out),
        in_specs=[pl.BlockSpec(memory_space=pltpu.VMEM)]
        + [pl.BlockSpec(memory_space=pl.ANY)] * len(extra),
        out_specs=pl.BlockSpec(memory_space=pltpu.VMEM),
        scratch_shapes=[pltpu.VMEM(*item) for item in landed_shapes]
        + [pltpu.VMEM(*item) for item in staged_shapes]
        + [pltpu.VMEM(item.shape, item.dtype) for item in extra]
        + [pltpu.SemaphoreType.DMA((max(len(extra), 1),))]
        + semaphores
        + [pltpu.SemaphoreType.DMA((len(spec),))],
        compiler_params=pltpu.CompilerParams(
            collective_id=cid, has_side_effects=True
        ),
    )(x, *extra)


def merged_2(array, axis, combine):
    everything = jax.tree.map(lambda part: lax.all_gather(part, axis), array)
    first = jax.tree.map(lambda part: part[0], everything)

    def hop(k, so_far):
        return combine(so_far, jax.tree.map(lambda part: part[k], everything))

    return lax.fori_loop(1, lax.axis_size(axis), hop, first)


def rms_norm(matrix, gain_vec):
    widened = matrix.astype(jnp.float32)
    factor = lax.rsqrt(jnp.mean(widened * widened, axis=-1, keepdims=True) + EPSILON)
    return (widened * factor * gain_vec.astype(jnp.float32)).astype(jnp.bfloat16)


def rotate(vectors, positions):
    half_dim = vectors.shape[-1] // 2
    frequency = ROTARY_BASE ** (-2.0 * jnp.arange(half_dim, dtype=jnp.float32) / vectors.shape[-1])
    angles = positions.astype(jnp.float32)[..., None, None] * frequency
    cosine = jnp.cos(angles)
    sine_part = jnp.sin(angles)
    front_half = vectors[..., :half_dim]
    back_half = vectors[..., half_dim:]
    return jnp.concatenate(
        [front_half * cosine - back_half * sine_part, back_half * cosine + front_half * sine_part],
        axis=-1,
    )


def softmax_join(earlier, later):
    first_max, first_sum, first_out = earlier
    second_max, second_sum, second_out = later
    overall = jnp.maximum(first_max, second_max)
    first_factor = jnp.exp(first_max - overall)
    second_factor = jnp.exp(second_max - overall)
    return (
        overall,
        first_sum * first_factor + second_sum * second_factor,
        first_out * first_factor[..., None] + second_out * second_factor[..., None],
    )


def body(
    given_token_index,
    hidden,
    token_embedding_table,
    attention_norm_gain,
    query_key_value_weight,
    rotated_key_cache,
    cached_value_pages,
    lengths,
    request_page_slots,
    attention_output_weight,
    feedforward_norm_gain,
    gate_weight,
    up_weight,
    adapter_down_map,
    adapter_gate_map,
    adapter_up_map,
    down_weight,
):
    seq_devices = lax.axis_size("seq")
    req_devices = lax.axis_size("req")
    seq_index = lax.axis_index("seq")
    req_index = lax.axis_index("req")
    group_rows = hidden.shape[0]
    requests = lengths.shape[0]
    steps_each = group_rows // requests
    vocab_rows = token_embedding_table.shape[0]
    first_id = (seq_index * req_devices + req_index) * vocab_rows
    local_ids = given_token_index - first_id
    present = (local_ids >= 0) & (local_ids < vocab_rows)
    looked = jnp.take(token_embedding_table, jnp.clip(local_ids, 0, vocab_rows - 1), axis=0).astype(
        jnp.float32
    )
    looked = jnp.where(present[:, None], looked, 0.0).astype(jnp.bfloat16)
    row_share = group_rows // seq_devices
    lanes = 128
    by_group = looked.reshape(req_devices, seq_devices, row_share * looked.shape[1] // lanes, lanes)
    row_parts = two_rounds(
        by_group,
        ("req", False),
        ("seq", False),
        lambda landed: _block_sum(landed).astype(jnp.bfloat16),
        by_group.shape[1:],
        jnp.bfloat16,
        10,
    )
    embedded_rows = (
        jnp.sum(row_parts.astype(jnp.float32), axis=0)
        .astype(jnp.bfloat16)
        .reshape(row_share, looked.shape[1])
    )
    own_hidden = lax.dynamic_slice_in_dim(hidden, seq_index * row_share, row_share, 0)
    own_rows = jnp.concatenate([own_hidden, embedded_rows], axis=1)
    normed_rows = rms_norm(own_rows, attention_norm_gain)
    model_width = own_rows.shape[1]
    width_share = model_width // req_devices

    def to_owners(landed, weight):
        rows = landed[...].reshape(group_rows, model_width)
        return jnp.stack(
            [rows[:, part * width_share : (part + 1) * width_share] for part in range(req_devices)]
        )

    qkv_cols = query_key_value_weight.shape[1]

    def project(landed, weight):
        flat = landed[...].reshape(req_devices * group_rows, width_share)
        product = jnp.dot(flat, weight[...], preferred_element_type=jnp.float32)
        return product.reshape(req_devices, group_rows, qkv_cols)

    qkv_all = chain(
        normed_rows.reshape(-1, lanes),
        [
            ("seq", True, to_owners, ((req_devices, group_rows, width_share), jnp.bfloat16)),
            ("req", False, project, ((req_devices, group_rows, qkv_cols), jnp.float32)),
            (
                "req",
                False,
                lambda landed, weight: _block_sum(landed).astype(jnp.bfloat16),
                ((group_rows, qkv_cols), jnp.bfloat16),
            ),
            ("seq", True, None, None),
        ],
        4,
        extra=(query_key_value_weight,),
    )
    projected = jnp.transpose(qkv_all, (1, 0, 2)).reshape(group_rows, seq_devices * qkv_all.shape[2])
    head_cols = HEADS * HD
    queries = projected[:, :head_cols].reshape(requests, steps_each, HEADS, HD)
    new_keys = projected[:, head_cols : 2 * head_cols].reshape(requests, steps_each, HEADS, HD)
    new_values = projected[:, 2 * head_cols :].reshape(requests, steps_each, HEADS, HD)
    positions = lengths[:, None] + jnp.arange(steps_each, dtype=jnp.int32)[None, :]
    queries = rotate(queries.astype(jnp.float32), positions).astype(jnp.bfloat16)
    new_keys = rotate(new_keys.astype(jnp.float32), positions).astype(jnp.bfloat16)
    slots = rotated_key_cache.shape[0]
    page_len = rotated_key_cache.shape[2]
    cache_k = rotated_key_cache.reshape(slots * page_len, head_cols)
    cache_v = cached_value_pages.reshape(slots * page_len, head_cols)
    slot_ids = seq_index * slots + jnp.arange(slots, dtype=jnp.int32)
    page_ids = jnp.arange(request_page_slots.shape[1], dtype=jnp.int32)
    is_live = page_ids[None, :] < ((lengths + page_len - 1) // page_len)[:, None]
    matches = (request_page_slots[:, :, None] == slot_ids[None, None, :]) & is_live[:, :, None]
    is_owned = jnp.any(matches, axis=1)
    page_of = jnp.sum(jnp.where(matches, page_ids[None, :, None], 0), axis=1)
    token_pos = (
        page_of[:, :, None] * page_len + jnp.arange(page_len, dtype=jnp.int32)[None, None, :]
    )
    is_valid = (is_owned[:, :, None] & (token_pos < lengths[:, None, None])).reshape(
        requests, slots * page_len
    )
    score_scale = 1.0 / math.sqrt(HD)
    head_mask = (jnp.arange(head_cols, dtype=jnp.int32)[None, :] // HD) == jnp.arange(
        HEADS, dtype=jnp.int32
    )[:, None]
    query_rows = queries.reshape(group_rows, head_cols)
    spread_queries = jnp.where(head_mask[None], query_rows[:, None, :], jnp.zeros((), jnp.bfloat16))
    scores = (
        jnp.dot(
            spread_queries.reshape(group_rows * HEADS, head_cols),
            cache_k.T,
            preferred_element_type=jnp.float32,
        )
        * score_scale
    ).reshape(requests, steps_each, HEADS, slots * page_len)
    mask_b = is_valid[:, None, None, :]
    local_max = jnp.max(jnp.where(mask_b, scores, NEGATIVE), axis=-1)
    weights = jnp.where(mask_b, jnp.exp(scores - local_max[..., None]), 0.0)
    local_sum = jnp.sum(weights, axis=-1)
    spread_out = jnp.dot(
        weights.astype(jnp.bfloat16).reshape(group_rows * HEADS, slots * page_len),
        cache_v,
        preferred_element_type=jnp.float32,
    ).reshape(group_rows, HEADS, head_cols)
    local_out = jnp.sum(jnp.where(head_mask[None], spread_out, 0.0), axis=1).reshape(
        requests, steps_each, HEADS, HD
    )
    fresh_scores = (
        jnp.einsum("rthd,rshd->rths", queries, new_keys, preferred_element_type=jnp.float32)
        * score_scale
    )
    causal = jnp.arange(steps_each)[:, None] >= jnp.arange(steps_each)[None, :]
    fresh_mask = causal[None, :, None, :]
    fresh_max = jnp.max(jnp.where(fresh_mask, fresh_scores, NEGATIVE), axis=-1)
    fresh_w = jnp.where(fresh_mask, jnp.exp(fresh_scores - fresh_max[..., None]), 0.0)
    fresh_sum = jnp.sum(fresh_w, axis=-1)
    fresh_out = jnp.einsum(
        "rths,rshd->rthd",
        fresh_w.astype(jnp.bfloat16),
        new_values,
        preferred_element_type=jnp.float32,
    )
    own_heads = HEADS // seq_devices
    first_head = seq_index * own_heads

    def own_slice(member):
        return lax.dynamic_slice_in_dim(member, first_head, own_heads, 2)

    pad_cols = 256 - HD - 2
    packed = jnp.concatenate(
        [
            local_out,
            local_max[..., None],
            local_sum[..., None],
            jnp.zeros(local_out.shape[:-1] + (pad_cols,), jnp.float32),
        ],
        axis=-1,
    )
    packed = packed.reshape(requests * steps_each, seq_devices, own_heads, 256)
    packed = jnp.transpose(packed, (1, 0, 2, 3)).reshape(seq_devices, group_rows * own_heads, 256)
    model_width = attention_output_weight.shape[1]
    head_rows = group_rows * own_heads
    tile_rows = row_share * model_width // lanes

    def merge_and_project(landed, fresh_max_ref, fresh_sum_ref, fresh_out_ref, weight, own, gain):
        part_o = landed[:, :, :HD]
        part_m = landed[:, :, HD : HD + 1]
        part_l = landed[:, :, HD + 1 : HD + 2]
        f_max = fresh_max_ref[...]
        overall = jnp.maximum(jnp.max(part_m, axis=0), f_max)
        part_factor = jnp.exp(part_m - overall[None])
        fresh_factor = jnp.exp(f_max - overall)
        denominator = jnp.sum(part_l * part_factor, axis=0) + fresh_sum_ref[...] * fresh_factor
        numerator = jnp.sum(part_o * part_factor, axis=0) + fresh_out_ref[...] * fresh_factor
        attention = (numerator / denominator).astype(jnp.bfloat16).reshape(
            group_rows, own_heads * HD
        )
        product = jnp.dot(attention, weight[...], preferred_element_type=jnp.float32)
        return product.reshape(seq_devices, tile_rows, lanes)

    def add_residual(landed, fresh_max_ref, fresh_sum_ref, fresh_out_ref, weight, own, gain):
        after = (own[...].astype(jnp.float32) + _block_sum(landed)).astype(jnp.bfloat16)
        widened = after.astype(jnp.float32)
        factor = lax.rsqrt(jnp.sum(widened * widened) / model_width + EPSILON)
        normed_two = (widened * factor * gain[...].astype(jnp.float32)).astype(jnp.bfloat16)
        return jnp.stack([after, normed_two])

    both_rows = chain(
        packed,
        [
            ("seq", False, merge_and_project, ((seq_devices, tile_rows, lanes), jnp.float32)),
            ("seq", False, add_residual, ((2, tile_rows, lanes), jnp.bfloat16)),
            ("seq", True, None, None),
        ],
        1,
        extra=(
            own_slice(fresh_max).reshape(head_rows, 1),
            own_slice(fresh_sum).reshape(head_rows, 1),
            own_slice(fresh_out).reshape(head_rows, HD),
            attention_output_weight,
            own_rows.reshape(tile_rows, lanes),
            feedforward_norm_gain.reshape(tile_rows, lanes),
        ),
    )
    block_out, _ = fused_mlp(
        both_rows, gate_weight, up_weight, adapter_down_map, adapter_gate_map, adapter_up_map, down_weight, 7
    )
    return block_out


def solution(mesh):
    placed = (
        P(),
        P("req", None),
        P(("seq", "req"), None),
        P(),
        P("req", "seq"),
        P("seq", "req", None, None),
        P("seq", "req", None, None),
        P("req"),
        P("req", None),
        P("seq", None),
        P(),
        P("req", "seq"),
        P("req", "seq"),
        P("req", None),
        P(None, "seq"),
        P(None, "seq"),
        P("seq", "req"),
    )
    return jax.shard_map(
        body, mesh=mesh, in_specs=placed, out_specs=P("seq", "req"), check_vma=False
    )
```

```python
import functools
import math

import jax
import jax.numpy as jnp
from jax import lax
from jax.experimental import pallas as pl
from jax.experimental.pallas import tpu as pltpu
from jax.sharding import PartitionSpec as P

HEADS = 16
HD = 224


NEGATIVE = -1e30
EPSILON = 1e-05
ROTARY_BASE = 10000.0


MESH_ID = pl.DeviceIdType.MESH


def _exchange_kernel(axis, n, gather, x_ref, y_ref, send_sem, recv_sem, local_sem):
    me = lax.axis_index(axis)
    barrier = pltpu.get_barrier_semaphore()
    for k in range(1, n):
        peer = lax.rem(me + k, n)
        pl.semaphore_signal(barrier, 1, device_id={axis: peer}, device_id_type=MESH_ID)
    pl.semaphore_wait(barrier, n - 1)
    copies = []
    for k in range(1, n):
        peer = lax.rem(me + k, n)
        source = x_ref if gather else x_ref.at[peer]
        copy = pltpu.make_async_remote_copy(
            src_ref=source,
            dst_ref=y_ref.at[me],
            send_sem=send_sem.at[k],
            recv_sem=recv_sem.at[k],
            device_id={axis: peer},
            device_id_type=MESH_ID,
        )
        copy.start()
        copies.append(copy)
    local = pltpu.make_async_copy(x_ref if gather else x_ref.at[me], y_ref.at[me], local_sem)
    local.start()
    local.wait()
    for copy in copies:
        copy.wait()


def exchange(x, axis, cid, gather=False):
    n = lax.axis_size(axis)
    out_shape = (n,) + x.shape if gather else x.shape
    return pl.pallas_call(
        functools.partial(_exchange_kernel, axis, n, gather),
        out_shape=jax.ShapeDtypeStruct(out_shape, x.dtype),
        in_specs=[pl.BlockSpec(memory_space=pltpu.VMEM)],
        out_specs=pl.BlockSpec(memory_space=pltpu.VMEM),
        scratch_shapes=[
            pltpu.SemaphoreType.DMA((n,)),
            pltpu.SemaphoreType.DMA((n,)),
            pltpu.SemaphoreType.DMA(()),
        ],
        compiler_params=pltpu.CompilerParams(collective_id=cid, has_side_effects=True),
    )(x)


def _greet(axes_sizes):
    barrier = pltpu.get_barrier_semaphore()
    total = 0
    for axis, n in axes_sizes:
        me = lax.axis_index(axis)
        for k in range(1, n):
            peer = lax.rem(me + k, n)
            pl.semaphore_signal(barrier, 1, device_id={axis: peer}, device_id_type=MESH_ID)
        total += n - 1
    pl.semaphore_wait(barrier, total)


def _start_round(axis, n, gather, source, target, send_sem, recv_sem, local_sem):
    me = lax.axis_index(axis)
    copies = []
    for k in range(1, n):
        peer = lax.rem(me + k, n)
        copy = pltpu.make_async_remote_copy(
            src_ref=source if gather else source.at[peer],
            dst_ref=target.at[me],
            send_sem=send_sem.at[k],
            recv_sem=recv_sem.at[k],
            device_id={axis: peer},
            device_id_type=MESH_ID,
        )
        copy.start()
        copies.append(copy)
    local = pltpu.make_async_copy(source if gather else source.at[me], target.at[me], local_sem)
    local.start()
    copies.append(local)
    return copies


def _two_round_kernel(first, second, mid, n_extra, x_ref, *refs):
    extra = refs[:n_extra]
    y_ref, landed, staged, send_a, recv_a, send_b, recv_b, local_sems = refs[n_extra:]
    axis_a, n_a, gather_a = first
    axis_b, n_b, gather_b = second
    greeted = [(axis_a, n_a)] if axis_a == axis_b else [(axis_a, n_a), (axis_b, n_b)]
    _greet(greeted)
    for copy in _start_round(axis_a, n_a, gather_a, x_ref, landed, send_a, recv_a, local_sems.at[0]):
        copy.wait()
    staged[...] = mid(landed, *extra)
    for copy in _start_round(axis_b, n_b, gather_b, staged, y_ref, send_b, recv_b, local_sems.at[1]):
        copy.wait()


def two_rounds(x, first, second, mid, staged_shape, staged_dtype, cid, extra=()):
    axis_a, gather_a = first
    axis_b, gather_b = second
    n_a, n_b = lax.axis_size(axis_a), lax.axis_size(axis_b)
    landed_shape = (n_a,) + x.shape if gather_a else x.shape
    out_shape = (n_b,) + staged_shape if gather_b else staged_shape
    return pl.pallas_call(
        functools.partial(
            _two_round_kernel, (axis_a, n_a, gather_a), (axis_b, n_b, gather_b), mid, len(extra)
        ),
        out_shape=jax.ShapeDtypeStruct(out_shape, staged_dtype),
        in_specs=[pl.BlockSpec(memory_space=pltpu.VMEM)] * (1 + len(extra)),
        out_specs=pl.BlockSpec(memory_space=pltpu.VMEM),
        scratch_shapes=[
            pltpu.VMEM(landed_shape, x.dtype),
            pltpu.VMEM(staged_shape, staged_dtype),
            pltpu.SemaphoreType.DMA((n_a,)),
            pltpu.SemaphoreType.DMA((n_a,)),
            pltpu.SemaphoreType.DMA((n_b,)),
            pltpu.SemaphoreType.DMA((n_b,)),
            pltpu.SemaphoreType.DMA((2,)),
        ],
        compiler_params=pltpu.CompilerParams(collective_id=cid, has_side_effects=True),
    )(x, *extra)


def _block_sum(landed):
    total = landed[0].astype(jnp.float32)
    for k in range(1, landed.shape[0]):
        total = total + landed[k].astype(jnp.float32)
    return total


def _mlp_kernel(
    x_ref, gate_hbm, up_hbm, down_map_hbm, gate_map_hbm, up_map_hbm, down_hbm,
    out_ref, spread_ref, landed1, staged1, staged2, landed2, staged3, landed3,
    send0, recv0, send1, recv1, send2, recv2, send3, recv3, local_sems,
    gate_ref, up_ref, down_map_ref, gate_map_ref, up_map_ref, down_ref, weight_sems, staged0,
):
    n_req = spread_ref.shape[0]
    n_seq = landed3.shape[0]
    rows = n_req * spread_ref.shape[2]
    units = gate_ref.shape[1]
    loads = []
    pairs = (
        (gate_hbm, gate_ref), (up_hbm, up_ref), (down_map_hbm, down_map_ref),
        (gate_map_hbm, gate_map_ref), (up_map_hbm, up_map_ref), (down_hbm, down_ref),
    )
    for index, (source, target) in enumerate(pairs):
        load = pltpu.make_async_copy(source, target, weight_sems.at[index])
        load.start()
        loads.append(load)
    _greet([("req", n_req), ("seq", n_seq)])
    share = staged0.shape[3]
    for kind in range(staged0.shape[1]):
        full_rows = x_ref[:, kind].reshape(staged0.shape[2], n_req * share)
        for part in range(n_req):
            staged0[part, kind] = full_rows[:, part * share : (part + 1) * share]
    for copy in _start_round("req", n_req, False, staged0, spread_ref, send0, recv0, local_sems.at[0]):
        copy.wait()
    for load in loads[:3]:
        load.wait()
    normed_all = spread_ref[:, 1].reshape(rows, spread_ref.shape[3])
    staged1[:, :, :units] = jnp.dot(
        normed_all, gate_ref[...], preferred_element_type=jnp.float32
    ).reshape(staged1.shape[0], staged1.shape[1], units)
    staged1[:, :, units : 2 * units] = jnp.dot(
        normed_all, up_ref[...], preferred_element_type=jnp.float32
    ).reshape(staged1.shape[0], staged1.shape[1], units)
    staged1[:, :, 2 * units :] = jnp.dot(
        normed_all, down_map_ref[...], preferred_element_type=jnp.float32
    ).reshape(staged1.shape[0], staged1.shape[1], staged1.shape[2] - 2 * units)
    for copy in _start_round("req", n_req, False, staged1, landed1, send1, recv1, local_sems.at[1]):
        copy.wait()
    for load in loads[3:5]:
        load.wait()
    total = _block_sum(landed1)
    low = total[:, 2 * units :].astype(jnp.bfloat16)
    gate_pre = total[:, :units] + jnp.dot(low, gate_map_ref[...], preferred_element_type=jnp.float32)
    up_part = total[:, units : 2 * units] + jnp.dot(
        low, up_map_ref[...], preferred_element_type=jnp.float32
    )
    staged2[...] = (gate_pre / (1.0 + jnp.exp(-gate_pre)) * up_part).astype(jnp.bfloat16)
    for copy in _start_round("req", n_req, True, staged2, landed2, send2, recv2, local_sems.at[2]):
        copy.wait()
    loads[5].wait()
    inner = landed2[...].reshape(rows, units)
    staged3[...] = jnp.dot(inner, down_ref[...], preferred_element_type=jnp.float32).reshape(
        staged3.shape
    )
    for copy in _start_round("seq", n_seq, False, staged3, landed3, send3, recv3, local_sems.at[3]):
        copy.wait()
    out_rows = landed3.shape[1]
    group_rows = spread_ref.shape[2]
    first_row = lax.axis_index("seq") * out_rows
    group_rows_all = spread_ref[first_row // group_rows, 0].astype(jnp.float32)
    chunk = (first_row % group_rows) // out_rows
    residual = group_rows_all[:out_rows]
    for index in range(1, group_rows // out_rows):
        piece = group_rows_all[index * out_rows : (index + 1) * out_rows]
        residual = jnp.where(chunk == index, piece, residual)
    out_ref[...] = (residual + _block_sum(landed3)).astype(out_ref.dtype)


def fused_mlp(both, gate_weight, up_weight, down_map, gate_map, up_map, down_weight, cid):
    n_req, n_seq = lax.axis_size("req"), lax.axis_size("seq")
    group_rows = both.shape[0]
    spread_shape = (n_req, both.shape[1], group_rows, both.shape[2] * both.shape[3] // n_req)
    rows = n_req * group_rows
    units = gate_weight.shape[1]
    wide = 2 * units + down_map.shape[1]
    out_rows = rows // n_seq
    vmem = pltpu.VMEM
    return pl.pallas_call(
        _mlp_kernel,
        out_shape=(
            jax.ShapeDtypeStruct((out_rows, down_weight.shape[1]), jnp.bfloat16),
            jax.ShapeDtypeStruct(spread_shape, both.dtype),
        ),
        in_specs=[pl.BlockSpec(memory_space=vmem)] + [pl.BlockSpec(memory_space=pl.ANY)] * 6,
        out_specs=(pl.BlockSpec(memory_space=vmem), pl.BlockSpec(memory_space=vmem)),
        scratch_shapes=[
            vmem((n_req, group_rows, wide), jnp.float32),
            vmem((n_req, group_rows, wide), jnp.float32),
            vmem((group_rows, units), jnp.bfloat16),
            vmem((n_req, group_rows, units), jnp.bfloat16),
            vmem((n_seq, out_rows, down_weight.shape[1]), jnp.float32),
            vmem((n_seq, out_rows, down_weight.shape[1]), jnp.float32),
            pltpu.SemaphoreType.DMA((n_req,)),
            pltpu.SemaphoreType.DMA((n_req,)),
            pltpu.SemaphoreType.DMA((n_req,)),
            pltpu.SemaphoreType.DMA((n_req,)),
            pltpu.SemaphoreType.DMA((n_req,)),
            pltpu.SemaphoreType.DMA((n_req,)),
            pltpu.SemaphoreType.DMA((n_seq,)),
            pltpu.SemaphoreType.DMA((n_seq,)),
            pltpu.SemaphoreType.DMA((4,)),
        ]
        + [
            vmem(weight.shape, weight.dtype)
            for weight in (gate_weight, up_weight, down_map, gate_map, up_map, down_weight)
        ]
        + [pltpu.SemaphoreType.DMA((6,)), vmem(spread_shape, both.dtype)],
        compiler_params=pltpu.CompilerParams(
            collective_id=cid, has_side_effects=True
        ),
    )(both, gate_weight, up_weight, down_map, gate_map, up_map, down_weight)


def _chain_kernel(spec, n_extra, pre, x_ref, *refs):
    extra_hbm = refs[:n_extra]
    y_ref = refs[n_extra]
    scratch = refs[n_extra + 1 :]
    count = len(spec)
    landed = list(scratch[: count - 1]) + [y_ref]
    staged = scratch[count - 1 : 2 * count - 2]
    extra = scratch[2 * count - 2 : 2 * count - 2 + n_extra]
    extra_sems = scratch[2 * count - 2 + n_extra]
    sems = scratch[2 * count - 1 + n_extra : len(scratch) - (pre is not None)]
    loads = []
    for index in range(n_extra):
        load = pltpu.make_async_copy(extra_hbm[index], extra[index], extra_sems.at[index])
        load.start()
        loads.append(load)
    if pre is not None:
        for load in loads:
            load.wait()
        loads = []
        scratch[-1][...] = pre(x_ref, *extra)
        x_ref = scratch[-1]
    axes = []
    for axis, n, _, _ in spec:
        if (axis, n) not in axes:
            axes.append((axis, n))
    _greet(axes)
    source = x_ref
    for k, (axis, n, gather, mid) in enumerate(spec):
        copies = _start_round(
            axis, n, gather, source, landed[k], sems[2 * k], sems[2 * k + 1], sems[-1].at[k]
        )
        for copy in copies:
            copy.wait()
        if k == 0:
            for load in loads:
                load.wait()
        if mid is not None:
            staged[k][...] = mid(landed[k], *extra)
            source = staged[k]


def chain(x, rounds, cid, extra=(), pre=None):
    spec, landed_shapes, staged_shapes = [], [], []
    block = (x.shape, x.dtype)
    for index, (axis, gather, mid, made) in enumerate(rounds):
        n = lax.axis_size(axis)
        shape, dtype = block
        landed = ((n,) + shape if gather else shape, dtype)
        spec.append((axis, n, gather, mid))
        if index < len(rounds) - 1:
            landed_shapes.append(landed)
            staged_shapes.append(made)
            block = made
        else:
            out = landed
    sizes = [n for _, n, _, _ in spec]
    semaphores = []
    for n in sizes:
        semaphores += [pltpu.SemaphoreType.DMA((n,)), pltpu.SemaphoreType.DMA((n,))]
    return pl.pallas_call(
        functools.partial(_chain_kernel, spec, len(extra), pre),
        out_shape=jax.ShapeDtypeStruct(*out),
        in_specs=[pl.BlockSpec(memory_space=pltpu.VMEM)]
        + [pl.BlockSpec(memory_space=pl.ANY)] * len(extra),
        out_specs=pl.BlockSpec(memory_space=pltpu.VMEM),
        scratch_shapes=[pltpu.VMEM(*item) for item in landed_shapes]
        + [pltpu.VMEM(*item) for item in staged_shapes]
        + [pltpu.VMEM(item.shape, item.dtype) for item in extra]
        + [pltpu.SemaphoreType.DMA((max(len(extra), 1),))]
        + semaphores
        + [pltpu.SemaphoreType.DMA((len(spec),))]
        + ([pltpu.VMEM(x.shape, x.dtype)] if pre is not None else []),
        compiler_params=pltpu.CompilerParams(
            collective_id=cid, has_side_effects=True
        ),
    )(x, *extra)


def merged_2(array, axis, combine):
    everything = jax.tree.map(lambda part: lax.all_gather(part, axis), array)
    first = jax.tree.map(lambda part: part[0], everything)

    def hop(k, so_far):
        return combine(so_far, jax.tree.map(lambda part: part[k], everything))

    return lax.fori_loop(1, lax.axis_size(axis), hop, first)


def rms_norm(matrix, gain_vec):
    widened = matrix.astype(jnp.float32)
    factor = lax.rsqrt(jnp.mean(widened * widened, axis=-1, keepdims=True) + EPSILON)
    return (widened * factor * gain_vec.astype(jnp.float32)).astype(jnp.bfloat16)


def rotate(vectors, positions):
    half_dim = vectors.shape[-1] // 2
    frequency = ROTARY_BASE ** (-2.0 * jnp.arange(half_dim, dtype=jnp.float32) / vectors.shape[-1])
    angles = positions.astype(jnp.float32)[..., None, None] * frequency
    cosine = jnp.cos(angles)
    sine_part = jnp.sin(angles)
    front_half = vectors[..., :half_dim]
    back_half = vectors[..., half_dim:]
    return jnp.concatenate(
        [front_half * cosine - back_half * sine_part, back_half * cosine + front_half * sine_part],
        axis=-1,
    )


def softmax_join(earlier, later):
    first_max, first_sum, first_out = earlier
    second_max, second_sum, second_out = later
    overall = jnp.maximum(first_max, second_max)
    first_factor = jnp.exp(first_max - overall)
    second_factor = jnp.exp(second_max - overall)
    return (
        overall,
        first_sum * first_factor + second_sum * second_factor,
        first_out * first_factor[..., None] + second_out * second_factor[..., None],
    )


def body(
    given_token_index,
    hidden,
    token_embedding_table,
    attention_norm_gain,
    query_key_value_weight,
    rotated_key_cache,
    cached_value_pages,
    lengths,
    request_page_slots,
    attention_output_weight,
    feedforward_norm_gain,
    gate_weight,
    up_weight,
    adapter_down_map,
    adapter_gate_map,
    adapter_up_map,
    down_weight,
):
    seq_devices = lax.axis_size("seq")
    req_devices = lax.axis_size("req")
    seq_index = lax.axis_index("seq")
    req_index = lax.axis_index("req")
    group_rows = hidden.shape[0]
    requests = lengths.shape[0]
    steps_each = group_rows // requests
    vocab_rows = token_embedding_table.shape[0]
    first_id = (seq_index * req_devices + req_index) * vocab_rows
    local_ids = given_token_index - first_id
    present = (local_ids >= 0) & (local_ids < vocab_rows)
    looked = jnp.take(token_embedding_table, jnp.clip(local_ids, 0, vocab_rows - 1), axis=0).astype(
        jnp.float32
    )
    looked = jnp.where(present[:, None], looked, 0.0).astype(jnp.bfloat16)
    row_share = group_rows // seq_devices
    lanes = 128
    by_group = looked.reshape(req_devices, seq_devices, row_share * looked.shape[1] // lanes, lanes)
    row_parts = two_rounds(
        by_group,
        ("req", False),
        ("seq", False),
        lambda landed: _block_sum(landed).astype(jnp.bfloat16),
        by_group.shape[1:],
        jnp.bfloat16,
        10,
    )
    embedded_rows = (
        jnp.sum(row_parts.astype(jnp.float32), axis=0)
        .astype(jnp.bfloat16)
        .reshape(row_share, looked.shape[1])
    )
    own_hidden = lax.dynamic_slice_in_dim(hidden, seq_index * row_share, row_share, 0)
    own_rows = jnp.concatenate([own_hidden, embedded_rows], axis=1)
    model_width = own_rows.shape[1]
    width_share = model_width // req_devices

    def normalize(joined_tiles, weight, gain):
        widened = joined_tiles[...].astype(jnp.float32)
        factor = lax.rsqrt(jnp.sum(widened * widened) / model_width + EPSILON)
        return (widened * factor * gain[...].astype(jnp.float32)).astype(jnp.bfloat16)

    def to_owners(landed, weight, gain):
        rows = landed[...].reshape(group_rows, model_width)
        return jnp.stack(
            [rows[:, part * width_share : (part + 1) * width_share] for part in range(req_devices)]
        )

    qkv_cols = query_key_value_weight.shape[1]

    def project(landed, weight, gain):
        flat = landed[...].reshape(req_devices * group_rows, width_share)
        product = jnp.dot(flat, weight[...], preferred_element_type=jnp.float32)
        return product.reshape(req_devices, group_rows, qkv_cols)

    qkv_all = chain(
        own_rows.reshape(-1, lanes),
        [
            ("seq", True, to_owners, ((req_devices, group_rows, width_share), jnp.bfloat16)),
            ("req", False, project, ((req_devices, group_rows, qkv_cols), jnp.float32)),
            (
                "req",
                False,
                lambda landed, weight, gain: _block_sum(landed).astype(jnp.bfloat16),
                ((group_rows, qkv_cols), jnp.bfloat16),
            ),
            ("seq", True, None, None),
        ],
        4,
        extra=(query_key_value_weight, attention_norm_gain.reshape(-1, lanes)),
        pre=normalize,
    )
    projected = jnp.transpose(qkv_all, (1, 0, 2)).reshape(group_rows, seq_devices * qkv_all.shape[2])
    head_cols = HEADS * HD
    queries = projected[:, :head_cols].reshape(requests, steps_each, HEADS, HD)
    new_keys = projected[:, head_cols : 2 * head_cols].reshape(requests, steps_each, HEADS, HD)
    new_values = projected[:, 2 * head_cols :].reshape(requests, steps_each, HEADS, HD)
    positions = lengths[:, None] + jnp.arange(steps_each, dtype=jnp.int32)[None, :]
    queries = rotate(queries.astype(jnp.float32), positions).astype(jnp.bfloat16)
    new_keys = rotate(new_keys.astype(jnp.float32), positions).astype(jnp.bfloat16)
    slots = rotated_key_cache.shape[0]
    page_len = rotated_key_cache.shape[2]
    cache_k = rotated_key_cache.reshape(slots * page_len, head_cols)
    cache_v = cached_value_pages.reshape(slots * page_len, head_cols)
    slot_ids = seq_index * slots + jnp.arange(slots, dtype=jnp.int32)
    page_ids = jnp.arange(request_page_slots.shape[1], dtype=jnp.int32)
    is_live = page_ids[None, :] < ((lengths + page_len - 1) // page_len)[:, None]
    matches = (request_page_slots[:, :, None] == slot_ids[None, None, :]) & is_live[:, :, None]
    is_owned = jnp.any(matches, axis=1)
    page_of = jnp.sum(jnp.where(matches, page_ids[None, :, None], 0), axis=1)
    token_pos = (
        page_of[:, :, None] * page_len + jnp.arange(page_len, dtype=jnp.int32)[None, None, :]
    )
    is_valid = (is_owned[:, :, None] & (token_pos < lengths[:, None, None])).reshape(
        requests, slots * page_len
    )
    score_scale = 1.0 / math.sqrt(HD)
    head_mask = (jnp.arange(head_cols, dtype=jnp.int32)[None, :] // HD) == jnp.arange(
        HEADS, dtype=jnp.int32
    )[:, None]
    query_rows = queries.reshape(group_rows, head_cols)
    spread_queries = jnp.where(head_mask[None], query_rows[:, None, :], jnp.zeros((), jnp.bfloat16))
    scores = (
        jnp.dot(
            spread_queries.reshape(group_rows * HEADS, head_cols),
            cache_k.T,
            preferred_element_type=jnp.float32,
        )
        * score_scale
    ).reshape(requests, steps_each, HEADS, slots * page_len)
    mask_b = is_valid[:, None, None, :]
    local_max = jnp.max(jnp.where(mask_b, scores, NEGATIVE), axis=-1)
    weights = jnp.where(mask_b, jnp.exp(scores - local_max[..., None]), 0.0)
    local_sum = jnp.sum(weights, axis=-1)
    spread_out = jnp.dot(
        weights.astype(jnp.bfloat16).reshape(group_rows * HEADS, slots * page_len),
        cache_v,
        preferred_element_type=jnp.float32,
    ).reshape(group_rows, HEADS, head_cols)
    local_out = jnp.sum(jnp.where(head_mask[None], spread_out, 0.0), axis=1).reshape(
        requests, steps_each, HEADS, HD
    )
    fresh_scores = (
        jnp.einsum("rthd,rshd->rths", queries, new_keys, preferred_element_type=jnp.float32)
        * score_scale
    )
    causal = jnp.arange(steps_each)[:, None] >= jnp.arange(steps_each)[None, :]
    fresh_mask = causal[None, :, None, :]
    fresh_max = jnp.max(jnp.where(fresh_mask, fresh_scores, NEGATIVE), axis=-1)
    fresh_w = jnp.where(fresh_mask, jnp.exp(fresh_scores - fresh_max[..., None]), 0.0)
    fresh_sum = jnp.sum(fresh_w, axis=-1)
    fresh_out = jnp.einsum(
        "rths,rshd->rthd",
        fresh_w.astype(jnp.bfloat16),
        new_values,
        preferred_element_type=jnp.float32,
    )
    own_heads = HEADS // seq_devices
    first_head = seq_index * own_heads

    def own_slice(member):
        return lax.dynamic_slice_in_dim(member, first_head, own_heads, 2)

    pad_cols = 256 - HD - 2
    packed = jnp.concatenate(
        [
            local_out,
            local_max[..., None],
            local_sum[..., None],
            jnp.zeros(local_out.shape[:-1] + (pad_cols,), jnp.float32),
        ],
        axis=-1,
    )
    packed = packed.reshape(requests * steps_each, seq_devices, own_heads, 256)
    packed = jnp.transpose(packed, (1, 0, 2, 3)).reshape(seq_devices, group_rows * own_heads, 256)
    model_width = attention_output_weight.shape[1]
    head_rows = group_rows * own_heads
    tile_rows = row_share * model_width // lanes

    def merge_and_project(landed, fresh_max_ref, fresh_sum_ref, fresh_out_ref, weight, own, gain):
        part_o = landed[:, :, :HD]
        part_m = landed[:, :, HD : HD + 1]
        part_l = landed[:, :, HD + 1 : HD + 2]
        f_max = fresh_max_ref[...]
        overall = jnp.maximum(jnp.max(part_m, axis=0), f_max)
        part_factor = jnp.exp(part_m - overall[None])
        fresh_factor = jnp.exp(f_max - overall)
        denominator = jnp.sum(part_l * part_factor, axis=0) + fresh_sum_ref[...] * fresh_factor
        numerator = jnp.sum(part_o * part_factor, axis=0) + fresh_out_ref[...] * fresh_factor
        attention = (numerator / denominator).astype(jnp.bfloat16).reshape(
            group_rows, own_heads * HD
        )
        product = jnp.dot(attention, weight[...], preferred_element_type=jnp.float32)
        return product.reshape(seq_devices, tile_rows, lanes)

    def add_residual(landed, fresh_max_ref, fresh_sum_ref, fresh_out_ref, weight, own, gain):
        after = (own[...].astype(jnp.float32) + _block_sum(landed)).astype(jnp.bfloat16)
        widened = after.astype(jnp.float32)
        factor = lax.rsqrt(jnp.sum(widened * widened) / model_width + EPSILON)
        normed_two = (widened * factor * gain[...].astype(jnp.float32)).astype(jnp.bfloat16)
        return jnp.stack([after, normed_two])

    both_rows = chain(
        packed,
        [
            ("seq", False, merge_and_project, ((seq_devices, tile_rows, lanes), jnp.float32)),
            ("seq", False, add_residual, ((2, tile_rows, lanes), jnp.bfloat16)),
            ("seq", True, None, None),
        ],
        1,
        extra=(
            own_slice(fresh_max).reshape(head_rows, 1),
            own_slice(fresh_sum).reshape(head_rows, 1),
            own_slice(fresh_out).reshape(head_rows, HD),
            attention_output_weight,
            own_rows.reshape(tile_rows, lanes),
            feedforward_norm_gain.reshape(tile_rows, lanes),
        ),
    )
    block_out, _ = fused_mlp(
        both_rows, gate_weight, up_weight, adapter_down_map, adapter_gate_map, adapter_up_map, down_weight, 7
    )
    return block_out


def solution(mesh):
    placed = (
        P(),
        P("req", None),
        P(("seq", "req"), None),
        P(),
        P("req", "seq"),
        P("seq", "req", None, None),
        P("seq", "req", None, None),
        P("req"),
        P("req", None),
        P("seq", None),
        P(),
        P("req", "seq"),
        P("req", "seq"),
        P("req", None),
        P(None, "seq"),
        P(None, "seq"),
        P("seq", "req"),
    )
    return jax.shard_map(
        body, mesh=mesh, in_specs=placed, out_specs=P("seq", "req"), check_vma=False
    )
```

```python
import functools
import math

import jax
import jax.numpy as jnp
from jax import lax
from jax.experimental import pallas as pl
from jax.experimental.pallas import tpu as pltpu
from jax.sharding import PartitionSpec as P

HEADS = 16
HD = 224


NEGATIVE = -1e30
EPSILON = 1e-05
ROTARY_BASE = 10000.0


MESH_ID = pl.DeviceIdType.MESH


def _exchange_kernel(axis, n, gather, x_ref, y_ref, send_sem, recv_sem, local_sem):
    me = lax.axis_index(axis)
    barrier = pltpu.get_barrier_semaphore()
    for k in range(1, n):
        peer = lax.rem(me + k, n)
        pl.semaphore_signal(barrier, 1, device_id={axis: peer}, device_id_type=MESH_ID)
    pl.semaphore_wait(barrier, n - 1)
    copies = []
    for k in range(1, n):
        peer = lax.rem(me + k, n)
        source = x_ref if gather else x_ref.at[peer]
        copy = pltpu.make_async_remote_copy(
            src_ref=source,
            dst_ref=y_ref.at[me],
            send_sem=send_sem.at[k],
            recv_sem=recv_sem.at[k],
            device_id={axis: peer},
            device_id_type=MESH_ID,
        )
        copy.start()
        copies.append(copy)
    local = pltpu.make_async_copy(x_ref if gather else x_ref.at[me], y_ref.at[me], local_sem)
    local.start()
    local.wait()
    for copy in copies:
        copy.wait()


def exchange(x, axis, cid, gather=False):
    n = lax.axis_size(axis)
    out_shape = (n,) + x.shape if gather else x.shape
    return pl.pallas_call(
        functools.partial(_exchange_kernel, axis, n, gather),
        out_shape=jax.ShapeDtypeStruct(out_shape, x.dtype),
        in_specs=[pl.BlockSpec(memory_space=pltpu.VMEM)],
        out_specs=pl.BlockSpec(memory_space=pltpu.VMEM),
        scratch_shapes=[
            pltpu.SemaphoreType.DMA((n,)),
            pltpu.SemaphoreType.DMA((n,)),
            pltpu.SemaphoreType.DMA(()),
        ],
        compiler_params=pltpu.CompilerParams(collective_id=cid, has_side_effects=True),
    )(x)


def _greet(axes_sizes):
    barrier = pltpu.get_barrier_semaphore()
    total = 0
    for axis, n in axes_sizes:
        me = lax.axis_index(axis)
        for k in range(1, n):
            peer = lax.rem(me + k, n)
            pl.semaphore_signal(barrier, 1, device_id={axis: peer}, device_id_type=MESH_ID)
        total += n - 1
    pl.semaphore_wait(barrier, total)


def _start_round(axis, n, gather, source, target, send_sem, recv_sem, local_sem):
    me = lax.axis_index(axis)
    copies = []
    for k in range(1, n):
        peer = lax.rem(me + k, n)
        copy = pltpu.make_async_remote_copy(
            src_ref=source if gather else source.at[peer],
            dst_ref=target.at[me],
            send_sem=send_sem.at[k],
            recv_sem=recv_sem.at[k],
            device_id={axis: peer},
            device_id_type=MESH_ID,
        )
        copy.start()
        copies.append(copy)
    local = pltpu.make_async_copy(source if gather else source.at[me], target.at[me], local_sem)
    local.start()
    copies.append(local)
    return copies


def _two_round_kernel(first, second, mid, n_extra, x_ref, *refs):
    extra = refs[:n_extra]
    y_ref, landed, staged, send_a, recv_a, send_b, recv_b, local_sems = refs[n_extra:]
    axis_a, n_a, gather_a = first
    axis_b, n_b, gather_b = second
    greeted = [(axis_a, n_a)] if axis_a == axis_b else [(axis_a, n_a), (axis_b, n_b)]
    _greet(greeted)
    for copy in _start_round(axis_a, n_a, gather_a, x_ref, landed, send_a, recv_a, local_sems.at[0]):
        copy.wait()
    staged[...] = mid(landed, *extra)
    for copy in _start_round(axis_b, n_b, gather_b, staged, y_ref, send_b, recv_b, local_sems.at[1]):
        copy.wait()


def two_rounds(x, first, second, mid, staged_shape, staged_dtype, cid, extra=()):
    axis_a, gather_a = first
    axis_b, gather_b = second
    n_a, n_b = lax.axis_size(axis_a), lax.axis_size(axis_b)
    landed_shape = (n_a,) + x.shape if gather_a else x.shape
    out_shape = (n_b,) + staged_shape if gather_b else staged_shape
    return pl.pallas_call(
        functools.partial(
            _two_round_kernel, (axis_a, n_a, gather_a), (axis_b, n_b, gather_b), mid, len(extra)
        ),
        out_shape=jax.ShapeDtypeStruct(out_shape, staged_dtype),
        in_specs=[pl.BlockSpec(memory_space=pltpu.VMEM)] * (1 + len(extra)),
        out_specs=pl.BlockSpec(memory_space=pltpu.VMEM),
        scratch_shapes=[
            pltpu.VMEM(landed_shape, x.dtype),
            pltpu.VMEM(staged_shape, staged_dtype),
            pltpu.SemaphoreType.DMA((n_a,)),
            pltpu.SemaphoreType.DMA((n_a,)),
            pltpu.SemaphoreType.DMA((n_b,)),
            pltpu.SemaphoreType.DMA((n_b,)),
            pltpu.SemaphoreType.DMA((2,)),
        ],
        compiler_params=pltpu.CompilerParams(collective_id=cid, has_side_effects=True),
    )(x, *extra)


def _block_sum(landed):
    total = landed[0].astype(jnp.float32)
    for k in range(1, landed.shape[0]):
        total = total + landed[k].astype(jnp.float32)
    return total


def _mlp_kernel(
    x_ref, gate_hbm, up_hbm, down_map_hbm, gate_map_hbm, up_map_hbm, down_hbm,
    out_ref, spread_ref, landed1, staged1, staged2, landed2, staged3, landed3,
    send0, recv0, send1, recv1, send2, recv2, send3, recv3, local_sems,
    gate_ref, up_ref, down_map_ref, gate_map_ref, up_map_ref, down_ref, weight_sems, staged0,
):
    n_req = spread_ref.shape[0]
    n_seq = landed3.shape[0]
    rows = n_req * spread_ref.shape[2]
    units = gate_ref.shape[1]
    loads = []
    pairs = (
        (gate_hbm, gate_ref), (up_hbm, up_ref), (down_map_hbm, down_map_ref),
        (gate_map_hbm, gate_map_ref), (up_map_hbm, up_map_ref), (down_hbm, down_ref),
    )
    for index, (source, target) in enumerate(pairs):
        load = pltpu.make_async_copy(source, target, weight_sems.at[index])
        load.start()
        loads.append(load)
    _greet([("req", n_req), ("seq", n_seq)])
    share = staged0.shape[3]
    for kind in range(staged0.shape[1]):
        full_rows = x_ref[:, kind].reshape(staged0.shape[2], n_req * share)
        for part in range(n_req):
            staged0[part, kind] = full_rows[:, part * share : (part + 1) * share]
    for copy in _start_round("req", n_req, False, staged0, spread_ref, send0, recv0, local_sems.at[0]):
        copy.wait()
    for load in loads[:3]:
        load.wait()
    normed_all = spread_ref[:, 1].reshape(rows, spread_ref.shape[3])
    staged1[:, :, :units] = jnp.dot(
        normed_all, gate_ref[...], preferred_element_type=jnp.float32
    ).reshape(staged1.shape[0], staged1.shape[1], units)
    staged1[:, :, units : 2 * units] = jnp.dot(
        normed_all, up_ref[...], preferred_element_type=jnp.float32
    ).reshape(staged1.shape[0], staged1.shape[1], units)
    staged1[:, :, 2 * units :] = jnp.dot(
        normed_all, down_map_ref[...], preferred_element_type=jnp.float32
    ).reshape(staged1.shape[0], staged1.shape[1], staged1.shape[2] - 2 * units)
    for copy in _start_round("req", n_req, False, staged1, landed1, send1, recv1, local_sems.at[1]):
        copy.wait()
    for load in loads[3:5]:
        load.wait()
    total = _block_sum(landed1)
    low = total[:, 2 * units :].astype(jnp.bfloat16)
    gate_pre = total[:, :units] + jnp.dot(low, gate_map_ref[...], preferred_element_type=jnp.float32)
    up_part = total[:, units : 2 * units] + jnp.dot(
        low, up_map_ref[...], preferred_element_type=jnp.float32
    )
    staged2[...] = (gate_pre / (1.0 + jnp.exp(-gate_pre)) * up_part).astype(jnp.bfloat16)
    for copy in _start_round("req", n_req, True, staged2, landed2, send2, recv2, local_sems.at[2]):
        copy.wait()
    loads[5].wait()
    inner = landed2[...].reshape(rows, units)
    staged3[...] = jnp.dot(inner, down_ref[...], preferred_element_type=jnp.float32).reshape(
        staged3.shape
    )
    for copy in _start_round("seq", n_seq, False, staged3, landed3, send3, recv3, local_sems.at[3]):
        copy.wait()
    out_rows = landed3.shape[1]
    group_rows = spread_ref.shape[2]
    first_row = lax.axis_index("seq") * out_rows
    group_rows_all = spread_ref[first_row // group_rows, 0].astype(jnp.float32)
    chunk = (first_row % group_rows) // out_rows
    residual = group_rows_all[:out_rows]
    for index in range(1, group_rows // out_rows):
        piece = group_rows_all[index * out_rows : (index + 1) * out_rows]
        residual = jnp.where(chunk == index, piece, residual)
    out_ref[...] = (residual + _block_sum(landed3)).astype(out_ref.dtype)


def fused_mlp(both, gate_weight, up_weight, down_map, gate_map, up_map, down_weight, cid):
    n_req, n_seq = lax.axis_size("req"), lax.axis_size("seq")
    group_rows = both.shape[0]
    spread_shape = (n_req, both.shape[1], group_rows, both.shape[2] * both.shape[3] // n_req)
    rows = n_req * group_rows
    units = gate_weight.shape[1]
    wide = 2 * units + down_map.shape[1]
    out_rows = rows // n_seq
    vmem = pltpu.VMEM
    return pl.pallas_call(
        _mlp_kernel,
        out_shape=(
            jax.ShapeDtypeStruct((out_rows, down_weight.shape[1]), jnp.bfloat16),
            jax.ShapeDtypeStruct(spread_shape, both.dtype),
        ),
        in_specs=[pl.BlockSpec(memory_space=vmem)] + [pl.BlockSpec(memory_space=pl.ANY)] * 6,
        out_specs=(pl.BlockSpec(memory_space=vmem), pl.BlockSpec(memory_space=vmem)),
        scratch_shapes=[
            vmem((n_req, group_rows, wide), jnp.float32),
            vmem((n_req, group_rows, wide), jnp.float32),
            vmem((group_rows, units), jnp.bfloat16),
            vmem((n_req, group_rows, units), jnp.bfloat16),
            vmem((n_seq, out_rows, down_weight.shape[1]), jnp.float32),
            vmem((n_seq, out_rows, down_weight.shape[1]), jnp.float32),
            pltpu.SemaphoreType.DMA((n_req,)),
            pltpu.SemaphoreType.DMA((n_req,)),
            pltpu.SemaphoreType.DMA((n_req,)),
            pltpu.SemaphoreType.DMA((n_req,)),
            pltpu.SemaphoreType.DMA((n_req,)),
            pltpu.SemaphoreType.DMA((n_req,)),
            pltpu.SemaphoreType.DMA((n_seq,)),
            pltpu.SemaphoreType.DMA((n_seq,)),
            pltpu.SemaphoreType.DMA((4,)),
        ]
        + [
            vmem(weight.shape, weight.dtype)
            for weight in (gate_weight, up_weight, down_map, gate_map, up_map, down_weight)
        ]
        + [pltpu.SemaphoreType.DMA((6,)), vmem(spread_shape, both.dtype)],
        compiler_params=pltpu.CompilerParams(
            collective_id=cid, has_side_effects=True
        ),
    )(both, gate_weight, up_weight, down_map, gate_map, up_map, down_weight)


def _chain_kernel(spec, n_extra, pre, x_ref, *refs):
    extra_hbm = refs[:n_extra]
    y_ref = refs[n_extra]
    scratch = refs[n_extra + 1 :]
    count = len(spec)
    landed = list(scratch[: count - 1]) + [y_ref]
    staged = scratch[count - 1 : 2 * count - 2]
    extra = scratch[2 * count - 2 : 2 * count - 2 + n_extra]
    extra_sems = scratch[2 * count - 2 + n_extra]
    sems = scratch[2 * count - 1 + n_extra : len(scratch) - (pre is not None)]
    loads = []
    for index in range(n_extra):
        load = pltpu.make_async_copy(extra_hbm[index], extra[index], extra_sems.at[index])
        load.start()
        loads.append(load)
    if pre is not None:
        for load in loads:
            load.wait()
        loads = []
        scratch[-1][...] = pre(x_ref, *extra)
        x_ref = scratch[-1]
    axes = []
    for axis, n, _, _ in spec:
        if (axis, n) not in axes:
            axes.append((axis, n))
    _greet(axes)
    source = x_ref
    for k, (axis, n, gather, mid) in enumerate(spec):
        copies = _start_round(
            axis, n, gather, source, landed[k], sems[2 * k], sems[2 * k + 1], sems[-1].at[k]
        )
        for copy in copies:
            copy.wait()
        if k == 0:
            for load in loads:
                load.wait()
        if mid is not None:
            staged[k][...] = mid(landed[k], *extra)
            source = staged[k]


def chain(x, rounds, cid, extra=(), pre=None):
    spec, landed_shapes, staged_shapes = [], [], []
    block = (x.shape, x.dtype)
    for index, (axis, gather, mid, made) in enumerate(rounds):
        n = lax.axis_size(axis)
        shape, dtype = block
        landed = ((n,) + shape if gather else shape, dtype)
        spec.append((axis, n, gather, mid))
        if index < len(rounds) - 1:
            landed_shapes.append(landed)
            staged_shapes.append(made)
            block = made
        else:
            out = landed
    sizes = [n for _, n, _, _ in spec]
    semaphores = []
    for n in sizes:
        semaphores += [pltpu.SemaphoreType.DMA((n,)), pltpu.SemaphoreType.DMA((n,))]
    return pl.pallas_call(
        functools.partial(_chain_kernel, spec, len(extra), pre),
        out_shape=jax.ShapeDtypeStruct(*out),
        in_specs=[pl.BlockSpec(memory_space=pltpu.VMEM)]
        + [pl.BlockSpec(memory_space=pl.ANY)] * len(extra),
        out_specs=pl.BlockSpec(memory_space=pltpu.VMEM),
        scratch_shapes=[pltpu.VMEM(*item) for item in landed_shapes]
        + [pltpu.VMEM(*item) for item in staged_shapes]
        + [pltpu.VMEM(item.shape, item.dtype) for item in extra]
        + [pltpu.SemaphoreType.DMA((max(len(extra), 1),))]
        + semaphores
        + [pltpu.SemaphoreType.DMA((len(spec),))]
        + ([pltpu.VMEM(x.shape, x.dtype)] if pre is not None else []),
        compiler_params=pltpu.CompilerParams(
            collective_id=cid, has_side_effects=True
        ),
    )(x, *extra)


def merged_2(array, axis, combine):
    everything = jax.tree.map(lambda part: lax.all_gather(part, axis), array)
    first = jax.tree.map(lambda part: part[0], everything)

    def hop(k, so_far):
        return combine(so_far, jax.tree.map(lambda part: part[k], everything))

    return lax.fori_loop(1, lax.axis_size(axis), hop, first)


def rms_norm(matrix, gain_vec):
    widened = matrix.astype(jnp.float32)
    factor = lax.rsqrt(jnp.mean(widened * widened, axis=-1, keepdims=True) + EPSILON)
    return (widened * factor * gain_vec.astype(jnp.float32)).astype(jnp.bfloat16)


def rotate(vectors, positions):
    half_dim = vectors.shape[-1] // 2
    frequency = ROTARY_BASE ** (-2.0 * jnp.arange(half_dim, dtype=jnp.float32) / vectors.shape[-1])
    angles = positions.astype(jnp.float32)[..., None, None] * frequency
    cosine = jnp.cos(angles)
    sine_part = jnp.sin(angles)
    front_half = vectors[..., :half_dim]
    back_half = vectors[..., half_dim:]
    return jnp.concatenate(
        [front_half * cosine - back_half * sine_part, back_half * cosine + front_half * sine_part],
        axis=-1,
    )


def softmax_join(earlier, later):
    first_max, first_sum, first_out = earlier
    second_max, second_sum, second_out = later
    overall = jnp.maximum(first_max, second_max)
    first_factor = jnp.exp(first_max - overall)
    second_factor = jnp.exp(second_max - overall)
    return (
        overall,
        first_sum * first_factor + second_sum * second_factor,
        first_out * first_factor[..., None] + second_out * second_factor[..., None],
    )


def body(
    given_token_index,
    hidden,
    token_embedding_table,
    attention_norm_gain,
    query_key_value_weight,
    rotated_key_cache,
    cached_value_pages,
    lengths,
    request_page_slots,
    attention_output_weight,
    feedforward_norm_gain,
    gate_weight,
    up_weight,
    adapter_down_map,
    adapter_gate_map,
    adapter_up_map,
    down_weight,
):
    seq_devices = lax.axis_size("seq")
    req_devices = lax.axis_size("req")
    seq_index = lax.axis_index("seq")
    req_index = lax.axis_index("req")
    group_rows = hidden.shape[0]
    requests = lengths.shape[0]
    steps_each = group_rows // requests
    vocab_rows = token_embedding_table.shape[0]
    first_id = (seq_index * req_devices + req_index) * vocab_rows
    local_ids = given_token_index - first_id
    present = (local_ids >= 0) & (local_ids < vocab_rows)
    looked = jnp.take(token_embedding_table, jnp.clip(local_ids, 0, vocab_rows - 1), axis=0)
    looked = jnp.where(present[:, None], looked, jnp.zeros((), looked.dtype))
    row_share = group_rows // seq_devices
    lanes = 128
    by_group = looked.reshape(req_devices, seq_devices, row_share * looked.shape[1] // lanes, lanes)
    row_parts = two_rounds(
        by_group,
        ("req", False),
        ("seq", False),
        lambda landed: _block_sum(landed).astype(jnp.bfloat16),
        by_group.shape[1:],
        jnp.bfloat16,
        10,
    )
    embedded_rows = (
        jnp.sum(row_parts.astype(jnp.float32), axis=0)
        .astype(jnp.bfloat16)
        .reshape(row_share, looked.shape[1])
    )
    own_hidden = lax.dynamic_slice_in_dim(hidden, seq_index * row_share, row_share, 0)
    own_rows = jnp.concatenate([own_hidden, embedded_rows], axis=1)
    model_width = own_rows.shape[1]
    width_share = model_width // req_devices

    def normalize(joined_tiles, weight, gain):
        widened = joined_tiles[...].astype(jnp.float32)
        factor = lax.rsqrt(jnp.sum(widened * widened) / model_width + EPSILON)
        return (widened * factor * gain[...].astype(jnp.float32)).astype(jnp.bfloat16)

    def to_owners(landed, weight, gain):
        rows = landed[...].reshape(group_rows, model_width)
        return jnp.stack(
            [rows[:, part * width_share : (part + 1) * width_share] for part in range(req_devices)]
        )

    qkv_cols = query_key_value_weight.shape[1]

    def project(landed, weight, gain):
        flat = landed[...].reshape(req_devices * group_rows, width_share)
        product = jnp.dot(flat, weight[...], preferred_element_type=jnp.float32)
        return product.reshape(req_devices, group_rows, qkv_cols)

    qkv_all = chain(
        own_rows.reshape(-1, lanes),
        [
            ("seq", True, to_owners, ((req_devices, group_rows, width_share), jnp.bfloat16)),
            ("req", False, project, ((req_devices, group_rows, qkv_cols), jnp.float32)),
            (
                "req",
                False,
                lambda landed, weight, gain: _block_sum(landed).astype(jnp.bfloat16),
                ((group_rows, qkv_cols), jnp.bfloat16),
            ),
            ("seq", True, None, None),
        ],
        4,
        extra=(query_key_value_weight, attention_norm_gain.reshape(-1, lanes)),
        pre=normalize,
    )
    projected = jnp.transpose(qkv_all, (1, 0, 2)).reshape(group_rows, seq_devices * qkv_all.shape[2])
    head_cols = HEADS * HD
    queries = projected[:, :head_cols].reshape(requests, steps_each, HEADS, HD)
    new_keys = projected[:, head_cols : 2 * head_cols].reshape(requests, steps_each, HEADS, HD)
    new_values = projected[:, 2 * head_cols :].reshape(requests, steps_each, HEADS, HD)
    positions = lengths[:, None] + jnp.arange(steps_each, dtype=jnp.int32)[None, :]
    queries = rotate(queries.astype(jnp.float32), positions).astype(jnp.bfloat16)
    new_keys = rotate(new_keys.astype(jnp.float32), positions).astype(jnp.bfloat16)
    slots = rotated_key_cache.shape[0]
    page_len = rotated_key_cache.shape[2]
    cache_k = rotated_key_cache.reshape(slots * page_len, head_cols)
    cache_v = cached_value_pages.reshape(slots * page_len, head_cols)
    slot_ids = seq_index * slots + jnp.arange(slots, dtype=jnp.int32)
    page_ids = jnp.arange(request_page_slots.shape[1], dtype=jnp.int32)
    is_live = page_ids[None, :] < ((lengths + page_len - 1) // page_len)[:, None]
    matches = (request_page_slots[:, :, None] == slot_ids[None, None, :]) & is_live[:, :, None]
    is_owned = jnp.any(matches, axis=1)
    page_of = jnp.sum(jnp.where(matches, page_ids[None, :, None], 0), axis=1)
    token_pos = (
        page_of[:, :, None] * page_len + jnp.arange(page_len, dtype=jnp.int32)[None, None, :]
    )
    is_valid = (is_owned[:, :, None] & (token_pos < lengths[:, None, None])).reshape(
        requests, slots * page_len
    )
    score_scale = 1.0 / math.sqrt(HD)
    head_mask = (jnp.arange(head_cols, dtype=jnp.int32)[None, :] // HD) == jnp.arange(
        HEADS, dtype=jnp.int32
    )[:, None]
    query_rows = queries.reshape(group_rows, head_cols)
    spread_queries = jnp.where(head_mask[None], query_rows[:, None, :], jnp.zeros((), jnp.bfloat16))
    scores = (
        jnp.dot(
            spread_queries.reshape(group_rows * HEADS, head_cols),
            cache_k.T,
            preferred_element_type=jnp.float32,
        )
        * score_scale
    ).reshape(requests, steps_each, HEADS, slots * page_len)
    mask_b = is_valid[:, None, None, :]
    local_max = jnp.max(jnp.where(mask_b, scores, NEGATIVE), axis=-1)
    weights = jnp.where(mask_b, jnp.exp(scores - local_max[..., None]), 0.0)
    local_sum = jnp.sum(weights, axis=-1)
    spread_out = jnp.dot(
        weights.astype(jnp.bfloat16).reshape(group_rows * HEADS, slots * page_len),
        cache_v,
        preferred_element_type=jnp.float32,
    ).reshape(group_rows, HEADS, head_cols)
    local_out = jnp.sum(jnp.where(head_mask[None], spread_out, 0.0), axis=1).reshape(
        requests, steps_each, HEADS, HD
    )
    fresh_scores = (
        jnp.einsum("rthd,rshd->rths", queries, new_keys, preferred_element_type=jnp.float32)
        * score_scale
    )
    causal = jnp.arange(steps_each)[:, None] >= jnp.arange(steps_each)[None, :]
    fresh_mask = causal[None, :, None, :]
    fresh_max = jnp.max(jnp.where(fresh_mask, fresh_scores, NEGATIVE), axis=-1)
    fresh_w = jnp.where(fresh_mask, jnp.exp(fresh_scores - fresh_max[..., None]), 0.0)
    fresh_sum = jnp.sum(fresh_w, axis=-1)
    fresh_out = jnp.einsum(
        "rths,rshd->rthd",
        fresh_w.astype(jnp.bfloat16),
        new_values,
        preferred_element_type=jnp.float32,
    )
    own_heads = HEADS // seq_devices
    first_head = seq_index * own_heads

    def own_slice(member):
        return lax.dynamic_slice_in_dim(member, first_head, own_heads, 2)

    pad_cols = 256 - HD - 2
    packed = jnp.concatenate(
        [
            local_out,
            local_max[..., None],
            local_sum[..., None],
            jnp.zeros(local_out.shape[:-1] + (pad_cols,), jnp.float32),
        ],
        axis=-1,
    )
    packed = packed.reshape(requests * steps_each, seq_devices, own_heads, 256)
    packed = jnp.transpose(packed, (1, 0, 2, 3)).reshape(seq_devices, group_rows * own_heads, 256)
    model_width = attention_output_weight.shape[1]
    head_rows = group_rows * own_heads
    tile_rows = row_share * model_width // lanes

    def merge_and_project(landed, fresh_max_ref, fresh_sum_ref, fresh_out_ref, weight, own, gain):
        part_o = landed[:, :, :HD]
        part_m = landed[:, :, HD : HD + 1]
        part_l = landed[:, :, HD + 1 : HD + 2]
        f_max = fresh_max_ref[...]
        overall = jnp.maximum(jnp.max(part_m, axis=0), f_max)
        part_factor = jnp.exp(part_m - overall[None])
        fresh_factor = jnp.exp(f_max - overall)
        denominator = jnp.sum(part_l * part_factor, axis=0) + fresh_sum_ref[...] * fresh_factor
        numerator = jnp.sum(part_o * part_factor, axis=0) + fresh_out_ref[...] * fresh_factor
        attention = (numerator / denominator).astype(jnp.bfloat16).reshape(
            group_rows, own_heads * HD
        )
        product = jnp.dot(attention, weight[...], preferred_element_type=jnp.float32)
        return product.reshape(seq_devices, tile_rows, lanes)

    def add_residual(landed, fresh_max_ref, fresh_sum_ref, fresh_out_ref, weight, own, gain):
        after = (own[...].astype(jnp.float32) + _block_sum(landed)).astype(jnp.bfloat16)
        widened = after.astype(jnp.float32)
        factor = lax.rsqrt(jnp.sum(widened * widened) / model_width + EPSILON)
        normed_two = (widened * factor * gain[...].astype(jnp.float32)).astype(jnp.bfloat16)
        return jnp.stack([after, normed_two])

    both_rows = chain(
        packed,
        [
            ("seq", False, merge_and_project, ((seq_devices, tile_rows, lanes), jnp.float32)),
            ("seq", False, add_residual, ((2, tile_rows, lanes), jnp.bfloat16)),
            ("seq", True, None, None),
        ],
        1,
        extra=(
            own_slice(fresh_max).reshape(head_rows, 1),
            own_slice(fresh_sum).reshape(head_rows, 1),
            own_slice(fresh_out).reshape(head_rows, HD),
            attention_output_weight,
            own_rows.reshape(tile_rows, lanes),
            feedforward_norm_gain.reshape(tile_rows, lanes),
        ),
    )
    block_out, _ = fused_mlp(
        both_rows, gate_weight, up_weight, adapter_down_map, adapter_gate_map, adapter_up_map, down_weight, 7
    )
    return block_out


def solution(mesh):
    placed = (
        P(),
        P("req", None),
        P(("seq", "req"), None),
        P(),
        P("req", "seq"),
        P("seq", "req", None, None),
        P("seq", "req", None, None),
        P("req"),
        P("req", None),
        P("seq", None),
        P(),
        P("req", "seq"),
        P("req", "seq"),
        P("req", None),
        P(None, "seq"),
        P(None, "seq"),
        P("seq", "req"),
    )
    return jax.shard_map(
        body, mesh=mesh, in_specs=placed, out_specs=P("seq", "req"), check_vma=False
    )
```
